32 devices in a mesh: group: 4 (over z), replica: 8 (over y, x, core).
Axes of the slice: x: 2, y: 2, z: 4, core: 2. Of those that a mesh axis runs over, the one named last changes fastest.
Arguments:
- tokens: bfloat16 [16, 1024, 1024], P('replica', 'group'), may hold values from -6 to 6
- cotangent: bfloat16 [16, 1024, 1024], P('replica', 'group'), may hold values from -6 to 6
- slot_order: int32 [16, 4], P('replica'), may hold values from 0 to 3, each once within a row
- attn_gain: bfloat16 [1024], P('group'), may hold values from 0.5 to 1.5
- q_gain: bfloat16 [128], replicated, may hold values from 0.5 to 1.5
- k_gain: bfloat16 [128], replicated, may hold values from 0.5 to 1.5
- w_qkv: bfloat16 [1024, 4096], P('group'), may hold values from -0.1875 to 0.1875
- w_out: bfloat16 [2048, 1024], P('group'), may hold values from -0.75 to 0.75
- mlp_gain: bfloat16 [1024], P('group'), may hold values from 0.5 to 1.5
- w_gate_up: bfloat16 [1024, 6144], P('group'), may hold values from -0.1875 to 0.1875
- w_down: bfloat16 [3072, 1024], P('group'), may hold values from -0.109375 to 0.109375
Outputs:
- block_out: bfloat16 [16, 1024, 1024], P('replica', 'group')
- input_grad: bfloat16 [16, 1024, 1024], P('replica', 'group')
- attn_gain_grad: float32 [1024], P('group')
- q_gain_grad: float32 [128], replicated
- k_gain_grad: float32 [128], replicated
- qkv_grad: float32 [1024, 4096], P('group')
- out_grad: float32 [2048, 1024], P('group')
- mlp_gain_grad: float32 [1024], P('group')
- gate_up_grad: float32 [1024, 6144], P('group')
- down_grad: float32 [3072, 1024], P('group')
The draws below stay inside these ranges and needn't reach their ends.
Inputs may be any that keep to these rules, and one draw needn't show every extreme that they name: Each row of slot_order names every block of 256 positions of a sequence exactly once.
All inputs are finite; a program needn't handle non-finite values.
Results may differ from the reference program's by a relative error of at most 0.02.
Values may be sent and summed in bfloat16 or wider, within the bound.
A program may use at most 256 MiB of HBM per device.

```python
import math
import jax
import jax.numpy as jnp
from jax import lax

D = 1024
HEADS = 16
KV_HEADS = 8
HD = 128
FF = 3072
LENGTH = 1024
QKV = 4096
SLOT_LEN = 256
SEQS = 16
N_GROUP = 4


def block_scale(rng, extent, cuts, smallest, high):
    loudness, own = 1.0, jax.random.fold_in(rng, 6)
    for axis_at, parts in cuts:
        steps = jnp.exp(jax.random.uniform(jax.random.fold_in(own, axis_at), (parts,), jnp.float32, smallest / len(cuts), high / len(cuts)))
        loudness = loudness * jnp.repeat(steps, extent[axis_at] // parts).reshape([-1 if axis == axis_at else 1 for axis in range(len(extent))])
    return loudness


def scatter_about(rng, dims, scale, reach, cuts=(), held_as=jnp.bfloat16):
    loudness = block_scale(rng, dims, cuts, -0.22, 0.18) if cuts else 1.0
    entries = jax.random.normal(rng, dims, jnp.float32) * scale * loudness
    return jnp.minimum(jnp.maximum(entries, -reach), reach).astype(held_as)


def setup_inputs(seed: int = 0) -> dict:
    seeds = jax.random.split(jax.random.key(seed), 12)
    tokens = scatter_about(seeds[0], (SEQS, LENGTH, D), 1.0, 6.0, ((0, 8), (1, 4)))
    cotangent = scatter_about(seeds[1], (SEQS, LENGTH, D), 1.0, 6.0, ((0, 8), (1, 4)))
    slot_order = jax.vmap(lambda own: jax.random.permutation(own, N_GROUP))(jax.random.split(seeds[2], SEQS)).reshape((SEQS, N_GROUP)).astype(jnp.int32)
    attn_gain = jnp.clip(1.0 + 0.1 * jax.random.normal(seeds[3], (D,), jnp.float32), 0.5, 1.5).astype(jnp.bfloat16)
    q_gain = jnp.clip(1.0 + 0.1 * jax.random.normal(seeds[4], (HD,), jnp.float32), 0.5, 1.5).astype(jnp.bfloat16)
    k_gain = jnp.clip(1.0 + 0.1 * jax.random.normal(seeds[5], (HD,), jnp.float32), 0.5, 1.5).astype(jnp.bfloat16)
    w_qkv = scatter_about(seeds[6], (D, QKV), D ** -0.5, 0.1875, ((0, 4),))
    w_out = scatter_about(seeds[7], (HEADS * HD, D), (HEADS * HD // 32) ** -0.5, 0.75, ((0, 4),))
    mlp_gain = jnp.clip(1.0 + 0.1 * jax.random.normal(seeds[8], (D,), jnp.float32), 0.5, 1.5).astype(jnp.bfloat16)
    w_gate_up = scatter_about(seeds[9], (D, 2 * FF), D ** -0.5, 0.1875, ((0, 4),))
    w_down = scatter_about(seeds[10], (FF, D), FF ** -0.5, 0.109375, ((0, 4),))
    return dict(tokens=tokens, cotangent=cotangent, slot_order=slot_order, attn_gain=attn_gain, q_gain=q_gain, k_gain=k_gain, w_qkv=w_qkv, w_out=w_out, mlp_gain=mlp_gain, w_gate_up=w_gate_up, w_down=w_down)


EPSILON = 1e-06
THETA_BASE = 1000000.0
MASKED = -1e+30

@jax.custom_vjp
def low(v):
    return lax.optimization_barrier(v.astype(jnp.bfloat16)).astype(jnp.float32)

@jax.custom_vjp
def low_back(v):
    return v

def low_keep(v):
    return (low(v), None)

def low_pass(kept, grad):
    return (grad,)

def back_keep(v):
    return (v, None)

def back_low(kept, grad):
    return (low(grad),)
low.defvjp(low_keep, low_pass)
low_back.defvjp(back_keep, back_low)

def exact_dot(a, b):
    return jnp.dot(a, b, precision=lax.Precision.HIGHEST, preferred_element_type=jnp.float32)

def norm_rows(v):
    return v * lax.rsqrt(lax.optimization_barrier(jnp.mean(v * v, axis=-1, keepdims=True)) + EPSILON)

def rotate(v, cosines, sines):
    half_size = v.shape[-1] // 2
    leading = v[..., :half_size]
    trailing = v[..., half_size:]
    return jnp.concatenate([leading * cosines - trailing * sines, trailing * cosines + leading * sines], axis=-1)

def rope_tables(positions):
    half_size = HD // 2
    counter = jnp.arange(half_size).astype(jnp.float32)
    frequency = THETA_BASE ** (-2.0 * counter / HD)
    angles = positions.astype(jnp.float32)[:, None] * frequency[None, :]
    return (jnp.cos(angles), jnp.sin(angles))

def attend(query_rot, key_rot, values_low, positions):
    length = query_rot.shape[0]
    block_rows = math.gcd(length, 512)
    groups = HEADS // KV_HEADS
    score_scale = 1.0 / math.sqrt(HD)
    key_heads = key_rot.reshape(length, KV_HEADS, HD)
    value_heads = values_low.reshape(length, KV_HEADS, HD)

    def one_block(block_item):
        query_block, query_pos = block_item
        query_heads = query_block.reshape(block_rows, KV_HEADS, groups, HD)
        scores = jnp.einsum('qkgd,skd->kgqs', query_heads, key_heads, precision=lax.Precision.HIGHEST)
        scores = low_back(scores * score_scale)
        allowed = positions[None, :] <= query_pos[:, None]
        scores = jnp.where(allowed[None, None], scores, MASKED)
        probabilities = jax.nn.softmax(scores, axis=-1)
        combined = jnp.einsum('kgqs,skd->qkgd', low(probabilities), value_heads, precision=lax.Precision.HIGHEST)
        return combined.reshape(block_rows, HEADS * HD)
    blocks = lax.map(jax.checkpoint(one_block), (query_rot.reshape(length // block_rows, block_rows, HEADS * HD), positions.reshape(length // block_rows, block_rows)))
    return blocks.reshape(length, HEADS * HD)

def block_layer(source, positions, attn_gain, q_gain, k_gain, w_qkv, w_out, mlp_gain, w_gate_up, w_down):
    length = source.shape[0]
    q_width = HEADS * HD
    kv_width = KV_HEADS * HD
    cosines, sines = rope_tables(positions)
    first_low = low(norm_rows(source) * attn_gain)
    qkv = low_back(exact_dot(first_low, w_qkv))
    queries = qkv[:, :q_width].reshape(length, HEADS, HD)
    keys_raw = qkv[:, q_width:q_width + kv_width].reshape(length, KV_HEADS, HD)
    values_raw = qkv[:, q_width + kv_width:]
    query_rot = low(rotate(norm_rows(queries) * q_gain, cosines[:, None, :], sines[:, None, :]))
    key_rot = low(rotate(norm_rows(keys_raw) * k_gain, cosines[:, None, :], sines[:, None, :]))
    attn = attend(query_rot.reshape(length, q_width), key_rot.reshape(length, kv_width), low(values_raw), positions)
    attended = low(low_back(attn))
    middle = source + low_back(exact_dot(attended, w_out))
    second_low = low(norm_rows(middle) * mlp_gain)
    gate_up = low_back(exact_dot(second_low, w_gate_up))
    gate_part = gate_up[:, :FF]
    up_part = gate_up[:, FF:]
    hidden = low(jax.nn.silu(gate_part) * up_part)
    return middle + low_back(exact_dot(hidden, w_down))

def reference(tokens, cotangent, slot_order, attn_gain, q_gain, k_gain, w_qkv, w_out, mlp_gain, w_gate_up, w_down):
    params = tuple((p.astype(jnp.float32) for p in (attn_gain, q_gain, k_gain, w_qkv, w_out, mlp_gain, w_gate_up, w_down)))
    offsets = jnp.arange(SLOT_LEN).astype(jnp.int32)

    def advance(totals, sample):
        source, grad_output, slots = sample
        positions = (slots[:, None].astype(jnp.int32) * SLOT_LEN + offsets[None, :]).reshape(-1).astype(jnp.int32)

        def forward(source_in, *weights):
            return block_layer(source_in, positions, *weights)
        output, pullback = jax.vjp(forward, source.astype(jnp.float32), *params)
        gradients = pullback(grad_output.astype(jnp.float32))
        totals = tuple((a + b for a, b in zip(totals, gradients[1:])))
        return (totals, (output.astype(jnp.bfloat16), gradients[0].astype(jnp.bfloat16)))
    initial = tuple((jnp.zeros(p.shape, jnp.float32) for p in params))
    totals, (results, input_back) = lax.scan(advance, initial, (tokens, cotangent, slot_order))
    return (results, input_back, totals[0], totals[1], totals[2], totals[3], totals[4], totals[5], totals[6], totals[7])
```

```python
import functools
import math

import jax
import jax.numpy as jnp
from jax import lax
from jax.experimental import pallas as pl
from jax.experimental.pallas import tpu as pltpu
from jax.sharding import Mesh
from jax.sharding import PartitionSpec as P

HEADS = 16
KV_HEADS = 8
HD = 128
FF = 3072


EPSILON = 1e-06
THETA_BASE = 1000000.0
MASKED = -1e30


def norm_rows(v):
    return v * lax.rsqrt(jnp.mean(v * v, axis=-1, keepdims=True) + EPSILON)


def norm_back(source, grad):
    inverse = lax.rsqrt(jnp.mean(source * source, axis=-1, keepdims=True) + EPSILON)
    normed = source * inverse
    return inverse * (grad - normed * jnp.mean(grad * normed, axis=-1, keepdims=True))


def rotate(v, cosines, sines):
    half_size = v.shape[-1] // 2
    leading = v[..., :half_size]
    trailing = v[..., half_size:]
    return jnp.concatenate(
        [leading * cosines - trailing * sines, trailing * cosines + leading * sines], axis=-1
    )


def rope_tables(positions):
    half_size = HD // 2
    counter = jnp.arange(half_size).astype(jnp.float32)
    frequency = THETA_BASE ** (-2.0 * counter / HD)
    angles = positions.astype(jnp.float32)[:, None] * frequency[None, :]
    return (jnp.cos(angles), jnp.sin(angles))


def matmul(a, b):
    return jnp.dot(a, b, preferred_element_type=jnp.float32)


def matmul_right(a, b):
    return lax.dot_general(a, b, (((1,), (1,)), ((), ())), preferred_element_type=jnp.float32)


def matmul_left(a, b):
    return lax.dot_general(a, b, (((0,), (0,)), ((), ())), preferred_element_type=jnp.float32)


def per_device(
    tokens,
    cotangent,
    slot_order,
    attn_gain,
    q_gain,
    k_gain,
    w_qkv,
    w_out,
    mlp_gain,
    w_gate_up,
    w_down,
):
    member_count = lax.axis_size("group")
    member = lax.axis_index("group")
    micro, slot_len, width = tokens.shape
    rows = micro * slot_len
    length = slot_len * member_count
    q_width = HEADS * HD
    kv_width = KV_HEADS * HD
    groups = HEADS // KV_HEADS
    score_scale = 1.0 / math.sqrt(HD)
    key_block = math.gcd(length, 512)
    block_count = length // key_block
    head_gain_q = q_gain.astype(jnp.float32)
    head_gain_k = k_gain.astype(jnp.float32)
    offsets = jnp.arange(slot_len, dtype=jnp.int32)
    source = tokens.reshape(rows, width).astype(jnp.float32)
    all_pos = (slot_order[:, :, None] * slot_len + offsets[None, None, :]).reshape(micro, length)
    my_pos = lax.dynamic_slice_in_dim(all_pos, member * slot_len, slot_len, 1)
    query_top = jnp.max(my_pos, axis=1)
    cosines, sines = rope_tables(my_pos.reshape(rows))
    normed_first = norm_rows(source)
    gain_piece = lax.all_gather(attn_gain, "group", axis=0, tiled=True)
    weight_piece = lax.all_gather(w_qkv, "group", axis=0, tiled=True)
    columns = normed_first
    low_cols = (columns * gain_piece.astype(jnp.float32)).astype(jnp.bfloat16)
    qkv = matmul(low_cols, weight_piece)
    first_low = low_cols
    gain_first = gain_piece.astype(jnp.float32)
    queries = qkv[:, :q_width].reshape(rows, HEADS, HD)
    keys_raw = qkv[:, q_width : q_width + kv_width].reshape(rows, KV_HEADS, HD)
    values_low = qkv[:, q_width + kv_width :].astype(jnp.bfloat16)
    queries_normed = norm_rows(queries)
    keys_normed = norm_rows(keys_raw)
    query_rot = rotate(queries_normed * head_gain_q, cosines[:, None, :], sines[:, None, :]).astype(
        jnp.bfloat16
    )
    key_rot = rotate(keys_normed * head_gain_k, cosines[:, None, :], sines[:, None, :]).astype(
        jnp.bfloat16
    )
    key_all, value_all = (
        lax.all_gather(key_rot.reshape(micro, slot_len, kv_width), "group", axis=1, tiled=True),
        lax.all_gather(values_low.reshape(micro, slot_len, kv_width), "group", axis=1, tiled=True),
    )
    query_heads = query_rot.reshape(micro, slot_len, KV_HEADS, groups, HD)

    def block_live(block_index):
        key_pos = lax.dynamic_slice_in_dim(all_pos, block_index * key_block, key_block, 1)
        return jnp.any(jnp.min(key_pos, axis=1) <= query_top)

    def block_scores(block_index):
        begin = block_index * key_block
        key_piece = lax.dynamic_slice_in_dim(key_all, begin, key_block, 1).reshape(
            micro, key_block, KV_HEADS, HD
        )
        key_pos = lax.dynamic_slice_in_dim(all_pos, begin, key_block, 1)
        raw = (
            jnp.einsum(
                "mqkgd,mskd->mkgqs", query_heads, key_piece, preferred_element_type=jnp.float32
            )
            * score_scale
        )
        allowed = (key_pos[:, None, :] <= my_pos[:, :, None])[:, None, None]
        return (jnp.where(allowed, raw, MASKED), allowed, key_piece)

    def stats_step(block_index, carry):

        def stats_visit_block(carry_in):
            top_in, total_in = carry_in
            scores, allowed, key_piece = block_scores(block_index)
            new_top = jnp.maximum(top_in, jnp.max(scores, axis=-1))
            summed = jnp.sum(jnp.where(allowed, jnp.exp(scores - new_top[..., None]), 0.0), axis=-1)
            return (new_top, total_in * jnp.exp(top_in - new_top) + summed)

        return lax.cond(
            block_live(block_index), stats_visit_block, lambda carry_in: carry_in, carry
        )

    stat_shape = (micro, KV_HEADS, groups, slot_len)
    top_final, total_final = lax.fori_loop(
        0,
        block_count,
        stats_step,
        (jnp.full(stat_shape, MASKED, jnp.float32), jnp.zeros(stat_shape, jnp.float32)),
    )
    log_total = top_final + jnp.log(total_final)

    def output_step(block_index, accum):

        def output_visit_block(accum_in):
            scores, allowed, key_piece = block_scores(block_index)
            probabilities = jnp.where(allowed, jnp.exp(scores - log_total[..., None]), 0.0)
            value_piece = lax.dynamic_slice_in_dim(
                value_all, block_index * key_block, key_block, 1
            ).reshape(micro, key_block, KV_HEADS, HD)
            return accum_in + jnp.einsum(
                "mkgqs,mskd->mqkgd",
                probabilities.astype(jnp.bfloat16),
                value_piece,
                preferred_element_type=jnp.float32,
            )

        return lax.cond(
            block_live(block_index), output_visit_block, lambda accum_in: accum_in, accum
        )

    attn_heads = lax.fori_loop(
        0, block_count, output_step, jnp.zeros((micro, slot_len, KV_HEADS, groups, HD), jnp.float32)
    )
    attended = attn_heads.reshape(rows, q_width).astype(jnp.bfloat16)
    columns = attended
    branch = matmul(columns, lax.all_gather(w_out, "group", axis=0, tiled=True))
    middle = source + branch
    normed_second = norm_rows(middle)
    gain_piece = lax.all_gather(mlp_gain, "group", axis=0, tiled=True)
    weight_piece = lax.all_gather(w_gate_up, "group", axis=0, tiled=True)
    columns = normed_second
    low_cols = (columns * gain_piece.astype(jnp.float32)).astype(jnp.bfloat16)
    gate_up = matmul(low_cols, weight_piece)
    gain_second = gain_piece.astype(jnp.float32)
    gate_part = gate_up[:, :FF]
    up_part = gate_up[:, FF:]
    sigmoid_gate = jax.nn.sigmoid(gate_part)
    silu_gate = gate_part * sigmoid_gate
    hidden = (silu_gate * up_part).astype(jnp.bfloat16)
    columns = hidden
    down_out = matmul(columns, lax.all_gather(w_down, "group", axis=0, tiled=True))
    block_out = (middle + down_out).astype(jnp.bfloat16).reshape(micro, slot_len, width)
    grad_low = cotangent.reshape(rows, width)
    grad_output = grad_low.astype(jnp.float32)
    down_full = matmul_left(hidden, grad_low)
    grad_hidden = matmul_right(grad_low, lax.all_gather(w_down, "group", axis=0, tiled=True))
    grad_gate = grad_hidden * up_part * (sigmoid_gate * (1.0 + gate_part * (1.0 - sigmoid_gate)))
    grad_upper = grad_hidden * silu_gate
    grad_gate_up = jnp.concatenate([grad_gate, grad_upper], axis=1).astype(jnp.bfloat16)
    gate_up_full = matmul_left(low_cols, grad_gate_up)
    grad_second = matmul_right(grad_gate_up, lax.all_gather(w_gate_up, "group", axis=0, tiled=True))
    gain_second_full = jnp.sum(normed_second * grad_second, axis=0)
    grad_middle = grad_output + norm_back(middle, grad_second * gain_second)
    grad_mid_low = grad_middle.astype(jnp.bfloat16)
    out_full = matmul_left(attended, grad_mid_low)
    grad_attn_full = matmul_right(grad_mid_low, lax.all_gather(w_out, "group", axis=0, tiled=True))
    grad_attn = grad_attn_full.astype(jnp.bfloat16)
    grad_heads = grad_attn.reshape(micro, slot_len, KV_HEADS, groups, HD)
    delta = jnp.transpose(
        jnp.sum(grad_heads.astype(jnp.float32) * attn_heads, axis=-1), (0, 2, 3, 1)
    )

    def back_step(block_index, carry):

        def back_visit_block(carry_in):
            grad_query_in, grad_key_in, grad_value_in = carry_in
            begin = block_index * key_block
            scores, allowed, key_piece = block_scores(block_index)
            probabilities = jnp.where(allowed, jnp.exp(scores - log_total[..., None]), 0.0)
            value_piece = lax.dynamic_slice_in_dim(value_all, begin, key_block, 1).reshape(
                micro, key_block, KV_HEADS, HD
            )
            grad_probs = jnp.einsum(
                "mqkgd,mskd->mkgqs", grad_heads, value_piece, preferred_element_type=jnp.float32
            )
            grad_scores = (probabilities * (grad_probs - delta[..., None])).astype(jnp.bfloat16)
            grad_query_out = (
                grad_query_in
                + jnp.einsum(
                    "mkgqs,mskd->mqkgd", grad_scores, key_piece, preferred_element_type=jnp.float32
                )
                * score_scale
            )
            key_term = (
                jnp.einsum(
                    "mkgqs,mqkgd->mskd",
                    grad_scores,
                    query_heads,
                    preferred_element_type=jnp.float32,
                )
                * score_scale
            )
            value_term = jnp.einsum(
                "mkgqs,mqkgd->mskd",
                probabilities.astype(jnp.bfloat16),
                grad_heads,
                preferred_element_type=jnp.float32,
            )
            key_old = lax.dynamic_slice_in_dim(grad_key_in, begin, key_block, 1)
            value_old = lax.dynamic_slice_in_dim(grad_value_in, begin, key_block, 1)
            grad_key_out = lax.dynamic_update_slice_in_dim(
                grad_key_in, key_old + key_term, begin, 1
            )
            grad_value_out = lax.dynamic_update_slice_in_dim(
                grad_value_in, value_old + value_term, begin, 1
            )
            return (grad_query_out, grad_key_out, grad_value_out)

        return lax.cond(block_live(block_index), back_visit_block, lambda carry_in: carry_in, carry)

    back_start = (
        jnp.zeros((micro, slot_len, KV_HEADS, groups, HD), jnp.float32),
        jnp.zeros((micro, length, KV_HEADS, HD), jnp.float32),
        jnp.zeros((micro, length, KV_HEADS, HD), jnp.float32),
    )
    grad_query_rot, grad_key_all, grad_value_all = lax.fori_loop(
        0, block_count, back_step, back_start
    )
    grad_key_mine, grad_value_mine = (
        lax.psum_scatter(
            grad_key_all.reshape(micro, length, kv_width).astype(jnp.bfloat16),
            "group",
            scatter_dimension=1,
            tiled=True,
        ).astype(jnp.float32),
        lax.psum_scatter(
            grad_value_all.reshape(micro, length, kv_width).astype(jnp.bfloat16),
            "group",
            scatter_dimension=1,
            tiled=True,
        ).astype(jnp.float32),
    )
    grad_query_norm = rotate(
        grad_query_rot.reshape(rows, HEADS, HD), cosines[:, None, :], -sines[:, None, :]
    )
    grad_key_norm = rotate(
        grad_key_mine.reshape(rows, KV_HEADS, HD), cosines[:, None, :], -sines[:, None, :]
    )
    q_gain_total = jnp.sum(queries_normed * grad_query_norm, axis=(0, 1))
    k_gain_total = jnp.sum(keys_normed * grad_key_norm, axis=(0, 1))
    grad_queries = norm_back(queries, grad_query_norm * head_gain_q).reshape(rows, q_width)
    grad_keys = norm_back(keys_raw, grad_key_norm * head_gain_k).reshape(rows, kv_width)
    grad_qkv = jnp.concatenate(
        [grad_queries, grad_keys, grad_value_mine.reshape(rows, kv_width)], axis=1
    ).astype(jnp.bfloat16)
    qkv_full = matmul_left(first_low, grad_qkv)
    grad_first = matmul_right(grad_qkv, lax.all_gather(w_qkv, "group", axis=0, tiled=True))
    gain_first_full = jnp.sum(normed_first * grad_first, axis=0)
    input_grad = (
        (grad_middle + norm_back(source, grad_first * gain_first))
        .astype(jnp.bfloat16)
        .reshape(micro, slot_len, width)
    )
    owned = (
        lax.psum_scatter(
            gain_first_full.astype(jnp.bfloat16), "group", scatter_dimension=0, tiled=True
        ).astype(jnp.float32),
        lax.psum_scatter(
            qkv_full.astype(jnp.bfloat16), "group", scatter_dimension=0, tiled=True
        ).astype(jnp.float32),
        lax.psum_scatter(
            out_full.astype(jnp.bfloat16), "group", scatter_dimension=0, tiled=True
        ).astype(jnp.float32),
        lax.psum_scatter(
            gain_second_full.astype(jnp.bfloat16), "group", scatter_dimension=0, tiled=True
        ).astype(jnp.float32),
        lax.psum_scatter(
            gate_up_full.astype(jnp.bfloat16), "group", scatter_dimension=0, tiled=True
        ).astype(jnp.float32),
        lax.psum_scatter(
            down_full.astype(jnp.bfloat16), "group", scatter_dimension=0, tiled=True
        ).astype(jnp.float32),
    )
    summed = (
        lax.psum(owned[0].astype(jnp.bfloat16), "replica").astype(jnp.float32),
        lax.psum(owned[1].astype(jnp.bfloat16), "replica").astype(jnp.float32),
        lax.psum(owned[2].astype(jnp.bfloat16), "replica").astype(jnp.float32),
        lax.psum(owned[3].astype(jnp.bfloat16), "replica").astype(jnp.float32),
        lax.psum(owned[4].astype(jnp.bfloat16), "replica").astype(jnp.float32),
        lax.psum(owned[5].astype(jnp.bfloat16), "replica").astype(jnp.float32),
    )
    head_sums = lax.psum((q_gain_total, k_gain_total), ("group", "replica"))
    return (
        block_out,
        input_grad,
        summed[0],
        head_sums[0],
        head_sums[1],
        summed[1],
        summed[2],
        summed[3],
        summed[4],
        summed[5],
    )


MESH_ID = pl.DeviceIdType.MESH
HBM = pltpu.MemorySpace.HBM
VMEM_LIMIT = 64 * 1024 * 1024 - 65536
NZ = 4


class Place:
    def __init__(self):
        self.z = lax.axis_index("z")
        self.y = lax.axis_index("y")
        self.x = lax.axis_index("x")
        self.c = lax.axis_index("core")
        self.h = self.z // 2
        self.m = self.at(self.z)
        self.inner = {"z": self.at(self.m + 1)}
        self.outer = {"z": self.at(lax.rem(self.m + 3, 4))}
        self.across_x = {"x": 1 - self.x}
        self.across_y = {"y": 1 - self.y}
        self.partner = {"core": 1 - self.c}

    def at(self, t):
        return t * (1 - 2 * self.h) + 3 * self.h

    def greet(self):
        barrier = pltpu.get_barrier_semaphore()
        peers = [self.across_x, self.across_y, self.partner]
        peers += [{"z": lax.rem(self.z + hop, NZ)} for hop in range(1, NZ)]
        for peer in peers:
            pl.semaphore_signal(barrier, inc=1, device_id=peer, device_id_type=MESH_ID)
        pl.semaphore_wait(barrier, len(peers))


def remote(src, dst, send, recv, peer):
    return pltpu.make_async_remote_copy(
        src_ref=src, dst_ref=dst, send_sem=send, recv_sem=recv, device_id=peer, device_id_type=MESH_ID
    )


def gather_kernel(count, gains, *refs):
    shards = refs[:count]
    gains_all = refs[count]
    fulls = refs[count + 1 : 2 * count + 1]
    held = refs[2 * count + 1 : 3 * count + 1]
    load_sem, keep_sem, gain_send, gain_recv, z_send, z_recv, f_send, xy_send, xy_recv = refs[3 * count + 1 :]
    me = Place()
    z, y, x, c, m = me.z, me.y, me.x, me.c, me.m
    stage_t = (1 - m, 2, 3)
    loads = [pltpu.make_async_copy(shards[w], held[w], load_sem.at[w]) for w in range(count)]
    keeps = [pltpu.make_async_copy(held[w], fulls[w].at[z], keep_sem.at[w]) for w in range(count)]
    for load in loads:
        load.start()
    me.greet()

    def own(w, peer, k, slot):
        piece = shards[w].at[c, x, y]
        return remote(piece, fulls[w].at[z, c, x, y], z_send.at[w, slot], z_recv.at[w, k], peer)

    def send_own(w):
        own(w, me.inner, m, 0).start()

        @pl.when(m == 1)
        def _():
            own(w, me.outer, 0, 1).start()

    def place(w, k, cc, xx, yy):
        return fulls[w].at[me.at(stage_t[k]), cc, xx, yy]

    def half(ref, which):
        rows = ref.shape[0] // 2
        return ref.at[pl.ds(which * rows, rows), :]

    def forward(w, k):
        piece = place(w, k, c, x, y)
        peer, slot = ((me.inner, 2), (me.outer, 1), (me.outer, 2))[k]
        return remote(piece, piece, f_send.at[w, k], z_recv.at[w, slot], peer)

    def hop(w, k, kind):
        mine, px = place(w, k, c, x, y), place(w, k, c, 1 - x, y)
        py, pd = place(w, k, c, x, 1 - y), place(w, k, c, 1 - x, 1 - y)
        src, peer = {
            "x": (mine, me.across_x),
            "y": (mine, me.across_y),
            "yx": (half(px, 0), me.across_y),
            "xy": (half(py, 1), me.across_x),
            "c": (mine, me.partner),
            "cx": (px, me.partner),
            "cy": (py, me.partner),
            "cd": (pd, me.partner),
        }[kind]
        index = KINDS.index(kind)
        return remote(src, src, xy_send.at[w, k, index], xy_recv.at[w, k, index], peer)

    def arrived(w, k, kind):
        dst = {
            "x": lambda: place(w, k, c, 1 - x, y),
            "y": lambda: place(w, k, c, x, 1 - y),
            "yx": lambda: half(place(w, k, c, 1 - x, 1 - y), 0),
            "xy": lambda: half(place(w, k, c, 1 - x, 1 - y), 1),
            "c": lambda: place(w, k, 1 - c, x, y),
            "cx": lambda: place(w, k, 1 - c, 1 - x, y),
            "cy": lambda: place(w, k, 1 - c, x, 1 - y),
            "cd": lambda: place(w, k, 1 - c, 1 - x, 1 - y),
        }[kind]()
        index = KINDS.index(kind)
        remote(dst, dst, xy_send.at[w, k, index], xy_recv.at[w, k, index], me.partner).wait_recv()

    gain_copies = []
    for j in range(1, NZ):
        there = {"z": lax.rem(z + j, NZ)}
        gain_copies.append(remote(gains, gains_all.at[z], gain_send.at[j], gain_recv.at[j], there))
    gain_own = pltpu.make_async_copy(gains, gains_all.at[z], gain_send.at[0])
    send_own(0)
    for copy in gain_copies:
        copy.start()
    gain_own.start()

    def first(w, k):
        if k == 0 and w + 1 < count:
            send_own(w + 1)
        mine = place(w, k, c, x, y)
        remote(mine, mine, f_send.at[w, k], z_recv.at[w, k], me.partner).wait_recv()

        @pl.when(m == 1)
        def _():
            forward(w, k).start()

        for kind in ("x", "y", "c"):
            hop(w, k, kind).start()
        if k == 0:
            loads[w].wait()
            keeps[w].start()

    def second(w, k):
        arrived(w, k, "x")
        hop(w, k, "yx").start()
        hop(w, k, "cx").start()
        arrived(w, k, "y")
        hop(w, k, "xy").start()
        hop(w, k, "cy").start()

    def third(w, k):
        arrived(w, k, "yx")
        arrived(w, k, "xy")
        hop(w, k, "cd").start()

    steps = [(w, k) for w in range(count) for k in range(3)]
    for i in range(len(steps) + 2):
        if i < len(steps):
            first(*steps[i])
        if 0 <= i - 1 < len(steps):
            second(*steps[i - 1])
        if 0 <= i - 2:
            third(*steps[i - 2])
    for w, k in steps:
        for kind in ("c", "cx", "cy", "cd"):
            arrived(w, k, kind)
        for kind in KINDS:
            hop(w, k, kind).wait_send()
    for w in range(count):
        keeps[w].wait()
        own(w, me.inner, m, 0).wait_send()

        @pl.when(m == 1)
        def _(w=w):
            own(w, me.outer, 0, 1).wait_send()
            for k in range(3):
                forward(w, k).wait_send()

    gain_own.wait()
    for j in range(1, NZ):
        gain_copies[j - 1].wait_send()
        there = gains_all.at[lax.rem(z + NZ - j, NZ)]
        remote(gains, there, gain_send.at[j], gain_recv.at[j], me.partner).wait_recv()


KINDS = ("x", "y", "yx", "xy", "c", "cx", "cy", "cd")


def gather_weights(gains, shards):
    count = len(shards)
    cut = [s.reshape(2, 2, 2, s.shape[0] // 8, s.shape[1]) for s in shards]
    shapes = [jax.ShapeDtypeStruct((NZ, *s.shape), s.dtype) for s in cut]
    out = pl.pallas_call(
        functools.partial(gather_kernel, count),
        out_shape=[jax.ShapeDtypeStruct((NZ, *gains.shape), gains.dtype), *shapes],
        in_specs=[pl.BlockSpec(memory_space=HBM)] * (count + 1),
        out_specs=[pl.BlockSpec(memory_space=HBM)] * (count + 1),
        scratch_shapes=[pltpu.VMEM(s.shape, s.dtype) for s in cut]
        + [
            pltpu.SemaphoreType.DMA((count,)),
            pltpu.SemaphoreType.DMA((count,)),
            pltpu.SemaphoreType.DMA((NZ,)),
            pltpu.SemaphoreType.DMA((NZ,)),
            pltpu.SemaphoreType.DMA((count, 2)),
            pltpu.SemaphoreType.DMA((count, 3)),
            pltpu.SemaphoreType.DMA((count, 3)),
            pltpu.SemaphoreType.DMA((count, 3, len(KINDS))),
            pltpu.SemaphoreType.DMA((count, 3, len(KINDS))),
        ],
        compiler_params=pltpu.CompilerParams(collective_id=0, has_side_effects=True, vmem_limit_bytes=VMEM_LIMIT),
        name="weight_gather",
    )(gains, *cut)
    fulls = [f.reshape(NZ * s.shape[0], s.shape[1]) for f, s in zip(out[1:], shards)]
    return out[0], fulls


def add_rows(dst, src, rows):
    def body(i, carry):
        at = pl.ds(pl.multiple_of(i * 16, 16), 16)
        total = dst[at, :].astype(jnp.float32) + src[at, :].astype(jnp.float32)
        dst[at, :] = total.astype(dst.dtype)
        return carry

    lax.fori_loop(0, rows // 16, body, 0)


REDUCE_STEPS = ("core", "x1", "y1", "y2", "x2", "z")
SPREAD = ("x", "y", "yx", "xy", "c", "cx", "cy", "cd")


def reduce_kernel(count, small, *refs):
    grads = refs[:count]
    small_out = refs[count]
    outs = refs[count + 1 : 2 * count + 1]
    rest = refs[2 * count + 1 :]
    acc, own, rx1, ry1, rx2, ry2, rz = (rest[i * count : (i + 1) * count] for i in range(7))
    small_mid, small_got, small_z = rest[7 * count : 7 * count + 3]
    own_sem, keep_sem, c_send, c_recv, r_send, r_recv, z_send, z_recv, o_send, o_recv, s_send, s_recv = rest[
        7 * count + 3 :
    ]
    me = Place()
    z, y, x, c, m = me.z, me.y, me.x, me.c, me.m
    stage_t = (3, 2, 1 - m, m)
    me.greet()
    chunks = [(w, k) for w in range(count) for k in range(4)]

    def zk(k):
        return me.at(stage_t[k])

    def to_partner(w, k):
        return remote(grads[w].at[zk(k), 1 - c], acc[w].at[zk(k)], c_send.at[w, k], c_recv.at[w, k], me.partner)

    def load(n):
        w, k = chunks[n]
        return pltpu.make_async_copy(grads[w].at[zk(k), c], own[w].at[k % 2], own_sem.at[w, k % 2])

    def exchange(w, k, kind):
        a = acc[w].at[zk(k)]
        half = a.shape[-1] // 2
        lo, hi = pl.ds(0, half), pl.ds(half, half)
        src, dst, peer = {
            "x1": lambda: (a.at[1 - x, :, :, lo], rx1[w].at[k], me.across_x),
            "y1": lambda: (a.at[:, 1 - y, :, hi], ry1[w].at[k], me.across_y),
            "y2": lambda: (a.at[x, 1 - y, :, lo], ry2[w].at[k], me.across_y),
            "x2": lambda: (a.at[1 - x, y, :, hi], rx2[w].at[k], me.across_x),
        }[kind]()
        index = ("x1", "y1", "y2", "x2").index(kind)
        return remote(src, dst, r_send.at[w, k, index], r_recv.at[w, k, index], peer)

    def along(w, k, slot, peer):
        return remote(acc[w].at[zk(k), x, y], rz[w].at[slot], z_send.at[w, k], z_recv.at[w, slot], peer)

    def z_arrived(w, slot):
        there = rz[w].at[slot]
        remote(there, there, z_send.at[w, 0], z_recv.at[w, slot], me.partner).wait_recv()

    def s0(n):
        w, k = chunks[n]
        a = acc[w].at[zk(k)]
        to_partner(w, k).wait_recv()
        load(n).wait()
        rows = a.shape[2]
        for i in range(2):
            for j in range(2):
                add_rows(a.at[i, j], own[w].at[k % 2, i, j], rows)
        exchange(w, k, "x1").start()
        exchange(w, k, "y1").start()
        if n + 2 < len(chunks):
            load(n + 2).start()

    def s1(n):
        w, k = chunks[n]
        a = acc[w].at[zk(k)]
        rows, half = a.shape[2], a.shape[3] // 2
        exchange(w, k, "x1").wait_recv()
        for j in range(2):
            add_rows(a.at[x, j, :, pl.ds(0, half)], rx1[w].at[k, j], rows)
        exchange(w, k, "y1").wait_recv()
        for i in range(2):
            add_rows(a.at[i, y, :, pl.ds(half, half)], ry1[w].at[k, i], rows)
        exchange(w, k, "y2").start()
        exchange(w, k, "x2").start()

    def s2(n):
        w, k = chunks[n]
        a = acc[w].at[zk(k), x, y]
        rows, half = a.shape[0], a.shape[1] // 2
        exchange(w, k, "y2").wait_recv()
        add_rows(a.at[:, pl.ds(0, half)], ry2[w].at[k], rows)
        exchange(w, k, "x2").wait_recv()
        add_rows(a.at[:, pl.ds(half, half)], rx2[w].at[k], rows)

    def s3(n):
        w, k = chunks[n]
        a = acc[w].at[zk(k), x, y]
        rows = a.shape[0]

        def take(slot):
            z_arrived(w, slot)
            add_rows(a, rz[w].at[slot], rows)

        @pl.when(m == 0)
        def _():
            if k < 3:
                along(w, k, k, me.inner).start()
            else:
                take(0)

        @pl.when(m == 1)
        def _():
            if k == 0:
                take(0)
                along(w, k, 3, me.inner).start()
            elif k == 1:
                take(1)
                along(w, k, 4, me.inner).start()
            elif k == 2:
                take(3)
                along(w, k, 0, me.outer).start()
            else:
                take(2)
                take(4)

    def out_at(w, cc, xx, yy):
        return outs[w].at[cc, xx, yy]

    def half_of(ref, which):
        rows = ref.shape[0] // 2
        return ref.at[pl.ds(which * rows, rows), :]

    def keep(w):
        return pltpu.make_async_copy(acc[w].at[z, x, y], out_at(w, c, x, y), keep_sem.at[w])

    def spread(w, kind):
        final, mine = acc[w].at[z, x, y], out_at(w, c, x, y)
        px, py, pd = out_at(w, c, 1 - x, y), out_at(w, c, x, 1 - y), out_at(w, c, 1 - x, 1 - y)
        src, dst, peer = {
            "x": (final, mine, me.across_x),
            "y": (final, mine, me.across_y),
            "c": (final, mine, me.partner),
            "yx": (half_of(px, 0), half_of(px, 0), me.across_y),
            "xy": (half_of(py, 1), half_of(py, 1), me.across_x),
            "cx": (px, px, me.partner),
            "cy": (py, py, me.partner),
            "cd": (pd, pd, me.partner),
        }[kind]
        index = SPREAD.index(kind)
        return remote(src, dst, o_send.at[w, index], o_recv.at[w, index], peer)

    def spread_arrived(w, kind):
        dst = {
            "x": lambda: out_at(w, c, 1 - x, y),
            "y": lambda: out_at(w, c, x, 1 - y),
            "yx": lambda: half_of(out_at(w, c, 1 - x, 1 - y), 0),
            "xy": lambda: half_of(out_at(w, c, 1 - x, 1 - y), 1),
            "c": lambda: out_at(w, 1 - c, x, y),
            "cx": lambda: out_at(w, 1 - c, 1 - x, y),
            "cy": lambda: out_at(w, 1 - c, x, 1 - y),
            "cd": lambda: out_at(w, 1 - c, 1 - x, 1 - y),
        }[kind]()
        index = SPREAD.index(kind)
        remote(dst, dst, o_send.at[w, index], o_recv.at[w, index], me.partner).wait_recv()

    def s4(w):
        keep(w).start()
        for kind in ("x", "y", "c"):
            spread(w, kind).start()

    def s5(w):
        spread_arrived(w, "x")
        spread(w, "yx").start()
        spread(w, "cx").start()
        spread_arrived(w, "y")
        spread(w, "xy").start()
        spread(w, "cy").start()

    def s6(w):
        spread_arrived(w, "yx")
        spread_arrived(w, "xy")
        spread(w, "cd").start()

    small_peers = (me.partner, me.across_x, me.across_y)

    def small_copy(step):
        return remote(small_mid.at[step], small_got.at[step], s_send.at[step], s_recv.at[step], small_peers[step])

    def small_along(j):
        return remote(
            small_mid.at[3], small_z.at[z], s_send.at[3 + j], s_recv.at[3 + j], {"z": lax.rem(z + 1 + j, NZ)}
        )

    def small_step(n):
        if n == 0:
            small_mid[0] = small[...]
        elif n in (1, 3, 5):
            small_copy(n // 2).start()
        elif n in (2, 4, 6):
            step = n // 2 - 1
            small_copy(step).wait()
            small_mid[step + 1] = small_mid[step] + small_got[step]
        elif n == 7:
            for j in range(3):
                small_along(j).start()
        elif n == 8:
            for j in range(3):
                small_along(j).wait_send()
                there = small_z.at[lax.rem(z + 3 - j, NZ)]
                remote(there, there, s_send.at[3 + j], s_recv.at[3 + j], me.partner).wait_recv()
            small_z[pl.ds(z, 1)] = small_mid[pl.ds(3, 1)]
            small_out[...] = (small_z[0] + small_z[1]) + (small_z[2] + small_z[3])

    for w, k in chunks[:4]:
        to_partner(w, k).start()
    load(0).start()
    load(1).start()
    total = len(chunks)
    for n in range(total + 6):
        if n < total:
            if n + 4 < total:
                to_partner(*chunks[n + 4]).start()
            s0(n)
        if 0 <= n - 1 < total:
            s1(n - 1)
        if 0 <= n - 2 < total:
            s2(n - 2)
        if 0 <= n - 3 < total:
            s3(n - 3)
            if chunks[n - 3][1] == 3:
                s4(chunks[n - 3][0])
        if 0 <= n - 4 < total and chunks[n - 4][1] == 3:
            s5(chunks[n - 4][0])
        if 0 <= n - 5 < total and chunks[n - 5][1] == 3:
            s6(chunks[n - 5][0])
        if n < 9:
            small_step(n)
    for w, k in chunks:
        to_partner(w, k).wait_send()
        for kind in ("x1", "y1", "y2", "x2"):
            exchange(w, k, kind).wait_send()
        if k < 3:
            along(w, k, k, me.inner).wait_send()
    for w in range(count):
        keep(w).wait()
        for kind in SPREAD:
            spread(w, kind).wait_send()
        for kind in ("c", "cx", "cy", "cd"):
            spread_arrived(w, kind)


def reduce_gradients(small, grads):
    count = len(grads)
    cut = [g.reshape(NZ, 2, 2, 2, g.shape[0] // 32, g.shape[1]) for g in grads]
    low = jnp.bfloat16

    def buffers(make):
        return [pltpu.VMEM(make(*g.shape[-2:]), low) for g in cut]

    dma = pltpu.SemaphoreType.DMA
    out = pl.pallas_call(
        functools.partial(reduce_kernel, count),
        out_shape=[jax.ShapeDtypeStruct(small.shape, jnp.float32)]
        + [jax.ShapeDtypeStruct((2, 2, 2, *g.shape[-2:]), low) for g in cut],
        in_specs=[pl.BlockSpec(memory_space=pltpu.VMEM)] + [pl.BlockSpec(memory_space=HBM)] * count,
        out_specs=[pl.BlockSpec(memory_space=pltpu.VMEM)] + [pl.BlockSpec(memory_space=HBM)] * count,
        scratch_shapes=buffers(lambda r, n: (NZ, 2, 2, r, n))
        + buffers(lambda r, n: (2, 2, 2, r, n))
        + buffers(lambda r, n: (NZ, 2, r, n // 2))
        + buffers(lambda r, n: (NZ, 2, r, n // 2))
        + buffers(lambda r, n: (NZ, r, n // 2))
        + buffers(lambda r, n: (NZ, r, n // 2))
        + buffers(lambda r, n: (5, r, n))
        + [
            pltpu.VMEM((4, *small.shape), jnp.float32),
            pltpu.VMEM((3, *small.shape), jnp.float32),
            pltpu.VMEM((NZ, *small.shape), jnp.float32),
            dma((count, 2)),
            dma((count,)),
            dma((count, 4)),
            dma((count, 4)),
            dma((count, 4, 4)),
            dma((count, 4, 4)),
            dma((count, 4)),
            dma((count, 5)),
            dma((count, len(SPREAD))),
            dma((count, len(SPREAD))),
            dma((6,)),
            dma((6,)),
        ],
        compiler_params=pltpu.CompilerParams(collective_id=1, has_side_effects=True, vmem_limit_bytes=VMEM_LIMIT),
        name="gradient_reduce",
    )(small, *cut)
    owned = [o.reshape(g.shape[0] // NZ, g.shape[1]) for o, g in zip(out[1:], grads)]
    return out[0], owned


PER_HEAD = 4 * HD
HALF_HEADS = KV_HEADS // 2
BLOCKS = 4


def turn(v):
    return pltpu.roll(v, HD // 2, 1)


def project_kernel(h1, wq, wk, wv, gain_q, gain_k, cosines, sines, raw, rot):
    weight = jnp.concatenate([wq[...], wk[...], wv[...]], axis=1)
    out = jnp.dot(h1[...], weight, preferred_element_type=jnp.float32)
    raw[...] = out.astype(raw.dtype)
    cos, sin = cosines[...], sines[...]
    for i, gain in enumerate((gain_q, gain_q, gain_k)):
        v = out[:, i * HD : (i + 1) * HD]
        v = v * lax.rsqrt(jnp.mean(v * v, axis=-1, keepdims=True) + EPSILON) * gain[...]
        rot[:, i * HD : (i + 1) * HD] = (v * cos + turn(v) * sin).astype(rot.dtype)
    rot[:, 3 * HD :] = out[:, 3 * HD :].astype(rot.dtype)


def project(h1, w_qkv, gain_q, gain_k, cosines, sines):
    rows, width = h1.shape
    whole = lambda shape: pl.BlockSpec(shape, lambda i: (0, 0))
    out_spec = pl.BlockSpec((None, rows, PER_HEAD), lambda i: (i // HALF_HEADS, 0, i % HALF_HEADS))
    shape = jax.ShapeDtypeStruct((2, rows, HALF_HEADS * PER_HEAD), jnp.bfloat16)
    return pl.pallas_call(
        project_kernel,
        grid=(KV_HEADS,),
        out_shape=[shape, shape],
        in_specs=[
            whole((rows, width)),
            pl.BlockSpec((width, 2 * HD), lambda i: (0, i)),
            pl.BlockSpec((width, HD), lambda i: (0, HEADS + i)),
            pl.BlockSpec((width, HD), lambda i: (0, HEADS + KV_HEADS + i)),
            whole((1, HD)),
            whole((1, HD)),
            whole((rows, HD)),
            whole((rows, HD)),
        ],
        out_specs=[out_spec, out_spec],
        cost_estimate=pl.CostEstimate(flops=2 * rows * width * 4096, bytes_accessed=2 * 4096 * (width + 2 * rows), transcendentals=0),
        name="qkv_project",
    )(h1, w_qkv, w_qkv, w_qkv, gain_q, gain_k, cosines, sines)


def block_rows(scalars, i, block):
    return pl.ds(pl.multiple_of(scalars[i] * block, block), block)


def stacked(two_heads):
    return jnp.concatenate([two_heads[:, :HD], two_heads[:, HD:]], axis=0)


def attend_kernel(scalars, mine, theirs, out, probs, tokens, keys, values):
    rows = mine.shape[0]
    block = 2 * rows // BLOCKS
    scale = 1.0 / math.sqrt(HD)
    tokens[:rows] = mine[...]
    tokens[rows:] = theirs[...]
    for i in range(BLOCKS):
        at = block_rows(scalars, i, block)
        keys[i * block : (i + 1) * block] = tokens[at, 2 * HD : 3 * HD]
        values[i * block : (i + 1) * block] = tokens[at, 3 * HD :]
    above = lax.broadcasted_iota(jnp.int32, (2 * block, block), 0) % block
    above = above < lax.broadcasted_iota(jnp.int32, (2 * block, block), 1)
    column = 0
    for i in range(BLOCKS):
        at = block_rows(scalars, i, block)
        n = (i + 1) * block
        query = stacked(tokens[at, : 2 * HD])
        scores = lax.dot_general(
            query, keys[:n], (((1,), (1,)), ((), ())), preferred_element_type=jnp.float32
        )
        last = jnp.where(above, MASKED, scores[:, i * block :])
        scores = last if i == 0 else jnp.concatenate([scores[:, : i * block], last], axis=1)
        top = jnp.max(scores, axis=-1, keepdims=True)
        weights = jnp.exp((scores - top) * scale)
        weights = weights * (1.0 / jnp.sum(weights, axis=-1, keepdims=True))
        low = weights.astype(jnp.bfloat16)
        probs[:, column : column + n] = low
        column += n
        mixed = jnp.dot(low, values[:n], preferred_element_type=jnp.float32).astype(out.dtype)
        out[at, :HD] = mixed[:block]
        out[at, HD:] = mixed[block:]


def attend(scalars, rot, theirs):
    _, rows, width = rot.shape
    heads = width // PER_HEAD
    block = 2 * rows // BLOCKS
    area = block * BLOCKS * (BLOCKS + 1) // 2
    return pl.pallas_call(
        attend_kernel,
        out_shape=[
            jax.ShapeDtypeStruct((2 * rows, heads * 2 * HD), jnp.bfloat16),
            jax.ShapeDtypeStruct((heads, 2 * block, area), jnp.bfloat16),
        ],
        grid_spec=pltpu.PrefetchScalarGridSpec(
            num_scalar_prefetch=1,
            grid=(heads,),
            in_specs=[
                pl.BlockSpec((None, rows, PER_HEAD), lambda i, s: (s[BLOCKS], 0, i)),
                pl.BlockSpec((rows, PER_HEAD), lambda i, s: (0, i)),
            ],
            out_specs=[
                pl.BlockSpec((2 * rows, 2 * HD), lambda i, s: (0, i)),
                pl.BlockSpec((None, 2 * block, area), lambda i, s: (i, 0, 0)),
            ],
            scratch_shapes=[
                pltpu.VMEM((2 * rows, PER_HEAD), jnp.bfloat16),
                pltpu.VMEM((2 * rows, HD), jnp.bfloat16),
                pltpu.VMEM((2 * rows, HD), jnp.bfloat16),
            ],
        ),
        cost_estimate=pl.CostEstimate(
            flops=heads * 4 * HD * 2 * block * area, bytes_accessed=2 * heads * 2 * block * area, transcendentals=heads * 2 * block * area
        ),
        name="attention",
    )(scalars, rot, theirs)


def attend_back_kernel(scalars, mine, theirs, grad_mine, grad_theirs, probs, out, tokens, grads, keys, values, grad_k, grad_v):
    rows = mine.shape[0]
    block = 2 * rows // BLOCKS
    scale = 1.0 / math.sqrt(HD)
    tokens[:rows] = mine[...]
    tokens[rows:] = theirs[...]
    grads[:rows] = grad_mine[...]
    grads[rows:] = grad_theirs[...]
    for i in range(BLOCKS):
        at = block_rows(scalars, i, block)
        keys[i * block : (i + 1) * block] = tokens[at, 2 * HD : 3 * HD]
        values[i * block : (i + 1) * block] = tokens[at, 3 * HD :]
    column = BLOCKS * (BLOCKS + 1) // 2 * block
    for i in reversed(range(BLOCKS)):
        at = block_rows(scalars, i, block)
        n = (i + 1) * block
        column -= n
        query = stacked(tokens[at, : 2 * HD])
        grad = stacked(grads[at, :])
        low = probs[:, column : column + n]
        weights = low.astype(jnp.float32)
        grad_probs = lax.dot_general(
            grad, values[:n], (((1,), (1,)), ((), ())), preferred_element_type=jnp.float32
        )
        delta = jnp.sum(weights * grad_probs, axis=-1, keepdims=True)
        grad_scores = (weights * (grad_probs - delta)).astype(jnp.bfloat16)
        grad_q = jnp.dot(grad_scores, keys[:n], preferred_element_type=jnp.float32) * scale
        out[at, :HD] = grad_q[:block].astype(out.dtype)
        out[at, HD : 2 * HD] = grad_q[block:].astype(out.dtype)
        across = (((0,), (0,)), ((), ()))
        part_k = lax.dot_general(query, grad_scores, across, preferred_element_type=jnp.float32)
        part_v = lax.dot_general(grad, low, across, preferred_element_type=jnp.float32)
        if i == BLOCKS - 1:
            grad_k[...] = part_k
            grad_v[...] = part_v
        else:
            grad_k[:, :n] += part_k
            grad_v[:, :n] += part_v
    for i in range(BLOCKS):
        at = block_rows(scalars, i, block)
        here = slice(i * block, (i + 1) * block)
        out[at, 2 * HD : 3 * HD] = jnp.transpose(grad_k[:, here] * scale).astype(out.dtype)
        out[at, 3 * HD :] = jnp.transpose(grad_v[:, here]).astype(out.dtype)


def attend_back(scalars, rot, theirs, grad_mine, grad_theirs, probs):
    _, rows, width = rot.shape
    heads = width // PER_HEAD
    block = 2 * rows // BLOCKS
    area = probs.shape[-1]
    return pl.pallas_call(
        attend_back_kernel,
        out_shape=jax.ShapeDtypeStruct((2 * rows, width), jnp.bfloat16),
        grid_spec=pltpu.PrefetchScalarGridSpec(
            num_scalar_prefetch=1,
            grid=(heads,),
            in_specs=[
                pl.BlockSpec((None, rows, PER_HEAD), lambda i, s: (s[BLOCKS], 0, i)),
                pl.BlockSpec((rows, PER_HEAD), lambda i, s: (0, i)),
                pl.BlockSpec((rows, 2 * HD), lambda i, s: (0, s[BLOCKS] * HALF_HEADS + i)),
                pl.BlockSpec((rows, 2 * HD), lambda i, s: (0, i)),
                pl.BlockSpec((None, 2 * block, area), lambda i, s: (i, 0, 0)),
            ],
            out_specs=pl.BlockSpec((2 * rows, PER_HEAD), lambda i, s: (0, i)),
            scratch_shapes=[
                pltpu.VMEM((2 * rows, PER_HEAD), jnp.bfloat16),
                pltpu.VMEM((2 * rows, 2 * HD), jnp.bfloat16),
                pltpu.VMEM((2 * rows, HD), jnp.bfloat16),
                pltpu.VMEM((2 * rows, HD), jnp.bfloat16),
                pltpu.VMEM((HD, 2 * rows), jnp.float32),
                pltpu.VMEM((HD, 2 * rows), jnp.float32),
            ],
        ),
        cost_estimate=pl.CostEstimate(
            flops=heads * 8 * HD * 2 * block * area, bytes_accessed=2 * heads * 2 * block * area, transcendentals=0
        ),
        name="attention_back",
    )(scalars, rot, theirs, grad_mine, grad_theirs, probs)


def unproject_kernel(scalars, mine, theirs, raw, gain_q, gain_k, cosines, sines, out, gains):
    i = pl.program_id(0)
    mine_here = i // HALF_HEADS == scalars[BLOCKS]
    grad = jnp.where(mine_here, mine[...], theirs[...]).astype(jnp.float32)
    cos, sin = cosines[...], sines[...]
    totals = []
    backs = []
    for j, gain in enumerate((gain_q, gain_q, gain_k)):
        v = raw[:, j * HD : (j + 1) * HD].astype(jnp.float32)
        inverse = lax.rsqrt(jnp.mean(v * v, axis=-1, keepdims=True) + EPSILON)
        normed = v * inverse
        g = grad[:, j * HD : (j + 1) * HD]
        g = g * cos - turn(g) * sin
        totals.append(jnp.sum(normed * g, axis=0, keepdims=True))
        g = g * gain[...]
        backs.append(inverse * (g - normed * jnp.mean(g * normed, axis=-1, keepdims=True)))

    @pl.when(i == 0)
    def _():
        gains[...] = jnp.zeros_like(gains)

    gains[0:1, :] += totals[0] + totals[1]
    gains[1:2, :] += totals[2]
    at = pl.multiple_of(i * 2 * HD, 2 * HD)
    out[:, pl.ds(at, HD)] = backs[0].astype(out.dtype)
    out[:, pl.ds(pl.multiple_of(at + HD, HD), HD)] = backs[1].astype(out.dtype)
    out[:, pl.ds(pl.multiple_of((HEADS + i) * HD, HD), HD)] = backs[2].astype(out.dtype)
    out[:, pl.ds(pl.multiple_of((HEADS + KV_HEADS + i) * HD, HD), HD)] = grad[:, 3 * HD :].astype(out.dtype)


def unproject(scalars, mine, theirs, raw, gain_q, gain_k, cosines, sines):
    _, rows, width = raw.shape
    whole = lambda shape: pl.BlockSpec(shape, lambda i, s: (0, 0))
    columns = (HEADS + 2 * KV_HEADS) * HD
    return pl.pallas_call(
        unproject_kernel,
        out_shape=[
            jax.ShapeDtypeStruct((rows, columns), jnp.bfloat16),
            jax.ShapeDtypeStruct((8, HD), jnp.float32),
        ],
        grid_spec=pltpu.PrefetchScalarGridSpec(
            num_scalar_prefetch=1,
            grid=(KV_HEADS,),
            in_specs=[
                pl.BlockSpec((rows, PER_HEAD), lambda i, s: (0, i % HALF_HEADS)),
                pl.BlockSpec((rows, PER_HEAD), lambda i, s: (0, i % HALF_HEADS)),
                pl.BlockSpec((None, rows, PER_HEAD), lambda i, s: (i // HALF_HEADS, 0, i % HALF_HEADS)),
                whole((1, HD)),
                whole((1, HD)),
                whole((rows, HD)),
                whole((rows, HD)),
            ],
            out_specs=[whole((rows, columns)), whole((8, HD))],
        ),
        cost_estimate=pl.CostEstimate(flops=rows * columns * 20, bytes_accessed=rows * columns * 10, transcendentals=0),
        name="qkv_back",
    )(scalars, mine, theirs, raw, gain_q, gain_k, cosines, sines)


def swap(v):
    return lax.ppermute(v, "core", [(0, 1), (1, 0)])


def half_of(v, which, size):
    return lax.dynamic_slice_in_dim(v, which * size, size, 1)


def first_route():
    return [(2 * s + c, 2 * (2 * c + s % 2) + s // 2) for s in range(4) for c in range(2)]


def second_route():
    return [(2 * s + c, 2 * (2 * c + 1 - s % 2) + s // 2) for s in range(4) for c in range(2)]


def back(route):
    return [(b, a) for a, b in route]


LINE = ("z", "core")


def to_sequences(v):
    odd = lax.axis_index("z") % 2
    first = lax.ppermute(lax.dynamic_index_in_dim(v, odd, 0, False), LINE, first_route())
    second = lax.ppermute(lax.dynamic_index_in_dim(v, 1 - odd, 0, False), LINE, second_route())
    return jnp.concatenate([first, second], axis=0)


def from_sequences(v):
    odd = lax.axis_index("z") % 2
    rows = v.shape[0] // 2
    first = lax.ppermute(v[:rows], LINE, back(first_route()))
    second = lax.ppermute(v[rows:], LINE, back(second_route()))
    return jnp.where(odd == 0, jnp.stack([first, second]), jnp.stack([second, first]))


def per_chip(
    tokens,
    cotangent,
    slot_order,
    attn_gain,
    q_gain,
    k_gain,
    w_qkv,
    w_out,
    mlp_gain,
    w_gate_up,
    w_down,
):
    z, core = lax.axis_index("z"), lax.axis_index("core")
    _, slot_len, width = tokens.shape
    f32, low = jnp.float32, jnp.bfloat16
    odd = z % 2
    source_low = to_sequences(tokens)
    grad_low = to_sequences(cotangent)
    orders = jnp.where(z // 2 == core, slot_order, swap(slot_order))
    order = lax.dynamic_index_in_dim(orders, odd, 0, False)
    slots = jnp.stack([2 * core + odd, 2 * core + 1 - odd, 2 - 2 * core + odd, 3 - 2 * core - odd])
    blocks = order[slots]
    where_is = jnp.sum(
        jnp.where(blocks[None, :] == jnp.arange(4)[:, None], jnp.arange(4)[None, :], 0), axis=1
    )
    scalars = jnp.concatenate([where_is, core[None], jnp.zeros((3,), jnp.int32)]).astype(jnp.int32)
    positions = (blocks[:2, None] * slot_len + jnp.arange(slot_len)[None, :]).reshape(-1)
    cos, sin = rope_tables(positions)
    cosines = jnp.concatenate([cos, cos], axis=1)
    sines = jnp.concatenate([-sin, sin], axis=1)
    gain_q, gain_k = q_gain.astype(f32)[None, :], k_gain.astype(f32)[None, :]

    gains = jnp.zeros((8, attn_gain.shape[0]), f32)
    gains = gains.at[0].set(attn_gain.astype(f32)).at[1].set(mlp_gain.astype(f32))
    gains_all, (full_qkv, full_out, full_gate_up, full_down) = gather_weights(
        gains, [w_qkv, w_out, w_gate_up, w_down]
    )
    gain_first, gain_second = gains_all[:, 0].reshape(-1), gains_all[:, 1].reshape(-1)

    source = source_low.astype(f32)
    normed_first = norm_rows(source)
    first_low = (normed_first * gain_first).astype(low)
    raw, rot = project(first_low, full_qkv, gain_q, gain_k, cosines, sines)
    theirs = swap(lax.dynamic_index_in_dim(rot, 1 - core, 0, False))
    mixed, probs = attend(scalars, rot, theirs)
    rows = source.shape[0]
    mixed_back = swap(mixed[rows:])
    attended = jnp.where(
        core == 0,
        jnp.concatenate([mixed[:rows], mixed_back], axis=1),
        jnp.concatenate([mixed_back, mixed[:rows]], axis=1),
    )
    middle = source + matmul(attended, full_out)
    normed_second = norm_rows(middle)
    second_low = (normed_second * gain_second).astype(low)
    gate_up = matmul(second_low, full_gate_up).astype(low)
    gate_part, up_part = gate_up[:, :FF].astype(f32), gate_up[:, FF:].astype(f32)
    sigmoid_gate = jax.nn.sigmoid(gate_part)
    silu_gate = gate_part * sigmoid_gate
    hidden = (silu_gate * up_part).astype(low)
    block_out = from_sequences((middle + matmul(hidden, full_down)).astype(low))

    grad_output = grad_low.astype(f32)
    down_full = matmul_left(hidden, grad_low).astype(low)
    grad_hidden = matmul_right(grad_low, full_down)
    grad_gate = grad_hidden * up_part * (sigmoid_gate * (1.0 + gate_part * (1.0 - sigmoid_gate)))
    grad_upper = grad_hidden * silu_gate
    grad_gate_up = jnp.concatenate([grad_gate, grad_upper], axis=1).astype(low)
    gate_up_full = matmul_left(second_low, grad_gate_up).astype(low)
    grad_second = matmul_right(grad_gate_up, full_gate_up)
    gain_second_sum = jnp.sum(normed_second * grad_second, axis=0)
    grad_middle = grad_output + norm_back(middle, grad_second * gain_second)
    grad_mid_low = grad_middle.astype(low)
    out_full = matmul_left(attended, grad_mid_low).astype(low)
    grad_attn = matmul_right(grad_mid_low, full_out).astype(low)
    half = HEADS * HD // 2
    grad_theirs = swap(half_of(grad_attn, 1 - core, half))
    grad_rot = attend_back(scalars, rot, theirs, grad_attn, grad_theirs, probs)
    grad_rot_theirs = swap(grad_rot[rows:])
    grad_qkv, head_gains = unproject(
        scalars, grad_rot, grad_rot_theirs, raw, gain_q, gain_k, cosines, sines
    )
    qkv_full = matmul_left(first_low, grad_qkv).astype(low)
    grad_first = matmul_right(grad_qkv, full_qkv)
    gain_first_sum = jnp.sum(normed_first * grad_first, axis=0)
    input_grad = from_sequences(
        (grad_middle + norm_back(source, grad_first * gain_first)).astype(low)
    )
    small = jnp.concatenate(
        [gain_first_sum.reshape(-1, HD), gain_second_sum.reshape(-1, HD), head_gains], axis=0
    )
    sums, (down_sum, gate_up_sum, out_sum, qkv_sum) = reduce_gradients(
        small, [down_full, gate_up_full, out_full, qkv_full]
    )
    count = width // HD
    share = width // NZ
    return (
        block_out,
        input_grad,
        lax.dynamic_slice_in_dim(sums[:count].reshape(-1), z * share, share, 0),
        sums[2 * count],
        sums[2 * count + 1],
        qkv_sum.astype(f32),
        out_sum.astype(f32),
        lax.dynamic_slice_in_dim(sums[count : 2 * count].reshape(-1), z * share, share, 0),
        gate_up_sum.astype(f32),
        down_sum.astype(f32),
    )


def solution(mesh):
    group, replica, body = "group", "replica", per_device
    if (mesh.shape["group"], mesh.shape["replica"]) == (NZ, 8):
        mesh = Mesh(mesh.devices.reshape(NZ, 2, 2, 2), ("z", "y", "x", "core"))
        group, replica, body = "z", ("y", "x", "core"), per_chip
    in_specs = (
        P(replica, group, None),
        P(replica, group, None),
        P(replica, None),
        P(group),
        P(),
        P(),
        P(group, None),
        P(group, None),
        P(group),
        P(group, None),
        P(group, None),
    )
    out_specs = (
        P(replica, group, None),
        P(replica, group, None),
        P(group),
        P(),
        P(),
        P(group, None),
        P(group, None),
        P(group),
        P(group, None),
        P(group, None),
    )
    return jax.shard_map(
        body, mesh=mesh, in_specs=in_specs, out_specs=out_specs, check_vma=False
    )
```

```python
import functools
import math

import jax
import jax.numpy as jnp
from jax import lax
from jax.experimental import pallas as pl
from jax.experimental.pallas import tpu as pltpu
from jax.sharding import Mesh
from jax.sharding import PartitionSpec as P

HEADS = 16
KV_HEADS = 8
HD = 128
FF = 3072


EPSILON = 1e-06
THETA_BASE = 1000000.0
MASKED = -1e30


def norm_rows(v):
    return v * lax.rsqrt(jnp.mean(v * v, axis=-1, keepdims=True) + EPSILON)


def norm_back(source, grad):
    inverse = lax.rsqrt(jnp.mean(source * source, axis=-1, keepdims=True) + EPSILON)
    normed = source * inverse
    return inverse * (grad - normed * jnp.mean(grad * normed, axis=-1, keepdims=True))


def rotate(v, cosines, sines):
    half_size = v.shape[-1] // 2
    leading = v[..., :half_size]
    trailing = v[..., half_size:]
    return jnp.concatenate(
        [leading * cosines - trailing * sines, trailing * cosines + leading * sines], axis=-1
    )


def rope_tables(positions):
    half_size = HD // 2
    counter = jnp.arange(half_size).astype(jnp.float32)
    frequency = THETA_BASE ** (-2.0 * counter / HD)
    angles = positions.astype(jnp.float32)[:, None] * frequency[None, :]
    return (jnp.cos(angles), jnp.sin(angles))


def matmul(a, b):
    return jnp.dot(a, b, preferred_element_type=jnp.float32)


def matmul_right(a, b):
    return lax.dot_general(a, b, (((1,), (1,)), ((), ())), preferred_element_type=jnp.float32)


def matmul_left(a, b):
    return lax.dot_general(a, b, (((0,), (0,)), ((), ())), preferred_element_type=jnp.float32)


def per_device(
    tokens,
    cotangent,
    slot_order,
    attn_gain,
    q_gain,
    k_gain,
    w_qkv,
    w_out,
    mlp_gain,
    w_gate_up,
    w_down,
):
    member_count = lax.axis_size("group")
    member = lax.axis_index("group")
    micro, slot_len, width = tokens.shape
    rows = micro * slot_len
    length = slot_len * member_count
    q_width = HEADS * HD
    kv_width = KV_HEADS * HD
    groups = HEADS // KV_HEADS
    score_scale = 1.0 / math.sqrt(HD)
    key_block = math.gcd(length, 512)
    block_count = length // key_block
    head_gain_q = q_gain.astype(jnp.float32)
    head_gain_k = k_gain.astype(jnp.float32)
    offsets = jnp.arange(slot_len, dtype=jnp.int32)
    source = tokens.reshape(rows, width).astype(jnp.float32)
    all_pos = (slot_order[:, :, None] * slot_len + offsets[None, None, :]).reshape(micro, length)
    my_pos = lax.dynamic_slice_in_dim(all_pos, member * slot_len, slot_len, 1)
    query_top = jnp.max(my_pos, axis=1)
    cosines, sines = rope_tables(my_pos.reshape(rows))
    normed_first = norm_rows(source)
    gain_piece = lax.all_gather(attn_gain, "group", axis=0, tiled=True)
    weight_piece = lax.all_gather(w_qkv, "group", axis=0, tiled=True)
    columns = normed_first
    low_cols = (columns * gain_piece.astype(jnp.float32)).astype(jnp.bfloat16)
    qkv = matmul(low_cols, weight_piece)
    first_low = low_cols
    gain_first = gain_piece.astype(jnp.float32)
    queries = qkv[:, :q_width].reshape(rows, HEADS, HD)
    keys_raw = qkv[:, q_width : q_width + kv_width].reshape(rows, KV_HEADS, HD)
    values_low = qkv[:, q_width + kv_width :].astype(jnp.bfloat16)
    queries_normed = norm_rows(queries)
    keys_normed = norm_rows(keys_raw)
    query_rot = rotate(queries_normed * head_gain_q, cosines[:, None, :], sines[:, None, :]).astype(
        jnp.bfloat16
    )
    key_rot = rotate(keys_normed * head_gain_k, cosines[:, None, :], sines[:, None, :]).astype(
        jnp.bfloat16
    )
    key_all, value_all = (
        lax.all_gather(key_rot.reshape(micro, slot_len, kv_width), "group", axis=1, tiled=True),
        lax.all_gather(values_low.reshape(micro, slot_len, kv_width), "group", axis=1, tiled=True),
    )
    query_heads = query_rot.reshape(micro, slot_len, KV_HEADS, groups, HD)

    def block_live(block_index):
        key_pos = lax.dynamic_slice_in_dim(all_pos, block_index * key_block, key_block, 1)
        return jnp.any(jnp.min(key_pos, axis=1) <= query_top)

    def block_scores(block_index):
        begin = block_index * key_block
        key_piece = lax.dynamic_slice_in_dim(key_all, begin, key_block, 1).reshape(
            micro, key_block, KV_HEADS, HD
        )
        key_pos = lax.dynamic_slice_in_dim(all_pos, begin, key_block, 1)
        raw = (
            jnp.einsum(
                "mqkgd,mskd->mkgqs", query_heads, key_piece, preferred_element_type=jnp.float32
            )
            * score_scale
        )
        allowed = (key_pos[:, None, :] <= my_pos[:, :, None])[:, None, None]
        return (jnp.where(allowed, raw, MASKED), allowed, key_piece)

    def stats_step(block_index, carry):

        def stats_visit_block(carry_in):
            top_in, total_in = carry_in
            scores, allowed, key_piece = block_scores(block_index)
            new_top = jnp.maximum(top_in, jnp.max(scores, axis=-1))
            summed = jnp.sum(jnp.where(allowed, jnp.exp(scores - new_top[..., None]), 0.0), axis=-1)
            return (new_top, total_in * jnp.exp(top_in - new_top) + summed)

        return lax.cond(
            block_live(block_index), stats_visit_block, lambda carry_in: carry_in, carry
        )

    stat_shape = (micro, KV_HEADS, groups, slot_len)
    top_final, total_final = lax.fori_loop(
        0,
        block_count,
        stats_step,
        (jnp.full(stat_shape, MASKED, jnp.float32), jnp.zeros(stat_shape, jnp.float32)),
    )
    log_total = top_final + jnp.log(total_final)

    def output_step(block_index, accum):

        def output_visit_block(accum_in):
            scores, allowed, key_piece = block_scores(block_index)
            probabilities = jnp.where(allowed, jnp.exp(scores - log_total[..., None]), 0.0)
            value_piece = lax.dynamic_slice_in_dim(
                value_all, block_index * key_block, key_block, 1
            ).reshape(micro, key_block, KV_HEADS, HD)
            return accum_in + jnp.einsum(
                "mkgqs,mskd->mqkgd",
                probabilities.astype(jnp.bfloat16),
                value_piece,
                preferred_element_type=jnp.float32,
            )

        return lax.cond(
            block_live(block_index), output_visit_block, lambda accum_in: accum_in, accum
        )

    attn_heads = lax.fori_loop(
        0, block_count, output_step, jnp.zeros((micro, slot_len, KV_HEADS, groups, HD), jnp.float32)
    )
    attended = attn_heads.reshape(rows, q_width).astype(jnp.bfloat16)
    columns = attended
    branch = matmul(columns, lax.all_gather(w_out, "group", axis=0, tiled=True))
    middle = source + branch
    normed_second = norm_rows(middle)
    gain_piece = lax.all_gather(mlp_gain, "group", axis=0, tiled=True)
    weight_piece = lax.all_gather(w_gate_up, "group", axis=0, tiled=True)
    columns = normed_second
    low_cols = (columns * gain_piece.astype(jnp.float32)).astype(jnp.bfloat16)
    gate_up = matmul(low_cols, weight_piece)
    gain_second = gain_piece.astype(jnp.float32)
    gate_part = gate_up[:, :FF]
    up_part = gate_up[:, FF:]
    sigmoid_gate = jax.nn.sigmoid(gate_part)
    silu_gate = gate_part * sigmoid_gate
    hidden = (silu_gate * up_part).astype(jnp.bfloat16)
    columns = hidden
    down_out = matmul(columns, lax.all_gather(w_down, "group", axis=0, tiled=True))
    block_out = (middle + down_out).astype(jnp.bfloat16).reshape(micro, slot_len, width)
    grad_low = cotangent.reshape(rows, width)
    grad_output = grad_low.astype(jnp.float32)
    down_full = matmul_left(hidden, grad_low)
    grad_hidden = matmul_right(grad_low, lax.all_gather(w_down, "group", axis=0, tiled=True))
    grad_gate = grad_hidden * up_part * (sigmoid_gate * (1.0 + gate_part * (1.0 - sigmoid_gate)))
    grad_upper = grad_hidden * silu_gate
    grad_gate_up = jnp.concatenate([grad_gate, grad_upper], axis=1).astype(jnp.bfloat16)
    gate_up_full = matmul_left(low_cols, grad_gate_up)
    grad_second = matmul_right(grad_gate_up, lax.all_gather(w_gate_up, "group", axis=0, tiled=True))
    gain_second_full = jnp.sum(normed_second * grad_second, axis=0)
    grad_middle = grad_output + norm_back(middle, grad_second * gain_second)
    grad_mid_low = grad_middle.astype(jnp.bfloat16)
    out_full = matmul_left(attended, grad_mid_low)
    grad_attn_full = matmul_right(grad_mid_low, lax.all_gather(w_out, "group", axis=0, tiled=True))
    grad_attn = grad_attn_full.astype(jnp.bfloat16)
    grad_heads = grad_attn.reshape(micro, slot_len, KV_HEADS, groups, HD)
    delta = jnp.transpose(
        jnp.sum(grad_heads.astype(jnp.float32) * attn_heads, axis=-1), (0, 2, 3, 1)
    )

    def back_step(block_index, carry):

        def back_visit_block(carry_in):
            grad_query_in, grad_key_in, grad_value_in = carry_in
            begin = block_index * key_block
            scores, allowed, key_piece = block_scores(block_index)
            probabilities = jnp.where(allowed, jnp.exp(scores - log_total[..., None]), 0.0)
            value_piece = lax.dynamic_slice_in_dim(value_all, begin, key_block, 1).reshape(
                micro, key_block, KV_HEADS, HD
            )
            grad_probs = jnp.einsum(
                "mqkgd,mskd->mkgqs", grad_heads, value_piece, preferred_element_type=jnp.float32
            )
            grad_scores = (probabilities * (grad_probs - delta[..., None])).astype(jnp.bfloat16)
            grad_query_out = (
                grad_query_in
                + jnp.einsum(
                    "mkgqs,mskd->mqkgd", grad_scores, key_piece, preferred_element_type=jnp.float32
                )
                * score_scale
            )
            key_term = (
                jnp.einsum(
                    "mkgqs,mqkgd->mskd",
                    grad_scores,
                    query_heads,
                    preferred_element_type=jnp.float32,
                )
                * score_scale
            )
            value_term = jnp.einsum(
                "mkgqs,mqkgd->mskd",
                probabilities.astype(jnp.bfloat16),
                grad_heads,
                preferred_element_type=jnp.float32,
            )
            key_old = lax.dynamic_slice_in_dim(grad_key_in, begin, key_block, 1)
            value_old = lax.dynamic_slice_in_dim(grad_value_in, begin, key_block, 1)
            grad_key_out = lax.dynamic_update_slice_in_dim(
                grad_key_in, key_old + key_term, begin, 1
            )
            grad_value_out = lax.dynamic_update_slice_in_dim(
                grad_value_in, value_old + value_term, begin, 1
            )
            return (grad_query_out, grad_key_out, grad_value_out)

        return lax.cond(block_live(block_index), back_visit_block, lambda carry_in: carry_in, carry)

    back_start = (
        jnp.zeros((micro, slot_len, KV_HEADS, groups, HD), jnp.float32),
        jnp.zeros((micro, length, KV_HEADS, HD), jnp.float32),
        jnp.zeros((micro, length, KV_HEADS, HD), jnp.float32),
    )
    grad_query_rot, grad_key_all, grad_value_all = lax.fori_loop(
        0, block_count, back_step, back_start
    )
    grad_key_mine, grad_value_mine = (
        lax.psum_scatter(
            grad_key_all.reshape(micro, length, kv_width).astype(jnp.bfloat16),
            "group",
            scatter_dimension=1,
            tiled=True,
        ).astype(jnp.float32),
        lax.psum_scatter(
            grad_value_all.reshape(micro, length, kv_width).astype(jnp.bfloat16),
            "group",
            scatter_dimension=1,
            tiled=True,
        ).astype(jnp.float32),
    )
    grad_query_norm = rotate(
        grad_query_rot.reshape(rows, HEADS, HD), cosines[:, None, :], -sines[:, None, :]
    )
    grad_key_norm = rotate(
        grad_key_mine.reshape(rows, KV_HEADS, HD), cosines[:, None, :], -sines[:, None, :]
    )
    q_gain_total = jnp.sum(queries_normed * grad_query_norm, axis=(0, 1))
    k_gain_total = jnp.sum(keys_normed * grad_key_norm, axis=(0, 1))
    grad_queries = norm_back(queries, grad_query_norm * head_gain_q).reshape(rows, q_width)
    grad_keys = norm_back(keys_raw, grad_key_norm * head_gain_k).reshape(rows, kv_width)
    grad_qkv = jnp.concatenate(
        [grad_queries, grad_keys, grad_value_mine.reshape(rows, kv_width)], axis=1
    ).astype(jnp.bfloat16)
    qkv_full = matmul_left(first_low, grad_qkv)
    grad_first = matmul_right(grad_qkv, lax.all_gather(w_qkv, "group", axis=0, tiled=True))
    gain_first_full = jnp.sum(normed_first * grad_first, axis=0)
    input_grad = (
        (grad_middle + norm_back(source, grad_first * gain_first))
        .astype(jnp.bfloat16)
        .reshape(micro, slot_len, width)
    )
    owned = (
        lax.psum_scatter(
            gain_first_full.astype(jnp.bfloat16), "group", scatter_dimension=0, tiled=True
        ).astype(jnp.float32),
        lax.psum_scatter(
            qkv_full.astype(jnp.bfloat16), "group", scatter_dimension=0, tiled=True
        ).astype(jnp.float32),
        lax.psum_scatter(
            out_full.astype(jnp.bfloat16), "group", scatter_dimension=0, tiled=True
        ).astype(jnp.float32),
        lax.psum_scatter(
            gain_second_full.astype(jnp.bfloat16), "group", scatter_dimension=0, tiled=True
        ).astype(jnp.float32),
        lax.psum_scatter(
            gate_up_full.astype(jnp.bfloat16), "group", scatter_dimension=0, tiled=True
        ).astype(jnp.float32),
        lax.psum_scatter(
            down_full.astype(jnp.bfloat16), "group", scatter_dimension=0, tiled=True
        ).astype(jnp.float32),
    )
    summed = (
        lax.psum(owned[0].astype(jnp.bfloat16), "replica").astype(jnp.float32),
        lax.psum(owned[1].astype(jnp.bfloat16), "replica").astype(jnp.float32),
        lax.psum(owned[2].astype(jnp.bfloat16), "replica").astype(jnp.float32),
        lax.psum(owned[3].astype(jnp.bfloat16), "replica").astype(jnp.float32),
        lax.psum(owned[4].astype(jnp.bfloat16), "replica").astype(jnp.float32),
        lax.psum(owned[5].astype(jnp.bfloat16), "replica").astype(jnp.float32),
    )
    head_sums = lax.psum((q_gain_total, k_gain_total), ("group", "replica"))
    return (
        block_out,
        input_grad,
        summed[0],
        head_sums[0],
        head_sums[1],
        summed[1],
        summed[2],
        summed[3],
        summed[4],
        summed[5],
    )


MESH_ID = pl.DeviceIdType.MESH
HBM = pltpu.MemorySpace.HBM
VMEM_LIMIT = 64 * 1024 * 1024 - 65536
NZ = 4


class Place:
    def __init__(self):
        self.z = lax.axis_index("z")
        self.y = lax.axis_index("y")
        self.x = lax.axis_index("x")
        self.c = lax.axis_index("core")
        self.h = self.z // 2
        self.m = self.at(self.z)
        self.inner = {"z": self.at(self.m + 1)}
        self.outer = {"z": self.at(lax.rem(self.m + 3, 4))}
        self.across_x = {"x": 1 - self.x}
        self.across_y = {"y": 1 - self.y}
        self.partner = {"core": 1 - self.c}

    def at(self, t):
        return t * (1 - 2 * self.h) + 3 * self.h

    def greet(self):
        barrier = pltpu.get_barrier_semaphore()
        peers = [self.across_x, self.across_y, self.partner]
        for hop in range(1, NZ):
            there = lax.rem(self.z + hop, NZ)
            peers += [{"z": there}, {"z": there, "core": 1 - self.c}]
        for peer in peers:
            pl.semaphore_signal(barrier, inc=1, device_id=peer, device_id_type=MESH_ID)
        pl.semaphore_wait(barrier, len(peers))


def remote(src, dst, send, recv, peer):
    return pltpu.make_async_remote_copy(
        src_ref=src, dst_ref=dst, send_sem=send, recv_sem=recv, device_id=peer, device_id_type=MESH_ID
    )


KINDS = ("x", "y", "yx", "xy", "c", "cx", "cy", "cd")


def half_rows(ref, which):
    rows = ref.shape[0] // 2
    return ref.at[pl.ds(which * rows, rows), :]


class Gather:
    def __init__(self, me, shards, fulls, sems):
        self.me, self.shards, self.fulls = me, shards, fulls
        self.z_send, self.z_recv, self.f_send, self.xy_send, self.xy_recv = sems
        self.stage_t = (1 - me.m, 2, 3)
        self.stages = [(w, k) for w in range(len(shards)) for k in range(3)]

    def piece(self, c, x, y):
        return c * 4 + x * 2 + y

    def shard_z(self, k):
        return self.me.at(self.stage_t[k])

    def own(self, w, peer, k, slot):
        me = self.me
        piece = self.piece(me.c, me.x, me.y)
        return remote(
            self.shards[w].at[piece],
            self.fulls[w].at[me.z, piece],
            self.z_send.at[w, slot],
            self.z_recv.at[w, k],
            peer,
        )

    def send_own(self, w):
        me = self.me
        self.own(w, me.inner, me.m, 0).start()

        @pl.when(me.m == 1)
        def _():
            self.own(w, me.outer, 0, 1).start()

    def place(self, w, k, cc, xx, yy):
        return self.fulls[w].at[self.shard_z(k), self.piece(cc, xx, yy)]

    def forward(self, w, k):
        me = self.me
        piece = self.place(w, k, me.c, me.x, me.y)
        peer, slot = ((me.inner, 2), (me.outer, 1), (me.outer, 2))[k]
        return remote(piece, piece, self.f_send.at[w, k], self.z_recv.at[w, slot], peer)

    def hop(self, w, k, kind):
        me = self.me
        c, x, y = me.c, me.x, me.y
        mine, px = self.place(w, k, c, x, y), self.place(w, k, c, 1 - x, y)
        py, pd = self.place(w, k, c, x, 1 - y), self.place(w, k, c, 1 - x, 1 - y)
        src, peer = {
            "x": (mine, me.across_x),
            "y": (mine, me.across_y),
            "yx": (half_rows(px, 0), me.across_y),
            "xy": (half_rows(py, 1), me.across_x),
            "c": (mine, me.partner),
            "cx": (px, me.partner),
            "cy": (py, me.partner),
            "cd": (pd, me.partner),
        }[kind]
        index = KINDS.index(kind)
        return remote(src, src, self.xy_send.at[w, k, index], self.xy_recv.at[w, k, index], peer)

    def arrived(self, w, k, kind):
        me = self.me
        c, x, y = me.c, me.x, me.y
        dst = {
            "x": lambda: self.place(w, k, c, 1 - x, y),
            "y": lambda: self.place(w, k, c, x, 1 - y),
            "yx": lambda: half_rows(self.place(w, k, c, 1 - x, 1 - y), 0),
            "xy": lambda: half_rows(self.place(w, k, c, 1 - x, 1 - y), 1),
            "c": lambda: self.place(w, k, 1 - c, x, y),
            "cx": lambda: self.place(w, k, 1 - c, 1 - x, y),
            "cy": lambda: self.place(w, k, 1 - c, x, 1 - y),
            "cd": lambda: self.place(w, k, 1 - c, 1 - x, 1 - y),
        }[kind]()
        index = KINDS.index(kind)
        remote(dst, dst, self.xy_send.at[w, k, index], self.xy_recv.at[w, k, index], me.partner).wait_recv()

    def first(self, i):
        w, k = self.stages[i]
        me = self.me
        mine = self.place(w, k, me.c, me.x, me.y)
        remote(mine, mine, self.f_send.at[w, k], self.z_recv.at[w, k], me.partner).wait_recv()

        @pl.when(me.m == 1)
        def _():
            self.forward(w, k).start()

        if k == 1 and w + 1 < len(self.shards):
            self.send_own(w + 1)
        for kind in ("x", "y", "c"):
            self.hop(w, k, kind).start()

    def second(self, i):
        w, k = self.stages[i]
        self.arrived(w, k, "x")
        self.hop(w, k, "yx").start()
        self.hop(w, k, "cx").start()
        self.arrived(w, k, "y")
        self.hop(w, k, "xy").start()
        self.hop(w, k, "cy").start()

    def third(self, i):
        w, k = self.stages[i]
        self.arrived(w, k, "yx")
        self.arrived(w, k, "xy")
        self.hop(w, k, "cd").start()

    def step(self, i):
        total = len(self.stages)
        if i < total:
            self.first(i)
        if 0 <= i - 3 < total:
            self.third(i - 3)
        if 0 <= i - 2 < total:
            self.second(i - 2)

    def require(self, w, k):
        for kind in ("c", "cx", "cy", "cd"):
            self.arrived(w, k, kind)

    def finish(self):
        me = self.me
        for w, k in self.stages:
            for kind in KINDS:
                self.hop(w, k, kind).wait_send()
        for w in range(len(self.shards)):
            self.own(w, me.inner, me.m, 0).wait_send()

            @pl.when(me.m == 1)
            def _(w=w):
                self.own(w, me.outer, 0, 1).wait_send()
                for k in range(3):
                    self.forward(w, k).wait_send()


class Route:
    def __init__(self, me):
        z, c = me.z, me.c
        odd = lax.rem(z, 2)
        self.stays = z // 2 == c
        self.order = (odd, 1 - odd)
        self.to = ({"z": 2 * c + odd, "core": z // 2}, {"z": 2 * c + 1 - odd, "core": z // 2})
        self.back_to = self.to
        self.back_at = odd

    def start(self, copies):
        first_local, first, second = copies

        @pl.when(self.stays)
        def _():
            first_local.start()

        @pl.when(jnp.logical_not(self.stays))
        def _():
            first.start()

        second.start()

    def out(self, held, there, sems):
        a, b = self.order
        return (
            pltpu.make_async_copy(held.at[a], there.at[0], sems.at[0]),
            remote(held.at[a], there.at[0], sems.at[1], sems.at[2], self.to[0]),
            remote(held.at[b], there.at[1], sems.at[3], sems.at[4], self.to[1]),
        )

    def wait(self, copies):
        first_local, first, second = copies

        @pl.when(self.stays)
        def _():
            first_local.wait()

        @pl.when(jnp.logical_not(self.stays))
        def _():
            first.wait()

        second.wait()


def turn(v):
    return pltpu.roll(v, HD // 2, 1)


def stacked(two_heads):
    return jnp.concatenate([two_heads[:, :HD], two_heads[:, HD:]], axis=0)


def pick(which, values):
    out = values[0]
    for i in range(1, len(values)):
        out = jnp.where(which == i, values[i], out)
    return out


def row_loop(rows, step, body):
    def run(i, carry):
        body(pl.ds(pl.multiple_of(i * step, step), step))
        return carry

    lax.fori_loop(0, rows // step, run, 0)


PER_HEAD = 4 * HD
HALF_HEADS = KV_HEADS // 2
BLOCKS = 4
COUNT = 4


def forward_kernel(scalars, gains, head_gains, cosines, sines, tokens, cotangent, *refs):
    shards = refs[:COUNT]
    (
        block_out,
        gains_all,
        source,
        grad,
        h1_out,
        raw_out,
        tok_out,
        probs_out,
        attended_out,
        middle_out,
        h2_out,
        gate_up_out,
    ) = refs[COUNT : COUNT + 12]
    fulls = refs[COUNT + 12 : 2 * COUNT + 12]
    (
        acc,
        acc_small,
        wide,
        narrow,
        x,
        h1,
        h2,
        tok,
        outgoing,
        raw,
        p0,
        p1,
        p2,
        p3,
        ordered,
        mixed,
        mixed_out,
        attended,
        middle,
        hidden,
        gate_up,
        low_out,
        z_send,
        z_recv,
        f_send,
        xy_send,
        xy_recv,
        load_sem,
        keep_sem,
        gain_sem,
        token_sem,
        cot_sem,
        swap_sem,
        save_sem,
        prob_sem,
        gate_sem,
    ) = refs[2 * COUNT + 12 :]
    prob_slots = (p0, p1, p2, p3)
    low, f32 = jnp.bfloat16, jnp.float32
    me = Place()
    z, c = me.z, me.c
    rows, width = x.shape
    block = rows // 2
    comm = Gather(me, shards, fulls, (z_send, z_recv, f_send, xy_send, xy_recv))
    route = Route(me)
    me.greet()
    comm.send_own(0)
    gain_copies = []
    for j in range(1, NZ):
        there = {"z": lax.rem(z + j, NZ)}
        gain_copies.append(remote(gains, gains_all.at[z], gain_sem.at[0, j], gain_sem.at[1, j], there))
    for copy in gain_copies:
        copy.start()
    gains_all[pl.ds(z, 1)] = gains[...][None]
    token_copies = route.out(tokens, source, token_sem)
    cot_copies = route.out(cotangent, grad, cot_sem)

    def buffer(w, kk):
        if w in (0, 2):
            return wide.at[kk % 2, :, :, pl.ds(0, shards[w].shape[2])]
        return narrow.at[kk % 2, :, pl.ds(0, shards[w].shape[1]), :]

    def load(w, kk):
        src = shards[w] if kk == 0 else fulls[w].at[comm.shard_z(kk - 1)]
        return pltpu.make_async_copy(src, buffer(w, kk), load_sem.at[w, kk])

    def keep(w):
        return pltpu.make_async_copy(buffer(w, 0), fulls[w].at[z], keep_sem.at[w])

    def chunk(w, kk, lhs, out, tile):
        depth = 8 * shards[w].shape[1]
        columns = shards[w].shape[2]
        own_z = z if kk == 0 else comm.shard_z(kk - 1)
        if kk > 0:
            comm.require(w, kk - 1)
            if kk == 2:
                keep(w).wait()
            load(w, kk).start()
        load(w, kk).wait()
        if kk == 0:
            keep(w).start()
        left = lhs[:, pl.ds(pl.multiple_of(own_z * depth, depth), depth)]
        weight = buffer(w, kk)

        def body(i, carry):
            at = pl.ds(pl.multiple_of(i * tile, tile), tile)
            right = weight[:, :, at].reshape(depth, tile)
            part = jnp.dot(left, right, preferred_element_type=f32)
            if kk == 0:
                out[:, at] = part
            else:
                out[:, at] += part
            return carry

        lax.fori_loop(0, columns // tile, body, 0)

    def save(i, src, dst):
        return pltpu.make_async_copy(src, dst, save_sem.at[i])

    load(0, 0).start()
    load(1, 0).start()
    comm.step(0)
    comm.step(1)
    comm.first(2)
    route.start(token_copies)
    comm.second(0)
    comm.first(3)
    comm.third(0)
    comm.second(1)
    comm.third(1)
    comm.second(2)
    comm.third(2)
    for j in range(1, NZ):
        gain_copies[j - 1].wait_send()
        there = gains_all.at[lax.rem(z + NZ - j, NZ)]
        remote(gains, there, gain_sem.at[0, j], gain_sem.at[1, j], me.partner).wait_recv()
    route.wait(token_copies)
    for part in range(2):
        pltpu.make_async_copy(source.at[part], x.at[pl.ds(part * block, block)], token_sem.at[5 + part]).start()
    for part in range(2):
        pltpu.make_async_copy(source.at[part], x.at[pl.ds(part * block, block)], token_sem.at[5 + part]).wait()

    def normed_times(v, index):
        v = v * lax.rsqrt(jnp.mean(v * v, axis=-1, keepdims=True) + EPSILON)
        gain = jnp.concatenate([gains_all[s, index : index + 1, :] for s in range(NZ)], axis=1)
        return (v * gain).astype(low)

    def first_norm(at):
        h1[at, :] = normed_times(x[at, :].astype(f32), 0)

    row_loop(rows, 64, first_norm)
    save(0, h1, h1_out).start()
    comm.first(4)
    chunk(0, 0, h1, acc, 512)
    chunk(0, 1, h1, acc, 512)
    comm.first(5)
    comm.second(3)
    chunk(0, 2, h1, acc, 512)
    comm.third(3)
    comm.second(4)
    chunk(0, 3, h1, acc, 512)
    load(2, 0).start()
    comm.first(6)
    comm.third(4)

    def head(h, target, column):
        parts = []
        for start, size in ((h * 2 * HD, 2 * HD), ((HEADS + h) * HD, HD), ((HEADS + KV_HEADS + h) * HD, HD)):
            parts.append(acc[:, pl.ds(pl.multiple_of(start, HD), size)])
        half, at = h // HALF_HEADS, pl.multiple_of(lax.rem(h, HALF_HEADS) * PER_HEAD, PER_HEAD)
        for i, (v, gain_row) in enumerate(((parts[0][:, :HD], 0), (parts[0][:, HD:], 0), (parts[1], 1))):
            raw[half, :, pl.ds(pl.multiple_of(at + i * HD, HD), HD)] = v.astype(low)
            v = v * lax.rsqrt(jnp.mean(v * v, axis=-1, keepdims=True) + EPSILON)
            v = v * head_gains[gain_row : gain_row + 1, :]
            v = (v * cosines[...] + turn(v) * sines[...]).astype(low)
            for j in range(2):
                target[j, :, pl.ds(pl.multiple_of(column + i * HD, HD), HD)] = v[j * block : (j + 1) * block]
        v = parts[2].astype(low)
        for j in range(2):
            target[j, :, pl.ds(pl.multiple_of(column + 3 * HD, HD), HD)] = v[j * block : (j + 1) * block]

    def other_head(i, carry):
        head(i + HALF_HEADS * (1 - c), outgoing, i * PER_HEAD)
        return carry

    def own_head(i, carry):
        head(i + HALF_HEADS * c, tok, i * PER_HEAD)
        return carry

    lax.fori_loop(0, HALF_HEADS, other_head, 0)
    swap_out = remote(outgoing, tok.at[pl.ds(2, 2)], swap_sem.at[0], swap_sem.at[1], me.partner)
    comm.first(7)
    swap_out.start()
    lax.fori_loop(0, HALF_HEADS, own_head, 0)
    save(1, raw, raw_out).start()
    comm.second(5)
    comm.third(5)
    swap_out.wait()
    save(2, tok, tok_out).start()

    scale = 1.0 / math.sqrt(HD)
    above = lax.rem(lax.broadcasted_iota(jnp.int32, (2 * block, block), 0), block)
    above = above < lax.broadcasted_iota(jnp.int32, (2 * block, block), 1)

    def save_probs(h, i):
        n = (i + 1) * block
        column = i * (i + 1) // 2 * block
        return pltpu.make_async_copy(prob_slots[i], probs_out.at[h, :, pl.ds(column, n)], prob_sem.at[i])

    def attend(h, carry):
        at = pl.multiple_of(h * PER_HEAD, PER_HEAD)
        for i in range(BLOCKS):
            ordered[i * block : (i + 1) * block] = pick(
                scalars[i], [tok[j, :, pl.ds(at, PER_HEAD)] for j in range(BLOCKS)]
            )
        for i in range(BLOCKS):
            n = (i + 1) * block
            query = stacked(ordered[i * block : n, : 2 * HD])
            keys, values = ordered[:n, 2 * HD : 3 * HD], ordered[:n, 3 * HD :]
            scores = lax.dot_general(query, keys, (((1,), (1,)), ((), ())), preferred_element_type=f32)
            last = jnp.where(above, MASKED, scores[:, i * block :])
            scores = last if i == 0 else jnp.concatenate([scores[:, : i * block], last], axis=1)
            top = jnp.max(scores, axis=-1, keepdims=True)
            weights = jnp.exp((scores - top) * scale)
            weights = weights * (1.0 / jnp.sum(weights, axis=-1, keepdims=True))
            probs = weights.astype(low)

            @pl.when(h > 0)
            def _():
                save_probs(h - 1, i).wait()

            prob_slots[i][...] = probs
            save_probs(h, i).start()
            out = jnp.dot(probs, values, preferred_element_type=f32).astype(low)
            there = pl.multiple_of(h * 2 * HD, 2 * HD)
            mixed[i * block : (i + 1) * block, pl.ds(there, HD)] = out[:block]
            mixed[i * block : (i + 1) * block, pl.ds(pl.multiple_of(there + HD, HD), HD)] = out[block:]
            for now, steps in ATTEND_STEPS.items():
                if now[1] == i:

                    @pl.when(h == now[0])
                    def _(steps=steps):
                        for name, index in steps:
                            getattr(comm, name)(index)

        return carry

    lax.fori_loop(0, HALF_HEADS, attend, 0)
    half = HEADS * HD // 2
    mine = pl.ds(pl.multiple_of(c * half, half), half)
    for j in range(2):
        blocks = [mixed[i * block : (i + 1) * block] for i in range(BLOCKS)]
        mixed_out[j * block : (j + 1) * block] = pick(scalars[BLOCKS + 2 + j], blocks)
    for j in range(2):
        blocks = [mixed[i * block : (i + 1) * block] for i in range(BLOCKS)]
        attended[j * block : (j + 1) * block, mine] = pick(scalars[BLOCKS + j], blocks)
    mixed_swap = remote(mixed_out, attended.at[:, mine], swap_sem.at[2], swap_sem.at[3], me.partner)
    mixed_swap.start()
    for i in range(BLOCKS):
        save_probs(HALF_HEADS - 1, i).wait()
    mixed_swap.wait()
    save(3, attended, attended_out).start()
    for kk in range(4):
        chunk(1, kk, attended, acc_small, 512)
    load(3, 0).start()

    def second_norm(at):
        v = x[at, :].astype(f32) + acc_small[at, :]
        middle[at, :] = v
        h2[at, :] = normed_times(v, 1)

    row_loop(rows, 64, second_norm)
    save(4, middle, middle_out).start()
    save(5, h2, h2_out).start()
    chunk(2, 0, h2, acc, 512)
    chunk(2, 1, h2, acc, 512)
    comm.first(10)
    comm.third(7)
    comm.second(8)
    route.start(cot_copies)
    chunk(2, 2, h2, acc, 512)
    comm.first(11)
    comm.third(8)
    comm.second(9)
    chunk(2, 3, h2, acc, 512)
    comm.third(9)
    comm.second(10)

    def save_gate_up(i, part, slot):
        at = pl.multiple_of(part * FF + i * 512, 512)
        return pltpu.make_async_copy(gate_up.at[slot, part], gate_up_out.at[:, pl.ds(at, 512)], gate_sem.at[slot, part])

    def activate(i, carry):
        slot = lax.rem(i, 2)
        at = pl.multiple_of(i * 512, 512)

        @pl.when(i >= 2)
        def _():
            for part in range(2):
                save_gate_up(i - 2, part, slot).wait()

        gate = acc[:, pl.ds(at, 512)]
        up = acc[:, pl.ds(pl.multiple_of(FF + at, 512), 512)]
        gate_up[slot, 0] = gate.astype(low)
        gate_up[slot, 1] = up.astype(low)
        hidden[:, pl.ds(at, 512)] = (gate * jax.nn.sigmoid(gate) * up).astype(low)
        for part in range(2):
            save_gate_up(i, part, slot).start()
        return carry

    tiles = FF // 512
    lax.fori_loop(0, tiles, activate, 0)
    chunk(3, 0, hidden, acc_small, 512)
    chunk(3, 1, hidden, acc_small, 512)
    comm.third(10)
    comm.second(11)
    chunk(3, 2, hidden, acc_small, 512)
    comm.third(11)
    chunk(3, 3, hidden, acc_small, 512)

    def final(at):
        low_out[at, :] = (middle[at, :] + acc_small[at, :]).astype(low)

    row_loop(rows, 64, final)
    save(6, low_out, block_out).start()
    comm.finish()
    for slot in range(2):
        for part in range(2):
            save_gate_up(tiles - 2 + slot, part, slot).wait()
    for i, (src, dst) in enumerate(
        (
            (h1, h1_out),
            (raw, raw_out),
            (tok, tok_out),
            (attended, attended_out),
            (middle, middle_out),
            (h2, h2_out),
            (low_out, block_out),
        )
    ):
        save(i, src, dst).wait()
    route.wait(cot_copies)


ATTEND_STEPS = {
    (1, 0): (("first", 8), ("second", 6)),
    (2, 0): (("third", 6),),
    (3, 1): (("first", 9), ("second", 7)),
}


def run_forward(scalars, gains, head_gains, cosines, sines, tokens, cotangent, shards):
    low, f32 = jnp.bfloat16, jnp.float32
    _, slot_len, width = tokens.shape
    rows = 2 * slot_len
    cut = [s.reshape(8, s.shape[0] // 8, s.shape[1]) for s in shards]
    area = slot_len * BLOCKS * (BLOCKS + 1) // 2
    shape = jax.ShapeDtypeStruct
    outs = [
        shape((rows, width), low),
        shape((NZ, *gains.shape), f32),
        shape((2, slot_len, width), low),
        shape((2, slot_len, width), low),
        shape((rows, width), low),
        shape((2, rows, HALF_HEADS * PER_HEAD), low),
        shape((4, slot_len, HALF_HEADS * PER_HEAD), low),
        shape((HALF_HEADS, 2 * slot_len, area), low),
        shape((rows, HEADS * HD), low),
        shape((rows, width), f32),
        shape((rows, width), low),
        shape((rows, 2 * FF), low),
    ] + [shape((NZ, *s.shape), low) for s in cut]
    hbm = pl.BlockSpec(memory_space=HBM)
    vmem = pl.BlockSpec(memory_space=pltpu.VMEM)
    dma = pltpu.SemaphoreType.DMA
    out = pl.pallas_call(
        forward_kernel,
        out_shape=outs,
        in_specs=[pl.BlockSpec(memory_space=pltpu.SMEM)] + [vmem] * 4 + [hbm] * (2 + COUNT),
        out_specs=[hbm, vmem] + [hbm] * (10 + COUNT),
        scratch_shapes=[
            pltpu.VMEM((rows, 2 * FF), f32),
            pltpu.VMEM((rows, width), f32),
            pltpu.VMEM((2, 8, cut[2].shape[1], 2 * FF), low),
            pltpu.VMEM((2, 8, cut[3].shape[1], width), low),
            pltpu.VMEM((rows, width), low),
            pltpu.VMEM((rows, width), low),
            pltpu.VMEM((rows, width), low),
            pltpu.VMEM((4, slot_len, HALF_HEADS * PER_HEAD), low),
            pltpu.VMEM((2, slot_len, HALF_HEADS * PER_HEAD), low),
            pltpu.VMEM((2, rows, HALF_HEADS * PER_HEAD), low),
        ]
        + [pltpu.VMEM((2 * slot_len, (i + 1) * slot_len), low) for i in range(BLOCKS)]
        + [
            pltpu.VMEM((4 * slot_len, PER_HEAD), low),
            pltpu.VMEM((4 * slot_len, HEADS * HD // 2), low),
            pltpu.VMEM((rows, HEADS * HD // 2), low),
            pltpu.VMEM((rows, HEADS * HD), low),
            pltpu.VMEM((rows, width), f32),
            pltpu.VMEM((rows, FF), low),
            pltpu.VMEM((2, 2, rows, 512), low),
            pltpu.VMEM((rows, width), low),
            dma((COUNT, 2)),
            dma((COUNT, 3)),
            dma((COUNT, 3)),
            dma((COUNT, 3, len(KINDS))),
            dma((COUNT, 3, len(KINDS))),
            dma((COUNT, 4)),
            dma((COUNT,)),
            dma((2, NZ)),
            dma((7,)),
            dma((5,)),
            dma((4,)),
            dma((7,)),
            dma((BLOCKS,)),
            dma((2, 2)),
        ],
        compiler_params=pltpu.CompilerParams(collective_id=0, has_side_effects=True, vmem_limit_bytes=VMEM_LIMIT),
        name="forward",
    )(scalars, gains, head_gains, cosines, sines, tokens, cotangent, *cut)
    return out[:12], [f.reshape(NZ * s.shape[0], s.shape[1]) for f, s in zip(out[12:], shards)]


def add_rows(dst, src, rows):
    def body(i, carry):
        at = pl.ds(pl.multiple_of(i * 16, 16), 16)
        total = dst[at, :].astype(jnp.float32) + src[at, :].astype(jnp.float32)
        dst[at, :] = total.astype(dst.dtype)
        return carry

    lax.fori_loop(0, rows // 16, body, 0)


SPREAD = ("x", "y", "yx", "xy", "c", "cx", "cy", "cd")


def reduce_kernel(shapes, small, *refs):
    count = len(shapes)
    pairs = refs[: 2 * count]
    small_out = refs[2 * count]
    outs = refs[2 * count + 1 : 3 * count + 1]
    rest = refs[3 * count + 1 :]
    lhs, rhs, stage, acc, rx1, ry1, rx2, ry2, rz = (rest[i * count : (i + 1) * count] for i in range(9))
    rest = rest[9 * count :]
    turned, small_mid, small_got, small_z = rest[:4]
    load_sem, keep_sem, c_send, c_recv, r_send, r_recv, z_send, z_recv, o_send, o_recv, s_send, s_recv = rest[4:]
    me = Place()
    z, y, x, c, m = me.z, me.y, me.x, me.c, me.m
    stage_t = (3, 2, 1 - m, m)
    chunks = [(w, k) for w in range(count) for k in range(4)]
    loads = [
        pltpu.make_async_copy(pairs[2 * w + i], (lhs[w], rhs[w])[i], load_sem.at[w, i])
        for w in range(count)
        for i in range(2)
    ]
    for load in loads:
        load.start()
    me.greet()

    def zk(k):
        return me.at(stage_t[k])

    def product(n, columns, store):
        w, k = chunks[n]
        rows = shapes[w][0]
        half = shapes[w][1] // 2
        tile = min(half, 512)

        def body(i, carry):
            at = pl.multiple_of(i * tile, tile)
            part = jnp.dot(
                turned[n % 2, :rows],
                rhs[w][:, pl.ds(pl.multiple_of(columns * half + at, tile), tile)],
                preferred_element_type=jnp.float32,
            )
            store(part, pl.ds(at, tile))
            return carry

        lax.fori_loop(0, half // tile, body, 0)

    def to_partner(w, k):
        return remote(stage[w], acc[w].at[zk(k)], c_send.at[w, k], c_recv.at[w, k], me.partner)

    def prepare(n):
        w, k = chunks[n]
        rows = shapes[w][0]
        if k == 0:
            loads[2 * w].wait()
            loads[2 * w + 1].wait()
        else:
            to_partner(w, k - 1).wait_send()
        at = pl.multiple_of(zk(k) * rows, rows)
        turned[n % 2, :rows] = jnp.transpose(lhs[w][:, pl.ds(at, rows)])

        def store(part, at):
            stage[w][:, :, :, at] = part.astype(jnp.bfloat16).reshape(2, 2, rows // 4, part.shape[1])

        product(n, 1 - c, store)

    def exchange(w, k, kind):
        a = acc[w].at[zk(k)]
        half = a.shape[-1] // 2
        lo, hi = pl.ds(0, half), pl.ds(half, half)
        src, dst, peer = {
            "x1": lambda: (a.at[1 - x, :, :, lo], rx1[w].at[k], me.across_x),
            "y1": lambda: (a.at[:, 1 - y, :, hi], ry1[w].at[k], me.across_y),
            "y2": lambda: (a.at[x, 1 - y, :, lo], ry2[w].at[k], me.across_y),
            "x2": lambda: (a.at[1 - x, y, :, hi], rx2[w].at[k], me.across_x),
        }[kind]()
        index = ("x1", "y1", "y2", "x2").index(kind)
        return remote(src, dst, r_send.at[w, k, index], r_recv.at[w, k, index], peer)

    def along(w, k, slot, peer):
        return remote(acc[w].at[zk(k), x, y], rz[w].at[slot], z_send.at[w, k], z_recv.at[w, slot], peer)

    def z_arrived(w, slot):
        there = rz[w].at[slot]
        remote(there, there, z_send.at[w, 0], z_recv.at[w, slot], me.partner).wait_recv()

    def s0(n):
        w, k = chunks[n]
        rows = shapes[w][0]
        a = acc[w].at[zk(k)]
        to_partner(w, k).wait_recv()

        def store(part, at):
            got = a[:, :, :, at].astype(jnp.float32)
            a[:, :, :, at] = (part.reshape(got.shape) + got).astype(jnp.bfloat16)

        product(n, c, store)

    def s0_send(n):
        w, k = chunks[n]
        exchange(w, k, "x1").start()
        exchange(w, k, "y1").start()

    def s1(n):
        w, k = chunks[n]
        a = acc[w].at[zk(k)]
        rows, half = a.shape[2], a.shape[3] // 2
        exchange(w, k, "x1").wait_recv()
        for j in range(2):
            add_rows(a.at[x, j, :, pl.ds(0, half)], rx1[w].at[k, j], rows)
        exchange(w, k, "y1").wait_recv()
        for i in range(2):
            add_rows(a.at[i, y, :, pl.ds(half, half)], ry1[w].at[k, i], rows)
        exchange(w, k, "y2").start()
        exchange(w, k, "x2").start()

    def s2(n):
        w, k = chunks[n]
        a = acc[w].at[zk(k), x, y]
        rows, half = a.shape[0], a.shape[1] // 2
        exchange(w, k, "y2").wait_recv()
        add_rows(a.at[:, pl.ds(0, half)], ry2[w].at[k], rows)
        exchange(w, k, "x2").wait_recv()
        add_rows(a.at[:, pl.ds(half, half)], rx2[w].at[k], rows)

    def s3(n):
        w, k = chunks[n]
        a = acc[w].at[zk(k), x, y]
        rows = a.shape[0]

        def take(slot):
            z_arrived(w, slot)
            add_rows(a, rz[w].at[slot], rows)

        @pl.when(m == 0)
        def _():
            if k < 3:
                along(w, k, k, me.inner).start()
            else:
                take(0)

        @pl.when(m == 1)
        def _():
            if k == 0:
                take(0)
                along(w, k, 3, me.inner).start()
            elif k == 1:
                take(1)
                along(w, k, 4, me.inner).start()
            elif k == 2:
                take(3)
                along(w, k, 0, me.outer).start()
            else:
                take(2)
                take(4)

    def out_at(w, cc, xx, yy):
        half = shapes[w][1] // 2
        return outs[w].at[xx, yy, :, pl.ds(pl.multiple_of(cc * half, half), half)]

    def half_of(ref, which):
        rows = ref.shape[0] // 2
        return ref.at[pl.ds(which * rows, rows), :]

    def keep(w):
        return pltpu.make_async_copy(acc[w].at[z, x, y], out_at(w, c, x, y), keep_sem.at[w])

    def spread(w, kind):
        final, mine = acc[w].at[z, x, y], out_at(w, c, x, y)
        px, py, pd = out_at(w, c, 1 - x, y), out_at(w, c, x, 1 - y), out_at(w, c, 1 - x, 1 - y)
        src, dst, peer = {
            "x": (final, mine, me.across_x),
            "y": (final, mine, me.across_y),
            "c": (final, mine, me.partner),
            "yx": (half_of(px, 0), half_of(px, 0), me.across_y),
            "xy": (half_of(py, 1), half_of(py, 1), me.across_x),
            "cx": (px, px, me.partner),
            "cy": (py, py, me.partner),
            "cd": (pd, pd, me.partner),
        }[kind]
        index = SPREAD.index(kind)
        return remote(src, dst, o_send.at[w, index], o_recv.at[w, index], peer)

    def spread_arrived(w, kind):
        dst = {
            "x": lambda: out_at(w, c, 1 - x, y),
            "y": lambda: out_at(w, c, x, 1 - y),
            "yx": lambda: half_of(out_at(w, c, 1 - x, 1 - y), 0),
            "xy": lambda: half_of(out_at(w, c, 1 - x, 1 - y), 1),
            "c": lambda: out_at(w, 1 - c, x, y),
            "cx": lambda: out_at(w, 1 - c, 1 - x, y),
            "cy": lambda: out_at(w, 1 - c, x, 1 - y),
            "cd": lambda: out_at(w, 1 - c, 1 - x, 1 - y),
        }[kind]()
        index = SPREAD.index(kind)
        remote(dst, dst, o_send.at[w, index], o_recv.at[w, index], me.partner).wait_recv()

    def s4(w):
        keep(w).start()
        for kind in ("x", "y", "c"):
            spread(w, kind).start()

    def s5(w):
        spread_arrived(w, "x")
        spread(w, "yx").start()
        spread(w, "cx").start()
        spread_arrived(w, "y")
        spread(w, "xy").start()
        spread(w, "cy").start()

    def s6(w):
        spread_arrived(w, "yx")
        spread_arrived(w, "xy")
        spread(w, "cd").start()

    small_peers = (me.partner, me.across_x, me.across_y)

    def small_copy(step):
        return remote(small_mid.at[step], small_got.at[step], s_send.at[step], s_recv.at[step], small_peers[step])

    def small_along(j):
        return remote(
            small_mid.at[3], small_z.at[z], s_send.at[3 + j], s_recv.at[3 + j], {"z": lax.rem(z + 1 + j, NZ)}
        )

    def small_step(n):
        if n == 0:
            small_mid[0] = small[...]
        elif n in (1, 3, 5):
            small_copy(n // 2).start()
        elif n in (2, 4, 6):
            step = n // 2 - 1
            small_copy(step).wait()
            small_mid[step + 1] = small_mid[step] + small_got[step]
        elif n == 7:
            for j in range(3):
                small_along(j).start()
        elif n == 8:
            for j in range(3):
                small_along(j).wait_send()
                there = small_z.at[lax.rem(z + 3 - j, NZ)]
                remote(there, there, s_send.at[3 + j], s_recv.at[3 + j], me.partner).wait_recv()
            small_z[pl.ds(z, 1)] = small_mid[pl.ds(3, 1)]
            small_out[...] = (small_z[0] + small_z[1]) + (small_z[2] + small_z[3])

    total = len(chunks)
    prepare(0)
    to_partner(*chunks[0]).start()
    for n in range(total + 6):
        if n + 1 < total:
            prepare(n + 1)
        if n < total:
            s0(n)
        if n + 1 < total:
            to_partner(*chunks[n + 1]).start()
        if n < total:
            s0_send(n)
        if 0 <= n - 1 < total:
            s1(n - 1)
        if 0 <= n - 2 < total:
            s2(n - 2)
        if 0 <= n - 3 < total:
            s3(n - 3)
            if chunks[n - 3][1] == 3:
                s4(chunks[n - 3][0])
        if 0 <= n - 4 < total and chunks[n - 4][1] == 3:
            s5(chunks[n - 4][0])
        if 0 <= n - 5 < total and chunks[n - 5][1] == 3:
            s6(chunks[n - 5][0])
        if n < 9:
            small_step(n)
    for w, k in chunks:
        if k == 3:
            to_partner(w, k).wait_send()
        for kind in ("x1", "y1", "y2", "x2"):
            exchange(w, k, kind).wait_send()
        if k < 3:
            along(w, k, k, me.inner).wait_send()
    for w in range(count):
        keep(w).wait()
        for kind in SPREAD:
            spread(w, kind).wait_send()
        for kind in ("c", "cx", "cy", "cd"):
            spread_arrived(w, kind)


def reduce_gradients(small, pairs):
    count = len(pairs)
    low = jnp.bfloat16
    shapes = [(a.shape[1] // NZ, b.shape[1]) for a, b in pairs]
    tokens = pairs[0][0].shape[0]
    deepest = max(r for r, _ in shapes)

    def buffers(make):
        return [pltpu.VMEM(make(r // 4, n // 2), low) for r, n in shapes]

    dma = pltpu.SemaphoreType.DMA
    out = pl.pallas_call(
        functools.partial(reduce_kernel, shapes),
        out_shape=[jax.ShapeDtypeStruct(small.shape, jnp.float32)]
        + [jax.ShapeDtypeStruct((2, 2, r // 4, n), low) for r, n in shapes],
        in_specs=[pl.BlockSpec(memory_space=pltpu.VMEM)] + [pl.BlockSpec(memory_space=HBM)] * (2 * count),
        out_specs=[pl.BlockSpec(memory_space=pltpu.VMEM)] + [pl.BlockSpec(memory_space=HBM)] * count,
        scratch_shapes=[pltpu.VMEM(a.shape, low) for a, _ in pairs]
        + [pltpu.VMEM(b.shape, low) for _, b in pairs]
        + buffers(lambda r, n: (2, 2, r, n))
        + buffers(lambda r, n: (NZ, 2, 2, r, n))
        + buffers(lambda r, n: (NZ, 2, r, n // 2))
        + buffers(lambda r, n: (NZ, 2, r, n // 2))
        + buffers(lambda r, n: (NZ, r, n // 2))
        + buffers(lambda r, n: (NZ, r, n // 2))
        + buffers(lambda r, n: (5, r, n))
        + [
            pltpu.VMEM((2, deepest, tokens), low),
            pltpu.VMEM((4, *small.shape), jnp.float32),
            pltpu.VMEM((3, *small.shape), jnp.float32),
            pltpu.VMEM((NZ, *small.shape), jnp.float32),
            dma((count, 2)),
            dma((count,)),
            dma((count, 4)),
            dma((count, 4)),
            dma((count, 4, 4)),
            dma((count, 4, 4)),
            dma((count, 4)),
            dma((count, 5)),
            dma((count, len(SPREAD))),
            dma((count, len(SPREAD))),
            dma((6,)),
            dma((6,)),
        ],
        compiler_params=pltpu.CompilerParams(collective_id=1, has_side_effects=True, vmem_limit_bytes=VMEM_LIMIT),
        name="gradient_reduce",
    )(small, *[v for pair in pairs for v in pair])
    return out[0], [o.reshape(r, n) for o, (r, n) in zip(out[1:], shapes)]


CORE_AT = 2 * BLOCKS


def block_rows(scalars, i, block):
    return pl.ds(pl.multiple_of(scalars[i] * block, block), block)


def attend_back_kernel(scalars, tokens, grad_mine, grad_theirs, probs, out, grads, keys, values, grad_k, grad_v):
    rows = grad_mine.shape[0]
    block = 2 * rows // BLOCKS
    scale = 1.0 / math.sqrt(HD)
    grads[:rows] = grad_mine[...]
    grads[rows:] = grad_theirs[...]
    for i in range(BLOCKS):
        at = block_rows(scalars, i, block)
        keys[i * block : (i + 1) * block] = tokens[at, 2 * HD : 3 * HD]
        values[i * block : (i + 1) * block] = tokens[at, 3 * HD :]
    column = BLOCKS * (BLOCKS + 1) // 2 * block
    for i in reversed(range(BLOCKS)):
        at = block_rows(scalars, i, block)
        n = (i + 1) * block
        column -= n
        query = stacked(tokens[at, : 2 * HD])
        grad = stacked(grads[at, :])
        low = probs[:, column : column + n]
        weights = low.astype(jnp.float32)
        grad_probs = lax.dot_general(
            grad, values[:n], (((1,), (1,)), ((), ())), preferred_element_type=jnp.float32
        )
        delta = jnp.sum(weights * grad_probs, axis=-1, keepdims=True)
        grad_scores = (weights * (grad_probs - delta)).astype(jnp.bfloat16)
        grad_q = jnp.dot(grad_scores, keys[:n], preferred_element_type=jnp.float32) * scale
        out[at, :HD] = grad_q[:block].astype(out.dtype)
        out[at, HD : 2 * HD] = grad_q[block:].astype(out.dtype)
        across = (((0,), (0,)), ((), ()))
        part_k = lax.dot_general(query, grad_scores, across, preferred_element_type=jnp.float32)
        part_v = lax.dot_general(grad, low, across, preferred_element_type=jnp.float32)
        if i == BLOCKS - 1:
            grad_k[...] = part_k
            grad_v[...] = part_v
        else:
            grad_k[:, :n] += part_k
            grad_v[:, :n] += part_v
    for i in range(BLOCKS):
        at = block_rows(scalars, i, block)
        here = slice(i * block, (i + 1) * block)
        out[at, 2 * HD : 3 * HD] = jnp.transpose(grad_k[:, here] * scale).astype(out.dtype)
        out[at, 3 * HD :] = jnp.transpose(grad_v[:, here]).astype(out.dtype)


def attend_back(scalars, tok, grad_mine, grad_theirs, probs):
    tok = tok.reshape(-1, tok.shape[-1])
    rows, width = tok.shape[0] // 2, tok.shape[1]
    heads = width // PER_HEAD
    block = 2 * rows // BLOCKS
    area = probs.shape[-1]
    return pl.pallas_call(
        attend_back_kernel,
        out_shape=jax.ShapeDtypeStruct((2 * rows, width), jnp.bfloat16),
        grid_spec=pltpu.PrefetchScalarGridSpec(
            num_scalar_prefetch=1,
            grid=(heads,),
            in_specs=[
                pl.BlockSpec((2 * rows, PER_HEAD), lambda i, s: (0, i)),
                pl.BlockSpec((rows, 2 * HD), lambda i, s: (0, s[CORE_AT] * HALF_HEADS + i)),
                pl.BlockSpec((rows, 2 * HD), lambda i, s: (0, i)),
                pl.BlockSpec((None, 2 * block, area), lambda i, s: (i, 0, 0)),
            ],
            out_specs=pl.BlockSpec((2 * rows, PER_HEAD), lambda i, s: (0, i)),
            scratch_shapes=[
                pltpu.VMEM((2 * rows, 2 * HD), jnp.bfloat16),
                pltpu.VMEM((2 * rows, HD), jnp.bfloat16),
                pltpu.VMEM((2 * rows, HD), jnp.bfloat16),
                pltpu.VMEM((HD, 2 * rows), jnp.float32),
                pltpu.VMEM((HD, 2 * rows), jnp.float32),
            ],
        ),
        cost_estimate=pl.CostEstimate(
            flops=heads * 8 * HD * 2 * block * area, bytes_accessed=2 * heads * 2 * block * area, transcendentals=0
        ),
        name="attention_back",
    )(scalars, tok, grad_mine, grad_theirs, probs)


def unproject_kernel(scalars, mine, theirs, raw, gain_q, gain_k, cosines, sines, out, gains):
    i = pl.program_id(0)
    mine_here = i // HALF_HEADS == scalars[CORE_AT]
    grad = jnp.where(mine_here, mine[...], theirs[...]).astype(jnp.float32)
    cos, sin = cosines[...], sines[...]
    totals = []
    backs = []
    for j, gain in enumerate((gain_q, gain_q, gain_k)):
        v = raw[:, j * HD : (j + 1) * HD].astype(jnp.float32)
        inverse = lax.rsqrt(jnp.mean(v * v, axis=-1, keepdims=True) + EPSILON)
        normed = v * inverse
        g = grad[:, j * HD : (j + 1) * HD]
        g = g * cos - turn(g) * sin
        totals.append(jnp.sum(normed * g, axis=0, keepdims=True))
        g = g * gain[...]
        backs.append(inverse * (g - normed * jnp.mean(g * normed, axis=-1, keepdims=True)))

    @pl.when(i == 0)
    def _():
        gains[...] = jnp.zeros_like(gains)

    gains[0:1, :] += totals[0] + totals[1]
    gains[1:2, :] += totals[2]
    at = pl.multiple_of(i * 2 * HD, 2 * HD)
    out[:, pl.ds(at, HD)] = backs[0].astype(out.dtype)
    out[:, pl.ds(pl.multiple_of(at + HD, HD), HD)] = backs[1].astype(out.dtype)
    out[:, pl.ds(pl.multiple_of((HEADS + i) * HD, HD), HD)] = backs[2].astype(out.dtype)
    out[:, pl.ds(pl.multiple_of((HEADS + KV_HEADS + i) * HD, HD), HD)] = grad[:, 3 * HD :].astype(out.dtype)


def unproject(scalars, mine, theirs, raw, gain_q, gain_k, cosines, sines):
    _, rows, width = raw.shape
    whole = lambda shape: pl.BlockSpec(shape, lambda i, s: (0, 0))
    columns = (HEADS + 2 * KV_HEADS) * HD
    return pl.pallas_call(
        unproject_kernel,
        out_shape=[
            jax.ShapeDtypeStruct((rows, columns), jnp.bfloat16),
            jax.ShapeDtypeStruct((8, HD), jnp.float32),
        ],
        grid_spec=pltpu.PrefetchScalarGridSpec(
            num_scalar_prefetch=1,
            grid=(KV_HEADS,),
            in_specs=[
                pl.BlockSpec((rows, PER_HEAD), lambda i, s: (0, i % HALF_HEADS)),
                pl.BlockSpec((rows, PER_HEAD), lambda i, s: (0, i % HALF_HEADS)),
                pl.BlockSpec((None, rows, PER_HEAD), lambda i, s: (i // HALF_HEADS, 0, i % HALF_HEADS)),
                whole((1, HD)),
                whole((1, HD)),
                whole((rows, HD)),
                whole((rows, HD)),
            ],
            out_specs=[whole((rows, columns)), whole((8, HD))],
        ),
        cost_estimate=pl.CostEstimate(flops=rows * columns * 20, bytes_accessed=rows * columns * 10, transcendentals=0),
        name="qkv_back",
    )(scalars, mine, theirs, raw, gain_q, gain_k, cosines, sines)


def swap(v):
    return lax.ppermute(v, "core", [(0, 1), (1, 0)])


def half_of(v, which, size):
    return lax.dynamic_slice_in_dim(v, which * size, size, 1)


def first_route():
    return [(2 * s + c, 2 * (2 * c + s % 2) + s // 2) for s in range(4) for c in range(2)]


def second_route():
    return [(2 * s + c, 2 * (2 * c + 1 - s % 2) + s // 2) for s in range(4) for c in range(2)]


def back(route):
    return [(b, a) for a, b in route]


LINE = ("z", "core")


def from_sequences(v):
    odd = lax.axis_index("z") % 2
    rows = v.shape[0] // 2
    first = lax.ppermute(v[:rows], LINE, back(first_route()))
    second = lax.ppermute(v[rows:], LINE, back(second_route()))
    return jnp.where(odd == 0, jnp.stack([first, second]), jnp.stack([second, first]))


def per_chip(
    tokens,
    cotangent,
    slot_order,
    attn_gain,
    q_gain,
    k_gain,
    w_qkv,
    w_out,
    mlp_gain,
    w_gate_up,
    w_down,
):
    z, core = lax.axis_index("z"), lax.axis_index("core")
    _, slot_len, width = tokens.shape
    f32, low = jnp.float32, jnp.bfloat16
    odd = z % 2
    orders = jnp.where(z // 2 == core, slot_order, swap(slot_order))
    order = lax.dynamic_index_in_dim(orders, odd, 0, False)
    slots = jnp.stack([2 * core + odd, 2 * core + 1 - odd, 2 - 2 * core + odd, 3 - 2 * core - odd])
    blocks = order[slots]
    where_is = jnp.sum(
        jnp.where(blocks[None, :] == jnp.arange(4)[:, None], jnp.arange(4)[None, :], 0), axis=1
    )
    scalars = jnp.concatenate([where_is, blocks, core[None], jnp.zeros((7,), jnp.int32)]).astype(jnp.int32)
    positions = (blocks[:2, None] * slot_len + jnp.arange(slot_len)[None, :]).reshape(-1)
    cos, sin = rope_tables(positions)
    cosines = jnp.concatenate([cos, cos], axis=1)
    sines = jnp.concatenate([-sin, sin], axis=1)
    gain_q, gain_k = q_gain.astype(f32)[None, :], k_gain.astype(f32)[None, :]
    head_gains = jnp.concatenate([gain_q, gain_k, jnp.zeros((6, HD), f32)], axis=0)
    gains = jnp.concatenate(
        [attn_gain.astype(f32)[None], mlp_gain.astype(f32)[None], jnp.zeros((6, attn_gain.shape[0]), f32)], axis=0
    )
    (
        (block_rows_out, gains_all, source_low, grad_low, first_low, raw, tok, probs, attended, middle, second_low, gate_up),
        (full_qkv, full_out, full_gate_up, full_down),
    ) = run_forward(
        scalars, gains, head_gains, cosines, sines, tokens, cotangent, [w_qkv, w_out, w_gate_up, w_down]
    )
    gain_first, gain_second = gains_all[:, 0].reshape(-1), gains_all[:, 1].reshape(-1)
    block_out = from_sequences(block_rows_out)
    source = source_low.reshape(-1, width).astype(f32)
    grad_low = grad_low.reshape(-1, width)
    rows = source.shape[0]
    normed_first = norm_rows(source)
    normed_second = norm_rows(middle)
    gate_part, up_part = gate_up[:, :FF].astype(f32), gate_up[:, FF:].astype(f32)
    sigmoid_gate = jax.nn.sigmoid(gate_part)
    silu_gate = gate_part * sigmoid_gate
    hidden = (silu_gate * up_part).astype(low)

    grad_output = grad_low.astype(f32)
    grad_hidden = matmul_right(grad_low, full_down)
    grad_gate = grad_hidden * up_part * (sigmoid_gate * (1.0 + gate_part * (1.0 - sigmoid_gate)))
    grad_upper = grad_hidden * silu_gate
    grad_gate_up = jnp.concatenate([grad_gate, grad_upper], axis=1).astype(low)
    grad_second = matmul_right(grad_gate_up, full_gate_up)
    gain_second_sum = jnp.sum(normed_second * grad_second, axis=0)
    grad_middle = grad_output + norm_back(middle, grad_second * gain_second)
    grad_mid_low = grad_middle.astype(low)
    grad_attn = matmul_right(grad_mid_low, full_out).astype(low)
    half = HEADS * HD // 2
    grad_theirs = swap(half_of(grad_attn, 1 - core, half))
    grad_rot = attend_back(scalars, tok, grad_attn, grad_theirs, probs)
    grad_rot_theirs = swap(grad_rot[rows:])
    grad_qkv, head_sums = unproject(
        scalars, grad_rot, grad_rot_theirs, raw, gain_q, gain_k, cosines, sines
    )
    grad_first = matmul_right(grad_qkv, full_qkv)
    gain_first_sum = jnp.sum(normed_first * grad_first, axis=0)
    input_grad = from_sequences(
        (grad_middle + norm_back(source, grad_first * gain_first)).astype(low)
    )
    small = jnp.concatenate(
        [gain_first_sum.reshape(-1, HD), gain_second_sum.reshape(-1, HD), head_sums], axis=0
    )
    sums, (down_sum, gate_up_sum, out_sum, qkv_sum) = reduce_gradients(
        small,
        [(hidden, grad_low), (second_low, grad_gate_up), (attended, grad_mid_low), (first_low, grad_qkv)],
    )
    count = width // HD
    share = width // NZ
    return (
        block_out,
        input_grad,
        lax.dynamic_slice_in_dim(sums[:count].reshape(-1), z * share, share, 0),
        sums[2 * count],
        sums[2 * count + 1],
        qkv_sum.astype(f32),
        out_sum.astype(f32),
        lax.dynamic_slice_in_dim(sums[count : 2 * count].reshape(-1), z * share, share, 0),
        gate_up_sum.astype(f32),
        down_sum.astype(f32),
    )


def solution(mesh):
    group, replica, body = "group", "replica", per_device
    if (mesh.shape["group"], mesh.shape["replica"]) == (NZ, 8):
        mesh = Mesh(mesh.devices.reshape(NZ, 2, 2, 2), ("z", "y", "x", "core"))
        group, replica, body = "z", ("y", "x", "core"), per_chip
    in_specs = (
        P(replica, group, None),
        P(replica, group, None),
        P(replica, None),
        P(group),
        P(),
        P(),
        P(group, None),
        P(group, None),
        P(group),
        P(group, None),
        P(group, None),
    )
    out_specs = (
        P(replica, group, None),
        P(replica, group, None),
        P(group),
        P(),
        P(),
        P(group, None),
        P(group, None),
        P(group),
        P(group, None),
        P(group, None),
    )
    return jax.shard_map(
        body, mesh=mesh, in_specs=in_specs, out_specs=out_specs, check_vma=False
    )
```

```python
import functools
import math

import jax
import jax.numpy as jnp
from jax import lax
from jax.experimental import pallas as pl
from jax.experimental.pallas import tpu as pltpu
from jax.sharding import Mesh
from jax.sharding import PartitionSpec as P

HEADS = 16
KV_HEADS = 8
HD = 128
FF = 3072


EPSILON = 1e-06
THETA_BASE = 1000000.0
MASKED = -1e30


def norm_rows(v):
    return v * lax.rsqrt(jnp.mean(v * v, axis=-1, keepdims=True) + EPSILON)


def norm_back(source, grad):
    inverse = lax.rsqrt(jnp.mean(source * source, axis=-1, keepdims=True) + EPSILON)
    normed = source * inverse
    return inverse * (grad - normed * jnp.mean(grad * normed, axis=-1, keepdims=True))


def rotate(v, cosines, sines):
    half_size = v.shape[-1] // 2
    leading = v[..., :half_size]
    trailing = v[..., half_size:]
    return jnp.concatenate(
        [leading * cosines - trailing * sines, trailing * cosines + leading * sines], axis=-1
    )


def rope_tables(positions):
    half_size = HD // 2
    counter = jnp.arange(half_size).astype(jnp.float32)
    frequency = THETA_BASE ** (-2.0 * counter / HD)
    angles = positions.astype(jnp.float32)[:, None] * frequency[None, :]
    return (jnp.cos(angles), jnp.sin(angles))


def matmul(a, b):
    return jnp.dot(a, b, preferred_element_type=jnp.float32)


def matmul_right(a, b):
    return lax.dot_general(a, b, (((1,), (1,)), ((), ())), preferred_element_type=jnp.float32)


def matmul_left(a, b):
    return lax.dot_general(a, b, (((0,), (0,)), ((), ())), preferred_element_type=jnp.float32)


def per_device(
    tokens,
    cotangent,
    slot_order,
    attn_gain,
    q_gain,
    k_gain,
    w_qkv,
    w_out,
    mlp_gain,
    w_gate_up,
    w_down,
):
    member_count = lax.axis_size("group")
    member = lax.axis_index("group")
    micro, slot_len, width = tokens.shape
    rows = micro * slot_len
    length = slot_len * member_count
    q_width = HEADS * HD
    kv_width = KV_HEADS * HD
    groups = HEADS // KV_HEADS
    score_scale = 1.0 / math.sqrt(HD)
    key_block = math.gcd(length, 512)
    block_count = length // key_block
    head_gain_q = q_gain.astype(jnp.float32)
    head_gain_k = k_gain.astype(jnp.float32)
    offsets = jnp.arange(slot_len, dtype=jnp.int32)
    source = tokens.reshape(rows, width).astype(jnp.float32)
    all_pos = (slot_order[:, :, None] * slot_len + offsets[None, None, :]).reshape(micro, length)
    my_pos = lax.dynamic_slice_in_dim(all_pos, member * slot_len, slot_len, 1)
    query_top = jnp.max(my_pos, axis=1)
    cosines, sines = rope_tables(my_pos.reshape(rows))
    normed_first = norm_rows(source)
    gain_piece = lax.all_gather(attn_gain, "group", axis=0, tiled=True)
    weight_piece = lax.all_gather(w_qkv, "group", axis=0, tiled=True)
    columns = normed_first
    low_cols = (columns * gain_piece.astype(jnp.float32)).astype(jnp.bfloat16)
    qkv = matmul(low_cols, weight_piece)
    first_low = low_cols
    gain_first = gain_piece.astype(jnp.float32)
    queries = qkv[:, :q_width].reshape(rows, HEADS, HD)
    keys_raw = qkv[:, q_width : q_width + kv_width].reshape(rows, KV_HEADS, HD)
    values_low = qkv[:, q_width + kv_width :].astype(jnp.bfloat16)
    queries_normed = norm_rows(queries)
    keys_normed = norm_rows(keys_raw)
    query_rot = rotate(queries_normed * head_gain_q, cosines[:, None, :], sines[:, None, :]).astype(
        jnp.bfloat16
    )
    key_rot = rotate(keys_normed * head_gain_k, cosines[:, None, :], sines[:, None, :]).astype(
        jnp.bfloat16
    )
    key_all, value_all = (
        lax.all_gather(key_rot.reshape(micro, slot_len, kv_width), "group", axis=1, tiled=True),
        lax.all_gather(values_low.reshape(micro, slot_len, kv_width), "group", axis=1, tiled=True),
    )
    query_heads = query_rot.reshape(micro, slot_len, KV_HEADS, groups, HD)

    def block_live(block_index):
        key_pos = lax.dynamic_slice_in_dim(all_pos, block_index * key_block, key_block, 1)
        return jnp.any(jnp.min(key_pos, axis=1) <= query_top)

    def block_scores(block_index):
        begin = block_index * key_block
        key_piece = lax.dynamic_slice_in_dim(key_all, begin, key_block, 1).reshape(
            micro, key_block, KV_HEADS, HD
        )
        key_pos = lax.dynamic_slice_in_dim(all_pos, begin, key_block, 1)
        raw = (
            jnp.einsum(
                "mqkgd,mskd->mkgqs", query_heads, key_piece, preferred_element_type=jnp.float32
            )
            * score_scale
        )
        allowed = (key_pos[:, None, :] <= my_pos[:, :, None])[:, None, None]
        return (jnp.where(allowed, raw, MASKED), allowed, key_piece)

    def stats_step(block_index, carry):

        def stats_visit_block(carry_in):
            top_in, total_in = carry_in
            scores, allowed, key_piece = block_scores(block_index)
            new_top = jnp.maximum(top_in, jnp.max(scores, axis=-1))
            summed = jnp.sum(jnp.where(allowed, jnp.exp(scores - new_top[..., None]), 0.0), axis=-1)
            return (new_top, total_in * jnp.exp(top_in - new_top) + summed)

        return lax.cond(
            block_live(block_index), stats_visit_block, lambda carry_in: carry_in, carry
        )

    stat_shape = (micro, KV_HEADS, groups, slot_len)
    top_final, total_final = lax.fori_loop(
        0,
        block_count,
        stats_step,
        (jnp.full(stat_shape, MASKED, jnp.float32), jnp.zeros(stat_shape, jnp.float32)),
    )
    log_total = top_final + jnp.log(total_final)

    def output_step(block_index, accum):

        def output_visit_block(accum_in):
            scores, allowed, key_piece = block_scores(block_index)
            probabilities = jnp.where(allowed, jnp.exp(scores - log_total[..., None]), 0.0)
            value_piece = lax.dynamic_slice_in_dim(
                value_all, block_index * key_block, key_block, 1
            ).reshape(micro, key_block, KV_HEADS, HD)
            return accum_in + jnp.einsum(
                "mkgqs,mskd->mqkgd",
                probabilities.astype(jnp.bfloat16),
                value_piece,
                preferred_element_type=jnp.float32,
            )

        return lax.cond(
            block_live(block_index), output_visit_block, lambda accum_in: accum_in, accum
        )

    attn_heads = lax.fori_loop(
        0, block_count, output_step, jnp.zeros((micro, slot_len, KV_HEADS, groups, HD), jnp.float32)
    )
    attended = attn_heads.reshape(rows, q_width).astype(jnp.bfloat16)
    columns = attended
    branch = matmul(columns, lax.all_gather(w_out, "group", axis=0, tiled=True))
    middle = source + branch
    normed_second = norm_rows(middle)
    gain_piece = lax.all_gather(mlp_gain, "group", axis=0, tiled=True)
    weight_piece = lax.all_gather(w_gate_up, "group", axis=0, tiled=True)
    columns = normed_second
    low_cols = (columns * gain_piece.astype(jnp.float32)).astype(jnp.bfloat16)
    gate_up = matmul(low_cols, weight_piece)
    gain_second = gain_piece.astype(jnp.float32)
    gate_part = gate_up[:, :FF]
    up_part = gate_up[:, FF:]
    sigmoid_gate = jax.nn.sigmoid(gate_part)
    silu_gate = gate_part * sigmoid_gate
    hidden = (silu_gate * up_part).astype(jnp.bfloat16)
    columns = hidden
    down_out = matmul(columns, lax.all_gather(w_down, "group", axis=0, tiled=True))
    block_out = (middle + down_out).astype(jnp.bfloat16).reshape(micro, slot_len, width)
    grad_low = cotangent.reshape(rows, width)
    grad_output = grad_low.astype(jnp.float32)
    down_full = matmul_left(hidden, grad_low)
    grad_hidden = matmul_right(grad_low, lax.all_gather(w_down, "group", axis=0, tiled=True))
    grad_gate = grad_hidden * up_part * (sigmoid_gate * (1.0 + gate_part * (1.0 - sigmoid_gate)))
    grad_upper = grad_hidden * silu_gate
    grad_gate_up = jnp.concatenate([grad_gate, grad_upper], axis=1).astype(jnp.bfloat16)
    gate_up_full = matmul_left(low_cols, grad_gate_up)
    grad_second = matmul_right(grad_gate_up, lax.all_gather(w_gate_up, "group", axis=0, tiled=True))
    gain_second_full = jnp.sum(normed_second * grad_second, axis=0)
    grad_middle = grad_output + norm_back(middle, grad_second * gain_second)
    grad_mid_low = grad_middle.astype(jnp.bfloat16)
    out_full = matmul_left(attended, grad_mid_low)
    grad_attn_full = matmul_right(grad_mid_low, lax.all_gather(w_out, "group", axis=0, tiled=True))
    grad_attn = grad_attn_full.astype(jnp.bfloat16)
    grad_heads = grad_attn.reshape(micro, slot_len, KV_HEADS, groups, HD)
    delta = jnp.transpose(
        jnp.sum(grad_heads.astype(jnp.float32) * attn_heads, axis=-1), (0, 2, 3, 1)
    )

    def back_step(block_index, carry):

        def back_visit_block(carry_in):
            grad_query_in, grad_key_in, grad_value_in = carry_in
            begin = block_index * key_block
            scores, allowed, key_piece = block_scores(block_index)
            probabilities = jnp.where(allowed, jnp.exp(scores - log_total[..., None]), 0.0)
            value_piece = lax.dynamic_slice_in_dim(value_all, begin, key_block, 1).reshape(
                micro, key_block, KV_HEADS, HD
            )
            grad_probs = jnp.einsum(
                "mqkgd,mskd->mkgqs", grad_heads, value_piece, preferred_element_type=jnp.float32
            )
            grad_scores = (probabilities * (grad_probs - delta[..., None])).astype(jnp.bfloat16)
            grad_query_out = (
                grad_query_in
                + jnp.einsum(
                    "mkgqs,mskd->mqkgd", grad_scores, key_piece, preferred_element_type=jnp.float32
                )
                * score_scale
            )
            key_term = (
                jnp.einsum(
                    "mkgqs,mqkgd->mskd",
                    grad_scores,
                    query_heads,
                    preferred_element_type=jnp.float32,
                )
                * score_scale
            )
            value_term = jnp.einsum(
                "mkgqs,mqkgd->mskd",
                probabilities.astype(jnp.bfloat16),
                grad_heads,
                preferred_element_type=jnp.float32,
            )
            key_old = lax.dynamic_slice_in_dim(grad_key_in, begin, key_block, 1)
            value_old = lax.dynamic_slice_in_dim(grad_value_in, begin, key_block, 1)
            grad_key_out = lax.dynamic_update_slice_in_dim(
                grad_key_in, key_old + key_term, begin, 1
            )
            grad_value_out = lax.dynamic_update_slice_in_dim(
                grad_value_in, value_old + value_term, begin, 1
            )
            return (grad_query_out, grad_key_out, grad_value_out)

        return lax.cond(block_live(block_index), back_visit_block, lambda carry_in: carry_in, carry)

    back_start = (
        jnp.zeros((micro, slot_len, KV_HEADS, groups, HD), jnp.float32),
        jnp.zeros((micro, length, KV_HEADS, HD), jnp.float32),
        jnp.zeros((micro, length, KV_HEADS, HD), jnp.float32),
    )
    grad_query_rot, grad_key_all, grad_value_all = lax.fori_loop(
        0, block_count, back_step, back_start
    )
    grad_key_mine, grad_value_mine = (
        lax.psum_scatter(
            grad_key_all.reshape(micro, length, kv_width).astype(jnp.bfloat16),
            "group",
            scatter_dimension=1,
            tiled=True,
        ).astype(jnp.float32),
        lax.psum_scatter(
            grad_value_all.reshape(micro, length, kv_width).astype(jnp.bfloat16),
            "group",
            scatter_dimension=1,
            tiled=True,
        ).astype(jnp.float32),
    )
    grad_query_norm = rotate(
        grad_query_rot.reshape(rows, HEADS, HD), cosines[:, None, :], -sines[:, None, :]
    )
    grad_key_norm = rotate(
        grad_key_mine.reshape(rows, KV_HEADS, HD), cosines[:, None, :], -sines[:, None, :]
    )
    q_gain_total = jnp.sum(queries_normed * grad_query_norm, axis=(0, 1))
    k_gain_total = jnp.sum(keys_normed * grad_key_norm, axis=(0, 1))
    grad_queries = norm_back(queries, grad_query_norm * head_gain_q).reshape(rows, q_width)
    grad_keys = norm_back(keys_raw, grad_key_norm * head_gain_k).reshape(rows, kv_width)
    grad_qkv = jnp.concatenate(
        [grad_queries, grad_keys, grad_value_mine.reshape(rows, kv_width)], axis=1
    ).astype(jnp.bfloat16)
    qkv_full = matmul_left(first_low, grad_qkv)
    grad_first = matmul_right(grad_qkv, lax.all_gather(w_qkv, "group", axis=0, tiled=True))
    gain_first_full = jnp.sum(normed_first * grad_first, axis=0)
    input_grad = (
        (grad_middle + norm_back(source, grad_first * gain_first))
        .astype(jnp.bfloat16)
        .reshape(micro, slot_len, width)
    )
    owned = (
        lax.psum_scatter(
            gain_first_full.astype(jnp.bfloat16), "group", scatter_dimension=0, tiled=True
        ).astype(jnp.float32),
        lax.psum_scatter(
            qkv_full.astype(jnp.bfloat16), "group", scatter_dimension=0, tiled=True
        ).astype(jnp.float32),
        lax.psum_scatter(
            out_full.astype(jnp.bfloat16), "group", scatter_dimension=0, tiled=True
        ).astype(jnp.float32),
        lax.psum_scatter(
            gain_second_full.astype(jnp.bfloat16), "group", scatter_dimension=0, tiled=True
        ).astype(jnp.float32),
        lax.psum_scatter(
            gate_up_full.astype(jnp.bfloat16), "group", scatter_dimension=0, tiled=True
        ).astype(jnp.float32),
        lax.psum_scatter(
            down_full.astype(jnp.bfloat16), "group", scatter_dimension=0, tiled=True
        ).astype(jnp.float32),
    )
    summed = (
        lax.psum(owned[0].astype(jnp.bfloat16), "replica").astype(jnp.float32),
        lax.psum(owned[1].astype(jnp.bfloat16), "replica").astype(jnp.float32),
        lax.psum(owned[2].astype(jnp.bfloat16), "replica").astype(jnp.float32),
        lax.psum(owned[3].astype(jnp.bfloat16), "replica").astype(jnp.float32),
        lax.psum(owned[4].astype(jnp.bfloat16), "replica").astype(jnp.float32),
        lax.psum(owned[5].astype(jnp.bfloat16), "replica").astype(jnp.float32),
    )
    head_sums = lax.psum((q_gain_total, k_gain_total), ("group", "replica"))
    return (
        block_out,
        input_grad,
        summed[0],
        head_sums[0],
        head_sums[1],
        summed[1],
        summed[2],
        summed[3],
        summed[4],
        summed[5],
    )


MESH_ID = pl.DeviceIdType.MESH
HBM = pltpu.MemorySpace.HBM
VMEM_LIMIT = 64 * 1024 * 1024 - 65536
NZ = 4


class Place:
    def __init__(self):
        self.z = lax.axis_index("z")
        self.y = lax.axis_index("y")
        self.x = lax.axis_index("x")
        self.c = lax.axis_index("core")
        self.h = self.z // 2
        self.m = self.at(self.z)
        self.inner = {"z": self.at(self.m + 1)}
        self.outer = {"z": self.at(lax.rem(self.m + 3, 4))}
        self.across_x = {"x": 1 - self.x}
        self.across_y = {"y": 1 - self.y}
        self.partner = {"core": 1 - self.c}

    def at(self, t):
        return t * (1 - 2 * self.h) + 3 * self.h

    def greet(self):
        barrier = pltpu.get_barrier_semaphore()
        peers = [self.across_x, self.across_y, self.partner]
        for hop in range(1, NZ):
            there = lax.rem(self.z + hop, NZ)
            peers += [{"z": there}, {"z": there, "core": 1 - self.c}]
        for peer in peers:
            pl.semaphore_signal(barrier, inc=1, device_id=peer, device_id_type=MESH_ID)
        pl.semaphore_wait(barrier, len(peers))


def remote(src, dst, send, recv, peer):
    return pltpu.make_async_remote_copy(
        src_ref=src, dst_ref=dst, send_sem=send, recv_sem=recv, device_id=peer, device_id_type=MESH_ID
    )


KINDS = ("x", "y", "yx", "xy", "c", "cx", "cy", "cd")


def half_rows(ref, which):
    rows = ref.shape[0] // 2
    return ref.at[pl.ds(which * rows, rows), :]


class Gather:
    def __init__(self, me, shards, fulls, sems):
        self.me, self.shards, self.fulls = me, shards, fulls
        self.z_send, self.z_recv, self.f_send, self.xy_send, self.xy_recv = sems
        self.stage_t = (1 - me.m, 2, 3)
        self.stages = [(w, k) for w in range(len(shards)) for k in range(3)]

    def piece(self, c, x, y):
        return c * 4 + x * 2 + y

    def shard_z(self, k):
        return self.me.at(self.stage_t[k])

    def own(self, w, peer, k, slot):
        me = self.me
        piece = self.piece(me.c, me.x, me.y)
        return remote(
            self.shards[w].at[piece],
            self.fulls[w].at[me.z, piece],
            self.z_send.at[w, slot],
            self.z_recv.at[w, k],
            peer,
        )

    def send_own(self, w):
        me = self.me
        self.own(w, me.inner, me.m, 0).start()

        @pl.when(me.m == 1)
        def _():
            self.own(w, me.outer, 0, 1).start()

    def place(self, w, k, cc, xx, yy):
        return self.fulls[w].at[self.shard_z(k), self.piece(cc, xx, yy)]

    def forward(self, w, k):
        me = self.me
        piece = self.place(w, k, me.c, me.x, me.y)
        peer, slot = ((me.inner, 2), (me.outer, 1), (me.outer, 2))[k]
        return remote(piece, piece, self.f_send.at[w, k], self.z_recv.at[w, slot], peer)

    def hop(self, w, k, kind):
        me = self.me
        c, x, y = me.c, me.x, me.y
        mine, px = self.place(w, k, c, x, y), self.place(w, k, c, 1 - x, y)
        py, pd = self.place(w, k, c, x, 1 - y), self.place(w, k, c, 1 - x, 1 - y)
        src, peer = {
            "x": (mine, me.across_x),
            "y": (mine, me.across_y),
            "yx": (half_rows(px, 0), me.across_y),
            "xy": (half_rows(py, 1), me.across_x),
            "c": (mine, me.partner),
            "cx": (px, me.partner),
            "cy": (py, me.partner),
            "cd": (pd, me.partner),
        }[kind]
        index = KINDS.index(kind)
        return remote(src, src, self.xy_send.at[w, k, index], self.xy_recv.at[w, k, index], peer)

    def arrived(self, w, k, kind):
        me = self.me
        c, x, y = me.c, me.x, me.y
        dst = {
            "x": lambda: self.place(w, k, c, 1 - x, y),
            "y": lambda: self.place(w, k, c, x, 1 - y),
            "yx": lambda: half_rows(self.place(w, k, c, 1 - x, 1 - y), 0),
            "xy": lambda: half_rows(self.place(w, k, c, 1 - x, 1 - y), 1),
            "c": lambda: self.place(w, k, 1 - c, x, y),
            "cx": lambda: self.place(w, k, 1 - c, 1 - x, y),
            "cy": lambda: self.place(w, k, 1 - c, x, 1 - y),
            "cd": lambda: self.place(w, k, 1 - c, 1 - x, 1 - y),
        }[kind]()
        index = KINDS.index(kind)
        remote(dst, dst, self.xy_send.at[w, k, index], self.xy_recv.at[w, k, index], me.partner).wait_recv()

    def relay(self, i):
        w, k = self.stages[i]
        me = self.me
        mine = self.place(w, k, me.c, me.x, me.y)
        remote(mine, mine, self.f_send.at[w, k], self.z_recv.at[w, k], me.partner).wait_recv()

        @pl.when(me.m == 1)
        def _():
            self.forward(w, k).start()

    def launch(self, i):
        w, k = self.stages[i]
        for kind in ("x", "y", "c"):
            self.hop(w, k, kind).start()

    def first(self, i):
        self.relay(i)
        if self.stages[i][1] == 1 and self.stages[i][0] + 1 < len(self.shards):
            self.send_own(self.stages[i][0] + 1)
        self.launch(i)

    def second(self, i):
        w, k = self.stages[i]
        self.arrived(w, k, "x")
        self.hop(w, k, "yx").start()
        self.hop(w, k, "cx").start()
        self.arrived(w, k, "y")
        self.hop(w, k, "xy").start()
        self.hop(w, k, "cy").start()

    def third(self, i):
        w, k = self.stages[i]
        self.arrived(w, k, "yx")
        self.arrived(w, k, "xy")
        self.hop(w, k, "cd").start()

    def step(self, i):
        total = len(self.stages)
        if i < total:
            self.first(i)
        if 0 <= i - 3 < total:
            self.third(i - 3)
        if 0 <= i - 2 < total:
            self.second(i - 2)

    def require(self, w, k):
        for kind in ("c", "cx", "cy", "cd"):
            self.arrived(w, k, kind)

    def finish(self):
        me = self.me
        for w, k in self.stages:
            for kind in KINDS:
                self.hop(w, k, kind).wait_send()
        for w in range(len(self.shards)):
            self.own(w, me.inner, me.m, 0).wait_send()

            @pl.when(me.m == 1)
            def _(w=w):
                self.own(w, me.outer, 0, 1).wait_send()
                for k in range(3):
                    self.forward(w, k).wait_send()


class Route:
    def __init__(self, me):
        z, c = me.z, me.c
        odd = lax.rem(z, 2)
        self.stays = z // 2 == c
        self.order = (odd, 1 - odd)
        self.to = ({"z": 2 * c + odd, "core": z // 2}, {"z": 2 * c + 1 - odd, "core": z // 2})

    def start(self, copies):
        first_local, first, second = copies

        @pl.when(self.stays)
        def _():
            first_local.start()

        @pl.when(jnp.logical_not(self.stays))
        def _():
            first.start()

        second.start()

    def out(self, held, there, sems):
        a, b = self.order
        return (
            pltpu.make_async_copy(held.at[a], there.at[0], sems.at[0]),
            remote(held.at[a], there.at[0], sems.at[1], sems.at[2], self.to[0]),
            remote(held.at[b], there.at[1], sems.at[3], sems.at[4], self.to[1]),
        )

    def back(self, held, there, sems):
        odd = self.order[0]
        return (
            pltpu.make_async_copy(held.at[0], there.at[odd], sems.at[0]),
            remote(held.at[0], there.at[odd], sems.at[1], sems.at[2], self.to[0]),
            remote(held.at[1], there.at[odd], sems.at[3], sems.at[4], self.to[1]),
        )

    def wait(self, copies):
        first_local, first, second = copies

        @pl.when(self.stays)
        def _():
            first_local.wait()

        @pl.when(jnp.logical_not(self.stays))
        def _():
            first.wait()

        second.wait()


def turn(v):
    return pltpu.roll(v, HD // 2, 1)


def stacked(two_heads):
    return jnp.concatenate([two_heads[:, :HD], two_heads[:, HD:]], axis=0)


def pick(which, values):
    out = values[0]
    for i in range(1, len(values)):
        out = jnp.where(which == i, values[i], out)
    return out


def row_loop(rows, step, body):
    def run(i, carry):
        body(pl.ds(pl.multiple_of(i * step, step), step))
        return carry

    lax.fori_loop(0, rows // step, run, 0)


PER_HEAD = 4 * HD
HALF_HEADS = KV_HEADS // 2
BLOCKS = 4
COUNT = 4


def forward_kernel(scalars, gains, head_gains, cosines, sines, tokens, cotangent, *refs):
    shards = refs[:COUNT]
    (
        block_out,
        gains_all,
        source,
        grad,
        h1_out,
        raw_out,
        tok_out,
        probs_out,
        attended_out,
        middle_out,
        h2_out,
        gate_up_out,
    ) = refs[COUNT : COUNT + 12]
    fulls = refs[COUNT + 12 : 2 * COUNT + 12]
    (
        acc,
        acc_small,
        wide,
        narrow,
        x,
        h1,
        h2,
        tok,
        outgoing,
        raw,
        p0,
        p1,
        p2,
        p3,
        ordered,
        mixed,
        mixed_out,
        attended,
        middle,
        hidden,
        gate_up,
        low_out,
        z_send,
        z_recv,
        f_send,
        xy_send,
        xy_recv,
        load_sem,
        keep_sem,
        gain_sem,
        token_sem,
        cot_sem,
        swap_sem,
        save_sem,
        prob_sem,
        gate_sem,
    ) = refs[2 * COUNT + 12 :]
    prob_slots = (p0, p1, p2, p3)
    low, f32 = jnp.bfloat16, jnp.float32
    me = Place()
    z, c = me.z, me.c
    rows, width = x.shape
    block = rows // 2
    comm = Gather(me, shards, fulls, (z_send, z_recv, f_send, xy_send, xy_recv))
    route = Route(me)
    me.greet()
    comm.send_own(0)
    gain_copies = []
    for j in range(1, NZ):
        there = {"z": lax.rem(z + j, NZ)}
        gain_copies.append(remote(gains, gains_all.at[z], gain_sem.at[0, j], gain_sem.at[1, j], there))
    for copy in gain_copies:
        copy.start()
    gains_all[pl.ds(z, 1)] = gains[...][None]
    token_copies = route.out(tokens, source, token_sem)
    cot_copies = route.out(cotangent, grad, cot_sem)

    def buffer(w, kk):
        if w in (0, 2):
            return wide.at[kk % 2, :, :, pl.ds(0, shards[w].shape[2])]
        return narrow.at[kk % 2, :, pl.ds(0, shards[w].shape[1]), :]

    def load(w, kk):
        src = shards[w] if kk == 0 else fulls[w].at[comm.shard_z(kk - 1)]
        return pltpu.make_async_copy(src, buffer(w, kk), load_sem.at[w, kk])

    def keep(w):
        return pltpu.make_async_copy(buffer(w, 0), fulls[w].at[z], keep_sem.at[w])

    def chunk(w, kk, lhs, out, tile):
        depth = 8 * shards[w].shape[1]
        columns = shards[w].shape[2]
        own_z = z if kk == 0 else comm.shard_z(kk - 1)
        if kk > 0:
            comm.require(w, kk - 1)
            if kk == 2:
                keep(w).wait()
            load(w, kk).start()
        load(w, kk).wait()
        if kk == 0:
            keep(w).start()
        left = lhs[:, pl.ds(pl.multiple_of(own_z * depth, depth), depth)]
        weight = buffer(w, kk)

        def body(i, carry):
            at = pl.ds(pl.multiple_of(i * tile, tile), tile)
            right = weight[:, :, at].reshape(depth, tile)
            part = jnp.dot(left, right, preferred_element_type=f32)
            if kk == 0:
                out[:, at] = part
            else:
                out[:, at] += part
            return carry

        lax.fori_loop(0, columns // tile, body, 0)

    def save(i, src, dst):
        return pltpu.make_async_copy(src, dst, save_sem.at[i])

    load(0, 0).start()
    load(1, 0).start()
    comm.step(0)
    comm.step(1)
    comm.first(2)
    route.start(token_copies)
    comm.second(0)
    comm.first(3)
    comm.third(0)
    comm.second(1)
    comm.third(1)
    comm.second(2)
    comm.third(2)
    for j in range(1, NZ):
        gain_copies[j - 1].wait_send()
        there = gains_all.at[lax.rem(z + NZ - j, NZ)]
        remote(gains, there, gain_sem.at[0, j], gain_sem.at[1, j], me.partner).wait_recv()
    route.wait(token_copies)
    for part in range(2):
        pltpu.make_async_copy(source.at[part], x.at[pl.ds(part * block, block)], token_sem.at[5 + part]).start()
    for part in range(2):
        pltpu.make_async_copy(source.at[part], x.at[pl.ds(part * block, block)], token_sem.at[5 + part]).wait()

    def normed_times(v, index):
        v = v * lax.rsqrt(jnp.mean(v * v, axis=-1, keepdims=True) + EPSILON)
        gain = jnp.concatenate([gains_all[s, index : index + 1, :] for s in range(NZ)], axis=1)
        return (v * gain).astype(low)

    def first_norm(at):
        h1[at, :] = normed_times(x[at, :].astype(f32), 0)

    row_loop(rows, 64, first_norm)
    save(0, h1, h1_out).start()
    comm.first(4)
    chunk(0, 0, h1, acc, 512)
    chunk(0, 1, h1, acc, 512)
    comm.first(5)
    comm.second(3)
    chunk(0, 2, h1, acc, 512)
    comm.third(3)
    comm.second(4)
    chunk(0, 3, h1, acc, 512)
    load(2, 0).start()
    comm.first(6)
    comm.third(4)

    def head(h, target, column):
        parts = []
        for start, size in ((h * 2 * HD, 2 * HD), ((HEADS + h) * HD, HD), ((HEADS + KV_HEADS + h) * HD, HD)):
            parts.append(acc[:, pl.ds(pl.multiple_of(start, HD), size)])
        half, at = h // HALF_HEADS, pl.multiple_of(lax.rem(h, HALF_HEADS) * PER_HEAD, PER_HEAD)
        for i, (v, gain_row) in enumerate(((parts[0][:, :HD], 0), (parts[0][:, HD:], 0), (parts[1], 1))):
            raw[half, :, pl.ds(pl.multiple_of(at + i * HD, HD), HD)] = v.astype(low)
            v = v * lax.rsqrt(jnp.mean(v * v, axis=-1, keepdims=True) + EPSILON)
            v = v * head_gains[gain_row : gain_row + 1, :]
            v = (v * cosines[...] + turn(v) * sines[...]).astype(low)
            for j in range(2):
                target[j, :, pl.ds(pl.multiple_of(column + i * HD, HD), HD)] = v[j * block : (j + 1) * block]
        v = parts[2].astype(low)
        for j in range(2):
            target[j, :, pl.ds(pl.multiple_of(column + 3 * HD, HD), HD)] = v[j * block : (j + 1) * block]

    def other_head(i, carry):
        head(i + HALF_HEADS * (1 - c), outgoing, i * PER_HEAD)
        return carry

    def own_head(i, carry):
        head(i + HALF_HEADS * c, tok, i * PER_HEAD)
        return carry

    lax.fori_loop(0, HALF_HEADS, other_head, 0)
    swap_out = remote(outgoing, tok.at[pl.ds(2, 2)], swap_sem.at[0], swap_sem.at[1], me.partner)
    comm.first(7)
    swap_out.start()
    lax.fori_loop(0, HALF_HEADS, own_head, 0)
    save(1, raw, raw_out).start()
    comm.second(5)
    comm.third(5)
    swap_out.wait()
    save(2, tok, tok_out).start()

    scale = 1.0 / math.sqrt(HD)
    above = lax.rem(lax.broadcasted_iota(jnp.int32, (2 * block, block), 0), block)
    above = above < lax.broadcasted_iota(jnp.int32, (2 * block, block), 1)

    def save_probs(h, i):
        n = (i + 1) * block
        column = i * (i + 1) // 2 * block
        return pltpu.make_async_copy(prob_slots[i], probs_out.at[h, :, pl.ds(column, n)], prob_sem.at[i])

    def attend(h, carry):
        at = pl.multiple_of(h * PER_HEAD, PER_HEAD)
        for i in range(BLOCKS):
            ordered[i * block : (i + 1) * block] = pick(
                scalars[i], [tok[j, :, pl.ds(at, PER_HEAD)] for j in range(BLOCKS)]
            )
        for i in range(BLOCKS):
            n = (i + 1) * block
            query = stacked(ordered[i * block : n, : 2 * HD])
            keys, values = ordered[:n, 2 * HD : 3 * HD], ordered[:n, 3 * HD :]
            scores = lax.dot_general(query, keys, (((1,), (1,)), ((), ())), preferred_element_type=f32)
            last = jnp.where(above, MASKED, scores[:, i * block :])
            scores = last if i == 0 else jnp.concatenate([scores[:, : i * block], last], axis=1)
            top = jnp.max(scores, axis=-1, keepdims=True)
            weights = jnp.exp((scores - top) * scale)
            weights = weights * (1.0 / jnp.sum(weights, axis=-1, keepdims=True))
            probs = weights.astype(low)

            @pl.when(h > 0)
            def _():
                save_probs(h - 1, i).wait()

            prob_slots[i][...] = probs
            save_probs(h, i).start()
            out = jnp.dot(probs, values, preferred_element_type=f32).astype(low)
            there = pl.multiple_of(h * 2 * HD, 2 * HD)
            mixed[i * block : (i + 1) * block, pl.ds(there, HD)] = out[:block]
            mixed[i * block : (i + 1) * block, pl.ds(pl.multiple_of(there + HD, HD), HD)] = out[block:]
            for now, steps in ATTEND_STEPS.items():
                if now[1] == i:

                    @pl.when(h == now[0])
                    def _(steps=steps):
                        for name, index in steps:
                            getattr(comm, name)(index)

        return carry

    lax.fori_loop(0, HALF_HEADS, attend, 0)
    half = HEADS * HD // 2
    mine = pl.ds(pl.multiple_of(c * half, half), half)
    for j in range(2):
        blocks = [mixed[i * block : (i + 1) * block] for i in range(BLOCKS)]
        mixed_out[j * block : (j + 1) * block] = pick(scalars[BLOCKS + 2 + j], blocks)
    for j in range(2):
        blocks = [mixed[i * block : (i + 1) * block] for i in range(BLOCKS)]
        attended[j * block : (j + 1) * block, mine] = pick(scalars[BLOCKS + j], blocks)
    mixed_swap = remote(mixed_out, attended.at[:, mine], swap_sem.at[2], swap_sem.at[3], me.partner)
    mixed_swap.start()
    for i in range(BLOCKS):
        save_probs(HALF_HEADS - 1, i).wait()
    mixed_swap.wait()
    save(3, attended, attended_out).start()
    for kk in range(4):
        chunk(1, kk, attended, acc_small, 512)
    load(3, 0).start()

    def second_norm(at):
        v = x[at, :].astype(f32) + acc_small[at, :]
        middle[at, :] = v
        h2[at, :] = normed_times(v, 1)

    row_loop(rows, 64, second_norm)
    save(4, middle, middle_out).start()
    save(5, h2, h2_out).start()
    chunk(2, 0, h2, acc, 512)
    chunk(2, 1, h2, acc, 512)
    comm.first(10)
    comm.third(7)
    comm.second(8)
    route.start(cot_copies)
    chunk(2, 2, h2, acc, 512)
    comm.first(11)
    comm.third(8)
    comm.second(9)
    chunk(2, 3, h2, acc, 512)
    comm.third(9)
    comm.second(10)

    def save_gate_up(i, part, slot):
        at = pl.multiple_of(part * FF + i * 512, 512)
        return pltpu.make_async_copy(gate_up.at[slot, part], gate_up_out.at[:, pl.ds(at, 512)], gate_sem.at[slot, part])

    def activate(i, carry):
        slot = lax.rem(i, 2)
        at = pl.multiple_of(i * 512, 512)

        @pl.when(i >= 2)
        def _():
            for part in range(2):
                save_gate_up(i - 2, part, slot).wait()

        gate = acc[:, pl.ds(at, 512)]
        up = acc[:, pl.ds(pl.multiple_of(FF + at, 512), 512)]
        gate_up[slot, 0] = gate.astype(low)
        gate_up[slot, 1] = up.astype(low)
        hidden[:, pl.ds(at, 512)] = (gate * jax.nn.sigmoid(gate) * up).astype(low)
        for part in range(2):
            save_gate_up(i, part, slot).start()
        return carry

    tiles = FF // 512
    lax.fori_loop(0, tiles, activate, 0)
    chunk(3, 0, hidden, acc_small, 512)
    chunk(3, 1, hidden, acc_small, 512)
    comm.third(10)
    comm.second(11)
    chunk(3, 2, hidden, acc_small, 512)
    comm.third(11)
    chunk(3, 3, hidden, acc_small, 512)

    def final(at):
        low_out[at, :] = (middle[at, :] + acc_small[at, :]).astype(low)

    row_loop(rows, 64, final)
    save(6, low_out, block_out).start()
    comm.finish()
    for slot in range(2):
        for part in range(2):
            save_gate_up(tiles - 2 + slot, part, slot).wait()
    for i, (src, dst) in enumerate(
        (
            (h1, h1_out),
            (raw, raw_out),
            (tok, tok_out),
            (attended, attended_out),
            (middle, middle_out),
            (h2, h2_out),
            (low_out, block_out),
        )
    ):
        save(i, src, dst).wait()
    route.wait(cot_copies)


ATTEND_STEPS = {
    (1, 0): (("first", 8), ("second", 6)),
    (2, 0): (("third", 6),),
    (3, 1): (("first", 9), ("second", 7)),
}


def run_forward(scalars, gains, head_gains, cosines, sines, tokens, cotangent, shards):
    low, f32 = jnp.bfloat16, jnp.float32
    _, slot_len, width = tokens.shape
    rows = 2 * slot_len
    cut = [s.reshape(8, s.shape[0] // 8, s.shape[1]) for s in shards]
    area = slot_len * BLOCKS * (BLOCKS + 1) // 2
    shape = jax.ShapeDtypeStruct
    outs = [
        shape((rows, width), low),
        shape((NZ, *gains.shape), f32),
        shape((2, slot_len, width), low),
        shape((2, slot_len, width), low),
        shape((rows, width), low),
        shape((2, rows, HALF_HEADS * PER_HEAD), low),
        shape((4, slot_len, HALF_HEADS * PER_HEAD), low),
        shape((HALF_HEADS, 2 * slot_len, area), low),
        shape((rows, HEADS * HD), low),
        shape((rows, width), f32),
        shape((rows, width), low),
        shape((rows, 2 * FF), low),
    ] + [shape((NZ, *s.shape), low) for s in cut]
    hbm = pl.BlockSpec(memory_space=HBM)
    vmem = pl.BlockSpec(memory_space=pltpu.VMEM)
    dma = pltpu.SemaphoreType.DMA
    out = pl.pallas_call(
        forward_kernel,
        out_shape=outs,
        in_specs=[pl.BlockSpec(memory_space=pltpu.SMEM)] + [vmem] * 4 + [hbm] * (2 + COUNT),
        out_specs=[hbm, vmem] + [hbm] * (10 + COUNT),
        scratch_shapes=[
            pltpu.VMEM((rows, 2 * FF), f32),
            pltpu.VMEM((rows, width), f32),
            pltpu.VMEM((2, 8, cut[2].shape[1], 2 * FF), low),
            pltpu.VMEM((2, 8, cut[3].shape[1], width), low),
            pltpu.VMEM((rows, width), low),
            pltpu.VMEM((rows, width), low),
            pltpu.VMEM((rows, width), low),
            pltpu.VMEM((4, slot_len, HALF_HEADS * PER_HEAD), low),
            pltpu.VMEM((2, slot_len, HALF_HEADS * PER_HEAD), low),
            pltpu.VMEM((2, rows, HALF_HEADS * PER_HEAD), low),
        ]
        + [pltpu.VMEM((2 * slot_len, (i + 1) * slot_len), low) for i in range(BLOCKS)]
        + [
            pltpu.VMEM((4 * slot_len, PER_HEAD), low),
            pltpu.VMEM((4 * slot_len, HEADS * HD // 2), low),
            pltpu.VMEM((rows, HEADS * HD // 2), low),
            pltpu.VMEM((rows, HEADS * HD), low),
            pltpu.VMEM((rows, width), f32),
            pltpu.VMEM((rows, FF), low),
            pltpu.VMEM((2, 2, rows, 512), low),
            pltpu.VMEM((rows, width), low),
            dma((COUNT, 2)),
            dma((COUNT, 3)),
            dma((COUNT, 3)),
            dma((COUNT, 3, len(KINDS))),
            dma((COUNT, 3, len(KINDS))),
            dma((COUNT, 4)),
            dma((COUNT,)),
            dma((2, NZ)),
            dma((7,)),
            dma((5,)),
            dma((4,)),
            dma((7,)),
            dma((BLOCKS,)),
            dma((2, 2)),
        ],
        compiler_params=pltpu.CompilerParams(collective_id=0, has_side_effects=True, vmem_limit_bytes=VMEM_LIMIT),
        name="forward",
    )(scalars, gains, head_gains, cosines, sines, tokens, cotangent, *cut)
    return out[:12], out[12:]


def add_rows(dst, src, rows):
    def body(i, carry):
        at = pl.ds(pl.multiple_of(i * 16, 16), 16)
        total = dst[at, :].astype(jnp.float32) + src[at, :].astype(jnp.float32)
        dst[at, :] = total.astype(dst.dtype)
        return carry

    lax.fori_loop(0, rows // 16, body, 0)


SPREAD = ("x", "y", "yx", "xy", "c", "cx", "cy", "cd")
ROUNDS = ("x1", "y1", "y2", "x2")


class Reduce:
    def __init__(self, me, shapes, refs, turned, sems):
        self.me, self.shapes, self.turned = me, shapes, turned
        self.stage, self.acc, self.rx1, self.ry1, self.rx2, self.ry2, self.rz, self.outs = refs
        (
            self.keep_sem,
            self.c_send,
            self.c_recv,
            self.r_send,
            self.r_recv,
            self.z_send,
            self.z_recv,
            self.o_send,
            self.o_recv,
        ) = sems
        self.stage_t = (3, 2, 1 - me.m, me.m)
        self.chunks = [(w, k) for w in range(len(shapes)) for k in range(4)]

    def zk(self, k):
        return self.me.at(self.stage_t[k])

    def product(self, n, rhs, columns, store):
        w, k = self.chunks[n]
        rows = self.shapes[w][0]
        half = self.shapes[w][1] // 2
        tile = min(half, 512)

        def body(i, carry):
            at = pl.multiple_of(i * tile, tile)
            part = jnp.dot(
                self.turned[n % 2, :rows],
                rhs[:, pl.ds(pl.multiple_of(columns * half + at, tile), tile)],
                preferred_element_type=jnp.float32,
            )
            store(part, pl.ds(at, tile))
            return carry

        lax.fori_loop(0, half // tile, body, 0)

    def to_partner(self, n):
        w, k = self.chunks[n]
        return remote(
            self.stage[w], self.acc[w].at[self.zk(k)], self.c_send.at[w, k], self.c_recv.at[w, k], self.me.partner
        )

    def turn_rows(self, n, lhs):
        w, k = self.chunks[n]
        rows = self.shapes[w][0]
        at = pl.multiple_of(self.zk(k) * rows, rows)
        self.turned[n % 2, :rows] = jnp.transpose(lhs[:, pl.ds(at, rows)])

    def theirs(self, n, rhs):
        w, k = self.chunks[n]
        rows = self.shapes[w][0]
        if k > 0:
            self.to_partner(n - 1).wait_send()

        def store(part, at):
            self.stage[w][:, :, :, at] = part.astype(jnp.bfloat16).reshape(2, 2, rows // 4, part.shape[1])

        self.product(n, rhs, 1 - self.me.c, store)

    def ours(self, n, rhs):
        w, k = self.chunks[n]
        a = self.acc[w].at[self.zk(k)]
        self.to_partner(n).wait_recv()

        def store(part, at):
            got = a[:, :, :, at].astype(jnp.float32)
            a[:, :, :, at] = (part.reshape(got.shape) + got).astype(jnp.bfloat16)

        self.product(n, rhs, self.me.c, store)

    def launch(self, n):
        w, k = self.chunks[n]
        self.exchange(w, k, "x1").start()
        self.exchange(w, k, "y1").start()

    def exchange(self, w, k, kind):
        me = self.me
        x, y = me.x, me.y
        a = self.acc[w].at[self.zk(k)]
        half = a.shape[-1] // 2
        lo, hi = pl.ds(0, half), pl.ds(half, half)
        src, dst, peer = {
            "x1": lambda: (a.at[1 - x, :, :, lo], self.rx1[w].at[k], me.across_x),
            "y1": lambda: (a.at[:, 1 - y, :, hi], self.ry1[w].at[k], me.across_y),
            "y2": lambda: (a.at[x, 1 - y, :, lo], self.ry2[w].at[k], me.across_y),
            "x2": lambda: (a.at[1 - x, y, :, hi], self.rx2[w].at[k], me.across_x),
        }[kind]()
        index = ROUNDS.index(kind)
        return remote(src, dst, self.r_send.at[w, k, index], self.r_recv.at[w, k, index], peer)

    def along(self, w, k, slot, peer):
        me = self.me
        return remote(
            self.acc[w].at[self.zk(k), me.x, me.y], self.rz[w].at[slot], self.z_send.at[w, k], self.z_recv.at[w, slot], peer
        )

    def s1(self, n):
        w, k = self.chunks[n]
        me = self.me
        a = self.acc[w].at[self.zk(k)]
        rows, half = a.shape[2], a.shape[3] // 2
        self.exchange(w, k, "x1").wait_recv()
        for j in range(2):
            add_rows(a.at[me.x, j, :, pl.ds(0, half)], self.rx1[w].at[k, j], rows)
        self.exchange(w, k, "y1").wait_recv()
        for i in range(2):
            add_rows(a.at[i, me.y, :, pl.ds(half, half)], self.ry1[w].at[k, i], rows)
        self.exchange(w, k, "y2").start()
        self.exchange(w, k, "x2").start()

    def s2(self, n):
        w, k = self.chunks[n]
        a = self.acc[w].at[self.zk(k), self.me.x, self.me.y]
        rows, half = a.shape[0], a.shape[1] // 2
        self.exchange(w, k, "y2").wait_recv()
        add_rows(a.at[:, pl.ds(0, half)], self.ry2[w].at[k], rows)
        self.exchange(w, k, "x2").wait_recv()
        add_rows(a.at[:, pl.ds(half, half)], self.rx2[w].at[k], rows)

    def s3(self, n):
        w, k = self.chunks[n]
        me = self.me
        a = self.acc[w].at[self.zk(k), me.x, me.y]
        rows = a.shape[0]

        def take(slot):
            there = self.rz[w].at[slot]
            remote(there, there, self.z_send.at[w, 0], self.z_recv.at[w, slot], me.partner).wait_recv()
            add_rows(a, there, rows)

        @pl.when(me.m == 0)
        def _():
            if k < 3:
                self.along(w, k, k, me.inner).start()
            else:
                take(0)

        @pl.when(me.m == 1)
        def _():
            if k == 0:
                take(0)
                self.along(w, k, 3, me.inner).start()
            elif k == 1:
                take(1)
                self.along(w, k, 4, me.inner).start()
            elif k == 2:
                take(3)
                self.along(w, k, 0, me.outer).start()
            else:
                take(2)
                take(4)

    def out_at(self, w, cc, xx, yy):
        half = self.shapes[w][1] // 2
        return self.outs[w].at[xx, yy, :, pl.ds(pl.multiple_of(cc * half, half), half)]

    def keep(self, w):
        me = self.me
        return pltpu.make_async_copy(
            self.acc[w].at[me.z, me.x, me.y], self.out_at(w, me.c, me.x, me.y), self.keep_sem.at[w]
        )

    def spread(self, w, kind):
        me = self.me
        c, x, y = me.c, me.x, me.y
        final, mine = self.acc[w].at[me.z, x, y], self.out_at(w, c, x, y)
        px, py = self.out_at(w, c, 1 - x, y), self.out_at(w, c, x, 1 - y)
        pd = self.out_at(w, c, 1 - x, 1 - y)
        src, dst, peer = {
            "x": (final, mine, me.across_x),
            "y": (final, mine, me.across_y),
            "c": (final, mine, me.partner),
            "yx": (half_rows(px, 0), half_rows(px, 0), me.across_y),
            "xy": (half_rows(py, 1), half_rows(py, 1), me.across_x),
            "cx": (px, px, me.partner),
            "cy": (py, py, me.partner),
            "cd": (pd, pd, me.partner),
        }[kind]
        index = SPREAD.index(kind)
        return remote(src, dst, self.o_send.at[w, index], self.o_recv.at[w, index], peer)

    def spread_arrived(self, w, kind):
        me = self.me
        c, x, y = me.c, me.x, me.y
        dst = {
            "x": lambda: self.out_at(w, c, 1 - x, y),
            "y": lambda: self.out_at(w, c, x, 1 - y),
            "yx": lambda: half_rows(self.out_at(w, c, 1 - x, 1 - y), 0),
            "xy": lambda: half_rows(self.out_at(w, c, 1 - x, 1 - y), 1),
            "c": lambda: self.out_at(w, 1 - c, x, y),
            "cx": lambda: self.out_at(w, 1 - c, 1 - x, y),
            "cy": lambda: self.out_at(w, 1 - c, x, 1 - y),
            "cd": lambda: self.out_at(w, 1 - c, 1 - x, 1 - y),
        }[kind]()
        index = SPREAD.index(kind)
        remote(dst, dst, self.o_send.at[w, index], self.o_recv.at[w, index], me.partner).wait_recv()

    def s4(self, w):
        self.keep(w).start()
        for kind in ("x", "y", "c"):
            self.spread(w, kind).start()

    def s5(self, w):
        self.spread_arrived(w, "x")
        self.spread(w, "yx").start()
        self.spread(w, "cx").start()
        self.spread_arrived(w, "y")
        self.spread(w, "xy").start()
        self.spread(w, "cy").start()

    def s6(self, w):
        self.spread_arrived(w, "yx")
        self.spread_arrived(w, "xy")
        self.spread(w, "cd").start()

    def group(self, n):
        total = len(self.chunks)
        if 0 <= n < total:
            self.s1(n)
        if 0 <= n - 1 < total:
            self.s2(n - 1)
        if 0 <= n - 2 < total:
            self.s3(n - 2)
            if self.chunks[n - 2][1] == 3:
                self.s4(self.chunks[n - 2][0])
        if 0 <= n - 4 < total and self.chunks[n - 4][1] == 3:
            self.s5(self.chunks[n - 4][0])
        if 0 <= n - 6 < total and self.chunks[n - 6][1] == 3:
            self.s6(self.chunks[n - 6][0])

    def finish(self):
        for n, (w, k) in enumerate(self.chunks):
            if k == 3:
                self.to_partner(n).wait_send()
            for kind in ROUNDS:
                self.exchange(w, k, kind).wait_send()
            if k < 3:
                self.along(w, k, k, self.me.inner).wait_send()
        for w in range(len(self.shapes)):
            self.keep(w).wait()
            for kind in SPREAD:
                self.spread(w, kind).wait_send()
            for kind in ("c", "cx", "cy", "cd"):
                self.spread_arrived(w, kind)


class Small:
    def __init__(self, me, mid, got, along, send, recv):
        self.me, self.mid, self.got, self.along_z, self.send, self.recv = me, mid, got, along, send, recv
        self.peers = (me.partner, me.across_x, me.across_y)

    def copy(self, step):
        return remote(self.mid.at[step], self.got.at[step], self.send.at[step], self.recv.at[step], self.peers[step])

    def along(self, j):
        there = {"z": lax.rem(self.me.z + 1 + j, NZ)}
        return remote(self.mid.at[3], self.along_z.at[self.me.z], self.send.at[3 + j], self.recv.at[3 + j], there)

    def step(self, n):
        if n < 6:
            step = n // 2
            if n % 2 == 0:
                self.copy(step).start()
            else:
                self.copy(step).wait()
                self.mid[step + 1] = self.mid[step] + self.got[step]
        elif n == 6:
            for j in range(3):
                self.along(j).start()
        else:
            for j in range(3):
                self.along(j).wait_send()
                there = self.along_z.at[lax.rem(self.me.z + 3 - j, NZ)]
                remote(there, there, self.send.at[3 + j], self.recv.at[3 + j], self.me.partner).wait_recv()
            self.along_z[pl.ds(self.me.z, 1)] = self.mid[pl.ds(3, 1)]

    def total(self):
        return (self.along_z[0] + self.along_z[1]) + (self.along_z[2] + self.along_z[3])


def backward_kernel(shapes, scalars, gains, head_gains, cosines, sines, *refs):
    (
        source,
        grad,
        h1_in,
        raw_in,
        tok_in,
        probs_in,
        attended_in,
        middle_in,
        h2_in,
        gate_up_in,
        block_rows_in,
        full_qkv,
        full_out,
        full_gate_up,
        full_down,
    ) = refs[:15]
    small_out, input_out, block_out = refs[15:18]
    outs = refs[18:22]
    rest = refs[22:]
    stage, acc, rz = rest[:4], rest[4:8], rest[8:12]
    rx1, ry1, rx2, ry2 = rest[12:14], rest[14:16], rest[16:18], rest[18:20]
    turned, wide, grad_mid, grads, outgoing, returned, small_mid, small_got, small_z, gain_sums, sums, input_low = rest[20:32]
    comm_sems = rest[32:41]
    (
        s_send,
        s_recv,
        load_sem,
        wide_sem,
        narrow_sem,
        gate_sem,
        prob_sem,
        tok_sem,
        raw_sem,
        swap_sem,
        out_sem,
        in_sem,
    ) = rest[41:]

    def like(refs, w):
        r, n = shapes[w]
        ref = refs[w % 2]
        if w < 2:
            return ref
        lead = (slice(None),) * (len(ref.shape) - 2)
        return ref.at[(*lead, pl.ds(0, r // 4), pl.ds(0, n // 4))]

    landing = [[like(group, w) for w in range(4)] for group in (rx1, ry1, rx2, ry2)]
    low, f32 = jnp.bfloat16, jnp.float32
    me = Place()
    z, c = me.z, me.c
    rows, width = grad_mid.shape
    block = rows // 2
    share = width // NZ
    comm = Reduce(me, shapes, (stage, acc, *landing, rz, outs), turned, comm_sems)
    small = Small(me, small_mid, small_got, small_z, s_send, s_recv)
    route = Route(me)
    me.greet()
    block_back = route.back(block_rows_in, block_out, out_sem)
    route.start(block_back)
    sums[...] = jnp.zeros_like(sums)
    gain_sums[...] = jnp.zeros_like(gain_sums)
    contract = (((1,), (1,)), ((), ()))
    depth = FF // NZ

    wide_loads = [(full_gate_up, k, t) for k in range(4) for t in range(3)]
    wide_loads += [(full_qkv, k, t) for k in range(4) for t in range(2)]
    wide_tile = wide.shape[3]

    def wide_load(j):
        full, k, t = wide_loads[j]
        src = full.at[comm.zk(k), :, :, pl.ds(t * wide_tile, wide_tile)]
        return pltpu.make_async_copy(src, wide.at[j % 2], wide_sem.at[j % 2])

    def against(j, count, left, target):
        k = wide_loads[j][1]
        total = None
        for t in range(count):
            wide_load(j + t).wait()
            if j + t + 1 < len(wide_loads):
                wide_load(j + t + 1).start()
            right = wide[(j + t) % 2].reshape(share, wide_tile)
            lhs = left[:, t * wide_tile : (t + 1) * wide_tile]
            part = lax.dot_general(lhs, right, contract, preferred_element_type=f32)
            total = part if t == 0 else total + part
        target[:, pl.ds(pl.multiple_of(comm.zk(k) * share, share), share)] = total

    def gain_row(index):
        return jnp.concatenate([gains[s, index : index + 1, :] for s in range(NZ)], axis=1)

    def norm_parts(v):
        inverse = lax.rsqrt(jnp.mean(v * v, axis=-1, keepdims=True) + EPSILON)
        return v * inverse, inverse

    def norm_grad(normed, inverse, g):
        return inverse * (g - normed * jnp.mean(g * normed, axis=-1, keepdims=True))

    def load(i, src, dst):
        return pltpu.make_async_copy(src, dst, load_sem.at[i])

    def feed_forward(g, h2, grad_gate_up, narrow, gate_up, middle):
        g_loads = [load(i, grad.at[i], g.at[pl.ds(i * block, block)]) for i in range(2)]

        def narrow_load(k):
            return pltpu.make_async_copy(full_down.at[comm.zk(k)], narrow.at[k % 2], narrow_sem.at[k % 2])

        def gate_load(k, part):
            at = pl.multiple_of(part * FF + comm.zk(k) * depth, depth)
            src = gate_up_in.at[:, pl.ds(at, depth)]
            return pltpu.make_async_copy(src, gate_up.at[k % 2, part], gate_sem.at[k % 2, part])

        def fetch(k):
            narrow_load(k).start()
            for part in range(2):
                gate_load(k, part).start()

        for copy in g_loads:
            copy.start()
        fetch(0)
        fetch(1)
        load(2, h2_in, h2).start()
        load(3, middle_in, middle).start()
        wide_load(0).start()
        for copy in g_loads:
            copy.wait()
        tile = depth // 2

        def hidden_part(k):
            narrow_load(k).wait()
            for part in range(2):
                gate_load(k, part).wait()

            def body(i, carry):
                at = pl.multiple_of(i * tile, tile)
                right = narrow[k % 2, pl.ds(i * 4, 4)].reshape(tile, width)
                grad_hidden = lax.dot_general(g[...], right, contract, preferred_element_type=f32)
                gate = gate_up[k % 2, 0, :, pl.ds(at, tile)].astype(f32)
                up = gate_up[k % 2, 1, :, pl.ds(at, tile)].astype(f32)
                sigmoid = jax.nn.sigmoid(gate)
                silu = gate * sigmoid
                turned[k % 2, pl.ds(at, tile), :] = jnp.transpose((silu * up).astype(low))
                there = pl.multiple_of(comm.zk(k) * depth + at, 128)
                grad_gate = grad_hidden * up * (sigmoid * (1.0 + gate * (1.0 - sigmoid)))
                grad_gate_up[:, pl.ds(there, tile)] = grad_gate.astype(low)
                grad_gate_up[:, pl.ds(pl.multiple_of(FF + there, 128), tile)] = (grad_hidden * silu).astype(low)
                return carry

            lax.fori_loop(0, 2, body, 0)
            if k + 2 < 4:
                fetch(k + 2)

        for n in range(4):
            hidden_part(n)
            comm.theirs(n, g)
            if n > 0:
                comm.ours(n - 1, g)
            comm.to_partner(n).start()
            if n > 0:
                comm.launch(n - 1)
            if n > 1:
                comm.group(n - 2)
        load(2, h2_in, h2).wait()
        for n in range(4, 8):
            comm.turn_rows(n, h2)
            comm.theirs(n, grad_gate_up)
            comm.ours(n - 1, g if n == 4 else grad_gate_up)
            comm.to_partner(n).start()
            comm.launch(n - 1)
            against((n - 4) * 3, 3, grad_gate_up, grad_mid)
            comm.group(n - 2)
        comm.ours(7, grad_gate_up)
        comm.launch(7)
        load(3, middle_in, middle).wait()

        def second_norm(at):
            normed, inverse = norm_parts(middle[at, :])
            grad_h2 = grad_mid[at, :]
            gain_sums[1:2, :] += jnp.sum(normed * grad_h2, axis=0, keepdims=True)
            grad_mid[at, :] = g[at, :].astype(f32) + norm_grad(normed, inverse, grad_h2 * gain_row(1))

        row_loop(rows, 64, second_norm)

    pl.run_scoped(
        feed_forward,
        pltpu.VMEM((rows, width), low),
        pltpu.VMEM((rows, width), low),
        pltpu.VMEM((rows, 2 * FF), low),
        pltpu.VMEM((2, *full_down.shape[1:]), low),
        pltpu.VMEM((2, 2, rows, depth), low),
        pltpu.VMEM((rows, width), f32),
    )

    half = HEADS * HD // 2

    def out_projection(attended, narrow, grad_low):
        def narrow_load(j):
            where = 2 * (1 - c) + j if j < 2 else 2 * c + j - 2
            return pltpu.make_async_copy(full_out.at[where], narrow.at[j % 2], narrow_sem.at[j % 2])

        narrow_load(0).start()
        narrow_load(1).start()
        load(0, attended_in, attended).start()

        def lower(at):
            grad_low[at, :] = grad_mid[at, :].astype(low)

        row_loop(rows, 64, lower)
        columns = half // 2
        swap = remote(outgoing, grads.at[pl.ds(2, 2)], swap_sem.at[0], swap_sem.at[1], me.partner)
        for j in range(4):
            narrow_load(j).wait()
            right = narrow[j % 2].reshape(columns, width)
            part = lax.dot_general(grad_low[...], right, contract, preferred_element_type=f32).astype(low)
            target = outgoing if j < 2 else grads
            for i in range(2):
                target[i, :, j % 2 * columns : (j % 2 + 1) * columns] = part[i * block : (i + 1) * block]
            if j + 2 < 4:
                narrow_load(j + 2).start()
            if j == 2:
                swap.start()
        load(0, attended_in, attended).wait()
        for n in range(8, 12):
            comm.turn_rows(n, attended)
            comm.theirs(n, grad_low)
            if n > 8:
                comm.ours(n - 1, grad_low)
            comm.to_partner(n).start()
            if n > 8:
                comm.launch(n - 1)
        comm.ours(11, grad_low)
        comm.launch(11)
        swap.wait()

    pl.run_scoped(
        out_projection,
        pltpu.VMEM((rows, HEADS * HD), low),
        pltpu.VMEM((2, *full_out.shape[1:]), low),
        pltpu.VMEM((rows, width), low),
    )
    comm.group(6)

    def sequence_part(own):
        def attention(tok, ordered, grad_ordered, p0, p1, p2, p3, grad_k, grad_v, placed, leaving):
            slots = (p0, p1, p2, p3)
            scale = 1.0 / math.sqrt(HD)

            def prob_load(h, i):
                n = (i + 1) * block
                src = probs_in.at[h, :, pl.ds(i * (i + 1) // 2 * block, n)]
                return pltpu.make_async_copy(src, slots[i], prob_sem.at[i])

            def tok_load(h, slot):
                at = pl.multiple_of(h * PER_HEAD, PER_HEAD)
                return pltpu.make_async_copy(tok_in.at[:, :, pl.ds(at, PER_HEAD)], tok.at[slot], tok_sem.at[slot])

            tok_load(0, 0).start()
            for i in reversed(range(BLOCKS)):
                prob_load(0, i).start()

            def one_head(h, carry):
                slot = lax.rem(h, 2)
                tok_load(h, slot).wait()

                @pl.when(h + 1 < HALF_HEADS)
                def _():
                    tok_load(h + 1, 1 - slot).start()

                at = pl.multiple_of(h * 2 * HD, 2 * HD)
                for i in range(BLOCKS):
                    here = slice(i * block, (i + 1) * block)
                    ordered[here] = pick(scalars[i], [tok[slot, j] for j in range(BLOCKS)])
                    grad_ordered[here] = pick(scalars[i], [grads[j, :, pl.ds(at, 2 * HD)] for j in range(BLOCKS)])
                for i in reversed(range(BLOCKS)):
                    n = (i + 1) * block
                    here = slice(i * block, n)
                    prob_load(h, i).wait()
                    query = stacked(ordered[here, : 2 * HD])
                    g = stacked(grad_ordered[here, :])
                    keys, values = ordered[:n, 2 * HD : 3 * HD], ordered[:n, 3 * HD :]
                    probs = slots[i][...]
                    weights = probs.astype(f32)
                    grad_probs = lax.dot_general(g, values, contract, preferred_element_type=f32)
                    delta = jnp.sum(weights * grad_probs, axis=-1, keepdims=True)
                    grad_scores = (weights * (grad_probs - delta)).astype(low)
                    grad_q = (jnp.dot(grad_scores, keys, preferred_element_type=f32) * scale).astype(low)
                    placed[here, :HD] = grad_q[:block]
                    placed[here, HD : 2 * HD] = grad_q[block:]
                    across = (((0,), (0,)), ((), ()))
                    part_k = lax.dot_general(query, grad_scores, across, preferred_element_type=f32)
                    part_v = lax.dot_general(g, probs, across, preferred_element_type=f32)
                    if i == BLOCKS - 1:
                        grad_k[...] = part_k
                        grad_v[...] = part_v
                    else:
                        grad_k[:, :n] += part_k
                        grad_v[:, :n] += part_v

                    @pl.when(h + 1 < HALF_HEADS)
                    def _():
                        prob_load(h + 1, i).start()

                for i in range(BLOCKS):
                    here = slice(i * block, (i + 1) * block)
                    placed[here, 2 * HD : 3 * HD] = jnp.transpose(grad_k[:, here] * scale).astype(low)
                    placed[here, 3 * HD :] = jnp.transpose(grad_v[:, here]).astype(low)
                columns = pl.ds(pl.multiple_of(h * PER_HEAD, PER_HEAD), PER_HEAD)
                for j in range(BLOCKS):
                    value = pick(scalars[BLOCKS + j], [placed[i * block : (i + 1) * block] for i in range(BLOCKS)])
                    target = own if j < 2 else leaving
                    target[j % 2 * block : (j % 2 + 1) * block, columns] = value
                for now, n in BACK_GROUPS.items():

                    @pl.when(h == now)
                    def _(n=n):
                        comm.group(n)

                return carry

            lax.fori_loop(0, HALF_HEADS, one_head, 0)
            swap = remote(leaving, returned, swap_sem.at[2], swap_sem.at[3], me.partner)
            swap.start()
            comm.group(10)
            swap.wait()

        pl.run_scoped(
            attention,
            pltpu.VMEM((2, 4, block, PER_HEAD), low),
            pltpu.VMEM((4 * block, PER_HEAD), low),
            pltpu.VMEM((4 * block, 2 * HD), low),
            *[pltpu.VMEM((2 * block, (i + 1) * block), low) for i in range(BLOCKS)],
            pltpu.VMEM((HD, 4 * block), f32),
            pltpu.VMEM((HD, 4 * block), f32),
            pltpu.VMEM((4 * block, PER_HEAD), low),
            pltpu.VMEM((rows, HALF_HEADS * PER_HEAD), low),
        )

        def projection(grad_qkv, raw, h1, x, grad_first):
            load(0, h1_in, h1).start()
            for i in range(2):
                load(2 + i, source.at[i], x.at[pl.ds(i * block, block)]).start()

            def raw_load(j, slot):
                which = c + j // HALF_HEADS * (1 - 2 * c)
                at = pl.multiple_of(lax.rem(j, HALF_HEADS) * PER_HEAD, PER_HEAD)
                return pltpu.make_async_copy(raw_in.at[which, :, pl.ds(at, PER_HEAD)], raw.at[slot], raw_sem.at[slot])

            raw_load(0, 0).start()

            def one_head(j, came):
                slot = lax.rem(j, 2)
                raw_load(j, slot).wait()

                @pl.when(j + 1 < KV_HEADS)
                def _():
                    raw_load(j + 1, 1 - slot).start()

                at = pl.multiple_of(lax.rem(j, HALF_HEADS) * PER_HEAD, PER_HEAD)
                h = lax.rem(j, HALF_HEADS) + HALF_HEADS * (c + j // HALF_HEADS * (1 - 2 * c))
                places = (h * 2 * HD, (h * 2 + 1) * HD, (HEADS + h) * HD)
                for i, (row, place) in enumerate(zip((0, 0, 1), places)):
                    normed, inverse = norm_parts(raw[slot, :, i * HD : (i + 1) * HD].astype(f32))
                    g = came[:, pl.ds(pl.multiple_of(at + i * HD, HD), HD)].astype(f32)
                    g = g * cosines[...] - turn(g) * sines[...]
                    sums[row : row + 1, :] += jnp.sum(normed * g, axis=0, keepdims=True)
                    back = norm_grad(normed, inverse, g * head_gains[row : row + 1, :])
                    grad_qkv[:, pl.ds(pl.multiple_of(place, HD), HD)] = back.astype(low)
                there = pl.multiple_of((HEADS + KV_HEADS + h) * HD, HD)
                grad_qkv[:, pl.ds(there, HD)] = came[:, pl.ds(pl.multiple_of(at + 3 * HD, HD), HD)]

            def own_head(i, carry):
                one_head(i, own)
                return carry

            def other_head(i, carry):
                one_head(i + HALF_HEADS, returned)
                return carry

            lax.fori_loop(0, HALF_HEADS, own_head, 0)
            comm.group(11)
            lax.fori_loop(0, HALF_HEADS, other_head, 0)
            load(0, h1_in, h1).wait()
            for n in range(12, 16):
                comm.turn_rows(n, h1)
                comm.theirs(n, grad_qkv)
                if n > 12:
                    comm.ours(n - 1, grad_qkv)
                comm.to_partner(n).start()
                if n > 12:
                    comm.launch(n - 1)
            comm.ours(15, grad_qkv)
            comm.launch(15)
            comm.group(12)
            for k in range(4):
                against(12 + k * 2, 2, grad_qkv, grad_first)
                if k == 1:
                    comm.group(13)
            for i in range(2):
                load(2 + i, source.at[i], x.at[pl.ds(i * block, block)]).wait()
            for i in range(2):

                def first_norm(at, i=i):
                    here = pl.ds(pl.multiple_of(i * block + at.start, 64), 64)
                    normed, inverse = norm_parts(x[here, :].astype(f32))
                    g = grad_first[here, :]
                    gain_sums[0:1, :] += jnp.sum(normed * g, axis=0, keepdims=True)
                    total = grad_mid[here, :] + norm_grad(normed, inverse, g * gain_row(0))
                    input_low[i, at, :] = total.astype(low)

                row_loop(block, 64, first_norm)

        pl.run_scoped(
            projection,
            pltpu.VMEM((rows, (HEADS + 2 * KV_HEADS) * HD), low),
            pltpu.VMEM((2, rows, PER_HEAD), low),
            pltpu.VMEM((rows, width), low),
            pltpu.VMEM((rows, width), low),
            pltpu.VMEM((rows, width), f32),
        )

    pl.run_scoped(sequence_part, pltpu.VMEM((rows, HALF_HEADS * PER_HEAD), low))

    small_mid[0] = jnp.zeros(small_mid.shape[1:], f32)
    for row in range(2):
        for i in range(width // HD):
            small_mid[0, row * 8 + i : row * 8 + i + 1, :] = gain_sums[row : row + 1, i * HD : (i + 1) * HD]
    small_mid[0, 16:24, :] = sums[...]
    input_back = route.back(input_low, input_out, in_sem)
    comm.group(14)
    route.start(input_back)
    for n in range(8):
        small.step(n)
        comm.group(15 + n)
    small_out[...] = small.total()
    comm.finish()
    route.wait(block_back)
    route.wait(input_back)


BACK_GROUPS = {1: 7, 2: 8, 3: 9}


def run_backward(scalars, gains_all, head_gains, cosines, sines, saved, block_rows, fulls):
    low, f32 = jnp.bfloat16, jnp.float32
    source = saved[0]
    _, slot_len, width = source.shape
    rows = 2 * slot_len
    full_qkv, full_out, full_gate_up, full_down = fulls
    order = (full_down, full_gate_up, full_out, full_qkv)
    shapes = [(8 * f.shape[2], f.shape[3]) for f in order]
    shape = jax.ShapeDtypeStruct
    hbm = pl.BlockSpec(memory_space=HBM)
    vmem = pl.BlockSpec(memory_space=pltpu.VMEM)
    dma = pltpu.SemaphoreType.DMA
    count = len(shapes)

    def buffers(make, which):
        return [pltpu.VMEM(make(r // 4, n // 2), low) for r, n in which]

    out = pl.pallas_call(
        functools.partial(backward_kernel, shapes),
        out_shape=[
            shape((24, HD), f32),
            shape(source.shape, low),
            shape(source.shape, low),
            *[shape((2, 2, r // 4, n), low) for r, n in shapes],
        ],
        in_specs=[pl.BlockSpec(memory_space=pltpu.SMEM)] + [vmem] * 4 + [hbm] * 15,
        out_specs=[vmem] + [hbm] * 6,
        scratch_shapes=buffers(lambda r, n: (2, 2, r, n), shapes)
        + buffers(lambda r, n: (NZ, 2, 2, r, n), shapes)
        + buffers(lambda r, n: (5, r, n), shapes)
        + buffers(lambda r, n: (NZ, 2, r, n // 2), shapes[:2])
        + buffers(lambda r, n: (NZ, 2, r, n // 2), shapes[:2])
        + buffers(lambda r, n: (NZ, r, n // 2), shapes[:2])
        + buffers(lambda r, n: (NZ, r, n // 2), shapes[:2])
        + [
            pltpu.VMEM((2, max(r for r, _ in shapes), rows), low),
            pltpu.VMEM((2, 8, full_gate_up.shape[2], 2 * width), low),
            pltpu.VMEM((rows, width), f32),
            pltpu.VMEM((4, slot_len, HEADS * HD // 2), low),
            pltpu.VMEM((2, slot_len, HEADS * HD // 2), low),
            pltpu.VMEM((rows, HALF_HEADS * PER_HEAD), low),
            pltpu.VMEM((4, 24, HD), f32),
            pltpu.VMEM((3, 24, HD), f32),
            pltpu.VMEM((NZ, 24, HD), f32),
            pltpu.VMEM((8, width), f32),
            pltpu.VMEM((8, HD), f32),
            pltpu.VMEM((2, slot_len, width), low),
            dma((count,)),
            dma((count, 4)),
            dma((count, 4)),
            dma((count, 4, 4)),
            dma((count, 4, 4)),
            dma((count, 4)),
            dma((count, 5)),
            dma((count, len(SPREAD))),
            dma((count, len(SPREAD))),
            dma((6,)),
            dma((6,)),
            dma((4,)),
            dma((2,)),
            dma((2,)),
            dma((2, 2)),
            dma((BLOCKS,)),
            dma((2,)),
            dma((2,)),
            dma((4,)),
            dma((5,)),
            dma((5,)),
        ],
        compiler_params=pltpu.CompilerParams(collective_id=1, has_side_effects=True, vmem_limit_bytes=VMEM_LIMIT),
        name="backward",
    )(scalars, gains_all, head_gains, cosines, sines, *saved, block_rows, *fulls)
    return out[0], out[1], out[2], [o.reshape(r, n) for o, (r, n) in zip(out[3:], shapes)]


def swap(v):
    return lax.ppermute(v, "core", [(0, 1), (1, 0)])


def per_chip(
    tokens,
    cotangent,
    slot_order,
    attn_gain,
    q_gain,
    k_gain,
    w_qkv,
    w_out,
    mlp_gain,
    w_gate_up,
    w_down,
):
    z, core = lax.axis_index("z"), lax.axis_index("core")
    _, slot_len, width = tokens.shape
    f32, low = jnp.float32, jnp.bfloat16
    odd = z % 2
    orders = jnp.where(z // 2 == core, slot_order, swap(slot_order))
    order = lax.dynamic_index_in_dim(orders, odd, 0, False)
    slots = jnp.stack([2 * core + odd, 2 * core + 1 - odd, 2 - 2 * core + odd, 3 - 2 * core - odd])
    blocks = order[slots]
    where_is = jnp.sum(
        jnp.where(blocks[None, :] == jnp.arange(4)[:, None], jnp.arange(4)[None, :], 0), axis=1
    )
    scalars = jnp.concatenate([where_is, blocks, core[None], jnp.zeros((7,), jnp.int32)]).astype(jnp.int32)
    positions = (blocks[:2, None] * slot_len + jnp.arange(slot_len)[None, :]).reshape(-1)
    cos, sin = rope_tables(positions)
    cosines = jnp.concatenate([cos, cos], axis=1)
    sines = jnp.concatenate([-sin, sin], axis=1)
    gain_q, gain_k = q_gain.astype(f32)[None, :], k_gain.astype(f32)[None, :]
    head_gains = jnp.concatenate([gain_q, gain_k, jnp.zeros((6, HD), f32)], axis=0)
    gains = jnp.concatenate(
        [attn_gain.astype(f32)[None], mlp_gain.astype(f32)[None], jnp.zeros((6, attn_gain.shape[0]), f32)], axis=0
    )
    (block_rows, gains_all, *saved), fulls = run_forward(
        scalars, gains, head_gains, cosines, sines, tokens, cotangent, [w_qkv, w_out, w_gate_up, w_down]
    )
    sums, input_grad, block_out, (down_sum, gate_up_sum, out_sum, qkv_sum) = run_backward(
        scalars, gains_all, head_gains, cosines, sines, saved, block_rows.reshape(2, slot_len, width), fulls
    )
    count = width // HD
    share = width // NZ
    return (
        block_out,
        input_grad,
        lax.dynamic_slice_in_dim(sums[:count].reshape(-1), z * share, share, 0),
        sums[2 * count],
        sums[2 * count + 1],
        qkv_sum.astype(f32),
        out_sum.astype(f32),
        lax.dynamic_slice_in_dim(sums[count : 2 * count].reshape(-1), z * share, share, 0),
        gate_up_sum.astype(f32),
        down_sum.astype(f32),
    )


def solution(mesh):
    group, replica, body = "group", "replica", per_device
    if (mesh.shape["group"], mesh.shape["replica"]) == (NZ, 8):
        mesh = Mesh(mesh.devices.reshape(NZ, 2, 2, 2), ("z", "y", "x", "core"))
        group, replica, body = "z", ("y", "x", "core"), per_chip
    in_specs = (
        P(replica, group, None),
        P(replica, group, None),
        P(replica, None),
        P(group),
        P(),
        P(),
        P(group, None),
        P(group, None),
        P(group),
        P(group, None),
        P(group, None),
    )
    out_specs = (
        P(replica, group, None),
        P(replica, group, None),
        P(group),
        P(),
        P(),
        P(group, None),
        P(group, None),
        P(group),
        P(group, None),
        P(group, None),
    )
    return jax.shard_map(
        body, mesh=mesh, in_specs=in_specs, out_specs=out_specs, check_vma=False
    )
```

```python
import functools
import math

import jax
import jax.numpy as jnp
from jax import lax
from jax.experimental import pallas as pl
from jax.experimental.pallas import tpu as pltpu
from jax.sharding import Mesh
from jax.sharding import PartitionSpec as P

HEADS = 16
KV_HEADS = 8
HD = 128
FF = 3072


EPSILON = 1e-06
THETA_BASE = 1000000.0
MASKED = -1e30


def norm_rows(v):
    return v * lax.rsqrt(jnp.mean(v * v, axis=-1, keepdims=True) + EPSILON)


def norm_back(source, grad):
    inverse = lax.rsqrt(jnp.mean(source * source, axis=-1, keepdims=True) + EPSILON)
    normed = source * inverse
    return inverse * (grad - normed * jnp.mean(grad * normed, axis=-1, keepdims=True))


def rotate(v, cosines, sines):
    half_size = v.shape[-1] // 2
    leading = v[..., :half_size]
    trailing = v[..., half_size:]
    return jnp.concatenate(
        [leading * cosines - trailing * sines, trailing * cosines + leading * sines], axis=-1
    )


def rope_tables(positions):
    half_size = HD // 2
    counter = jnp.arange(half_size).astype(jnp.float32)
    frequency = THETA_BASE ** (-2.0 * counter / HD)
    angles = positions.astype(jnp.float32)[:, None] * frequency[None, :]
    return (jnp.cos(angles), jnp.sin(angles))


def matmul(a, b):
    return jnp.dot(a, b, preferred_element_type=jnp.float32)


def matmul_right(a, b):
    return lax.dot_general(a, b, (((1,), (1,)), ((), ())), preferred_element_type=jnp.float32)


def matmul_left(a, b):
    return lax.dot_general(a, b, (((0,), (0,)), ((), ())), preferred_element_type=jnp.float32)


def per_device(
    tokens,
    cotangent,
    slot_order,
    attn_gain,
    q_gain,
    k_gain,
    w_qkv,
    w_out,
    mlp_gain,
    w_gate_up,
    w_down,
):
    member_count = lax.axis_size("group")
    member = lax.axis_index("group")
    micro, slot_len, width = tokens.shape
    rows = micro * slot_len
    length = slot_len * member_count
    q_width = HEADS * HD
    kv_width = KV_HEADS * HD
    groups = HEADS // KV_HEADS
    score_scale = 1.0 / math.sqrt(HD)
    key_block = math.gcd(length, 512)
    block_count = length // key_block
    head_gain_q = q_gain.astype(jnp.float32)
    head_gain_k = k_gain.astype(jnp.float32)
    offsets = jnp.arange(slot_len, dtype=jnp.int32)
    source = tokens.reshape(rows, width).astype(jnp.float32)
    all_pos = (slot_order[:, :, None] * slot_len + offsets[None, None, :]).reshape(micro, length)
    my_pos = lax.dynamic_slice_in_dim(all_pos, member * slot_len, slot_len, 1)
    query_top = jnp.max(my_pos, axis=1)
    cosines, sines = rope_tables(my_pos.reshape(rows))
    normed_first = norm_rows(source)
    gain_piece = lax.all_gather(attn_gain, "group", axis=0, tiled=True)
    weight_piece = lax.all_gather(w_qkv, "group", axis=0, tiled=True)
    columns = normed_first
    low_cols = (columns * gain_piece.astype(jnp.float32)).astype(jnp.bfloat16)
    qkv = matmul(low_cols, weight_piece)
    first_low = low_cols
    gain_first = gain_piece.astype(jnp.float32)
    queries = qkv[:, :q_width].reshape(rows, HEADS, HD)
    keys_raw = qkv[:, q_width : q_width + kv_width].reshape(rows, KV_HEADS, HD)
    values_low = qkv[:, q_width + kv_width :].astype(jnp.bfloat16)
    queries_normed = norm_rows(queries)
    keys_normed = norm_rows(keys_raw)
    query_rot = rotate(queries_normed * head_gain_q, cosines[:, None, :], sines[:, None, :]).astype(
        jnp.bfloat16
    )
    key_rot = rotate(keys_normed * head_gain_k, cosines[:, None, :], sines[:, None, :]).astype(
        jnp.bfloat16
    )
    key_all, value_all = (
        lax.all_gather(key_rot.reshape(micro, slot_len, kv_width), "group", axis=1, tiled=True),
        lax.all_gather(values_low.reshape(micro, slot_len, kv_width), "group", axis=1, tiled=True),
    )
    query_heads = query_rot.reshape(micro, slot_len, KV_HEADS, groups, HD)

    def block_live(block_index):
        key_pos = lax.dynamic_slice_in_dim(all_pos, block_index * key_block, key_block, 1)
        return jnp.any(jnp.min(key_pos, axis=1) <= query_top)

    def block_scores(block_index):
        begin = block_index * key_block
        key_piece = lax.dynamic_slice_in_dim(key_all, begin, key_block, 1).reshape(
            micro, key_block, KV_HEADS, HD
        )
        key_pos = lax.dynamic_slice_in_dim(all_pos, begin, key_block, 1)
        raw = (
            jnp.einsum(
                "mqkgd,mskd->mkgqs", query_heads, key_piece, preferred_element_type=jnp.float32
            )
            * score_scale
        )
        allowed = (key_pos[:, None, :] <= my_pos[:, :, None])[:, None, None]
        return (jnp.where(allowed, raw, MASKED), allowed, key_piece)

    def stats_step(block_index, carry):

        def stats_visit_block(carry_in):
            top_in, total_in = carry_in
            scores, allowed, key_piece = block_scores(block_index)
            new_top = jnp.maximum(top_in, jnp.max(scores, axis=-1))
            summed = jnp.sum(jnp.where(allowed, jnp.exp(scores - new_top[..., None]), 0.0), axis=-1)
            return (new_top, total_in * jnp.exp(top_in - new_top) + summed)

        return lax.cond(
            block_live(block_index), stats_visit_block, lambda carry_in: carry_in, carry
        )

    stat_shape = (micro, KV_HEADS, groups, slot_len)
    top_final, total_final = lax.fori_loop(
        0,
        block_count,
        stats_step,
        (jnp.full(stat_shape, MASKED, jnp.float32), jnp.zeros(stat_shape, jnp.float32)),
    )
    log_total = top_final + jnp.log(total_final)

    def output_step(block_index, accum):

        def output_visit_block(accum_in):
            scores, allowed, key_piece = block_scores(block_index)
            probabilities = jnp.where(allowed, jnp.exp(scores - log_total[..., None]), 0.0)
            value_piece = lax.dynamic_slice_in_dim(
                value_all, block_index * key_block, key_block, 1
            ).reshape(micro, key_block, KV_HEADS, HD)
            return accum_in + jnp.einsum(
                "mkgqs,mskd->mqkgd",
                probabilities.astype(jnp.bfloat16),
                value_piece,
                preferred_element_type=jnp.float32,
            )

        return lax.cond(
            block_live(block_index), output_visit_block, lambda accum_in: accum_in, accum
        )

    attn_heads = lax.fori_loop(
        0, block_count, output_step, jnp.zeros((micro, slot_len, KV_HEADS, groups, HD), jnp.float32)
    )
    attended = attn_heads.reshape(rows, q_width).astype(jnp.bfloat16)
    columns = attended
    branch = matmul(columns, lax.all_gather(w_out, "group", axis=0, tiled=True))
    middle = source + branch
    normed_second = norm_rows(middle)
    gain_piece = lax.all_gather(mlp_gain, "group", axis=0, tiled=True)
    weight_piece = lax.all_gather(w_gate_up, "group", axis=0, tiled=True)
    columns = normed_second
    low_cols = (columns * gain_piece.astype(jnp.float32)).astype(jnp.bfloat16)
    gate_up = matmul(low_cols, weight_piece)
    gain_second = gain_piece.astype(jnp.float32)
    gate_part = gate_up[:, :FF]
    up_part = gate_up[:, FF:]
    sigmoid_gate = jax.nn.sigmoid(gate_part)
    silu_gate = gate_part * sigmoid_gate
    hidden = (silu_gate * up_part).astype(jnp.bfloat16)
    columns = hidden
    down_out = matmul(columns, lax.all_gather(w_down, "group", axis=0, tiled=True))
    block_out = (middle + down_out).astype(jnp.bfloat16).reshape(micro, slot_len, width)
    grad_low = cotangent.reshape(rows, width)
    grad_output = grad_low.astype(jnp.float32)
    down_full = matmul_left(hidden, grad_low)
    grad_hidden = matmul_right(grad_low, lax.all_gather(w_down, "group", axis=0, tiled=True))
    grad_gate = grad_hidden * up_part * (sigmoid_gate * (1.0 + gate_part * (1.0 - sigmoid_gate)))
    grad_upper = grad_hidden * silu_gate
    grad_gate_up = jnp.concatenate([grad_gate, grad_upper], axis=1).astype(jnp.bfloat16)
    gate_up_full = matmul_left(low_cols, grad_gate_up)
    grad_second = matmul_right(grad_gate_up, lax.all_gather(w_gate_up, "group", axis=0, tiled=True))
    gain_second_full = jnp.sum(normed_second * grad_second, axis=0)
    grad_middle = grad_output + norm_back(middle, grad_second * gain_second)
    grad_mid_low = grad_middle.astype(jnp.bfloat16)
    out_full = matmul_left(attended, grad_mid_low)
    grad_attn_full = matmul_right(grad_mid_low, lax.all_gather(w_out, "group", axis=0, tiled=True))
    grad_attn = grad_attn_full.astype(jnp.bfloat16)
    grad_heads = grad_attn.reshape(micro, slot_len, KV_HEADS, groups, HD)
    delta = jnp.transpose(
        jnp.sum(grad_heads.astype(jnp.float32) * attn_heads, axis=-1), (0, 2, 3, 1)
    )

    def back_step(block_index, carry):

        def back_visit_block(carry_in):
            grad_query_in, grad_key_in, grad_value_in = carry_in
            begin = block_index * key_block
            scores, allowed, key_piece = block_scores(block_index)
            probabilities = jnp.where(allowed, jnp.exp(scores - log_total[..., None]), 0.0)
            value_piece = lax.dynamic_slice_in_dim(value_all, begin, key_block, 1).reshape(
                micro, key_block, KV_HEADS, HD
            )
            grad_probs = jnp.einsum(
                "mqkgd,mskd->mkgqs", grad_heads, value_piece, preferred_element_type=jnp.float32
            )
            grad_scores = (probabilities * (grad_probs - delta[..., None])).astype(jnp.bfloat16)
            grad_query_out = (
                grad_query_in
                + jnp.einsum(
                    "mkgqs,mskd->mqkgd", grad_scores, key_piece, preferred_element_type=jnp.float32
                )
                * score_scale
            )
            key_term = (
                jnp.einsum(
                    "mkgqs,mqkgd->mskd",
                    grad_scores,
                    query_heads,
                    preferred_element_type=jnp.float32,
                )
                * score_scale
            )
            value_term = jnp.einsum(
                "mkgqs,mqkgd->mskd",
                probabilities.astype(jnp.bfloat16),
                grad_heads,
                preferred_element_type=jnp.float32,
            )
            key_old = lax.dynamic_slice_in_dim(grad_key_in, begin, key_block, 1)
            value_old = lax.dynamic_slice_in_dim(grad_value_in, begin, key_block, 1)
            grad_key_out = lax.dynamic_update_slice_in_dim(
                grad_key_in, key_old + key_term, begin, 1
            )
            grad_value_out = lax.dynamic_update_slice_in_dim(
                grad_value_in, value_old + value_term, begin, 1
            )
            return (grad_query_out, grad_key_out, grad_value_out)

        return lax.cond(block_live(block_index), back_visit_block, lambda carry_in: carry_in, carry)

    back_start = (
        jnp.zeros((micro, slot_len, KV_HEADS, groups, HD), jnp.float32),
        jnp.zeros((micro, length, KV_HEADS, HD), jnp.float32),
        jnp.zeros((micro, length, KV_HEADS, HD), jnp.float32),
    )
    grad_query_rot, grad_key_all, grad_value_all = lax.fori_loop(
        0, block_count, back_step, back_start
    )
    grad_key_mine, grad_value_mine = (
        lax.psum_scatter(
            grad_key_all.reshape(micro, length, kv_width).astype(jnp.bfloat16),
            "group",
            scatter_dimension=1,
            tiled=True,
        ).astype(jnp.float32),
        lax.psum_scatter(
            grad_value_all.reshape(micro, length, kv_width).astype(jnp.bfloat16),
            "group",
            scatter_dimension=1,
            tiled=True,
        ).astype(jnp.float32),
    )
    grad_query_norm = rotate(
        grad_query_rot.reshape(rows, HEADS, HD), cosines[:, None, :], -sines[:, None, :]
    )
    grad_key_norm = rotate(
        grad_key_mine.reshape(rows, KV_HEADS, HD), cosines[:, None, :], -sines[:, None, :]
    )
    q_gain_total = jnp.sum(queries_normed * grad_query_norm, axis=(0, 1))
    k_gain_total = jnp.sum(keys_normed * grad_key_norm, axis=(0, 1))
    grad_queries = norm_back(queries, grad_query_norm * head_gain_q).reshape(rows, q_width)
    grad_keys = norm_back(keys_raw, grad_key_norm * head_gain_k).reshape(rows, kv_width)
    grad_qkv = jnp.concatenate(
        [grad_queries, grad_keys, grad_value_mine.reshape(rows, kv_width)], axis=1
    ).astype(jnp.bfloat16)
    qkv_full = matmul_left(first_low, grad_qkv)
    grad_first = matmul_right(grad_qkv, lax.all_gather(w_qkv, "group", axis=0, tiled=True))
    gain_first_full = jnp.sum(normed_first * grad_first, axis=0)
    input_grad = (
        (grad_middle + norm_back(source, grad_first * gain_first))
        .astype(jnp.bfloat16)
        .reshape(micro, slot_len, width)
    )
    owned = (
        lax.psum_scatter(
            gain_first_full.astype(jnp.bfloat16), "group", scatter_dimension=0, tiled=True
        ).astype(jnp.float32),
        lax.psum_scatter(
            qkv_full.astype(jnp.bfloat16), "group", scatter_dimension=0, tiled=True
        ).astype(jnp.float32),
        lax.psum_scatter(
            out_full.astype(jnp.bfloat16), "group", scatter_dimension=0, tiled=True
        ).astype(jnp.float32),
        lax.psum_scatter(
            gain_second_full.astype(jnp.bfloat16), "group", scatter_dimension=0, tiled=True
        ).astype(jnp.float32),
        lax.psum_scatter(
            gate_up_full.astype(jnp.bfloat16), "group", scatter_dimension=0, tiled=True
        ).astype(jnp.float32),
        lax.psum_scatter(
            down_full.astype(jnp.bfloat16), "group", scatter_dimension=0, tiled=True
        ).astype(jnp.float32),
    )
    summed = (
        lax.psum(owned[0].astype(jnp.bfloat16), "replica").astype(jnp.float32),
        lax.psum(owned[1].astype(jnp.bfloat16), "replica").astype(jnp.float32),
        lax.psum(owned[2].astype(jnp.bfloat16), "replica").astype(jnp.float32),
        lax.psum(owned[3].astype(jnp.bfloat16), "replica").astype(jnp.float32),
        lax.psum(owned[4].astype(jnp.bfloat16), "replica").astype(jnp.float32),
        lax.psum(owned[5].astype(jnp.bfloat16), "replica").astype(jnp.float32),
    )
    head_sums = lax.psum((q_gain_total, k_gain_total), ("group", "replica"))
    return (
        block_out,
        input_grad,
        summed[0],
        head_sums[0],
        head_sums[1],
        summed[1],
        summed[2],
        summed[3],
        summed[4],
        summed[5],
    )


MESH_ID = pl.DeviceIdType.MESH
HBM = pltpu.MemorySpace.HBM
VMEM_LIMIT = 64 * 1024 * 1024 - 65536
NZ = 4


class Place:
    def __init__(self):
        self.z = lax.axis_index("z")
        self.y = lax.axis_index("y")
        self.x = lax.axis_index("x")
        self.c = lax.axis_index("core")
        self.h = self.z // 2
        self.m = self.at(self.z)
        self.inner = {"z": self.at(self.m + 1)}
        self.outer = {"z": self.at(lax.rem(self.m + 3, 4))}
        self.across_x = {"x": 1 - self.x}
        self.across_y = {"y": 1 - self.y}
        self.partner = {"core": 1 - self.c}

    def at(self, t):
        return t * (1 - 2 * self.h) + 3 * self.h

    def greet(self):
        barrier = pltpu.get_barrier_semaphore()
        peers = [self.across_x, self.across_y, self.partner]
        for hop in range(1, NZ):
            there = lax.rem(self.z + hop, NZ)
            peers += [{"z": there}, {"z": there, "core": 1 - self.c}]
        for peer in peers:
            pl.semaphore_signal(barrier, inc=1, device_id=peer, device_id_type=MESH_ID)
        pl.semaphore_wait(barrier, len(peers))


def remote(src, dst, send, recv, peer):
    return pltpu.make_async_remote_copy(
        src_ref=src, dst_ref=dst, send_sem=send, recv_sem=recv, device_id=peer, device_id_type=MESH_ID
    )


KINDS = ("x", "y", "yx", "xy", "c", "cx", "cy", "cd")


def half_rows(ref, which):
    rows = ref.shape[0] // 2
    return ref.at[pl.ds(which * rows, rows), :]


class Gather:
    def __init__(self, me, shards, fulls, sems):
        self.me, self.shards, self.fulls = me, shards, fulls
        self.z_send, self.z_recv, self.f_send, self.xy_send, self.xy_recv = sems
        self.stage_t = (1 - me.m, 2, 3)
        self.stages = [(w, k) for w in range(len(shards)) for k in range(3)]

    def piece(self, c, x, y):
        return c * 4 + x * 2 + y

    def shard_z(self, k):
        return self.me.at(self.stage_t[k])

    def own_copy(self, w, peer, k, slot):
        me = self.me
        piece = self.piece(me.c, me.x, me.y)
        return remote(
            self.shards[w].at[piece],
            self.fulls[w].at[me.z, piece],
            self.z_send.at[w, slot],
            self.z_recv.at[w, k],
            peer,
        )

    def own(self, w):
        me = self.me
        self.own_copy(w, me.inner, me.m, 0).start()

        @pl.when(me.m == 1)
        def _():
            self.own_copy(w, me.outer, 0, 1).start()

    def place(self, w, k, cc, xx, yy):
        return self.fulls[w].at[self.shard_z(k), self.piece(cc, xx, yy)]

    def forward(self, w, k):
        me = self.me
        piece = self.place(w, k, me.c, me.x, me.y)
        peer, slot = ((me.inner, 2), (me.outer, 1), (me.outer, 2))[k]
        return remote(piece, piece, self.f_send.at[w, k], self.z_recv.at[w, slot], peer)

    def hop(self, w, k, kind):
        me = self.me
        c, x, y = me.c, me.x, me.y
        mine, px = self.place(w, k, c, x, y), self.place(w, k, c, 1 - x, y)
        py, pd = self.place(w, k, c, x, 1 - y), self.place(w, k, c, 1 - x, 1 - y)
        src, peer = {
            "x": (mine, me.across_x),
            "y": (mine, me.across_y),
            "yx": (half_rows(px, 0), me.across_y),
            "xy": (half_rows(py, 1), me.across_x),
            "c": (mine, me.partner),
            "cx": (px, me.partner),
            "cy": (py, me.partner),
            "cd": (pd, me.partner),
        }[kind]
        index = KINDS.index(kind)
        return remote(src, src, self.xy_send.at[w, k, index], self.xy_recv.at[w, k, index], peer)

    def arrived(self, w, k, kind):
        me = self.me
        c, x, y = me.c, me.x, me.y
        dst = {
            "x": lambda: self.place(w, k, c, 1 - x, y),
            "y": lambda: self.place(w, k, c, x, 1 - y),
            "yx": lambda: half_rows(self.place(w, k, c, 1 - x, 1 - y), 0),
            "xy": lambda: half_rows(self.place(w, k, c, 1 - x, 1 - y), 1),
            "c": lambda: self.place(w, k, 1 - c, x, y),
            "cx": lambda: self.place(w, k, 1 - c, 1 - x, y),
            "cy": lambda: self.place(w, k, 1 - c, x, 1 - y),
            "cd": lambda: self.place(w, k, 1 - c, 1 - x, 1 - y),
        }[kind]()
        index = KINDS.index(kind)
        remote(dst, dst, self.xy_send.at[w, k, index], self.xy_recv.at[w, k, index], me.partner).wait_recv()

    def relay(self, i):
        w, k = self.stages[i]
        me = self.me
        mine = self.place(w, k, me.c, me.x, me.y)
        remote(mine, mine, self.f_send.at[w, k], self.z_recv.at[w, k], me.partner).wait_recv()

        @pl.when(me.m == 1)
        def _():
            self.forward(w, k).start()

    def launch(self, i):
        w, k = self.stages[i]
        for kind in ("x", "y", "c"):
            self.hop(w, k, kind).start()

    def sx(self, i):
        w, k = self.stages[i]
        self.arrived(w, k, "x")
        self.hop(w, k, "yx").start()
        self.hop(w, k, "cx").start()

    def sy(self, i):
        w, k = self.stages[i]
        self.arrived(w, k, "y")
        self.hop(w, k, "xy").start()
        self.hop(w, k, "cy").start()

    def third(self, i):
        w, k = self.stages[i]
        self.arrived(w, k, "yx")
        self.arrived(w, k, "xy")
        self.hop(w, k, "cd").start()

    def require(self, w, k):
        for kind in ("c", "cx", "cy", "cd"):
            self.arrived(w, k, kind)

    def finish(self):
        me = self.me
        for w, k in self.stages:
            for kind in KINDS:
                self.hop(w, k, kind).wait_send()
        for w in range(len(self.shards)):
            self.own_copy(w, me.inner, me.m, 0).wait_send()

            @pl.when(me.m == 1)
            def _(w=w):
                self.own_copy(w, me.outer, 0, 1).wait_send()
                for k in range(3):
                    self.forward(w, k).wait_send()


class Route:
    def __init__(self, me):
        z, c = me.z, me.c
        odd = lax.rem(z, 2)
        self.stays = z // 2 == c
        self.order = (odd, 1 - odd)
        self.to = ({"z": 2 * c + odd, "core": z // 2}, {"z": 2 * c + 1 - odd, "core": z // 2})

    def start(self, copies):
        first_local, first, second = copies

        @pl.when(self.stays)
        def _():
            first_local.start()

        @pl.when(jnp.logical_not(self.stays))
        def _():
            first.start()

        second.start()

    def out(self, held, there, sems):
        a, b = self.order
        return (
            pltpu.make_async_copy(held.at[a], there.at[0], sems.at[0]),
            remote(held.at[a], there.at[0], sems.at[1], sems.at[2], self.to[0]),
            remote(held.at[b], there.at[1], sems.at[3], sems.at[4], self.to[1]),
        )

    def back(self, held, there, sems):
        odd = self.order[0]
        return (
            pltpu.make_async_copy(held.at[0], there.at[odd], sems.at[0]),
            remote(held.at[0], there.at[odd], sems.at[1], sems.at[2], self.to[0]),
            remote(held.at[1], there.at[odd], sems.at[3], sems.at[4], self.to[1]),
        )

    def wait(self, copies):
        first_local, first, second = copies

        @pl.when(self.stays)
        def _():
            first_local.wait()

        @pl.when(jnp.logical_not(self.stays))
        def _():
            first.wait()

        second.wait()


def turn(v):
    return pltpu.roll(v, HD // 2, 1)


def stacked(two_heads):
    return jnp.concatenate([two_heads[:, :HD], two_heads[:, HD:]], axis=0)


def pick(which, values):
    out = values[0]
    for i in range(1, len(values)):
        out = jnp.where(which == i, values[i], out)
    return out


def row_loop(rows, step, body):
    def run(i, carry):
        body(pl.ds(pl.multiple_of(i * step, step), step))
        return carry

    lax.fori_loop(0, rows // step, run, 0)


PER_HEAD = 4 * HD
HALF_HEADS = KV_HEADS // 2
BLOCKS = 4
COUNT = 4


def forward_kernel(scalars, gains, head_gains, cosines, sines, tokens, cotangent, *refs):
    shards = refs[:COUNT]
    (
        block_out,
        gains_all,
        source,
        grad,
        h1_out,
        raw_out,
        tok_out,
        probs_out,
        attended_out,
        middle_out,
        h2_out,
        gate_up_out,
    ) = refs[COUNT : COUNT + 12]
    fulls = refs[COUNT + 12 : 2 * COUNT + 12]
    (
        acc,
        acc_small,
        wide,
        narrow,
        x,
        h1,
        h2,
        tok,
        outgoing,
        raw,
        p0,
        p1,
        p2,
        p3,
        ordered,
        mixed,
        mixed_out,
        attended,
        middle,
        hidden,
        gate_up,
        low_out,
        z_send,
        z_recv,
        f_send,
        xy_send,
        xy_recv,
        load_sem,
        keep_sem,
        gain_sem,
        token_sem,
        cot_sem,
        swap_sem,
        save_sem,
        prob_sem,
        gate_sem,
    ) = refs[2 * COUNT + 12 :]
    prob_slots = (p0, p1, p2, p3)
    low, f32 = jnp.bfloat16, jnp.float32
    me = Place()
    z, c = me.z, me.c
    rows, width = x.shape
    block = rows // 2
    comm = Gather(me, shards, fulls, (z_send, z_recv, f_send, xy_send, xy_recv))
    route = Route(me)
    me.greet()
    gain_copies = []
    for j in range(1, NZ):
        there = {"z": lax.rem(z + j, NZ)}
        gain_copies.append(remote(gains, gains_all.at[z], gain_sem.at[0, j], gain_sem.at[1, j], there))
    for copy in gain_copies:
        copy.start()
    gains_all[pl.ds(z, 1)] = gains[...][None]
    token_copies = route.out(tokens, source, token_sem)
    cot_copies = route.out(cotangent, grad, cot_sem)

    def at_slot(slot):
        for name, index in FORWARD_PLAN.get(slot, ()):
            if name == "tok":
                route.start(token_copies)
            elif name == "cot":
                route.start(cot_copies)
            else:
                getattr(comm, name)(index)

    def buffer(w, kk):
        if w in (0, 2):
            return wide.at[kk % 2, :, :, pl.ds(0, shards[w].shape[2])]
        return narrow.at[kk % 2, :, pl.ds(0, shards[w].shape[1]), :]

    def load(w, kk):
        src = shards[w] if kk == 0 else fulls[w].at[comm.shard_z(kk - 1)]
        return pltpu.make_async_copy(src, buffer(w, kk), load_sem.at[w, kk])

    def keep(w):
        return pltpu.make_async_copy(buffer(w, 0), fulls[w].at[z], keep_sem.at[w])

    def fetch(w, kk):
        if kk > 0:
            comm.require(w, kk - 1)
        if kk == 2:
            keep(w).wait()
        load(w, kk).start()

    def chunk(w, kk, lhs, out, tile):
        depth = 8 * shards[w].shape[1]
        columns = shards[w].shape[2]
        own_z = z if kk == 0 else comm.shard_z(kk - 1)
        load(w, kk).wait()
        if kk == 0:
            keep(w).start()
        left = lhs[:, pl.ds(pl.multiple_of(own_z * depth, depth), depth)]
        weight = buffer(w, kk)

        def body(i, carry):
            at = pl.ds(pl.multiple_of(i * tile, tile), tile)
            right = weight[:, :, at].reshape(depth, tile)
            part = jnp.dot(left, right, preferred_element_type=f32)
            if kk == 0:
                out[:, at] = part
            else:
                out[:, at] += part
            return carry

        lax.fori_loop(0, columns // tile, body, 0)

    def save(i, src, dst):
        return pltpu.make_async_copy(src, dst, save_sem.at[i])

    fetch(0, 0)
    fetch(1, 0)
    at_slot("start")
    fetch(0, 1)
    for j in range(1, NZ):
        gain_copies[j - 1].wait_send()
        there = gains_all.at[lax.rem(z + NZ - j, NZ)]
        remote(gains, there, gain_sem.at[0, j], gain_sem.at[1, j], me.partner).wait_recv()
    route.wait(token_copies)
    for part in range(2):
        pltpu.make_async_copy(source.at[part], x.at[pl.ds(part * block, block)], token_sem.at[5 + part]).start()
    for part in range(2):
        pltpu.make_async_copy(source.at[part], x.at[pl.ds(part * block, block)], token_sem.at[5 + part]).wait()

    def normed_times(v, index):
        v = v * lax.rsqrt(jnp.mean(v * v, axis=-1, keepdims=True) + EPSILON)
        gain = jnp.concatenate([gains_all[s, index : index + 1, :] for s in range(NZ)], axis=1)
        return (v * gain).astype(low)

    def first_norm(at):
        h1[at, :] = normed_times(x[at, :].astype(f32), 0)

    row_loop(rows, 64, first_norm)
    save(0, h1, h1_out).start()
    at_slot("tw")
    chunk(0, 0, h1, acc, 512)
    at_slot("q0")
    fetch(0, 2)
    chunk(0, 1, h1, acc, 512)
    at_slot("q1")
    fetch(0, 3)
    chunk(0, 2, h1, acc, 512)
    fetch(2, 0)
    at_slot("q2")
    chunk(0, 3, h1, acc, 512)
    at_slot("q3")

    def head(h, target, column):
        parts = []
        for start, size in ((h * 2 * HD, 2 * HD), ((HEADS + h) * HD, HD), ((HEADS + KV_HEADS + h) * HD, HD)):
            parts.append(acc[:, pl.ds(pl.multiple_of(start, HD), size)])
        half, at = h // HALF_HEADS, pl.multiple_of(lax.rem(h, HALF_HEADS) * PER_HEAD, PER_HEAD)
        for i, (v, gain_row) in enumerate(((parts[0][:, :HD], 0), (parts[0][:, HD:], 0), (parts[1], 1))):
            raw[half, :, pl.ds(pl.multiple_of(at + i * HD, HD), HD)] = v.astype(low)
            v = v * lax.rsqrt(jnp.mean(v * v, axis=-1, keepdims=True) + EPSILON)
            v = v * head_gains[gain_row : gain_row + 1, :]
            v = (v * cosines[...] + turn(v) * sines[...]).astype(low)
            for j in range(2):
                target[j, :, pl.ds(pl.multiple_of(column + i * HD, HD), HD)] = v[j * block : (j + 1) * block]
        v = parts[2].astype(low)
        for j in range(2):
            target[j, :, pl.ds(pl.multiple_of(column + 3 * HD, HD), HD)] = v[j * block : (j + 1) * block]

    def other_head(i, carry):
        head(i + HALF_HEADS * (1 - c), outgoing, i * PER_HEAD)
        return carry

    def own_head(i, carry):
        head(i + HALF_HEADS * c, tok, i * PER_HEAD)
        return carry

    lax.fori_loop(0, HALF_HEADS, other_head, 0)
    swap_out = remote(outgoing, tok.at[pl.ds(2, 2)], swap_sem.at[0], swap_sem.at[1], me.partner)
    swap_out.start()
    at_slot("r0")
    lax.fori_loop(0, HALF_HEADS, own_head, 0)
    save(1, raw, raw_out).start()
    at_slot("r1")
    swap_out.wait()
    save(2, tok, tok_out).start()
    at_slot("sw")

    scale = 1.0 / math.sqrt(HD)
    above = lax.rem(lax.broadcasted_iota(jnp.int32, (2 * block, block), 0), block)
    above = above < lax.broadcasted_iota(jnp.int32, (2 * block, block), 1)

    def save_probs(h, i):
        n = (i + 1) * block
        column = i * (i + 1) // 2 * block
        return pltpu.make_async_copy(prob_slots[i], probs_out.at[h, :, pl.ds(column, n)], prob_sem.at[i])

    def attend(h, carry):
        at = pl.multiple_of(h * PER_HEAD, PER_HEAD)
        for i in range(BLOCKS):
            ordered[i * block : (i + 1) * block] = pick(
                scalars[i], [tok[j, :, pl.ds(at, PER_HEAD)] for j in range(BLOCKS)]
            )
        for i in range(BLOCKS):
            n = (i + 1) * block
            query = stacked(ordered[i * block : n, : 2 * HD])
            keys, values = ordered[:n, 2 * HD : 3 * HD], ordered[:n, 3 * HD :]
            scores = lax.dot_general(query, keys, (((1,), (1,)), ((), ())), preferred_element_type=f32)
            last = jnp.where(above, MASKED, scores[:, i * block :])
            scores = last if i == 0 else jnp.concatenate([scores[:, : i * block], last], axis=1)
            top = jnp.max(scores, axis=-1, keepdims=True)
            weights = jnp.exp((scores - top) * scale)
            weights = weights * (1.0 / jnp.sum(weights, axis=-1, keepdims=True))
            probs = weights.astype(low)

            @pl.when(h > 0)
            def _():
                save_probs(h - 1, i).wait()

            prob_slots[i][...] = probs
            save_probs(h, i).start()
            out = jnp.dot(probs, values, preferred_element_type=f32).astype(low)
            there = pl.multiple_of(h * 2 * HD, 2 * HD)
            mixed[i * block : (i + 1) * block, pl.ds(there, HD)] = out[:block]
            mixed[i * block : (i + 1) * block, pl.ds(pl.multiple_of(there + HD, HD), HD)] = out[block:]
            for now in range(HALF_HEADS):
                slot_name = f"t{now}{i}"
                if slot_name in FORWARD_PLAN:

                    @pl.when(h == now)
                    def _(slot_name=slot_name):
                        at_slot(slot_name)

        return carry

    lax.fori_loop(0, HALF_HEADS, attend, 0)
    fetch(1, 1)
    half = HEADS * HD // 2
    mine = pl.ds(pl.multiple_of(c * half, half), half)
    for j in range(2):
        blocks = [mixed[i * block : (i + 1) * block] for i in range(BLOCKS)]
        mixed_out[j * block : (j + 1) * block] = pick(scalars[BLOCKS + 2 + j], blocks)
    for j in range(2):
        blocks = [mixed[i * block : (i + 1) * block] for i in range(BLOCKS)]
        attended[j * block : (j + 1) * block, mine] = pick(scalars[BLOCKS + j], blocks)
    mixed_swap = remote(mixed_out, attended.at[:, mine], swap_sem.at[2], swap_sem.at[3], me.partner)
    mixed_swap.start()
    at_slot("m")
    for i in range(BLOCKS):
        save_probs(HALF_HEADS - 1, i).wait()
    mixed_swap.wait()
    save(3, attended, attended_out).start()
    for kk in range(4):
        chunk(1, kk, attended, acc_small, 512)
        at_slot(f"o{kk}")
        if kk < 2:
            fetch(1, kk + 2)
        elif kk == 2:
            fetch(3, 0)

    def second_norm(at):
        v = x[at, :].astype(f32) + acc_small[at, :]
        middle[at, :] = v
        h2[at, :] = normed_times(v, 1)

    row_loop(rows, 64, second_norm)
    save(4, middle, middle_out).start()
    save(5, h2, h2_out).start()
    at_slot("n2")
    fetch(2, 1)
    chunk(2, 0, h2, acc, 512)
    at_slot("g0")
    fetch(2, 2)
    chunk(2, 1, h2, acc, 512)
    at_slot("g1")
    chunk(2, 2, h2, acc, 512)
    at_slot("g2")
    fetch(2, 3)
    chunk(2, 3, h2, acc, 512)
    at_slot("g3")

    def save_gate_up(i, part, slot):
        at = pl.multiple_of(part * FF + i * 512, 512)
        return pltpu.make_async_copy(gate_up.at[slot, part], gate_up_out.at[:, pl.ds(at, 512)], gate_sem.at[slot, part])

    def activate(i, carry):
        slot = lax.rem(i, 2)
        at = pl.multiple_of(i * 512, 512)

        @pl.when(i >= 2)
        def _():
            for part in range(2):
                save_gate_up(i - 2, part, slot).wait()

        gate = acc[:, pl.ds(at, 512)]
        up = acc[:, pl.ds(pl.multiple_of(FF + at, 512), 512)]
        gate_up[slot, 0] = gate.astype(low)
        gate_up[slot, 1] = up.astype(low)
        hidden[:, pl.ds(at, 512)] = (gate * jax.nn.sigmoid(gate) * up).astype(low)
        for part in range(2):
            save_gate_up(i, part, slot).start()
        return carry

    tiles = FF // 512
    lax.fori_loop(0, tiles, activate, 0)
    at_slot("ac")
    fetch(3, 1)
    chunk(3, 0, hidden, acc_small, 512)
    at_slot("d0")
    chunk(3, 1, hidden, acc_small, 512)
    at_slot("d1")
    fetch(3, 2)
    chunk(3, 2, hidden, acc_small, 512)
    at_slot("d2")
    fetch(3, 3)
    chunk(3, 3, hidden, acc_small, 512)
    at_slot("d3")

    def final(at):
        low_out[at, :] = (middle[at, :] + acc_small[at, :]).astype(low)

    row_loop(rows, 64, final)
    save(6, low_out, block_out).start()
    at_slot("fin")
    comm.finish()
    for slot in range(2):
        for part in range(2):
            save_gate_up(tiles - 2 + slot, part, slot).wait()
    for i, (src, dst) in enumerate(
        (
            (h1, h1_out),
            (raw, raw_out),
            (tok, tok_out),
            (attended, attended_out),
            (middle, middle_out),
            (h2, h2_out),
            (low_out, block_out),
        )
    ):
        save(i, src, dst).wait()
    route.wait(cot_copies)


FORWARD_PLAN = {
    "start": (("own", 0), ("own", 1), ("relay", 0), ("launch", 0), ("own", 2), ("relay", 2), ("launch", 2), ("relay", 1), ("sx", 2), ("tok", 0), ("sy", 0), ("relay", 3), ("relay", 6), ("launch", 1), ("launch", 3), ("sx", 0), ("sy", 1), ("sx", 1), ("third", 0), ("sy", 2), ("sy", 3), ("launch", 6), ("relay", 7), ("third", 2), ("own", 3), ("launch", 7), ("third", 1), ("sx", 3),),
    "q0": (("relay", 4),),
    "q1": (("launch", 4),),
    "q2": (("relay", 5), ("launch", 5),),
    "r0": (("relay", 10), ("relay", 9), ("sy", 6), ("sx", 6), ("sy", 4), ("third", 3), ("sy", 5),),
    "r1": (("launch", 9), ("sx", 4), ("sx", 5), ("launch", 10),),
    "t00": (("relay", 8),),
    "t01": (("launch", 8),),
    "m": (("third", 4), ("sy", 7), ("sx", 7), ("relay", 11), ("third", 6), ("sy", 10), ("third", 5), ("sy", 9), ("sy", 8), ("sx", 8), ("sx", 10), ("launch", 11), ("cot", 0), ("sx", 9),),
    "o3": (("third", 7),),
    "g0": (("third", 8),),
    "g1": (("sy", 11), ("sx", 11), ("third", 9),),
    "g2": (("third", 10),),
    "ac": (("third", 11),),
}


def run_forward(scalars, gains, head_gains, cosines, sines, tokens, cotangent, shards):
    low, f32 = jnp.bfloat16, jnp.float32
    _, slot_len, width = tokens.shape
    rows = 2 * slot_len
    cut = [s.reshape(8, s.shape[0] // 8, s.shape[1]) for s in shards]
    area = slot_len * BLOCKS * (BLOCKS + 1) // 2
    shape = jax.ShapeDtypeStruct
    outs = [
        shape((rows, width), low),
        shape((NZ, *gains.shape), f32),
        shape((2, slot_len, width), low),
        shape((2, slot_len, width), low),
        shape((rows, width), low),
        shape((2, rows, HALF_HEADS * PER_HEAD), low),
        shape((4, slot_len, HALF_HEADS * PER_HEAD), low),
        shape((HALF_HEADS, 2 * slot_len, area), low),
        shape((rows, HEADS * HD), low),
        shape((rows, width), f32),
        shape((rows, width), low),
        shape((rows, 2 * FF), low),
    ] + [shape((NZ, *s.shape), low) for s in cut]
    hbm = pl.BlockSpec(memory_space=HBM)
    vmem = pl.BlockSpec(memory_space=pltpu.VMEM)
    dma = pltpu.SemaphoreType.DMA
    out = pl.pallas_call(
        forward_kernel,
        out_shape=outs,
        in_specs=[pl.BlockSpec(memory_space=pltpu.SMEM)] + [vmem] * 4 + [hbm] * (2 + COUNT),
        out_specs=[hbm, vmem] + [hbm] * (10 + COUNT),
        scratch_shapes=[
            pltpu.VMEM((rows, 2 * FF), f32),
            pltpu.VMEM((rows, width), f32),
            pltpu.VMEM((2, 8, cut[2].shape[1], 2 * FF), low),
            pltpu.VMEM((2, 8, cut[3].shape[1], width), low),
            pltpu.VMEM((rows, width), low),
            pltpu.VMEM((rows, width), low),
            pltpu.VMEM((rows, width), low),
            pltpu.VMEM((4, slot_len, HALF_HEADS * PER_HEAD), low),
            pltpu.VMEM((2, slot_len, HALF_HEADS * PER_HEAD), low),
            pltpu.VMEM((2, rows, HALF_HEADS * PER_HEAD), low),
        ]
        + [pltpu.VMEM((2 * slot_len, (i + 1) * slot_len), low) for i in range(BLOCKS)]
        + [
            pltpu.VMEM((4 * slot_len, PER_HEAD), low),
            pltpu.VMEM((4 * slot_len, HEADS * HD // 2), low),
            pltpu.VMEM((rows, HEADS * HD // 2), low),
            pltpu.VMEM((rows, HEADS * HD), low),
            pltpu.VMEM((rows, width), f32),
            pltpu.VMEM((rows, FF), low),
            pltpu.VMEM((2, 2, rows, 512), low),
            pltpu.VMEM((rows, width), low),
            dma((COUNT, 2)),
            dma((COUNT, 3)),
            dma((COUNT, 3)),
            dma((COUNT, 3, len(KINDS))),
            dma((COUNT, 3, len(KINDS))),
            dma((COUNT, 4)),
            dma((COUNT,)),
            dma((2, NZ)),
            dma((7,)),
            dma((5,)),
            dma((4,)),
            dma((7,)),
            dma((BLOCKS,)),
            dma((2, 2)),
        ],
        compiler_params=pltpu.CompilerParams(collective_id=0, has_side_effects=True, vmem_limit_bytes=VMEM_LIMIT),
        name="forward",
    )(scalars, gains, head_gains, cosines, sines, tokens, cotangent, *cut)
    return out[:12], out[12:]


def add_rows(dst, src, rows):
    def body(i, carry):
        at = pl.ds(pl.multiple_of(i * 16, 16), 16)
        total = dst[at, :].astype(jnp.float32) + src[at, :].astype(jnp.float32)
        dst[at, :] = total.astype(dst.dtype)
        return carry

    lax.fori_loop(0, rows // 16, body, 0)


SPREAD = ("x", "y", "yx", "xy", "c", "cx", "cy", "cd")
ROUNDS = ("x1", "y1", "y2", "x2")


class Reduce:
    def __init__(self, me, shapes, refs, turned, sems):
        self.me, self.shapes, self.turned = me, shapes, turned
        self.stage, self.acc, self.rx1, self.ry1, self.rx2, self.ry2, self.rz, self.outs = refs
        (
            self.keep_sem,
            self.c_send,
            self.c_recv,
            self.r_send,
            self.r_recv,
            self.z_send,
            self.z_recv,
            self.o_send,
            self.o_recv,
        ) = sems
        self.stage_t = (3, 2, 1 - me.m, me.m)
        self.chunks = [(w, k) for w in range(len(shapes)) for k in range(4)]

    def zk(self, k):
        return self.me.at(self.stage_t[k])

    def product(self, n, rhs, columns, store):
        w, k = self.chunks[n]
        rows = self.shapes[w][0]
        half = self.shapes[w][1] // 2
        tile = min(half, 512)

        def body(i, carry):
            at = pl.multiple_of(i * tile, tile)
            part = jnp.dot(
                self.turned[n % 2, :rows],
                rhs[:, pl.ds(pl.multiple_of(columns * half + at, tile), tile)],
                preferred_element_type=jnp.float32,
            )
            store(part, pl.ds(at, tile))
            return carry

        lax.fori_loop(0, half // tile, body, 0)

    def to_partner(self, n):
        w, k = self.chunks[n]
        return remote(
            self.stage[w], self.acc[w].at[self.zk(k)], self.c_send.at[w, k], self.c_recv.at[w, k], self.me.partner
        )

    def turn_rows(self, n, lhs):
        w, k = self.chunks[n]
        rows = self.shapes[w][0]
        at = pl.multiple_of(self.zk(k) * rows, rows)
        self.turned[n % 2, :rows] = jnp.transpose(lhs[:, pl.ds(at, rows)])

    def theirs(self, n, rhs):
        w, k = self.chunks[n]
        rows = self.shapes[w][0]
        if k > 0:
            self.to_partner(n - 1).wait_send()

        def store(part, at):
            self.stage[w][:, :, :, at] = part.astype(jnp.bfloat16).reshape(2, 2, rows // 4, part.shape[1])

        self.product(n, rhs, 1 - self.me.c, store)

    def ours(self, n, rhs):
        w, k = self.chunks[n]
        a = self.acc[w].at[self.zk(k)]
        self.to_partner(n).wait_recv()

        def store(part, at):
            got = a[:, :, :, at].astype(jnp.float32)
            a[:, :, :, at] = (part.reshape(got.shape) + got).astype(jnp.bfloat16)

        self.product(n, rhs, self.me.c, store)

    def launch(self, n):
        w, k = self.chunks[n]
        self.exchange(w, k, "x1").start()
        self.exchange(w, k, "y1").start()

    def exchange(self, w, k, kind):
        me = self.me
        x, y = me.x, me.y
        a = self.acc[w].at[self.zk(k)]
        half = a.shape[-1] // 2
        lo, hi = pl.ds(0, half), pl.ds(half, half)
        src, dst, peer = {
            "x1": lambda: (a.at[1 - x, :, :, lo], self.rx1[w].at[k], me.across_x),
            "y1": lambda: (a.at[:, 1 - y, :, hi], self.ry1[w].at[k], me.across_y),
            "y2": lambda: (a.at[x, 1 - y, :, lo], self.ry2[w].at[k], me.across_y),
            "x2": lambda: (a.at[1 - x, y, :, hi], self.rx2[w].at[k], me.across_x),
        }[kind]()
        index = ROUNDS.index(kind)
        return remote(src, dst, self.r_send.at[w, k, index], self.r_recv.at[w, k, index], peer)

    def along(self, w, k, slot, peer):
        me = self.me
        return remote(
            self.acc[w].at[self.zk(k), me.x, me.y], self.rz[w].at[slot], self.z_send.at[w, k], self.z_recv.at[w, slot], peer
        )

    def s1(self, n):
        w, k = self.chunks[n]
        me = self.me
        a = self.acc[w].at[self.zk(k)]
        rows, half = a.shape[2], a.shape[3] // 2
        self.exchange(w, k, "x1").wait_recv()
        for j in range(2):
            add_rows(a.at[me.x, j, :, pl.ds(0, half)], self.rx1[w].at[k, j], rows)
        self.exchange(w, k, "y1").wait_recv()
        for i in range(2):
            add_rows(a.at[i, me.y, :, pl.ds(half, half)], self.ry1[w].at[k, i], rows)
        self.exchange(w, k, "y2").start()
        self.exchange(w, k, "x2").start()

    def s2(self, n):
        w, k = self.chunks[n]
        a = self.acc[w].at[self.zk(k), self.me.x, self.me.y]
        rows, half = a.shape[0], a.shape[1] // 2
        self.exchange(w, k, "y2").wait_recv()
        add_rows(a.at[:, pl.ds(0, half)], self.ry2[w].at[k], rows)
        self.exchange(w, k, "x2").wait_recv()
        add_rows(a.at[:, pl.ds(half, half)], self.rx2[w].at[k], rows)

    def s3(self, n):
        w, k = self.chunks[n]
        me = self.me
        a = self.acc[w].at[self.zk(k), me.x, me.y]
        rows = a.shape[0]

        def take(slot):
            there = self.rz[w].at[slot]
            remote(there, there, self.z_send.at[w, 0], self.z_recv.at[w, slot], me.partner).wait_recv()
            add_rows(a, there, rows)

        @pl.when(me.m == 0)
        def _():
            if k < 3:
                self.along(w, k, k, me.inner).start()
            else:
                take(0)

        @pl.when(me.m == 1)
        def _():
            if k == 0:
                take(0)
                self.along(w, k, 3, me.inner).start()
            elif k == 1:
                take(1)
                self.along(w, k, 4, me.inner).start()
            elif k == 2:
                take(3)
                self.along(w, k, 0, me.outer).start()
            else:
                take(2)
                take(4)

    def out_at(self, w, cc, xx, yy):
        half = self.shapes[w][1] // 2
        return self.outs[w].at[xx, yy, :, pl.ds(pl.multiple_of(cc * half, half), half)]

    def keep(self, w):
        me = self.me
        return pltpu.make_async_copy(
            self.acc[w].at[me.z, me.x, me.y], self.out_at(w, me.c, me.x, me.y), self.keep_sem.at[w]
        )

    def spread(self, w, kind):
        me = self.me
        c, x, y = me.c, me.x, me.y
        final, mine = self.acc[w].at[me.z, x, y], self.out_at(w, c, x, y)
        px, py = self.out_at(w, c, 1 - x, y), self.out_at(w, c, x, 1 - y)
        pd = self.out_at(w, c, 1 - x, 1 - y)
        src, dst, peer = {
            "x": (final, mine, me.across_x),
            "y": (final, mine, me.across_y),
            "c": (final, mine, me.partner),
            "yx": (half_rows(px, 0), half_rows(px, 0), me.across_y),
            "xy": (half_rows(py, 1), half_rows(py, 1), me.across_x),
            "cx": (px, px, me.partner),
            "cy": (py, py, me.partner),
            "cd": (pd, pd, me.partner),
        }[kind]
        index = SPREAD.index(kind)
        return remote(src, dst, self.o_send.at[w, index], self.o_recv.at[w, index], peer)

    def spread_arrived(self, w, kind):
        me = self.me
        c, x, y = me.c, me.x, me.y
        dst = {
            "x": lambda: self.out_at(w, c, 1 - x, y),
            "y": lambda: self.out_at(w, c, x, 1 - y),
            "yx": lambda: half_rows(self.out_at(w, c, 1 - x, 1 - y), 0),
            "xy": lambda: half_rows(self.out_at(w, c, 1 - x, 1 - y), 1),
            "c": lambda: self.out_at(w, 1 - c, x, y),
            "cx": lambda: self.out_at(w, 1 - c, 1 - x, y),
            "cy": lambda: self.out_at(w, 1 - c, x, 1 - y),
            "cd": lambda: self.out_at(w, 1 - c, 1 - x, 1 - y),
        }[kind]()
        index = SPREAD.index(kind)
        remote(dst, dst, self.o_send.at[w, index], self.o_recv.at[w, index], me.partner).wait_recv()

    def s4(self, w):
        self.keep(w).start()
        for kind in ("x", "y", "c"):
            self.spread(w, kind).start()

    def s5(self, w):
        self.spread_arrived(w, "x")
        self.spread(w, "yx").start()
        self.spread(w, "cx").start()
        self.spread_arrived(w, "y")
        self.spread(w, "xy").start()
        self.spread(w, "cy").start()

    def s6(self, w):
        self.spread_arrived(w, "yx")
        self.spread_arrived(w, "xy")
        self.spread(w, "cd").start()

    def finish(self):
        for n, (w, k) in enumerate(self.chunks):
            if k == 3:
                self.to_partner(n).wait_send()
            for kind in ROUNDS:
                self.exchange(w, k, kind).wait_send()
            if k < 3:
                self.along(w, k, k, self.me.inner).wait_send()
        for w in range(len(self.shapes)):
            self.keep(w).wait()
            for kind in SPREAD:
                self.spread(w, kind).wait_send()
            for kind in ("c", "cx", "cy", "cd"):
                self.spread_arrived(w, kind)


class Small:
    def __init__(self, me, mid, got, along, send, recv):
        self.me, self.mid, self.got, self.along_z, self.send, self.recv = me, mid, got, along, send, recv
        self.peers = (me.partner, me.across_x, me.across_y)

    def copy(self, step):
        return remote(self.mid.at[step], self.got.at[step], self.send.at[step], self.recv.at[step], self.peers[step])

    def along(self, j):
        there = {"z": lax.rem(self.me.z + 1 + j, NZ)}
        return remote(self.mid.at[3], self.along_z.at[self.me.z], self.send.at[3 + j], self.recv.at[3 + j], there)

    def step(self, n):
        if n < 6:
            step = n // 2
            if n % 2 == 0:
                self.copy(step).start()
            else:
                self.copy(step).wait()
                self.mid[step + 1] = self.mid[step] + self.got[step]
        elif n == 6:
            for j in range(3):
                self.along(j).start()
        else:
            for j in range(3):
                self.along(j).wait_send()
                there = self.along_z.at[lax.rem(self.me.z + 3 - j, NZ)]
                remote(there, there, self.send.at[3 + j], self.recv.at[3 + j], self.me.partner).wait_recv()
            self.along_z[pl.ds(self.me.z, 1)] = self.mid[pl.ds(3, 1)]

    def total(self):
        return (self.along_z[0] + self.along_z[1]) + (self.along_z[2] + self.along_z[3])


def backward_kernel(shapes, scalars, gains, head_gains, cosines, sines, *refs):
    (
        source,
        grad,
        h1_in,
        raw_in,
        tok_in,
        probs_in,
        attended_in,
        middle_in,
        h2_in,
        gate_up_in,
        block_rows_in,
        full_qkv,
        full_out,
        full_gate_up,
        full_down,
    ) = refs[:15]
    small_out, input_out, block_out = refs[15:18]
    outs = refs[18:22]
    rest = refs[22:]
    stage, acc, rz = rest[:4], rest[4:8], rest[8:12]
    rx1, ry1, rx2, ry2 = rest[12:14], rest[14:16], rest[16:18], rest[18:20]
    turned, wide, grad_mid, grads, outgoing, returned, small_mid, small_got, small_z, gain_sums, sums, input_low = rest[20:32]
    comm_sems = rest[32:41]
    (
        s_send,
        s_recv,
        load_sem,
        wide_sem,
        narrow_sem,
        gate_sem,
        prob_sem,
        tok_sem,
        raw_sem,
        swap_sem,
        out_sem,
        in_sem,
    ) = rest[41:]

    def like(refs, w):
        r, n = shapes[w]
        ref = refs[w % 2]
        if w < 2:
            return ref
        lead = (slice(None),) * (len(ref.shape) - 2)
        return ref.at[(*lead, pl.ds(0, r // 4), pl.ds(0, n // 4))]

    landing = [[like(group, w) for w in range(4)] for group in (rx1, ry1, rx2, ry2)]
    low, f32 = jnp.bfloat16, jnp.float32
    me = Place()
    z, c = me.z, me.c
    rows, width = grad_mid.shape
    block = rows // 2
    share = width // NZ
    comm = Reduce(me, shapes, (stage, acc, *landing, rz, outs), turned, comm_sems)
    small = Small(me, small_mid, small_got, small_z, s_send, s_recv)

    def at_slot(slot):
        for name, index in BACK_PLAN.get(slot, ()):
            if name == "small":
                small.step(index)
            elif name == "inback":
                route.start(input_back)
            else:
                getattr(comm, name)(index)

    route = Route(me)
    me.greet()
    block_back = route.back(block_rows_in, block_out, out_sem)
    input_back = route.back(input_low, input_out, in_sem)
    route.start(block_back)
    sums[...] = jnp.zeros_like(sums)
    gain_sums[...] = jnp.zeros_like(gain_sums)
    contract = (((1,), (1,)), ((), ()))
    depth = FF // NZ

    wide_loads = [(full_gate_up, k, t) for k in range(4) for t in range(3)]
    wide_loads += [(full_qkv, k, t) for k in range(4) for t in range(2)]
    wide_tile = wide.shape[3]

    def wide_load(j):
        full, k, t = wide_loads[j]
        src = full.at[comm.zk(k), :, :, pl.ds(t * wide_tile, wide_tile)]
        return pltpu.make_async_copy(src, wide.at[j % 2], wide_sem.at[j % 2])

    def against(j, count, left, target):
        k = wide_loads[j][1]
        total = None
        for t in range(count):
            wide_load(j + t).wait()
            if j + t + 1 < len(wide_loads):
                wide_load(j + t + 1).start()
            right = wide[(j + t) % 2].reshape(share, wide_tile)
            lhs = left[:, t * wide_tile : (t + 1) * wide_tile]
            part = lax.dot_general(lhs, right, contract, preferred_element_type=f32)
            total = part if t == 0 else total + part
        target[:, pl.ds(pl.multiple_of(comm.zk(k) * share, share), share)] = total

    def gain_row(index):
        return jnp.concatenate([gains[s, index : index + 1, :] for s in range(NZ)], axis=1)

    def norm_parts(v):
        inverse = lax.rsqrt(jnp.mean(v * v, axis=-1, keepdims=True) + EPSILON)
        return v * inverse, inverse

    def norm_grad(normed, inverse, g):
        return inverse * (g - normed * jnp.mean(g * normed, axis=-1, keepdims=True))

    def load(i, src, dst):
        return pltpu.make_async_copy(src, dst, load_sem.at[i])

    def feed_forward(g, h2, grad_gate_up, narrow, gate_up, middle):
        g_loads = [load(i, grad.at[i], g.at[pl.ds(i * block, block)]) for i in range(2)]

        def narrow_load(k):
            return pltpu.make_async_copy(full_down.at[comm.zk(k)], narrow.at[k % 2], narrow_sem.at[k % 2])

        def gate_load(k, part):
            at = pl.multiple_of(part * FF + comm.zk(k) * depth, depth)
            src = gate_up_in.at[:, pl.ds(at, depth)]
            return pltpu.make_async_copy(src, gate_up.at[k % 2, part], gate_sem.at[k % 2, part])

        def fetch(k):
            narrow_load(k).start()
            for part in range(2):
                gate_load(k, part).start()

        for copy in g_loads:
            copy.start()
        fetch(0)
        fetch(1)
        load(2, h2_in, h2).start()
        load(3, middle_in, middle).start()
        wide_load(0).start()
        for copy in g_loads:
            copy.wait()
        tile = depth // 2

        def hidden_part(k):
            narrow_load(k).wait()
            for part in range(2):
                gate_load(k, part).wait()

            def body(i, carry):
                at = pl.multiple_of(i * tile, tile)
                right = narrow[k % 2, pl.ds(i * 4, 4)].reshape(tile, width)
                grad_hidden = lax.dot_general(g[...], right, contract, preferred_element_type=f32)
                gate = gate_up[k % 2, 0, :, pl.ds(at, tile)].astype(f32)
                up = gate_up[k % 2, 1, :, pl.ds(at, tile)].astype(f32)
                sigmoid = jax.nn.sigmoid(gate)
                silu = gate * sigmoid
                turned[k % 2, pl.ds(at, tile), :] = jnp.transpose((silu * up).astype(low))
                there = pl.multiple_of(comm.zk(k) * depth + at, 128)
                grad_gate = grad_hidden * up * (sigmoid * (1.0 + gate * (1.0 - sigmoid)))
                grad_gate_up[:, pl.ds(there, tile)] = grad_gate.astype(low)
                grad_gate_up[:, pl.ds(pl.multiple_of(FF + there, 128), tile)] = (grad_hidden * silu).astype(low)
                return carry

            lax.fori_loop(0, 2, body, 0)
            if k + 2 < 4:
                fetch(k + 2)

        for n in range(4):
            hidden_part(n)
            comm.theirs(n, g)
            if n > 0:
                comm.ours(n - 1, g)
            comm.to_partner(n).start()
            at_slot(f"h{n}")
        load(2, h2_in, h2).wait()
        for n in range(4, 8):
            comm.turn_rows(n, h2)
            comm.theirs(n, grad_gate_up)
            comm.ours(n - 1, g if n == 4 else grad_gate_up)
            comm.to_partner(n).start()
            at_slot(f"g{n}")
            against((n - 4) * 3, 3, grad_gate_up, grad_mid)
            at_slot(f"a{n}")
        comm.ours(7, grad_gate_up)
        at_slot("g8")
        load(3, middle_in, middle).wait()

        def second_norm(at):
            normed, inverse = norm_parts(middle[at, :])
            grad_h2 = grad_mid[at, :]
            gain_sums[1:2, :] += jnp.sum(normed * grad_h2, axis=0, keepdims=True)
            grad_mid[at, :] = g[at, :].astype(f32) + norm_grad(normed, inverse, grad_h2 * gain_row(1))

        row_loop(rows, 64, second_norm)
        at_slot("n2")

    pl.run_scoped(
        feed_forward,
        pltpu.VMEM((rows, width), low),
        pltpu.VMEM((rows, width), low),
        pltpu.VMEM((rows, 2 * FF), low),
        pltpu.VMEM((2, *full_down.shape[1:]), low),
        pltpu.VMEM((2, 2, rows, depth), low),
        pltpu.VMEM((rows, width), f32),
    )

    half = HEADS * HD // 2

    def out_projection(attended, narrow, grad_low):
        def narrow_load(j):
            where = 2 * (1 - c) + j if j < 2 else 2 * c + j - 2
            return pltpu.make_async_copy(full_out.at[where], narrow.at[j % 2], narrow_sem.at[j % 2])

        narrow_load(0).start()
        narrow_load(1).start()
        load(0, attended_in, attended).start()

        def lower(at):
            grad_low[at, :] = grad_mid[at, :].astype(low)

        row_loop(rows, 64, lower)
        columns = half // 2
        swap = remote(outgoing, grads.at[pl.ds(2, 2)], swap_sem.at[0], swap_sem.at[1], me.partner)
        for j in range(4):
            narrow_load(j).wait()
            right = narrow[j % 2].reshape(columns, width)
            part = lax.dot_general(grad_low[...], right, contract, preferred_element_type=f32).astype(low)
            target = outgoing if j < 2 else grads
            for i in range(2):
                target[i, :, j % 2 * columns : (j % 2 + 1) * columns] = part[i * block : (i + 1) * block]
            if j + 2 < 4:
                narrow_load(j + 2).start()
            if j == 2:
                swap.start()
        load(0, attended_in, attended).wait()
        at_slot("op")
        for n in range(8, 12):
            comm.turn_rows(n, attended)
            comm.theirs(n, grad_low)
            if n > 8:
                comm.ours(n - 1, grad_low)
            comm.to_partner(n).start()
            at_slot(f"o{n}")
        comm.ours(11, grad_low)
        swap.wait()
        at_slot("o12")

    pl.run_scoped(
        out_projection,
        pltpu.VMEM((rows, HEADS * HD), low),
        pltpu.VMEM((2, *full_out.shape[1:]), low),
        pltpu.VMEM((rows, width), low),
    )

    def sequence_part(own, leaving):
        swap = remote(leaving, returned, swap_sem.at[2], swap_sem.at[3], me.partner)

        def attention(tok, ordered, grad_ordered, p0, p1, p2, p3, grad_k, grad_v, placed):
            slots = (p0, p1, p2, p3)
            scale = 1.0 / math.sqrt(HD)

            def prob_load(h, i):
                n = (i + 1) * block
                src = probs_in.at[h, :, pl.ds(i * (i + 1) // 2 * block, n)]
                return pltpu.make_async_copy(src, slots[i], prob_sem.at[i])

            def tok_load(h, slot):
                at = pl.multiple_of(h * PER_HEAD, PER_HEAD)
                return pltpu.make_async_copy(tok_in.at[:, :, pl.ds(at, PER_HEAD)], tok.at[slot], tok_sem.at[slot])

            tok_load(0, 0).start()
            for i in reversed(range(BLOCKS)):
                prob_load(0, i).start()

            def one_head(h, carry):
                slot = lax.rem(h, 2)
                tok_load(h, slot).wait()

                @pl.when(h + 1 < HALF_HEADS)
                def _():
                    tok_load(h + 1, 1 - slot).start()

                at = pl.multiple_of(h * 2 * HD, 2 * HD)
                for i in range(BLOCKS):
                    here = slice(i * block, (i + 1) * block)
                    ordered[here] = pick(scalars[i], [tok[slot, j] for j in range(BLOCKS)])
                    grad_ordered[here] = pick(scalars[i], [grads[j, :, pl.ds(at, 2 * HD)] for j in range(BLOCKS)])
                for i in reversed(range(BLOCKS)):
                    n = (i + 1) * block
                    here = slice(i * block, n)
                    prob_load(h, i).wait()
                    query = stacked(ordered[here, : 2 * HD])
                    g = stacked(grad_ordered[here, :])
                    keys, values = ordered[:n, 2 * HD : 3 * HD], ordered[:n, 3 * HD :]
                    probs = slots[i][...]
                    weights = probs.astype(f32)
                    grad_probs = lax.dot_general(g, values, contract, preferred_element_type=f32)
                    delta = jnp.sum(weights * grad_probs, axis=-1, keepdims=True)
                    grad_scores = (weights * (grad_probs - delta)).astype(low)
                    grad_q = (jnp.dot(grad_scores, keys, preferred_element_type=f32) * scale).astype(low)
                    placed[here, :HD] = grad_q[:block]
                    placed[here, HD : 2 * HD] = grad_q[block:]
                    across = (((0,), (0,)), ((), ()))
                    part_k = lax.dot_general(query, grad_scores, across, preferred_element_type=f32)
                    part_v = lax.dot_general(g, probs, across, preferred_element_type=f32)
                    if i == BLOCKS - 1:
                        grad_k[...] = part_k
                        grad_v[...] = part_v
                    else:
                        grad_k[:, :n] += part_k
                        grad_v[:, :n] += part_v

                    @pl.when(h + 1 < HALF_HEADS)
                    def _():
                        prob_load(h + 1, i).start()

                    if i > 0:
                        for now in range(HALF_HEADS):
                            slot_name = f"t{now}{BLOCKS - 1 - i}"
                            if slot_name in BACK_PLAN:

                                @pl.when(h == now)
                                def _(slot_name=slot_name):
                                    at_slot(slot_name)

                for i in range(BLOCKS):
                    here = slice(i * block, (i + 1) * block)
                    placed[here, 2 * HD : 3 * HD] = jnp.transpose(grad_k[:, here] * scale).astype(low)
                    placed[here, 3 * HD :] = jnp.transpose(grad_v[:, here]).astype(low)
                columns = pl.ds(pl.multiple_of(h * PER_HEAD, PER_HEAD), PER_HEAD)
                for j in range(BLOCKS):
                    value = pick(scalars[BLOCKS + j], [placed[i * block : (i + 1) * block] for i in range(BLOCKS)])
                    target = own if j < 2 else leaving
                    target[j % 2 * block : (j % 2 + 1) * block, columns] = value
                for now in range(HALF_HEADS):
                    slot_name = f"t{now}{BLOCKS - 1}"
                    if slot_name in BACK_PLAN:

                        @pl.when(h == now)
                        def _(slot_name=slot_name):
                            at_slot(slot_name)

                return carry

            lax.fori_loop(0, HALF_HEADS, one_head, 0)
            swap.start()
            at_slot("sw")

        pl.run_scoped(
            attention,
            pltpu.VMEM((2, 4, block, PER_HEAD), low),
            pltpu.VMEM((4 * block, PER_HEAD), low),
            pltpu.VMEM((4 * block, 2 * HD), low),
            *[pltpu.VMEM((2 * block, (i + 1) * block), low) for i in range(BLOCKS)],
            pltpu.VMEM((HD, 4 * block), f32),
            pltpu.VMEM((HD, 4 * block), f32),
            pltpu.VMEM((4 * block, PER_HEAD), low),
        )

        def projection(grad_qkv, raw, h1, x, grad_first):
            load(0, h1_in, h1).start()
            for i in range(2):
                load(2 + i, source.at[i], x.at[pl.ds(i * block, block)]).start()

            def raw_load(j, slot):
                which = c + j // HALF_HEADS * (1 - 2 * c)
                at = pl.multiple_of(lax.rem(j, HALF_HEADS) * PER_HEAD, PER_HEAD)
                return pltpu.make_async_copy(raw_in.at[which, :, pl.ds(at, PER_HEAD)], raw.at[slot], raw_sem.at[slot])

            raw_load(0, 0).start()

            def one_head(j, came):
                slot = lax.rem(j, 2)
                raw_load(j, slot).wait()

                @pl.when(j + 1 < KV_HEADS)
                def _():
                    raw_load(j + 1, 1 - slot).start()

                at = pl.multiple_of(lax.rem(j, HALF_HEADS) * PER_HEAD, PER_HEAD)
                h = lax.rem(j, HALF_HEADS) + HALF_HEADS * (c + j // HALF_HEADS * (1 - 2 * c))
                places = (h * 2 * HD, (h * 2 + 1) * HD, (HEADS + h) * HD)
                for i, (row, place) in enumerate(zip((0, 0, 1), places)):
                    normed, inverse = norm_parts(raw[slot, :, i * HD : (i + 1) * HD].astype(f32))
                    g = came[:, pl.ds(pl.multiple_of(at + i * HD, HD), HD)].astype(f32)
                    g = g * cosines[...] - turn(g) * sines[...]
                    sums[row : row + 1, :] += jnp.sum(normed * g, axis=0, keepdims=True)
                    back = norm_grad(normed, inverse, g * head_gains[row : row + 1, :])
                    grad_qkv[:, pl.ds(pl.multiple_of(place, HD), HD)] = back.astype(low)
                there = pl.multiple_of((HEADS + KV_HEADS + h) * HD, HD)
                grad_qkv[:, pl.ds(there, HD)] = came[:, pl.ds(pl.multiple_of(at + 3 * HD, HD), HD)]

            def own_head(i, carry):
                one_head(i, own)
                return carry

            def other_head(i, carry):
                one_head(i + HALF_HEADS, returned)
                return carry

            lax.fori_loop(0, HALF_HEADS, own_head, 0)
            at_slot("b0")
            swap.wait()
            lax.fori_loop(0, HALF_HEADS, other_head, 0)
            load(0, h1_in, h1).wait()
            at_slot("b1")
            for n in range(12, 16):
                comm.turn_rows(n, h1)
                comm.theirs(n, grad_qkv)
                if n > 12:
                    comm.ours(n - 1, grad_qkv)
                comm.to_partner(n).start()
                at_slot(f"q{n}")
            comm.ours(15, grad_qkv)
            at_slot("q16")
            for k in range(4):
                against(12 + k * 2, 2, grad_qkv, grad_first)
                at_slot(f"f{k}")
            for i in range(2):
                load(2 + i, source.at[i], x.at[pl.ds(i * block, block)]).wait()
            for i in range(2):

                def first_norm(at, i=i):
                    here = pl.ds(pl.multiple_of(i * block + at.start, 64), 64)
                    normed, inverse = norm_parts(x[here, :].astype(f32))
                    g = grad_first[here, :]
                    gain_sums[0:1, :] += jnp.sum(normed * g, axis=0, keepdims=True)
                    total = grad_mid[here, :] + norm_grad(normed, inverse, g * gain_row(0))
                    input_low[i, at, :] = total.astype(low)

                row_loop(block, 64, first_norm)

        pl.run_scoped(
            projection,
            pltpu.VMEM((rows, (HEADS + 2 * KV_HEADS) * HD), low),
            pltpu.VMEM((2, rows, PER_HEAD), low),
            pltpu.VMEM((rows, width), low),
            pltpu.VMEM((rows, width), low),
            pltpu.VMEM((rows, width), f32),
        )

    pl.run_scoped(
        sequence_part,
        pltpu.VMEM((rows, HALF_HEADS * PER_HEAD), low),
        pltpu.VMEM((rows, HALF_HEADS * PER_HEAD), low),
    )

    small_mid[0] = jnp.zeros(small_mid.shape[1:], f32)
    for row in range(2):
        for i in range(width // HD):
            small_mid[0, row * 8 + i : row * 8 + i + 1, :] = gain_sums[row : row + 1, i * HD : (i + 1) * HD]
    small_mid[0, 16:24, :] = sums[...]
    at_slot("n1")
    small_out[...] = small.total()
    comm.finish()
    route.wait(block_back)
    route.wait(input_back)


BACK_PLAN = {
    "h1": (("launch", 0),),
    "h2": (("launch", 1),),
    "h3": (("launch", 2), ("s1", 1),),
    "g4": (("launch", 3),),
    "g5": (("launch", 4), ("s2", 1), ("s1", 2),),
    "g6": (("launch", 5), ("s1", 0),),
    "a7": (("launch", 6), ("s1", 4),),
    "o8": (("s1", 3), ("s2", 2),),
    "o9": (("s2", 0),),
    "o10": (("s3", 0), ("s1", 5), ("launch", 9),),
    "o11": (("s1", 6), ("s2", 3), ("s2", 4),),
    "t03": (("s3", 2), ("launch", 10),),
    "t11": (("launch", 8), ("s3", 1),),
    "t12": (("launch", 7), ("launch", 11),),
    "t22": (("s1", 10), ("s1", 9),),
    "t31": (("s1", 8),),
    "sw": (("s3", 3),),
    "b0": (("s4", 0),),
    "b1": (("s1", 11), ("s1", 7),),
    "q12": (("s3", 4), ("s5", 0),),
    "q13": (("launch", 12), ("s2", 5),),
    "q14": (("launch", 13), ("s3", 5), ("s2", 7),),
    "q15": (("s2", 6), ("s3", 6), ("s2", 8), ("s1", 12), ("s2", 9), ("s1", 13), ("launch", 14), ("s3", 9), ("s2", 11),),
    "q16": (("s3", 8), ("launch", 15),),
    "f0": (("s2", 13), ("s2", 10), ("s6", 0), ("s2", 12),),
    "f2": (("s3", 12), ("s3", 7), ("s1", 14), ("s3", 10), ("s4", 1),),
    "f3": (("s1", 15), ("s3", 13),),
    "n1": (("s2", 14), ("small", 0), ("s3", 14), ("small", 1), ("s3", 11), ("inback", 0), ("s5", 1), ("s2", 15), ("s3", 15), ("small", 2), ("s4", 3), ("small", 3), ("s4", 2), ("small", 4), ("s5", 3), ("s6", 1), ("small", 5), ("small", 6), ("s5", 2), ("s6", 3), ("small", 7), ("s6", 2),),
}


def run_backward(scalars, gains_all, head_gains, cosines, sines, saved, block_rows, fulls):
    low, f32 = jnp.bfloat16, jnp.float32
    source = saved[0]
    _, slot_len, width = source.shape
    rows = 2 * slot_len
    full_qkv, full_out, full_gate_up, full_down = fulls
    order = (full_down, full_gate_up, full_out, full_qkv)
    shapes = [(8 * f.shape[2], f.shape[3]) for f in order]
    shape = jax.ShapeDtypeStruct
    hbm = pl.BlockSpec(memory_space=HBM)
    vmem = pl.BlockSpec(memory_space=pltpu.VMEM)
    dma = pltpu.SemaphoreType.DMA
    count = len(shapes)

    def buffers(make, which):
        return [pltpu.VMEM(make(r // 4, n // 2), low) for r, n in which]

    out = pl.pallas_call(
        functools.partial(backward_kernel, shapes),
        out_shape=[
            shape((24, HD), f32),
            shape(source.shape, low),
            shape(source.shape, low),
            *[shape((2, 2, r // 4, n), low) for r, n in shapes],
        ],
        in_specs=[pl.BlockSpec(memory_space=pltpu.SMEM)] + [vmem] * 4 + [hbm] * 15,
        out_specs=[vmem] + [hbm] * 6,
        scratch_shapes=buffers(lambda r, n: (2, 2, r, n), shapes)
        + buffers(lambda r, n: (NZ, 2, 2, r, n), shapes)
        + buffers(lambda r, n: (5, r, n), shapes)
        + buffers(lambda r, n: (NZ, 2, r, n // 2), shapes[:2])
        + buffers(lambda r, n: (NZ, 2, r, n // 2), shapes[:2])
        + buffers(lambda r, n: (NZ, r, n // 2), shapes[:2])
        + buffers(lambda r, n: (NZ, r, n // 2), shapes[:2])
        + [
            pltpu.VMEM((2, max(r for r, _ in shapes), rows), low),
            pltpu.VMEM((2, 8, full_gate_up.shape[2], 2 * width), low),
            pltpu.VMEM((rows, width), f32),
            pltpu.VMEM((4, slot_len, HEADS * HD // 2), low),
            pltpu.VMEM((2, slot_len, HEADS * HD // 2), low),
            pltpu.VMEM((rows, HALF_HEADS * PER_HEAD), low),
            pltpu.VMEM((4, 24, HD), f32),
            pltpu.VMEM((3, 24, HD), f32),
            pltpu.VMEM((NZ, 24, HD), f32),
            pltpu.VMEM((8, width), f32),
            pltpu.VMEM((8, HD), f32),
            pltpu.VMEM((2, slot_len, width), low),
            dma((count,)),
            dma((count, 4)),
            dma((count, 4)),
            dma((count, 4, 4)),
            dma((count, 4, 4)),
            dma((count, 4)),
            dma((count, 5)),
            dma((count, len(SPREAD))),
            dma((count, len(SPREAD))),
            dma((6,)),
            dma((6,)),
            dma((4,)),
            dma((2,)),
            dma((2,)),
            dma((2, 2)),
            dma((BLOCKS,)),
            dma((2,)),
            dma((2,)),
            dma((4,)),
            dma((5,)),
            dma((5,)),
        ],
        compiler_params=pltpu.CompilerParams(collective_id=1, has_side_effects=True, vmem_limit_bytes=VMEM_LIMIT),
        name="backward",
    )(scalars, gains_all, head_gains, cosines, sines, *saved, block_rows, *fulls)
    return out[0], out[1], out[2], [o.reshape(r, n) for o, (r, n) in zip(out[3:], shapes)]


def swap(v):
    return lax.ppermute(v, "core", [(0, 1), (1, 0)])


def per_chip(
    tokens,
    cotangent,
    slot_order,
    attn_gain,
    q_gain,
    k_gain,
    w_qkv,
    w_out,
    mlp_gain,
    w_gate_up,
    w_down,
):
    z, core = lax.axis_index("z"), lax.axis_index("core")
    _, slot_len, width = tokens.shape
    f32, low = jnp.float32, jnp.bfloat16
    odd = z % 2
    orders = jnp.where(z // 2 == core, slot_order, swap(slot_order))
    order = lax.dynamic_index_in_dim(orders, odd, 0, False)
    slots = jnp.stack([2 * core + odd, 2 * core + 1 - odd, 2 - 2 * core + odd, 3 - 2 * core - odd])
    blocks = order[slots]
    where_is = jnp.sum(
        jnp.where(blocks[None, :] == jnp.arange(4)[:, None], jnp.arange(4)[None, :], 0), axis=1
    )
    scalars = jnp.concatenate([where_is, blocks, core[None], jnp.zeros((7,), jnp.int32)]).astype(jnp.int32)
    positions = (blocks[:2, None] * slot_len + jnp.arange(slot_len)[None, :]).reshape(-1)
    cos, sin = rope_tables(positions)
    cosines = jnp.concatenate([cos, cos], axis=1)
    sines = jnp.concatenate([-sin, sin], axis=1)
    gain_q, gain_k = q_gain.astype(f32)[None, :], k_gain.astype(f32)[None, :]
    head_gains = jnp.concatenate([gain_q, gain_k, jnp.zeros((6, HD), f32)], axis=0)
    gains = jnp.concatenate(
        [attn_gain.astype(f32)[None], mlp_gain.astype(f32)[None], jnp.zeros((6, attn_gain.shape[0]), f32)], axis=0
    )
    (block_rows, gains_all, *saved), fulls = run_forward(
        scalars, gains, head_gains, cosines, sines, tokens, cotangent, [w_qkv, w_out, w_gate_up, w_down]
    )
    sums, input_grad, block_out, (down_sum, gate_up_sum, out_sum, qkv_sum) = run_backward(
        scalars, gains_all, head_gains, cosines, sines, saved, block_rows.reshape(2, slot_len, width), fulls
    )
    count = width // HD
    share = width // NZ
    return (
        block_out,
        input_grad,
        lax.dynamic_slice_in_dim(sums[:count].reshape(-1), z * share, share, 0),
        sums[2 * count],
        sums[2 * count + 1],
        qkv_sum.astype(f32),
        out_sum.astype(f32),
        lax.dynamic_slice_in_dim(sums[count : 2 * count].reshape(-1), z * share, share, 0),
        gate_up_sum.astype(f32),
        down_sum.astype(f32),
    )


def solution(mesh):
    group, replica, body = "group", "replica", per_device
    if (mesh.shape["group"], mesh.shape["replica"]) == (NZ, 8):
        mesh = Mesh(mesh.devices.reshape(NZ, 2, 2, 2), ("z", "y", "x", "core"))
        group, replica, body = "z", ("y", "x", "core"), per_chip
    in_specs = (
        P(replica, group, None),
        P(replica, group, None),
        P(replica, None),
        P(group),
        P(),
        P(),
        P(group, None),
        P(group, None),
        P(group),
        P(group, None),
        P(group, None),
    )
    out_specs = (
        P(replica, group, None),
        P(replica, group, None),
        P(group),
        P(),
        P(),
        P(group, None),
        P(group, None),
        P(group),
        P(group, None),
        P(group, None),
    )
    return jax.shard_map(
        body, mesh=mesh, in_specs=in_specs, out_specs=out_specs, check_vma=False
    )
```

```python
import functools
import math

import jax
import jax.numpy as jnp
from jax import lax
from jax.experimental import pallas as pl
from jax.experimental.pallas import tpu as pltpu
from jax.sharding import Mesh
from jax.sharding import PartitionSpec as P

HEADS = 16
KV_HEADS = 8
HD = 128
FF = 3072


EPSILON = 1e-06
THETA_BASE = 1000000.0
MASKED = -1e30


def norm_rows(v):
    return v * lax.rsqrt(jnp.mean(v * v, axis=-1, keepdims=True) + EPSILON)


def norm_back(source, grad):
    inverse = lax.rsqrt(jnp.mean(source * source, axis=-1, keepdims=True) + EPSILON)
    normed = source * inverse
    return inverse * (grad - normed * jnp.mean(grad * normed, axis=-1, keepdims=True))


def rotate(v, cosines, sines):
    half_size = v.shape[-1] // 2
    leading = v[..., :half_size]
    trailing = v[..., half_size:]
    return jnp.concatenate(
        [leading * cosines - trailing * sines, trailing * cosines + leading * sines], axis=-1
    )


def rope_tables(positions):
    half_size = HD // 2
    counter = jnp.arange(half_size).astype(jnp.float32)
    frequency = THETA_BASE ** (-2.0 * counter / HD)
    angles = positions.astype(jnp.float32)[:, None] * frequency[None, :]
    return (jnp.cos(angles), jnp.sin(angles))


def matmul(a, b):
    return jnp.dot(a, b, preferred_element_type=jnp.float32)


def matmul_right(a, b):
    return lax.dot_general(a, b, (((1,), (1,)), ((), ())), preferred_element_type=jnp.float32)


def matmul_left(a, b):
    return lax.dot_general(a, b, (((0,), (0,)), ((), ())), preferred_element_type=jnp.float32)


def per_device(
    tokens,
    cotangent,
    slot_order,
    attn_gain,
    q_gain,
    k_gain,
    w_qkv,
    w_out,
    mlp_gain,
    w_gate_up,
    w_down,
):
    member_count = lax.axis_size("group")
    member = lax.axis_index("group")
    micro, slot_len, width = tokens.shape
    rows = micro * slot_len
    length = slot_len * member_count
    q_width = HEADS * HD
    kv_width = KV_HEADS * HD
    groups = HEADS // KV_HEADS
    score_scale = 1.0 / math.sqrt(HD)
    key_block = math.gcd(length, 512)
    block_count = length // key_block
    head_gain_q = q_gain.astype(jnp.float32)
    head_gain_k = k_gain.astype(jnp.float32)
    offsets = jnp.arange(slot_len, dtype=jnp.int32)
    source = tokens.reshape(rows, width).astype(jnp.float32)
    all_pos = (slot_order[:, :, None] * slot_len + offsets[None, None, :]).reshape(micro, length)
    my_pos = lax.dynamic_slice_in_dim(all_pos, member * slot_len, slot_len, 1)
    query_top = jnp.max(my_pos, axis=1)
    cosines, sines = rope_tables(my_pos.reshape(rows))
    normed_first = norm_rows(source)
    gain_piece = lax.all_gather(attn_gain, "group", axis=0, tiled=True)
    weight_piece = lax.all_gather(w_qkv, "group", axis=0, tiled=True)
    columns = normed_first
    low_cols = (columns * gain_piece.astype(jnp.float32)).astype(jnp.bfloat16)
    qkv = matmul(low_cols, weight_piece)
    first_low = low_cols
    gain_first = gain_piece.astype(jnp.float32)
    queries = qkv[:, :q_width].reshape(rows, HEADS, HD)
    keys_raw = qkv[:, q_width : q_width + kv_width].reshape(rows, KV_HEADS, HD)
    values_low = qkv[:, q_width + kv_width :].astype(jnp.bfloat16)
    queries_normed = norm_rows(queries)
    keys_normed = norm_rows(keys_raw)
    query_rot = rotate(queries_normed * head_gain_q, cosines[:, None, :], sines[:, None, :]).astype(
        jnp.bfloat16
    )
    key_rot = rotate(keys_normed * head_gain_k, cosines[:, None, :], sines[:, None, :]).astype(
        jnp.bfloat16
    )
    key_all, value_all = (
        lax.all_gather(key_rot.reshape(micro, slot_len, kv_width), "group", axis=1, tiled=True),
        lax.all_gather(values_low.reshape(micro, slot_len, kv_width), "group", axis=1, tiled=True),
    )
    query_heads = query_rot.reshape(micro, slot_len, KV_HEADS, groups, HD)

    def block_live(block_index):
        key_pos = lax.dynamic_slice_in_dim(all_pos, block_index * key_block, key_block, 1)
        return jnp.any(jnp.min(key_pos, axis=1) <= query_top)

    def block_scores(block_index):
        begin = block_index * key_block
        key_piece = lax.dynamic_slice_in_dim(key_all, begin, key_block, 1).reshape(
            micro, key_block, KV_HEADS, HD
        )
        key_pos = lax.dynamic_slice_in_dim(all_pos, begin, key_block, 1)
        raw = (
            jnp.einsum(
                "mqkgd,mskd->mkgqs", query_heads, key_piece, preferred_element_type=jnp.float32
            )
            * score_scale
        )
        allowed = (key_pos[:, None, :] <= my_pos[:, :, None])[:, None, None]
        return (jnp.where(allowed, raw, MASKED), allowed, key_piece)

    def stats_step(block_index, carry):

        def stats_visit_block(carry_in):
            top_in, total_in = carry_in
            scores, allowed, key_piece = block_scores(block_index)
            new_top = jnp.maximum(top_in, jnp.max(scores, axis=-1))
            summed = jnp.sum(jnp.where(allowed, jnp.exp(scores - new_top[..., None]), 0.0), axis=-1)
            return (new_top, total_in * jnp.exp(top_in - new_top) + summed)

        return lax.cond(
            block_live(block_index), stats_visit_block, lambda carry_in: carry_in, carry
        )

    stat_shape = (micro, KV_HEADS, groups, slot_len)
    top_final, total_final = lax.fori_loop(
        0,
        block_count,
        stats_step,
        (jnp.full(stat_shape, MASKED, jnp.float32), jnp.zeros(stat_shape, jnp.float32)),
    )
    log_total = top_final + jnp.log(total_final)

    def output_step(block_index, accum):

        def output_visit_block(accum_in):
            scores, allowed, key_piece = block_scores(block_index)
            probabilities = jnp.where(allowed, jnp.exp(scores - log_total[..., None]), 0.0)
            value_piece = lax.dynamic_slice_in_dim(
                value_all, block_index * key_block, key_block, 1
            ).reshape(micro, key_block, KV_HEADS, HD)
            return accum_in + jnp.einsum(
                "mkgqs,mskd->mqkgd",
                probabilities.astype(jnp.bfloat16),
                value_piece,
                preferred_element_type=jnp.float32,
            )

        return lax.cond(
            block_live(block_index), output_visit_block, lambda accum_in: accum_in, accum
        )

    attn_heads = lax.fori_loop(
        0, block_count, output_step, jnp.zeros((micro, slot_len, KV_HEADS, groups, HD), jnp.float32)
    )
    attended = attn_heads.reshape(rows, q_width).astype(jnp.bfloat16)
    columns = attended
    branch = matmul(columns, lax.all_gather(w_out, "group", axis=0, tiled=True))
    middle = source + branch
    normed_second = norm_rows(middle)
    gain_piece = lax.all_gather(mlp_gain, "group", axis=0, tiled=True)
    weight_piece = lax.all_gather(w_gate_up, "group", axis=0, tiled=True)
    columns = normed_second
    low_cols = (columns * gain_piece.astype(jnp.float32)).astype(jnp.bfloat16)
    gate_up = matmul(low_cols, weight_piece)
    gain_second = gain_piece.astype(jnp.float32)
    gate_part = gate_up[:, :FF]
    up_part = gate_up[:, FF:]
    sigmoid_gate = jax.nn.sigmoid(gate_part)
    silu_gate = gate_part * sigmoid_gate
    hidden = (silu_gate * up_part).astype(jnp.bfloat16)
    columns = hidden
    down_out = matmul(columns, lax.all_gather(w_down, "group", axis=0, tiled=True))
    block_out = (middle + down_out).astype(jnp.bfloat16).reshape(micro, slot_len, width)
    grad_low = cotangent.reshape(rows, width)
    grad_output = grad_low.astype(jnp.float32)
    down_full = matmul_left(hidden, grad_low)
    grad_hidden = matmul_right(grad_low, lax.all_gather(w_down, "group", axis=0, tiled=True))
    grad_gate = grad_hidden * up_part * (sigmoid_gate * (1.0 + gate_part * (1.0 - sigmoid_gate)))
    grad_upper = grad_hidden * silu_gate
    grad_gate_up = jnp.concatenate([grad_gate, grad_upper], axis=1).astype(jnp.bfloat16)
    gate_up_full = matmul_left(low_cols, grad_gate_up)
    grad_second = matmul_right(grad_gate_up, lax.all_gather(w_gate_up, "group", axis=0, tiled=True))
    gain_second_full = jnp.sum(normed_second * grad_second, axis=0)
    grad_middle = grad_output + norm_back(middle, grad_second * gain_second)
    grad_mid_low = grad_middle.astype(jnp.bfloat16)
    out_full = matmul_left(attended, grad_mid_low)
    grad_attn_full = matmul_right(grad_mid_low, lax.all_gather(w_out, "group", axis=0, tiled=True))
    grad_attn = grad_attn_full.astype(jnp.bfloat16)
    grad_heads = grad_attn.reshape(micro, slot_len, KV_HEADS, groups, HD)
    delta = jnp.transpose(
        jnp.sum(grad_heads.astype(jnp.float32) * attn_heads, axis=-1), (0, 2, 3, 1)
    )

    def back_step(block_index, carry):

        def back_visit_block(carry_in):
            grad_query_in, grad_key_in, grad_value_in = carry_in
            begin = block_index * key_block
            scores, allowed, key_piece = block_scores(block_index)
            probabilities = jnp.where(allowed, jnp.exp(scores - log_total[..., None]), 0.0)
            value_piece = lax.dynamic_slice_in_dim(value_all, begin, key_block, 1).reshape(
                micro, key_block, KV_HEADS, HD
            )
            grad_probs = jnp.einsum(
                "mqkgd,mskd->mkgqs", grad_heads, value_piece, preferred_element_type=jnp.float32
            )
            grad_scores = (probabilities * (grad_probs - delta[..., None])).astype(jnp.bfloat16)
            grad_query_out = (
                grad_query_in
                + jnp.einsum(
                    "mkgqs,mskd->mqkgd", grad_scores, key_piece, preferred_element_type=jnp.float32
                )
                * score_scale
            )
            key_term = (
                jnp.einsum(
                    "mkgqs,mqkgd->mskd",
                    grad_scores,
                    query_heads,
                    preferred_element_type=jnp.float32,
                )
                * score_scale
            )
            value_term = jnp.einsum(
                "mkgqs,mqkgd->mskd",
                probabilities.astype(jnp.bfloat16),
                grad_heads,
                preferred_element_type=jnp.float32,
            )
            key_old = lax.dynamic_slice_in_dim(grad_key_in, begin, key_block, 1)
            value_old = lax.dynamic_slice_in_dim(grad_value_in, begin, key_block, 1)
            grad_key_out = lax.dynamic_update_slice_in_dim(
                grad_key_in, key_old + key_term, begin, 1
            )
            grad_value_out = lax.dynamic_update_slice_in_dim(
                grad_value_in, value_old + value_term, begin, 1
            )
            return (grad_query_out, grad_key_out, grad_value_out)

        return lax.cond(block_live(block_index), back_visit_block, lambda carry_in: carry_in, carry)

    back_start = (
        jnp.zeros((micro, slot_len, KV_HEADS, groups, HD), jnp.float32),
        jnp.zeros((micro, length, KV_HEADS, HD), jnp.float32),
        jnp.zeros((micro, length, KV_HEADS, HD), jnp.float32),
    )
    grad_query_rot, grad_key_all, grad_value_all = lax.fori_loop(
        0, block_count, back_step, back_start
    )
    grad_key_mine, grad_value_mine = (
        lax.psum_scatter(
            grad_key_all.reshape(micro, length, kv_width).astype(jnp.bfloat16),
            "group",
            scatter_dimension=1,
            tiled=True,
        ).astype(jnp.float32),
        lax.psum_scatter(
            grad_value_all.reshape(micro, length, kv_width).astype(jnp.bfloat16),
            "group",
            scatter_dimension=1,
            tiled=True,
        ).astype(jnp.float32),
    )
    grad_query_norm = rotate(
        grad_query_rot.reshape(rows, HEADS, HD), cosines[:, None, :], -sines[:, None, :]
    )
    grad_key_norm = rotate(
        grad_key_mine.reshape(rows, KV_HEADS, HD), cosines[:, None, :], -sines[:, None, :]
    )
    q_gain_total = jnp.sum(queries_normed * grad_query_norm, axis=(0, 1))
    k_gain_total = jnp.sum(keys_normed * grad_key_norm, axis=(0, 1))
    grad_queries = norm_back(queries, grad_query_norm * head_gain_q).reshape(rows, q_width)
    grad_keys = norm_back(keys_raw, grad_key_norm * head_gain_k).reshape(rows, kv_width)
    grad_qkv = jnp.concatenate(
        [grad_queries, grad_keys, grad_value_mine.reshape(rows, kv_width)], axis=1
    ).astype(jnp.bfloat16)
    qkv_full = matmul_left(first_low, grad_qkv)
    grad_first = matmul_right(grad_qkv, lax.all_gather(w_qkv, "group", axis=0, tiled=True))
    gain_first_full = jnp.sum(normed_first * grad_first, axis=0)
    input_grad = (
        (grad_middle + norm_back(source, grad_first * gain_first))
        .astype(jnp.bfloat16)
        .reshape(micro, slot_len, width)
    )
    owned = (
        lax.psum_scatter(
            gain_first_full.astype(jnp.bfloat16), "group", scatter_dimension=0, tiled=True
        ).astype(jnp.float32),
        lax.psum_scatter(
            qkv_full.astype(jnp.bfloat16), "group", scatter_dimension=0, tiled=True
        ).astype(jnp.float32),
        lax.psum_scatter(
            out_full.astype(jnp.bfloat16), "group", scatter_dimension=0, tiled=True
        ).astype(jnp.float32),
        lax.psum_scatter(
            gain_second_full.astype(jnp.bfloat16), "group", scatter_dimension=0, tiled=True
        ).astype(jnp.float32),
        lax.psum_scatter(
            gate_up_full.astype(jnp.bfloat16), "group", scatter_dimension=0, tiled=True
        ).astype(jnp.float32),
        lax.psum_scatter(
            down_full.astype(jnp.bfloat16), "group", scatter_dimension=0, tiled=True
        ).astype(jnp.float32),
    )
    summed = (
        lax.psum(owned[0].astype(jnp.bfloat16), "replica").astype(jnp.float32),
        lax.psum(owned[1].astype(jnp.bfloat16), "replica").astype(jnp.float32),
        lax.psum(owned[2].astype(jnp.bfloat16), "replica").astype(jnp.float32),
        lax.psum(owned[3].astype(jnp.bfloat16), "replica").astype(jnp.float32),
        lax.psum(owned[4].astype(jnp.bfloat16), "replica").astype(jnp.float32),
        lax.psum(owned[5].astype(jnp.bfloat16), "replica").astype(jnp.float32),
    )
    head_sums = lax.psum((q_gain_total, k_gain_total), ("group", "replica"))
    return (
        block_out,
        input_grad,
        summed[0],
        head_sums[0],
        head_sums[1],
        summed[1],
        summed[2],
        summed[3],
        summed[4],
        summed[5],
    )


MESH_ID = pl.DeviceIdType.MESH
HBM = pltpu.MemorySpace.HBM
VMEM_LIMIT = 64 * 1024 * 1024 - 65536
NZ = 4


class Place:
    def __init__(self):
        self.z = lax.axis_index("z")
        self.y = lax.axis_index("y")
        self.x = lax.axis_index("x")
        self.c = lax.axis_index("core")
        self.h = self.z // 2
        self.m = self.at(self.z)
        self.inner = {"z": self.at(self.m + 1)}
        self.outer = {"z": self.at(lax.rem(self.m + 3, 4))}
        self.across_x = {"x": 1 - self.x}
        self.across_y = {"y": 1 - self.y}
        self.partner = {"core": 1 - self.c}

    def at(self, t):
        return t * (1 - 2 * self.h) + 3 * self.h

    def greet(self):
        barrier = pltpu.get_barrier_semaphore()
        peers = [self.across_x, self.across_y, self.partner]
        for hop in range(1, NZ):
            there = lax.rem(self.z + hop, NZ)
            peers += [{"z": there}, {"z": there, "core": 1 - self.c}]
        for peer in peers:
            pl.semaphore_signal(barrier, inc=1, device_id=peer, device_id_type=MESH_ID)
        pl.semaphore_wait(barrier, len(peers))


def remote(src, dst, send, recv, peer):
    return pltpu.make_async_remote_copy(
        src_ref=src, dst_ref=dst, send_sem=send, recv_sem=recv, device_id=peer, device_id_type=MESH_ID
    )


KINDS = ("x", "y", "yx", "xy", "c", "cx", "cy", "cd")


def half_rows(ref, which):
    rows = ref.shape[0] // 2
    return ref.at[pl.ds(which * rows, rows), :]


class Gather:
    def __init__(self, me, shards, fulls, sems):
        self.me, self.shards, self.fulls = me, shards, fulls
        self.z_send, self.z_recv, self.f_send, self.xy_send, self.xy_recv = sems
        self.stage_t = (1 - me.m, 2, 3)
        self.stages = [(w, k) for w in range(len(shards)) for k in range(3)]

    def piece(self, c, x, y):
        return c * 4 + x * 2 + y

    def shard_z(self, k):
        return self.me.at(self.stage_t[k])

    def own_copy(self, w, peer, k, slot):
        me = self.me
        piece = self.piece(me.c, me.x, me.y)
        return remote(
            self.shards[w].at[piece],
            self.fulls[w].at[me.z, piece],
            self.z_send.at[w, slot],
            self.z_recv.at[w, k],
            peer,
        )

    def own(self, w):
        me = self.me
        self.own_copy(w, me.inner, me.m, 0).start()

        @pl.when(me.m == 1)
        def _():
            self.own_copy(w, me.outer, 0, 1).start()

    def place(self, w, k, cc, xx, yy):
        return self.fulls[w].at[self.shard_z(k), self.piece(cc, xx, yy)]

    def forward(self, w, k):
        me = self.me
        piece = self.place(w, k, me.c, me.x, me.y)
        peer, slot = ((me.inner, 2), (me.outer, 1), (me.outer, 2))[k]
        return remote(piece, piece, self.f_send.at[w, k], self.z_recv.at[w, slot], peer)

    def hop(self, w, k, kind):
        me = self.me
        c, x, y = me.c, me.x, me.y
        mine, px = self.place(w, k, c, x, y), self.place(w, k, c, 1 - x, y)
        py, pd = self.place(w, k, c, x, 1 - y), self.place(w, k, c, 1 - x, 1 - y)
        src, peer = {
            "x": (mine, me.across_x),
            "y": (mine, me.across_y),
            "yx": (half_rows(px, 0), me.across_y),
            "xy": (half_rows(py, 1), me.across_x),
            "c": (mine, me.partner),
            "cx": (px, me.partner),
            "cy": (py, me.partner),
            "cd": (pd, me.partner),
        }[kind]
        index = KINDS.index(kind)
        return remote(src, src, self.xy_send.at[w, k, index], self.xy_recv.at[w, k, index], peer)

    def arrived(self, w, k, kind):
        me = self.me
        c, x, y = me.c, me.x, me.y
        dst = {
            "x": lambda: self.place(w, k, c, 1 - x, y),
            "y": lambda: self.place(w, k, c, x, 1 - y),
            "yx": lambda: half_rows(self.place(w, k, c, 1 - x, 1 - y), 0),
            "xy": lambda: half_rows(self.place(w, k, c, 1 - x, 1 - y), 1),
            "c": lambda: self.place(w, k, 1 - c, x, y),
            "cx": lambda: self.place(w, k, 1 - c, 1 - x, y),
            "cy": lambda: self.place(w, k, 1 - c, x, 1 - y),
            "cd": lambda: self.place(w, k, 1 - c, 1 - x, 1 - y),
        }[kind]()
        index = KINDS.index(kind)
        remote(dst, dst, self.xy_send.at[w, k, index], self.xy_recv.at[w, k, index], me.partner).wait_recv()

    def relay(self, i):
        w, k = self.stages[i]
        me = self.me
        mine = self.place(w, k, me.c, me.x, me.y)
        remote(mine, mine, self.f_send.at[w, k], self.z_recv.at[w, k], me.partner).wait_recv()

        @pl.when(me.m == 1)
        def _():
            self.forward(w, k).start()

    def launch(self, i):
        w, k = self.stages[i]
        for kind in ("x", "y", "c"):
            self.hop(w, k, kind).start()

    def sx(self, i):
        w, k = self.stages[i]
        self.arrived(w, k, "x")
        self.hop(w, k, "yx").start()
        self.hop(w, k, "cx").start()

    def sy(self, i):
        w, k = self.stages[i]
        self.arrived(w, k, "y")
        self.hop(w, k, "xy").start()
        self.hop(w, k, "cy").start()

    def third(self, i):
        w, k = self.stages[i]
        self.arrived(w, k, "yx")
        self.arrived(w, k, "xy")
        self.hop(w, k, "cd").start()

    def require(self, w, k):
        for kind in ("c", "cx", "cy", "cd"):
            self.arrived(w, k, kind)

    def finish(self):
        me = self.me
        for w, k in self.stages:
            for kind in KINDS:
                self.hop(w, k, kind).wait_send()
        for w in range(len(self.shards)):
            self.own_copy(w, me.inner, me.m, 0).wait_send()

            @pl.when(me.m == 1)
            def _(w=w):
                self.own_copy(w, me.outer, 0, 1).wait_send()
                for k in range(3):
                    self.forward(w, k).wait_send()


class Route:
    def __init__(self, me):
        z, c = me.z, me.c
        odd = lax.rem(z, 2)
        self.stays = z // 2 == c
        self.order = (odd, 1 - odd)
        self.to = ({"z": 2 * c + odd, "core": z // 2}, {"z": 2 * c + 1 - odd, "core": z // 2})

    def start(self, copies):
        first_local, first, second = copies

        @pl.when(self.stays)
        def _():
            first_local.start()

        @pl.when(jnp.logical_not(self.stays))
        def _():
            first.start()

        second.start()

    def out(self, held, there, sems):
        a, b = self.order
        return (
            pltpu.make_async_copy(held.at[a], there.at[0], sems.at[0]),
            remote(held.at[a], there.at[0], sems.at[1], sems.at[2], self.to[0]),
            remote(held.at[b], there.at[1], sems.at[3], sems.at[4], self.to[1]),
        )

    def back(self, held, there, sems):
        odd = self.order[0]
        return (
            pltpu.make_async_copy(held.at[0], there.at[odd], sems.at[0]),
            remote(held.at[0], there.at[odd], sems.at[1], sems.at[2], self.to[0]),
            remote(held.at[1], there.at[odd], sems.at[3], sems.at[4], self.to[1]),
        )

    def wait(self, copies):
        first_local, first, second = copies

        @pl.when(self.stays)
        def _():
            first_local.wait()

        @pl.when(jnp.logical_not(self.stays))
        def _():
            first.wait()

        second.wait()


def turn(v):
    return pltpu.roll(v, HD // 2, 1)


def stacked(two_heads):
    return jnp.concatenate([two_heads[:, :HD], two_heads[:, HD:]], axis=0)


def pick(which, values):
    out = values[0]
    for i in range(1, len(values)):
        out = jnp.where(which == i, values[i], out)
    return out


def row_loop(rows, step, body):
    def run(i, carry):
        body(pl.ds(pl.multiple_of(i * step, step), step))
        return carry

    lax.fori_loop(0, rows // step, run, 0)


PER_HEAD = 4 * HD
HALF_HEADS = KV_HEADS // 2
BLOCKS = 4
COUNT = 4


def forward_kernel(scalars, gains, head_gains, cosines, sines, tokens, cotangent, *refs):
    shards = refs[:COUNT]
    (
        block_out,
        gains_all,
        source,
        grad,
        h1_out,
        raw_out,
        tok_out,
        probs_out,
        attended_out,
        middle_out,
        h2_out,
        gate_up_out,
    ) = refs[COUNT : COUNT + 12]
    fulls = refs[COUNT + 12 : 2 * COUNT + 12]
    (
        acc,
        acc_small,
        wide,
        narrow,
        x,
        h1,
        h2,
        tok,
        outgoing,
        raw,
        p0,
        p1,
        p2,
        p3,
        ordered,
        mixed,
        mixed_out,
        attended,
        middle,
        hidden,
        gate_up,
        low_out,
        z_send,
        z_recv,
        f_send,
        xy_send,
        xy_recv,
        load_sem,
        keep_sem,
        gain_sem,
        token_sem,
        cot_sem,
        swap_sem,
        save_sem,
        prob_sem,
        gate_sem,
    ) = refs[2 * COUNT + 12 :]
    prob_slots = (p0, p1, p2, p3)
    low, f32 = jnp.bfloat16, jnp.float32
    me = Place()
    z, c = me.z, me.c
    rows, width = x.shape
    block = rows // 2
    comm = Gather(me, shards, fulls, (z_send, z_recv, f_send, xy_send, xy_recv))
    route = Route(me)
    me.greet()
    gain_copies = []
    for j in range(1, NZ):
        there = {"z": lax.rem(z + j, NZ)}
        gain_copies.append(remote(gains, gains_all.at[z], gain_sem.at[0, j], gain_sem.at[1, j], there))
    for copy in gain_copies:
        copy.start()
    gains_all[pl.ds(z, 1)] = gains[...][None]
    token_copies = route.out(tokens, source, token_sem)
    cot_copies = route.out(cotangent, grad, cot_sem)

    def at_slot(slot):
        for name, index in FORWARD_PLAN.get(slot, ()):
            if name == "tok":
                route.start(token_copies)
            elif name == "cot":
                route.start(cot_copies)
            else:
                getattr(comm, name)(index)

    def buffer(w, kk):
        if w in (0, 2):
            return wide.at[kk % 2, :, :, pl.ds(0, shards[w].shape[2])]
        return narrow.at[kk % 2, :, pl.ds(0, shards[w].shape[1]), :]

    def load(w, kk):
        src = shards[w] if kk == 0 else fulls[w].at[comm.shard_z(kk - 1)]
        return pltpu.make_async_copy(src, buffer(w, kk), load_sem.at[w, kk])

    def keep(w):
        return pltpu.make_async_copy(buffer(w, 0), fulls[w].at[z], keep_sem.at[w])

    def fetch(w, kk):
        if kk > 0:
            comm.require(w, kk - 1)
        if kk == 2:
            keep(w).wait()
        load(w, kk).start()

    def chunk(w, kk, lhs, out, tile):
        depth = 8 * shards[w].shape[1]
        columns = shards[w].shape[2]
        own_z = z if kk == 0 else comm.shard_z(kk - 1)
        load(w, kk).wait()
        if kk == 0:
            keep(w).start()
        from_left = pl.ds(pl.multiple_of(own_z * depth, depth), depth)
        weight = buffer(w, kk)

        def body(i, carry):
            at = pl.ds(pl.multiple_of(i * tile, tile), tile)
            right = weight[:, :, at].reshape(depth, tile)
            part = jnp.dot(lhs[:, from_left], right, preferred_element_type=f32)
            if kk == 0:
                out[:, at] = part
            else:
                out[:, at] += part
            return carry

        lax.fori_loop(0, columns // tile, body, 0)

    def save(i, src, dst):
        return pltpu.make_async_copy(src, dst, save_sem.at[i])

    fetch(0, 0)
    fetch(1, 0)
    at_slot("start")
    fetch(0, 1)
    for j in range(1, NZ):
        gain_copies[j - 1].wait_send()
        there = gains_all.at[lax.rem(z + NZ - j, NZ)]
        remote(gains, there, gain_sem.at[0, j], gain_sem.at[1, j], me.partner).wait_recv()
    route.wait(token_copies)
    for part in range(2):
        pltpu.make_async_copy(source.at[part], x.at[pl.ds(part * block, block)], token_sem.at[5 + part]).start()
    for part in range(2):
        pltpu.make_async_copy(source.at[part], x.at[pl.ds(part * block, block)], token_sem.at[5 + part]).wait()

    def normed_times(v, index):
        v = v * lax.rsqrt(jnp.mean(v * v, axis=-1, keepdims=True) + EPSILON)
        gain = jnp.concatenate([gains_all[s, index : index + 1, :] for s in range(NZ)], axis=1)
        return (v * gain).astype(low)

    def first_norm(at):
        h1[at, :] = normed_times(x[at, :].astype(f32), 0)

    row_loop(rows, 64, first_norm)
    save(0, h1, h1_out).start()
    at_slot("tw")
    chunk(0, 0, h1, acc, 512)
    at_slot("q0")
    fetch(0, 2)
    chunk(0, 1, h1, acc, 512)
    at_slot("q1")
    fetch(0, 3)
    chunk(0, 2, h1, acc, 512)
    fetch(2, 0)
    at_slot("q2")
    chunk(0, 3, h1, acc, 512)
    at_slot("q3")

    def head(h, target, column):
        parts = []
        for start, size in ((h * 2 * HD, 2 * HD), ((HEADS + h) * HD, HD), ((HEADS + KV_HEADS + h) * HD, HD)):
            parts.append(acc[:, pl.ds(pl.multiple_of(start, HD), size)])
        half, at = h // HALF_HEADS, pl.multiple_of(lax.rem(h, HALF_HEADS) * PER_HEAD, PER_HEAD)
        for i, (v, gain_row) in enumerate(((parts[0][:, :HD], 0), (parts[0][:, HD:], 0), (parts[1], 1))):
            raw[half, :, pl.ds(pl.multiple_of(at + i * HD, HD), HD)] = v.astype(low)
            v = v * lax.rsqrt(jnp.mean(v * v, axis=-1, keepdims=True) + EPSILON)
            v = v * head_gains[gain_row : gain_row + 1, :]
            v = (v * cosines[...] + turn(v) * sines[...]).astype(low)
            for j in range(2):
                target[j, :, pl.ds(pl.multiple_of(column + i * HD, HD), HD)] = v[j * block : (j + 1) * block]
        v = parts[2].astype(low)
        for j in range(2):
            target[j, :, pl.ds(pl.multiple_of(column + 3 * HD, HD), HD)] = v[j * block : (j + 1) * block]

    def other_head(i, carry):
        head(i + HALF_HEADS * (1 - c), outgoing, i * PER_HEAD)
        return carry

    def own_head(i, carry):
        head(i + HALF_HEADS * c, tok, i * PER_HEAD)
        return carry

    lax.fori_loop(0, HALF_HEADS, other_head, 0)
    swap_out = remote(outgoing, tok.at[pl.ds(2, 2)], swap_sem.at[0], swap_sem.at[1], me.partner)
    swap_out.start()
    at_slot("r0")
    lax.fori_loop(0, HALF_HEADS, own_head, 0)
    save(1, raw, raw_out).start()
    at_slot("r1")
    swap_out.wait()
    save(2, tok, tok_out).start()
    at_slot("sw")

    scale = 1.0 / math.sqrt(HD)
    above = lax.rem(lax.broadcasted_iota(jnp.int32, (2 * block, block), 0), block)
    above = above < lax.broadcasted_iota(jnp.int32, (2 * block, block), 1)

    def save_probs(h, i):
        n = (i + 1) * block
        column = i * (i + 1) // 2 * block
        return pltpu.make_async_copy(prob_slots[i], probs_out.at[h, :, pl.ds(column, n)], prob_sem.at[i])

    def attend(h, carry):
        at = pl.multiple_of(h * PER_HEAD, PER_HEAD)
        for i in range(BLOCKS):
            ordered[i * block : (i + 1) * block] = pick(
                scalars[i], [tok[j, :, pl.ds(at, PER_HEAD)] for j in range(BLOCKS)]
            )
        for i in range(BLOCKS):
            n = (i + 1) * block
            query = stacked(ordered[i * block : n, : 2 * HD])
            keys, values = ordered[:n, 2 * HD : 3 * HD], ordered[:n, 3 * HD :]
            scores = lax.dot_general(query, keys, (((1,), (1,)), ((), ())), preferred_element_type=f32)
            last = jnp.where(above, MASKED, scores[:, i * block :])
            scores = last if i == 0 else jnp.concatenate([scores[:, : i * block], last], axis=1)
            top = jnp.max(scores, axis=-1, keepdims=True)
            weights = jnp.exp((scores - top) * scale)
            weights = weights * (1.0 / jnp.sum(weights, axis=-1, keepdims=True))
            probs = weights.astype(low)

            @pl.when(h > 0)
            def _():
                save_probs(h - 1, i).wait()

            prob_slots[i][...] = probs
            save_probs(h, i).start()
            out = jnp.dot(probs, values, preferred_element_type=f32).astype(low)
            there = pl.multiple_of(h * 2 * HD, 2 * HD)
            mixed[i * block : (i + 1) * block, pl.ds(there, HD)] = out[:block]
            mixed[i * block : (i + 1) * block, pl.ds(pl.multiple_of(there + HD, HD), HD)] = out[block:]
            for now in range(HALF_HEADS):
                slot_name = f"t{now}{i}"
                if slot_name in FORWARD_PLAN:

                    @pl.when(h == now)
                    def _(slot_name=slot_name):
                        at_slot(slot_name)

        return carry

    lax.fori_loop(0, HALF_HEADS, attend, 0)
    fetch(1, 1)
    half = HEADS * HD // 2
    mine = pl.ds(pl.multiple_of(c * half, half), half)
    for j in range(2):
        blocks = [mixed[i * block : (i + 1) * block] for i in range(BLOCKS)]
        mixed_out[j * block : (j + 1) * block] = pick(scalars[BLOCKS + 2 + j], blocks)
    for j in range(2):
        blocks = [mixed[i * block : (i + 1) * block] for i in range(BLOCKS)]
        attended[j * block : (j + 1) * block, mine] = pick(scalars[BLOCKS + j], blocks)
    mixed_swap = remote(mixed_out, attended.at[:, mine], swap_sem.at[2], swap_sem.at[3], me.partner)
    mixed_swap.start()
    at_slot("m")
    for i in range(BLOCKS):
        save_probs(HALF_HEADS - 1, i).wait()
    mixed_swap.wait()
    save(3, attended, attended_out).start()
    for kk in range(4):
        chunk(1, kk, attended, acc_small, 512)
        at_slot(f"o{kk}")
        if kk < 2:
            fetch(1, kk + 2)
        elif kk == 2:
            fetch(3, 0)

    def second_norm(at):
        v = x[at, :].astype(f32) + acc_small[at, :]
        middle[at, :] = v
        h2[at, :] = normed_times(v, 1)

    row_loop(rows, 64, second_norm)
    save(4, middle, middle_out).start()
    save(5, h2, h2_out).start()
    at_slot("n2")
    fetch(2, 1)
    chunk(2, 0, h2, acc, 512)
    at_slot("g0")
    fetch(2, 2)
    chunk(2, 1, h2, acc, 512)
    at_slot("g1")
    chunk(2, 2, h2, acc, 512)
    at_slot("g2")
    fetch(2, 3)
    chunk(2, 3, h2, acc, 512)
    at_slot("g3")

    def save_gate_up(i, part, slot):
        at = pl.multiple_of(part * FF + i * 512, 512)
        return pltpu.make_async_copy(gate_up.at[slot, part], gate_up_out.at[:, pl.ds(at, 512)], gate_sem.at[slot, part])

    def activate(i, carry):
        slot = lax.rem(i, 2)
        at = pl.multiple_of(i * 512, 512)

        @pl.when(i >= 2)
        def _():
            for part in range(2):
                save_gate_up(i - 2, part, slot).wait()

        gate = acc[:, pl.ds(at, 512)]
        up = acc[:, pl.ds(pl.multiple_of(FF + at, 512), 512)]
        gate_up[slot, 0] = gate.astype(low)
        gate_up[slot, 1] = up.astype(low)
        hidden[:, pl.ds(at, 512)] = (gate * jax.nn.sigmoid(gate) * up).astype(low)
        for part in range(2):
            save_gate_up(i, part, slot).start()
        return carry

    tiles = FF // 512
    lax.fori_loop(0, tiles, activate, 0)
    at_slot("ac")
    fetch(3, 1)
    chunk(3, 0, hidden, acc_small, 512)
    at_slot("d0")
    chunk(3, 1, hidden, acc_small, 512)
    at_slot("d1")
    fetch(3, 2)
    chunk(3, 2, hidden, acc_small, 512)
    at_slot("d2")
    fetch(3, 3)
    chunk(3, 3, hidden, acc_small, 512)
    at_slot("d3")

    def final(at):
        low_out[at, :] = (middle[at, :] + acc_small[at, :]).astype(low)

    row_loop(rows, 64, final)
    save(6, low_out, block_out).start()
    at_slot("fin")
    comm.finish()
    for slot in range(2):
        for part in range(2):
            save_gate_up(tiles - 2 + slot, part, slot).wait()
    for i, (src, dst) in enumerate(
        (
            (h1, h1_out),
            (raw, raw_out),
            (tok, tok_out),
            (attended, attended_out),
            (middle, middle_out),
            (h2, h2_out),
            (low_out, block_out),
        )
    ):
        save(i, src, dst).wait()
    route.wait(cot_copies)


FORWARD_PLAN = {
    "start": (("own", 0), ("own", 1), ("relay", 0), ("launch", 0), ("own", 2), ("relay", 2), ("launch", 2), ("relay", 1), ("sx", 2), ("tok", 0), ("sy", 0), ("relay", 3), ("relay", 6), ("launch", 1), ("launch", 3), ("sx", 0), ("sy", 1), ("sx", 1), ("third", 0), ("sy", 2), ("sy", 3), ("launch", 6), ("relay", 7), ("third", 2), ("own", 3), ("launch", 7), ("third", 1), ("sx", 3),),
    "q0": (("relay", 4),),
    "q1": (("launch", 4),),
    "q2": (("relay", 5), ("launch", 5),),
    "r0": (("relay", 10), ("relay", 9), ("sy", 6), ("sx", 6), ("sy", 4), ("third", 3), ("sy", 5),),
    "r1": (("launch", 9), ("sx", 4), ("sx", 5), ("launch", 10),),
    "t00": (("relay", 8),),
    "t01": (("launch", 8),),
    "m": (("third", 4), ("sy", 7), ("sx", 7), ("relay", 11), ("third", 6), ("sy", 10), ("third", 5), ("sy", 9), ("sy", 8), ("sx", 8), ("sx", 10), ("launch", 11), ("cot", 0), ("sx", 9),),
    "o3": (("third", 7),),
    "g0": (("third", 8),),
    "g1": (("sy", 11), ("sx", 11), ("third", 9),),
    "g2": (("third", 10),),
    "ac": (("third", 11),),
}


def run_forward(scalars, gains, head_gains, cosines, sines, tokens, cotangent, shards):
    low, f32 = jnp.bfloat16, jnp.float32
    _, slot_len, width = tokens.shape
    rows = 2 * slot_len
    cut = [s.reshape(8, s.shape[0] // 8, s.shape[1]) for s in shards]
    area = slot_len * BLOCKS * (BLOCKS + 1) // 2
    shape = jax.ShapeDtypeStruct
    outs = [
        shape((rows, width), low),
        shape((NZ, *gains.shape), f32),
        shape((2, slot_len, width), low),
        shape((2, slot_len, width), low),
        shape((rows, width), low),
        shape((2, rows, HALF_HEADS * PER_HEAD), low),
        shape((4, slot_len, HALF_HEADS * PER_HEAD), low),
        shape((HALF_HEADS, 2 * slot_len, area), low),
        shape((rows, HEADS * HD), low),
        shape((rows, width), f32),
        shape((rows, width), low),
        shape((rows, 2 * FF), low),
    ] + [shape((NZ, *s.shape), low) for s in cut]
    hbm = pl.BlockSpec(memory_space=HBM)
    vmem = pl.BlockSpec(memory_space=pltpu.VMEM)
    dma = pltpu.SemaphoreType.DMA
    out = pl.pallas_call(
        forward_kernel,
        out_shape=outs,
        in_specs=[pl.BlockSpec(memory_space=pltpu.SMEM)] + [vmem] * 4 + [hbm] * (2 + COUNT),
        out_specs=[hbm, vmem] + [hbm] * (10 + COUNT),
        scratch_shapes=[
            pltpu.VMEM((rows, 2 * FF), f32),
            pltpu.VMEM((rows, width), f32),
            pltpu.VMEM((2, 8, cut[2].shape[1], 2 * FF), low),
            pltpu.VMEM((2, 8, cut[3].shape[1], width), low),
            pltpu.VMEM((rows, width), low),
            pltpu.VMEM((rows, width), low),
            pltpu.VMEM((rows, width), low),
            pltpu.VMEM((4, slot_len, HALF_HEADS * PER_HEAD), low),
            pltpu.VMEM((2, slot_len, HALF_HEADS * PER_HEAD), low),
            pltpu.VMEM((2, rows, HALF_HEADS * PER_HEAD), low),
        ]
        + [pltpu.VMEM((2 * slot_len, (i + 1) * slot_len), low) for i in range(BLOCKS)]
        + [
            pltpu.VMEM((4 * slot_len, PER_HEAD), low),
            pltpu.VMEM((4 * slot_len, HEADS * HD // 2), low),
            pltpu.VMEM((rows, HEADS * HD // 2), low),
            pltpu.VMEM((rows, HEADS * HD), low),
            pltpu.VMEM((rows, width), f32),
            pltpu.VMEM((rows, FF), low),
            pltpu.VMEM((2, 2, rows, 512), low),
            pltpu.VMEM((rows, width), low),
            dma((COUNT, 2)),
            dma((COUNT, 3)),
            dma((COUNT, 3)),
            dma((COUNT, 3, len(KINDS))),
            dma((COUNT, 3, len(KINDS))),
            dma((COUNT, 4)),
            dma((COUNT,)),
            dma((2, NZ)),
            dma((7,)),
            dma((5,)),
            dma((4,)),
            dma((7,)),
            dma((BLOCKS,)),
            dma((2, 2)),
        ],
        compiler_params=pltpu.CompilerParams(collective_id=0, has_side_effects=True, vmem_limit_bytes=VMEM_LIMIT),
        name="forward",
    )(scalars, gains, head_gains, cosines, sines, tokens, cotangent, *cut)
    return out[:12], out[12:]


def add_rows(dst, src, rows):
    def body(i, carry):
        at = pl.ds(pl.multiple_of(i * 16, 16), 16)
        total = dst[at, :].astype(jnp.float32) + src[at, :].astype(jnp.float32)
        dst[at, :] = total.astype(dst.dtype)
        return carry

    lax.fori_loop(0, rows // 16, body, 0)


SPREAD = ("x", "y", "yx", "xy", "c", "cx", "cy", "cd")
ROUNDS = ("x1", "y1", "y2", "x2")


class Reduce:
    def __init__(self, me, shapes, refs, turned, sems):
        self.me, self.shapes, self.turned = me, shapes, turned
        self.stage, self.acc, self.rx1, self.ry1, self.rx2, self.ry2, self.rz, self.outs = refs
        (
            self.keep_sem,
            self.c_send,
            self.c_recv,
            self.r_send,
            self.r_recv,
            self.z_send,
            self.z_recv,
            self.o_send,
            self.o_recv,
        ) = sems
        self.stage_t = (3, 2, 1 - me.m, me.m)
        self.chunks = [(w, k) for w in range(len(shapes)) for k in range(4)]

    def zk(self, k):
        return self.me.at(self.stage_t[k])

    def product(self, n, rhs, columns, store):
        w, k = self.chunks[n]
        rows = self.shapes[w][0]
        half = self.shapes[w][1] // 2
        tile = min(half, 512)

        steps = half // tile
        parts = 2 if rows > 256 else 1
        high = rows // parts

        def body(i, carry):
            at = pl.multiple_of(lax.rem(i, steps) * tile, tile)
            down = pl.multiple_of(i // steps * high, high)
            part = jnp.dot(
                self.turned[n % 2, pl.ds(down, high)],
                rhs[:, pl.ds(pl.multiple_of(columns * half + at, tile), tile)],
                preferred_element_type=jnp.float32,
            )
            store(part.reshape(2 // parts, 2, rows // 4, tile), pl.ds(i // steps, 2 // parts), pl.ds(at, tile))
            return carry

        lax.fori_loop(0, parts * steps, body, 0)

    def to_partner(self, n):
        w, k = self.chunks[n]
        return remote(
            self.stage[w], self.acc[w].at[self.zk(k)], self.c_send.at[w, k], self.c_recv.at[w, k], self.me.partner
        )

    def turn_rows(self, n, lhs):
        w, k = self.chunks[n]
        rows = self.shapes[w][0]
        at = pl.multiple_of(self.zk(k) * rows, rows)
        self.turned[n % 2, :rows] = jnp.transpose(lhs[:, pl.ds(at, rows)])

    def theirs(self, n, rhs):
        w, k = self.chunks[n]
        if k > 0:
            self.to_partner(n - 1).wait_send()

        def store(part, side, at):
            self.stage[w][side, :, :, at] = part.astype(jnp.bfloat16)

        self.product(n, rhs, 1 - self.me.c, store)

    def ours(self, n, rhs):
        w, k = self.chunks[n]
        a = self.acc[w].at[self.zk(k)]
        self.to_partner(n).wait_recv()

        def store(part, side, at):
            a[side, :, :, at] = (part + a[side, :, :, at].astype(jnp.float32)).astype(jnp.bfloat16)

        self.product(n, rhs, self.me.c, store)

    def launch(self, n):
        w, k = self.chunks[n]
        self.exchange(w, k, "x1").start()
        self.exchange(w, k, "y1").start()

    def exchange(self, w, k, kind):
        me = self.me
        x, y = me.x, me.y
        a = self.acc[w].at[self.zk(k)]
        half = a.shape[-1] // 2
        lo, hi = pl.ds(0, half), pl.ds(half, half)
        src, dst, peer = {
            "x1": lambda: (a.at[1 - x, :, :, lo], self.rx1[w].at[k], me.across_x),
            "y1": lambda: (a.at[:, 1 - y, :, hi], self.ry1[w].at[k], me.across_y),
            "y2": lambda: (a.at[x, 1 - y, :, lo], self.ry2[w].at[k], me.across_y),
            "x2": lambda: (a.at[1 - x, y, :, hi], self.rx2[w].at[k], me.across_x),
        }[kind]()
        index = ROUNDS.index(kind)
        return remote(src, dst, self.r_send.at[w, k, index], self.r_recv.at[w, k, index], peer)

    def along(self, w, k, slot, peer):
        me = self.me
        return remote(
            self.acc[w].at[self.zk(k), me.x, me.y], self.rz[w].at[slot], self.z_send.at[w, k], self.z_recv.at[w, slot], peer
        )

    def s1(self, n):
        w, k = self.chunks[n]
        me = self.me
        a = self.acc[w].at[self.zk(k)]
        rows, half = a.shape[2], a.shape[3] // 2
        self.exchange(w, k, "x1").wait_recv()
        for j in range(2):
            add_rows(a.at[me.x, j, :, pl.ds(0, half)], self.rx1[w].at[k, j], rows)
        self.exchange(w, k, "y1").wait_recv()
        for i in range(2):
            add_rows(a.at[i, me.y, :, pl.ds(half, half)], self.ry1[w].at[k, i], rows)
        self.exchange(w, k, "y2").start()
        self.exchange(w, k, "x2").start()

    def s2(self, n):
        w, k = self.chunks[n]
        a = self.acc[w].at[self.zk(k), self.me.x, self.me.y]
        rows, half = a.shape[0], a.shape[1] // 2
        self.exchange(w, k, "y2").wait_recv()
        add_rows(a.at[:, pl.ds(0, half)], self.ry2[w].at[k], rows)
        self.exchange(w, k, "x2").wait_recv()
        add_rows(a.at[:, pl.ds(half, half)], self.rx2[w].at[k], rows)

    def s3(self, n):
        w, k = self.chunks[n]
        me = self.me
        a = self.acc[w].at[self.zk(k), me.x, me.y]
        rows = a.shape[0]

        def take(slot):
            there = self.rz[w].at[slot]
            remote(there, there, self.z_send.at[w, 0], self.z_recv.at[w, slot], me.partner).wait_recv()
            add_rows(a, there, rows)

        @pl.when(me.m == 0)
        def _():
            if k < 3:
                self.along(w, k, k, me.inner).start()
            else:
                take(0)

        @pl.when(me.m == 1)
        def _():
            if k == 0:
                take(0)
                self.along(w, k, 3, me.inner).start()
            elif k == 1:
                take(1)
                self.along(w, k, 4, me.inner).start()
            elif k == 2:
                take(3)
                self.along(w, k, 0, me.outer).start()
            else:
                take(2)
                take(4)

    def out_at(self, w, cc, xx, yy):
        half = self.shapes[w][1] // 2
        return self.outs[w].at[xx, yy, :, pl.ds(pl.multiple_of(cc * half, half), half)]

    def keep(self, w):
        me = self.me
        return pltpu.make_async_copy(
            self.acc[w].at[me.z, me.x, me.y], self.out_at(w, me.c, me.x, me.y), self.keep_sem.at[w]
        )

    def spread(self, w, kind):
        me = self.me
        c, x, y = me.c, me.x, me.y
        final, mine = self.acc[w].at[me.z, x, y], self.out_at(w, c, x, y)
        px, py = self.out_at(w, c, 1 - x, y), self.out_at(w, c, x, 1 - y)
        pd = self.out_at(w, c, 1 - x, 1 - y)
        src, dst, peer = {
            "x": (final, mine, me.across_x),
            "y": (final, mine, me.across_y),
            "c": (final, mine, me.partner),
            "yx": (half_rows(px, 0), half_rows(px, 0), me.across_y),
            "xy": (half_rows(py, 1), half_rows(py, 1), me.across_x),
            "cx": (px, px, me.partner),
            "cy": (py, py, me.partner),
            "cd": (pd, pd, me.partner),
        }[kind]
        index = SPREAD.index(kind)
        return remote(src, dst, self.o_send.at[w, index], self.o_recv.at[w, index], peer)

    def spread_arrived(self, w, kind):
        me = self.me
        c, x, y = me.c, me.x, me.y
        dst = {
            "x": lambda: self.out_at(w, c, 1 - x, y),
            "y": lambda: self.out_at(w, c, x, 1 - y),
            "yx": lambda: half_rows(self.out_at(w, c, 1 - x, 1 - y), 0),
            "xy": lambda: half_rows(self.out_at(w, c, 1 - x, 1 - y), 1),
            "c": lambda: self.out_at(w, 1 - c, x, y),
            "cx": lambda: self.out_at(w, 1 - c, 1 - x, y),
            "cy": lambda: self.out_at(w, 1 - c, x, 1 - y),
            "cd": lambda: self.out_at(w, 1 - c, 1 - x, 1 - y),
        }[kind]()
        index = SPREAD.index(kind)
        remote(dst, dst, self.o_send.at[w, index], self.o_recv.at[w, index], me.partner).wait_recv()

    def s4(self, w):
        self.keep(w).start()
        for kind in ("x", "y", "c"):
            self.spread(w, kind).start()

    def s5(self, w):
        self.spread_arrived(w, "x")
        self.spread(w, "yx").start()
        self.spread(w, "cx").start()
        self.spread_arrived(w, "y")
        self.spread(w, "xy").start()
        self.spread(w, "cy").start()

    def s6(self, w):
        self.spread_arrived(w, "yx")
        self.spread_arrived(w, "xy")
        self.spread(w, "cd").start()

    def finish(self):
        for n, (w, k) in enumerate(self.chunks):
            if k == 3:
                self.to_partner(n).wait_send()
            for kind in ROUNDS:
                self.exchange(w, k, kind).wait_send()
            if k < 3:
                self.along(w, k, k, self.me.inner).wait_send()
        for w in range(len(self.shapes)):
            self.keep(w).wait()
            for kind in SPREAD:
                self.spread(w, kind).wait_send()
            for kind in ("c", "cx", "cy", "cd"):
                self.spread_arrived(w, kind)


class Small:
    def __init__(self, me, mid, got, along, send, recv):
        self.me, self.mid, self.got, self.along_z, self.send, self.recv = me, mid, got, along, send, recv
        self.peers = (me.partner, me.across_x, me.across_y)

    def copy(self, step):
        return remote(self.mid.at[step], self.got.at[step], self.send.at[step], self.recv.at[step], self.peers[step])

    def along(self, j):
        there = {"z": lax.rem(self.me.z + 1 + j, NZ)}
        return remote(self.mid.at[3], self.along_z.at[self.me.z], self.send.at[3 + j], self.recv.at[3 + j], there)

    def step(self, n):
        if n < 6:
            step = n // 2
            if n % 2 == 0:
                self.copy(step).start()
            else:
                self.copy(step).wait()
                self.mid[step + 1] = self.mid[step] + self.got[step]
        elif n == 6:
            for j in range(3):
                self.along(j).start()
        else:
            for j in range(3):
                self.along(j).wait_send()
                there = self.along_z.at[lax.rem(self.me.z + 3 - j, NZ)]
                remote(there, there, self.send.at[3 + j], self.recv.at[3 + j], self.me.partner).wait_recv()
            self.along_z[pl.ds(self.me.z, 1)] = self.mid[pl.ds(3, 1)]

    def total(self):
        return (self.along_z[0] + self.along_z[1]) + (self.along_z[2] + self.along_z[3])


def backward_kernel(shapes, scalars, gains, head_gains, cosines, sines, *refs):
    (
        source,
        grad,
        h1_in,
        raw_in,
        tok_in,
        probs_in,
        attended_in,
        middle_in,
        h2_in,
        gate_up_in,
        block_rows_in,
        full_qkv,
        full_out,
        full_gate_up,
        full_down,
    ) = refs[:15]
    small_out, input_out, block_out = refs[15:18]
    outs = refs[18:22]
    rest = refs[22:]
    stage, acc, rz = rest[:4], rest[4:8], rest[8:12]
    rx1, ry1, rx2, ry2 = rest[12:14], rest[14:16], rest[16:18], rest[18:20]
    turned, wide, grad_mid, grads, outgoing, returned, small_mid, small_got, small_z, gain_sums, sums, input_low = rest[20:32]
    comm_sems = rest[32:41]
    (
        s_send,
        s_recv,
        load_sem,
        wide_sem,
        narrow_sem,
        gate_sem,
        prob_sem,
        tok_sem,
        raw_sem,
        swap_sem,
        out_sem,
        in_sem,
    ) = rest[41:]

    def like(refs, w):
        r, n = shapes[w]
        ref = refs[w % 2]
        if w < 2:
            return ref
        lead = (slice(None),) * (len(ref.shape) - 2)
        return ref.at[(*lead, pl.ds(0, r // 4), pl.ds(0, n // 4))]

    landing = [[like(group, w) for w in range(4)] for group in (rx1, ry1, rx2, ry2)]
    low, f32 = jnp.bfloat16, jnp.float32
    me = Place()
    z, c = me.z, me.c
    rows, width = grad_mid.shape
    block = rows // 2
    share = width // NZ
    comm = Reduce(me, shapes, (stage, acc, *landing, rz, outs), turned, comm_sems)
    small = Small(me, small_mid, small_got, small_z, s_send, s_recv)

    def at_slot(slot):
        for name, index in BACK_PLAN.get(slot, ()):
            if name == "small":
                small.step(index)
            elif name == "inback":
                route.start(input_back)
            else:
                getattr(comm, name)(index)

    route = Route(me)
    me.greet()
    block_back = route.back(block_rows_in, block_out, out_sem)
    input_back = route.back(input_low, input_out, in_sem)
    route.start(block_back)
    sums[...] = jnp.zeros_like(sums)
    gain_sums[...] = jnp.zeros_like(gain_sums)
    contract = (((1,), (1,)), ((), ()))
    depth = FF // NZ

    wide_loads = [(full_gate_up, k, t) for k in range(4) for t in range(3)]
    wide_loads += [(full_qkv, k, t) for k in range(4) for t in range(2)]
    wide_tile = wide.shape[3]

    def wide_load(j):
        full, k, t = wide_loads[j]
        src = full.at[comm.zk(k), :, :, pl.ds(t * wide_tile, wide_tile)]
        return pltpu.make_async_copy(src, wide.at[j % 2], wide_sem.at[j % 2])

    def against(j, count, left, target):
        full, k, _ = wide_loads[j]
        at = pl.ds(pl.multiple_of(comm.zk(k) * share, share), share)
        deep = wide_tile // 2

        def tile_load(t, slot):
            here = pl.ds(pl.multiple_of(t * wide_tile, wide_tile), wide_tile)
            return pltpu.make_async_copy(full.at[comm.zk(k), :, :, here], wide.at[slot], wide_sem.at[slot])

        def body(t, carry):
            slot = lax.rem(j + t, 2)
            tile_load(t, slot).wait()

            @pl.when(t + 1 < count)
            def _():
                tile_load(t + 1, 1 - slot).start()

            if j + count < len(wide_loads):

                @pl.when(t + 1 == count)
                def _():
                    wide_load(j + count).start()

            def half_tile(i, carry):
                from_tile = pl.ds(pl.multiple_of(i * deep, deep), deep)
                from_left = pl.ds(pl.multiple_of(t * wide_tile + i * deep, deep), deep)
                right = wide[slot, :, :, from_tile].reshape(share, deep)
                part = lax.dot_general(left[:, from_left], right, contract, preferred_element_type=f32)

                @pl.when(t + i == 0)
                def _():
                    target[:, at] = part

                @pl.when(t + i > 0)
                def _():
                    target[:, at] += part

                return carry

            return lax.fori_loop(0, 2, half_tile, carry)

        lax.fori_loop(0, count, body, 0)

    def gain_row(index):
        return jnp.concatenate([gains[s, index : index + 1, :] for s in range(NZ)], axis=1)

    def norm_parts(v):
        inverse = lax.rsqrt(jnp.mean(v * v, axis=-1, keepdims=True) + EPSILON)
        return v * inverse, inverse

    def norm_grad(normed, inverse, g):
        return inverse * (g - normed * jnp.mean(g * normed, axis=-1, keepdims=True))

    def load(i, src, dst):
        return pltpu.make_async_copy(src, dst, load_sem.at[i])

    def feed_forward(g, h2, grad_gate_up, narrow, gate_up, middle):
        g_loads = [load(i, grad.at[i], g.at[pl.ds(i * block, block)]) for i in range(2)]

        def narrow_load(k):
            return pltpu.make_async_copy(full_down.at[comm.zk(k)], narrow.at[k % 2], narrow_sem.at[k % 2])

        def gate_load(k, part):
            at = pl.multiple_of(part * FF + comm.zk(k) * depth, depth)
            src = gate_up_in.at[:, pl.ds(at, depth)]
            return pltpu.make_async_copy(src, gate_up.at[k % 2, part], gate_sem.at[k % 2, part])

        def fetch(k):
            narrow_load(k).start()
            for part in range(2):
                gate_load(k, part).start()

        for copy in g_loads:
            copy.start()
        fetch(0)
        fetch(1)
        load(2, h2_in, h2).start()
        load(3, middle_in, middle).start()
        wide_load(0).start()
        for copy in g_loads:
            copy.wait()
        tile = depth // 2

        def hidden_part(k):
            narrow_load(k).wait()
            for part in range(2):
                gate_load(k, part).wait()

            def body(step, carry):
                at = pl.multiple_of(step // 2 * tile, tile)
                here = pl.ds(pl.multiple_of(lax.rem(step, 2) * block, block), block)
                right = narrow[k % 2, pl.ds(step // 2 * 4, 4)].reshape(tile, width)
                grad_hidden = lax.dot_general(g[here, :], right, contract, preferred_element_type=f32)
                gate = gate_up[k % 2, 0, here, pl.ds(at, tile)].astype(f32)
                up = gate_up[k % 2, 1, here, pl.ds(at, tile)].astype(f32)
                sigmoid = jax.nn.sigmoid(gate)
                silu = gate * sigmoid
                turned[k % 2, pl.ds(at, tile), here] = jnp.transpose((silu * up).astype(low))
                there = pl.multiple_of(comm.zk(k) * depth + at, 128)
                grad_gate = grad_hidden * up * (sigmoid * (1.0 + gate * (1.0 - sigmoid)))
                grad_gate_up[here, pl.ds(there, tile)] = grad_gate.astype(low)
                grad_gate_up[here, pl.ds(pl.multiple_of(FF + there, 128), tile)] = (grad_hidden * silu).astype(low)
                return carry

            lax.fori_loop(0, 4, body, 0)
            if k + 2 < 4:
                fetch(k + 2)

        for n in range(4):
            hidden_part(n)
            comm.theirs(n, g)
            if n > 0:
                comm.ours(n - 1, g)
            comm.to_partner(n).start()
            at_slot(f"h{n}")
        load(2, h2_in, h2).wait()
        for n in range(4, 8):
            comm.turn_rows(n, h2)
            comm.theirs(n, grad_gate_up)
            comm.ours(n - 1, g if n == 4 else grad_gate_up)
            comm.to_partner(n).start()
            at_slot(f"g{n}")
            against((n - 4) * 3, 3, grad_gate_up, grad_mid)
            at_slot(f"a{n}")
        comm.ours(7, grad_gate_up)
        at_slot("g8")
        load(3, middle_in, middle).wait()

        def second_norm(at):
            normed, inverse = norm_parts(middle[at, :])
            grad_h2 = grad_mid[at, :]
            gain_sums[1:2, :] += jnp.sum(normed * grad_h2, axis=0, keepdims=True)
            grad_mid[at, :] = g[at, :].astype(f32) + norm_grad(normed, inverse, grad_h2 * gain_row(1))

        row_loop(rows, 64, second_norm)
        at_slot("n2")

    pl.run_scoped(
        feed_forward,
        pltpu.VMEM((rows, width), low),
        pltpu.VMEM((rows, width), low),
        pltpu.VMEM((rows, 2 * FF), low),
        pltpu.VMEM((2, *full_down.shape[1:]), low),
        pltpu.VMEM((2, 2, rows, depth), low),
        pltpu.VMEM((rows, width), f32),
    )

    half = HEADS * HD // 2

    def out_projection(attended, narrow, grad_low):
        def narrow_load(j):
            ours = j // 2
            where = 2 * ((1 - c) * (1 - ours) + c * ours) + j % 2
            return pltpu.make_async_copy(full_out.at[where], narrow.at[j % 2], narrow_sem.at[j % 2])

        narrow_load(0).start()
        narrow_load(1).start()
        load(0, attended_in, attended).start()

        def lower(at):
            grad_low[at, :] = grad_mid[at, :].astype(low)

        row_loop(rows, 64, lower)
        columns = half // 2
        swap = remote(outgoing, grads.at[pl.ds(2, 2)], swap_sem.at[0], swap_sem.at[1], me.partner)

        def project(j, carry):
            narrow_load(j).wait()
            right = narrow[j % 2].reshape(columns, width)
            part = lax.dot_general(grad_low[...], right, contract, preferred_element_type=f32).astype(low)
            there = pl.ds(pl.multiple_of(j % 2 * columns, columns), columns)

            @pl.when(j < 2)
            def _():
                for i in range(2):
                    outgoing[i, :, there] = part[i * block : (i + 1) * block]
                narrow_load(j + 2).start()

            @pl.when(j >= 2)
            def _():
                for i in range(2):
                    grads[i, :, there] = part[i * block : (i + 1) * block]

            @pl.when(j == 2)
            def _():
                swap.start()

            return carry

        lax.fori_loop(0, 4, project, 0)
        load(0, attended_in, attended).wait()
        at_slot("op")
        for n in range(8, 12):
            comm.turn_rows(n, attended)
            comm.theirs(n, grad_low)
            if n > 8:
                comm.ours(n - 1, grad_low)
            comm.to_partner(n).start()
            at_slot(f"o{n}")
        comm.ours(11, grad_low)
        swap.wait()
        at_slot("o12")

    pl.run_scoped(
        out_projection,
        pltpu.VMEM((rows, HEADS * HD), low),
        pltpu.VMEM((2, *full_out.shape[1:]), low),
        pltpu.VMEM((rows, width), low),
    )

    def sequence_part(own, leaving):
        swap = remote(leaving, returned, swap_sem.at[2], swap_sem.at[3], me.partner)

        def attention(tok, ordered, grad_ordered, p0, p1, p2, p3, grad_k, grad_v, placed):
            slots = (p0, p1, p2, p3)
            scale = 1.0 / math.sqrt(HD)

            def prob_load(h, i):
                n = (i + 1) * block
                src = probs_in.at[h, :, pl.ds(i * (i + 1) // 2 * block, n)]
                return pltpu.make_async_copy(src, slots[i], prob_sem.at[i])

            def tok_load(h, slot):
                at = pl.multiple_of(h * PER_HEAD, PER_HEAD)
                return pltpu.make_async_copy(tok_in.at[:, :, pl.ds(at, PER_HEAD)], tok.at[slot], tok_sem.at[slot])

            tok_load(0, 0).start()
            for i in reversed(range(BLOCKS)):
                prob_load(0, i).start()

            def one_head(h, carry):
                slot = lax.rem(h, 2)
                tok_load(h, slot).wait()

                @pl.when(h + 1 < HALF_HEADS)
                def _():
                    tok_load(h + 1, 1 - slot).start()

                at = pl.multiple_of(h * 2 * HD, 2 * HD)
                for i in range(BLOCKS):
                    here = slice(i * block, (i + 1) * block)
                    ordered[here] = pick(scalars[i], [tok[slot, j] for j in range(BLOCKS)])
                    grad_ordered[here] = pick(scalars[i], [grads[j, :, pl.ds(at, 2 * HD)] for j in range(BLOCKS)])
                for i in reversed(range(BLOCKS)):
                    n = (i + 1) * block
                    here = slice(i * block, n)
                    prob_load(h, i).wait()
                    query = stacked(ordered[here, : 2 * HD])
                    g = stacked(grad_ordered[here, :])
                    keys, values = ordered[:n, 2 * HD : 3 * HD], ordered[:n, 3 * HD :]
                    probs = slots[i][...]
                    weights = probs.astype(f32)
                    grad_probs = lax.dot_general(g, values, contract, preferred_element_type=f32)
                    delta = jnp.sum(weights * grad_probs, axis=-1, keepdims=True)
                    grad_scores = (weights * (grad_probs - delta)).astype(low)
                    grad_q = (jnp.dot(grad_scores, keys, preferred_element_type=f32) * scale).astype(low)
                    placed[here, :HD] = grad_q[:block]
                    placed[here, HD : 2 * HD] = grad_q[block:]
                    across = (((0,), (0,)), ((), ()))
                    part_k = lax.dot_general(query, grad_scores, across, preferred_element_type=f32)
                    part_v = lax.dot_general(g, probs, across, preferred_element_type=f32)
                    if i == BLOCKS - 1:
                        grad_k[...] = part_k
                        grad_v[...] = part_v
                    else:
                        grad_k[:, :n] += part_k
                        grad_v[:, :n] += part_v

                    @pl.when(h + 1 < HALF_HEADS)
                    def _():
                        prob_load(h + 1, i).start()

                    if i > 0:
                        for now in range(HALF_HEADS):
                            slot_name = f"t{now}{BLOCKS - 1 - i}"
                            if slot_name in BACK_PLAN:

                                @pl.when(h == now)
                                def _(slot_name=slot_name):
                                    at_slot(slot_name)

                for i in range(BLOCKS):
                    here = slice(i * block, (i + 1) * block)
                    placed[here, 2 * HD : 3 * HD] = jnp.transpose(grad_k[:, here] * scale).astype(low)
                    placed[here, 3 * HD :] = jnp.transpose(grad_v[:, here]).astype(low)
                columns = pl.ds(pl.multiple_of(h * PER_HEAD, PER_HEAD), PER_HEAD)
                for j in range(BLOCKS):
                    value = pick(scalars[BLOCKS + j], [placed[i * block : (i + 1) * block] for i in range(BLOCKS)])
                    target = own if j < 2 else leaving
                    target[j % 2 * block : (j % 2 + 1) * block, columns] = value
                for now in range(HALF_HEADS):
                    slot_name = f"t{now}{BLOCKS - 1}"
                    if slot_name in BACK_PLAN:

                        @pl.when(h == now)
                        def _(slot_name=slot_name):
                            at_slot(slot_name)

                return carry

            lax.fori_loop(0, HALF_HEADS, one_head, 0)
            swap.start()
            at_slot("sw")

        pl.run_scoped(
            attention,
            pltpu.VMEM((2, 4, block, PER_HEAD), low),
            pltpu.VMEM((4 * block, PER_HEAD), low),
            pltpu.VMEM((4 * block, 2 * HD), low),
            *[pltpu.VMEM((2 * block, (i + 1) * block), low) for i in range(BLOCKS)],
            pltpu.VMEM((HD, 4 * block), f32),
            pltpu.VMEM((HD, 4 * block), f32),
            pltpu.VMEM((4 * block, PER_HEAD), low),
        )

        def projection(grad_qkv, raw, h1, x, grad_first):
            load(0, h1_in, h1).start()
            for i in range(2):
                load(2 + i, source.at[i], x.at[pl.ds(i * block, block)]).start()

            def raw_load(j, slot):
                which = c + j // HALF_HEADS * (1 - 2 * c)
                at = pl.multiple_of(lax.rem(j, HALF_HEADS) * PER_HEAD, PER_HEAD)
                return pltpu.make_async_copy(raw_in.at[which, :, pl.ds(at, PER_HEAD)], raw.at[slot], raw_sem.at[slot])

            raw_load(0, 0).start()

            def one_head(j, came):
                slot = lax.rem(j, 2)
                raw_load(j, slot).wait()

                @pl.when(j + 1 < KV_HEADS)
                def _():
                    raw_load(j + 1, 1 - slot).start()

                at = pl.multiple_of(lax.rem(j, HALF_HEADS) * PER_HEAD, PER_HEAD)
                h = lax.rem(j, HALF_HEADS) + HALF_HEADS * (c + j // HALF_HEADS * (1 - 2 * c))
                places = (h * 2 * HD, (h * 2 + 1) * HD, (HEADS + h) * HD)
                for i, (row, place) in enumerate(zip((0, 0, 1), places)):
                    normed, inverse = norm_parts(raw[slot, :, i * HD : (i + 1) * HD].astype(f32))
                    g = came[:, pl.ds(pl.multiple_of(at + i * HD, HD), HD)].astype(f32)
                    g = g * cosines[...] - turn(g) * sines[...]
                    sums[row : row + 1, :] += jnp.sum(normed * g, axis=0, keepdims=True)
                    back = norm_grad(normed, inverse, g * head_gains[row : row + 1, :])
                    grad_qkv[:, pl.ds(pl.multiple_of(place, HD), HD)] = back.astype(low)
                there = pl.multiple_of((HEADS + KV_HEADS + h) * HD, HD)
                grad_qkv[:, pl.ds(there, HD)] = came[:, pl.ds(pl.multiple_of(at + 3 * HD, HD), HD)]

            def own_head(i, carry):
                one_head(i, own)
                return carry

            def other_head(i, carry):
                one_head(i + HALF_HEADS, returned)
                return carry

            lax.fori_loop(0, HALF_HEADS, own_head, 0)
            at_slot("b0")
            swap.wait()
            lax.fori_loop(0, HALF_HEADS, other_head, 0)
            load(0, h1_in, h1).wait()
            at_slot("b1")
            for n in range(12, 16):
                comm.turn_rows(n, h1)
                comm.theirs(n, grad_qkv)
                if n > 12:
                    comm.ours(n - 1, grad_qkv)
                comm.to_partner(n).start()
                at_slot(f"q{n}")
            comm.ours(15, grad_qkv)
            at_slot("q16")
            for k in range(4):
                against(12 + k * 2, 2, grad_qkv, grad_first)
                at_slot(f"f{k}")
            for i in range(2):
                load(2 + i, source.at[i], x.at[pl.ds(i * block, block)]).wait()
            for i in range(2):

                def first_norm(at, i=i):
                    here = pl.ds(pl.multiple_of(i * block + at.start, 64), 64)
                    normed, inverse = norm_parts(x[here, :].astype(f32))
                    g = grad_first[here, :]
                    gain_sums[0:1, :] += jnp.sum(normed * g, axis=0, keepdims=True)
                    total = grad_mid[here, :] + norm_grad(normed, inverse, g * gain_row(0))
                    input_low[i, at, :] = total.astype(low)

                row_loop(block, 64, first_norm)

        pl.run_scoped(
            projection,
            pltpu.VMEM((rows, (HEADS + 2 * KV_HEADS) * HD), low),
            pltpu.VMEM((2, rows, PER_HEAD), low),
            pltpu.VMEM((rows, width), low),
            pltpu.VMEM((rows, width), low),
            pltpu.VMEM((rows, width), f32),
        )

    pl.run_scoped(
        sequence_part,
        pltpu.VMEM((rows, HALF_HEADS * PER_HEAD), low),
        pltpu.VMEM((rows, HALF_HEADS * PER_HEAD), low),
    )

    small_mid[0] = jnp.zeros(small_mid.shape[1:], f32)
    for row in range(2):
        for i in range(width // HD):
            small_mid[0, row * 8 + i : row * 8 + i + 1, :] = gain_sums[row : row + 1, i * HD : (i + 1) * HD]
    small_mid[0, 16:24, :] = sums[...]
    at_slot("n1")
    small_out[...] = small.total()
    comm.finish()
    route.wait(block_back)
    route.wait(input_back)


BACK_PLAN = {
    "h1": (("launch", 0),),
    "h2": (("launch", 1),),
    "h3": (("launch", 2), ("s1", 1),),
    "g4": (("launch", 3),),
    "g5": (("launch", 4), ("s2", 1), ("s1", 2),),
    "g6": (("launch", 5), ("s1", 0),),
    "a7": (("launch", 6), ("s1", 4),),
    "o8": (("s1", 3), ("s2", 2),),
    "o9": (("s2", 0),),
    "o10": (("s3", 0), ("s1", 5), ("launch", 9),),
    "o11": (("s1", 6), ("s2", 3), ("s2", 4),),
    "t03": (("s3", 2), ("launch", 10),),
    "t11": (("launch", 8), ("s3", 1),),
    "t12": (("launch", 7), ("launch", 11),),
    "t22": (("s1", 10), ("s1", 9),),
    "t31": (("s1", 8),),
    "sw": (("s3", 3),),
    "b0": (("s4", 0),),
    "b1": (("s1", 11), ("s1", 7),),
    "q12": (("s3", 4), ("s5", 0),),
    "q13": (("launch", 12), ("s2", 5),),
    "q14": (("launch", 13), ("s3", 5), ("s2", 7),),
    "q15": (("s2", 6), ("s3", 6), ("s2", 8), ("s1", 12), ("s2", 9), ("s1", 13), ("launch", 14), ("s3", 9), ("s2", 11),),
    "q16": (("s3", 8), ("launch", 15),),
    "f0": (("s2", 13), ("s2", 10), ("s6", 0), ("s2", 12),),
    "f2": (("s3", 12), ("s3", 7), ("s1", 14), ("s3", 10), ("s4", 1),),
    "f3": (("s1", 15), ("s3", 13),),
    "n1": (("s2", 14), ("small", 0), ("s3", 14), ("small", 1), ("s3", 11), ("inback", 0), ("s5", 1), ("s2", 15), ("s3", 15), ("small", 2), ("s4", 3), ("small", 3), ("s4", 2), ("small", 4), ("s5", 3), ("s6", 1), ("small", 5), ("small", 6), ("s5", 2), ("s6", 3), ("small", 7), ("s6", 2),),
}


def run_backward(scalars, gains_all, head_gains, cosines, sines, saved, block_rows, fulls):
    low, f32 = jnp.bfloat16, jnp.float32
    source = saved[0]
    _, slot_len, width = source.shape
    rows = 2 * slot_len
    full_qkv, full_out, full_gate_up, full_down = fulls
    order = (full_down, full_gate_up, full_out, full_qkv)
    shapes = [(8 * f.shape[2], f.shape[3]) for f in order]
    shape = jax.ShapeDtypeStruct
    hbm = pl.BlockSpec(memory_space=HBM)
    vmem = pl.BlockSpec(memory_space=pltpu.VMEM)
    dma = pltpu.SemaphoreType.DMA
    count = len(shapes)

    def buffers(make, which):
        return [pltpu.VMEM(make(r // 4, n // 2), low) for r, n in which]

    out = pl.pallas_call(
        functools.partial(backward_kernel, shapes),
        out_shape=[
            shape((24, HD), f32),
            shape(source.shape, low),
            shape(source.shape, low),
            *[shape((2, 2, r // 4, n), low) for r, n in shapes],
        ],
        in_specs=[pl.BlockSpec(memory_space=pltpu.SMEM)] + [vmem] * 4 + [hbm] * 15,
        out_specs=[vmem] + [hbm] * 6,
        scratch_shapes=buffers(lambda r, n: (2, 2, r, n), shapes)
        + buffers(lambda r, n: (NZ, 2, 2, r, n), shapes)
        + buffers(lambda r, n: (5, r, n), shapes)
        + buffers(lambda r, n: (NZ, 2, r, n // 2), shapes[:2])
        + buffers(lambda r, n: (NZ, 2, r, n // 2), shapes[:2])
        + buffers(lambda r, n: (NZ, r, n // 2), shapes[:2])
        + buffers(lambda r, n: (NZ, r, n // 2), shapes[:2])
        + [
            pltpu.VMEM((2, max(r for r, _ in shapes), rows), low),
            pltpu.VMEM((2, 8, full_gate_up.shape[2], 2 * width), low),
            pltpu.VMEM((rows, width), f32),
            pltpu.VMEM((4, slot_len, HEADS * HD // 2), low),
            pltpu.VMEM((2, slot_len, HEADS * HD // 2), low),
            pltpu.VMEM((rows, HALF_HEADS * PER_HEAD), low),
            pltpu.VMEM((4, 24, HD), f32),
            pltpu.VMEM((3, 24, HD), f32),
            pltpu.VMEM((NZ, 24, HD), f32),
            pltpu.VMEM((8, width), f32),
            pltpu.VMEM((8, HD), f32),
            pltpu.VMEM((2, slot_len, width), low),
            dma((count,)),
            dma((count, 4)),
            dma((count, 4)),
            dma((count, 4, 4)),
            dma((count, 4, 4)),
            dma((count, 4)),
            dma((count, 5)),
            dma((count, len(SPREAD))),
            dma((count, len(SPREAD))),
            dma((6,)),
            dma((6,)),
            dma((4,)),
            dma((2,)),
            dma((2,)),
            dma((2, 2)),
            dma((BLOCKS,)),
            dma((2,)),
            dma((2,)),
            dma((4,)),
            dma((5,)),
            dma((5,)),
        ],
        compiler_params=pltpu.CompilerParams(collective_id=1, has_side_effects=True, vmem_limit_bytes=VMEM_LIMIT),
        name="backward",
    )(scalars, gains_all, head_gains, cosines, sines, *saved, block_rows, *fulls)
    return out[0], out[1], out[2], [o.reshape(r, n) for o, (r, n) in zip(out[3:], shapes)]


def swap(v):
    return lax.ppermute(v, "core", [(0, 1), (1, 0)])


def per_chip(
    tokens,
    cotangent,
    slot_order,
    attn_gain,
    q_gain,
    k_gain,
    w_qkv,
    w_out,
    mlp_gain,
    w_gate_up,
    w_down,
):
    z, core = lax.axis_index("z"), lax.axis_index("core")
    _, slot_len, width = tokens.shape
    f32, low = jnp.float32, jnp.bfloat16
    odd = z % 2
    orders = jnp.where(z // 2 == core, slot_order, swap(slot_order))
    order = lax.dynamic_index_in_dim(orders, odd, 0, False)
    slots = jnp.stack([2 * core + odd, 2 * core + 1 - odd, 2 - 2 * core + odd, 3 - 2 * core - odd])
    blocks = order[slots]
    where_is = jnp.sum(
        jnp.where(blocks[None, :] == jnp.arange(4)[:, None], jnp.arange(4)[None, :], 0), axis=1
    )
    scalars = jnp.concatenate([where_is, blocks, core[None], jnp.zeros((7,), jnp.int32)]).astype(jnp.int32)
    positions = (blocks[:2, None] * slot_len + jnp.arange(slot_len)[None, :]).reshape(-1)
    cos, sin = rope_tables(positions)
    cosines = jnp.concatenate([cos, cos], axis=1)
    sines = jnp.concatenate([-sin, sin], axis=1)
    gain_q, gain_k = q_gain.astype(f32)[None, :], k_gain.astype(f32)[None, :]
    head_gains = jnp.concatenate([gain_q, gain_k, jnp.zeros((6, HD), f32)], axis=0)
    gains = jnp.concatenate(
        [attn_gain.astype(f32)[None], mlp_gain.astype(f32)[None], jnp.zeros((6, attn_gain.shape[0]), f32)], axis=0
    )
    (block_rows, gains_all, *saved), fulls = run_forward(
        scalars, gains, head_gains, cosines, sines, tokens, cotangent, [w_qkv, w_out, w_gate_up, w_down]
    )
    sums, input_grad, block_out, (down_sum, gate_up_sum, out_sum, qkv_sum) = run_backward(
        scalars, gains_all, head_gains, cosines, sines, saved, block_rows.reshape(2, slot_len, width), fulls
    )
    count = width // HD
    share = width // NZ
    return (
        block_out,
        input_grad,
        lax.dynamic_slice_in_dim(sums[:count].reshape(-1), z * share, share, 0),
        sums[2 * count],
        sums[2 * count + 1],
        qkv_sum.astype(f32),
        out_sum.astype(f32),
        lax.dynamic_slice_in_dim(sums[count : 2 * count].reshape(-1), z * share, share, 0),
        gate_up_sum.astype(f32),
        down_sum.astype(f32),
    )


def solution(mesh):
    group, replica, body = "group", "replica", per_device
    if (mesh.shape["group"], mesh.shape["replica"]) == (NZ, 8):
        mesh = Mesh(mesh.devices.reshape(NZ, 2, 2, 2), ("z", "y", "x", "core"))
        group, replica, body = "z", ("y", "x", "core"), per_chip
    in_specs = (
        P(replica, group, None),
        P(replica, group, None),
        P(replica, None),
        P(group),
        P(),
        P(),
        P(group, None),
        P(group, None),
        P(group),
        P(group, None),
        P(group, None),
    )
    out_specs = (
        P(replica, group, None),
        P(replica, group, None),
        P(group),
        P(),
        P(),
        P(group, None),
        P(group, None),
        P(group),
        P(group, None),
        P(group, None),
    )
    return jax.shard_map(
        body, mesh=mesh, in_specs=in_specs, out_specs=out_specs, check_vma=False
    )
```

```python
import functools
import math

import jax
import jax.numpy as jnp
from jax import lax
from jax.experimental import pallas as pl
from jax.experimental.pallas import tpu as pltpu
from jax.sharding import Mesh
from jax.sharding import PartitionSpec as P

HEADS = 16
KV_HEADS = 8
HD = 128
FF = 3072


EPSILON = 1e-06
THETA_BASE = 1000000.0
MASKED = -1e30


def norm_rows(v):
    return v * lax.rsqrt(jnp.mean(v * v, axis=-1, keepdims=True) + EPSILON)


def norm_back(source, grad):
    inverse = lax.rsqrt(jnp.mean(source * source, axis=-1, keepdims=True) + EPSILON)
    normed = source * inverse
    return inverse * (grad - normed * jnp.mean(grad * normed, axis=-1, keepdims=True))


def rotate(v, cosines, sines):
    half_size = v.shape[-1] // 2
    leading = v[..., :half_size]
    trailing = v[..., half_size:]
    return jnp.concatenate(
        [leading * cosines - trailing * sines, trailing * cosines + leading * sines], axis=-1
    )


def rope_tables(positions):
    half_size = HD // 2
    counter = jnp.arange(half_size).astype(jnp.float32)
    frequency = THETA_BASE ** (-2.0 * counter / HD)
    angles = positions.astype(jnp.float32)[:, None] * frequency[None, :]
    return (jnp.cos(angles), jnp.sin(angles))


def matmul(a, b):
    return jnp.dot(a, b, preferred_element_type=jnp.float32)


def matmul_right(a, b):
    return lax.dot_general(a, b, (((1,), (1,)), ((), ())), preferred_element_type=jnp.float32)


def matmul_left(a, b):
    return lax.dot_general(a, b, (((0,), (0,)), ((), ())), preferred_element_type=jnp.float32)


def per_device(
    tokens,
    cotangent,
    slot_order,
    attn_gain,
    q_gain,
    k_gain,
    w_qkv,
    w_out,
    mlp_gain,
    w_gate_up,
    w_down,
):
    member_count = lax.axis_size("group")
    member = lax.axis_index("group")
    micro, slot_len, width = tokens.shape
    rows = micro * slot_len
    length = slot_len * member_count
    q_width = HEADS * HD
    kv_width = KV_HEADS * HD
    groups = HEADS // KV_HEADS
    score_scale = 1.0 / math.sqrt(HD)
    key_block = math.gcd(length, 512)
    block_count = length // key_block
    head_gain_q = q_gain.astype(jnp.float32)
    head_gain_k = k_gain.astype(jnp.float32)
    offsets = jnp.arange(slot_len, dtype=jnp.int32)
    source = tokens.reshape(rows, width).astype(jnp.float32)
    all_pos = (slot_order[:, :, None] * slot_len + offsets[None, None, :]).reshape(micro, length)
    my_pos = lax.dynamic_slice_in_dim(all_pos, member * slot_len, slot_len, 1)
    query_top = jnp.max(my_pos, axis=1)
    cosines, sines = rope_tables(my_pos.reshape(rows))
    normed_first = norm_rows(source)
    gain_piece = lax.all_gather(attn_gain, "group", axis=0, tiled=True)
    weight_piece = lax.all_gather(w_qkv, "group", axis=0, tiled=True)
    columns = normed_first
    low_cols = (columns * gain_piece.astype(jnp.float32)).astype(jnp.bfloat16)
    qkv = matmul(low_cols, weight_piece)
    first_low = low_cols
    gain_first = gain_piece.astype(jnp.float32)
    queries = qkv[:, :q_width].reshape(rows, HEADS, HD)
    keys_raw = qkv[:, q_width : q_width + kv_width].reshape(rows, KV_HEADS, HD)
    values_low = qkv[:, q_width + kv_width :].astype(jnp.bfloat16)
    queries_normed = norm_rows(queries)
    keys_normed = norm_rows(keys_raw)
    query_rot = rotate(queries_normed * head_gain_q, cosines[:, None, :], sines[:, None, :]).astype(
        jnp.bfloat16
    )
    key_rot = rotate(keys_normed * head_gain_k, cosines[:, None, :], sines[:, None, :]).astype(
        jnp.bfloat16
    )
    key_all, value_all = (
        lax.all_gather(key_rot.reshape(micro, slot_len, kv_width), "group", axis=1, tiled=True),
        lax.all_gather(values_low.reshape(micro, slot_len, kv_width), "group", axis=1, tiled=True),
    )
    query_heads = query_rot.reshape(micro, slot_len, KV_HEADS, groups, HD)

    def block_live(block_index):
        key_pos = lax.dynamic_slice_in_dim(all_pos, block_index * key_block, key_block, 1)
        return jnp.any(jnp.min(key_pos, axis=1) <= query_top)

    def block_scores(block_index):
        begin = block_index * key_block
        key_piece = lax.dynamic_slice_in_dim(key_all, begin, key_block, 1).reshape(
            micro, key_block, KV_HEADS, HD
        )
        key_pos = lax.dynamic_slice_in_dim(all_pos, begin, key_block, 1)
        raw = (
            jnp.einsum(
                "mqkgd,mskd->mkgqs", query_heads, key_piece, preferred_element_type=jnp.float32
            )
            * score_scale
        )
        allowed = (key_pos[:, None, :] <= my_pos[:, :, None])[:, None, None]
        return (jnp.where(allowed, raw, MASKED), allowed, key_piece)

    def stats_step(block_index, carry):

        def stats_visit_block(carry_in):
            top_in, total_in = carry_in
            scores, allowed, key_piece = block_scores(block_index)
            new_top = jnp.maximum(top_in, jnp.max(scores, axis=-1))
            summed = jnp.sum(jnp.where(allowed, jnp.exp(scores - new_top[..., None]), 0.0), axis=-1)
            return (new_top, total_in * jnp.exp(top_in - new_top) + summed)

        return lax.cond(
            block_live(block_index), stats_visit_block, lambda carry_in: carry_in, carry
        )

    stat_shape = (micro, KV_HEADS, groups, slot_len)
    top_final, total_final = lax.fori_loop(
        0,
        block_count,
        stats_step,
        (jnp.full(stat_shape, MASKED, jnp.float32), jnp.zeros(stat_shape, jnp.float32)),
    )
    log_total = top_final + jnp.log(total_final)

    def output_step(block_index, accum):

        def output_visit_block(accum_in):
            scores, allowed, key_piece = block_scores(block_index)
            probabilities = jnp.where(allowed, jnp.exp(scores - log_total[..., None]), 0.0)
            value_piece = lax.dynamic_slice_in_dim(
                value_all, block_index * key_block, key_block, 1
            ).reshape(micro, key_block, KV_HEADS, HD)
            return accum_in + jnp.einsum(
                "mkgqs,mskd->mqkgd",
                probabilities.astype(jnp.bfloat16),
                value_piece,
                preferred_element_type=jnp.float32,
            )

        return lax.cond(
            block_live(block_index), output_visit_block, lambda accum_in: accum_in, accum
        )

    attn_heads = lax.fori_loop(
        0, block_count, output_step, jnp.zeros((micro, slot_len, KV_HEADS, groups, HD), jnp.float32)
    )
    attended = attn_heads.reshape(rows, q_width).astype(jnp.bfloat16)
    columns = attended
    branch = matmul(columns, lax.all_gather(w_out, "group", axis=0, tiled=True))
    middle = source + branch
    normed_second = norm_rows(middle)
    gain_piece = lax.all_gather(mlp_gain, "group", axis=0, tiled=True)
    weight_piece = lax.all_gather(w_gate_up, "group", axis=0, tiled=True)
    columns = normed_second
    low_cols = (columns * gain_piece.astype(jnp.float32)).astype(jnp.bfloat16)
    gate_up = matmul(low_cols, weight_piece)
    gain_second = gain_piece.astype(jnp.float32)
    gate_part = gate_up[:, :FF]
    up_part = gate_up[:, FF:]
    sigmoid_gate = jax.nn.sigmoid(gate_part)
    silu_gate = gate_part * sigmoid_gate
    hidden = (silu_gate * up_part).astype(jnp.bfloat16)
    columns = hidden
    down_out = matmul(columns, lax.all_gather(w_down, "group", axis=0, tiled=True))
    block_out = (middle + down_out).astype(jnp.bfloat16).reshape(micro, slot_len, width)
    grad_low = cotangent.reshape(rows, width)
    grad_output = grad_low.astype(jnp.float32)
    down_full = matmul_left(hidden, grad_low)
    grad_hidden = matmul_right(grad_low, lax.all_gather(w_down, "group", axis=0, tiled=True))
    grad_gate = grad_hidden * up_part * (sigmoid_gate * (1.0 + gate_part * (1.0 - sigmoid_gate)))
    grad_upper = grad_hidden * silu_gate
    grad_gate_up = jnp.concatenate([grad_gate, grad_upper], axis=1).astype(jnp.bfloat16)
    gate_up_full = matmul_left(low_cols, grad_gate_up)
    grad_second = matmul_right(grad_gate_up, lax.all_gather(w_gate_up, "group", axis=0, tiled=True))
    gain_second_full = jnp.sum(normed_second * grad_second, axis=0)
    grad_middle = grad_output + norm_back(middle, grad_second * gain_second)
    grad_mid_low = grad_middle.astype(jnp.bfloat16)
    out_full = matmul_left(attended, grad_mid_low)
    grad_attn_full = matmul_right(grad_mid_low, lax.all_gather(w_out, "group", axis=0, tiled=True))
    grad_attn = grad_attn_full.astype(jnp.bfloat16)
    grad_heads = grad_attn.reshape(micro, slot_len, KV_HEADS, groups, HD)
    delta = jnp.transpose(
        jnp.sum(grad_heads.astype(jnp.float32) * attn_heads, axis=-1), (0, 2, 3, 1)
    )

    def back_step(block_index, carry):

        def back_visit_block(carry_in):
            grad_query_in, grad_key_in, grad_value_in = carry_in
            begin = block_index * key_block
            scores, allowed, key_piece = block_scores(block_index)
            probabilities = jnp.where(allowed, jnp.exp(scores - log_total[..., None]), 0.0)
            value_piece = lax.dynamic_slice_in_dim(value_all, begin, key_block, 1).reshape(
                micro, key_block, KV_HEADS, HD
            )
            grad_probs = jnp.einsum(
                "mqkgd,mskd->mkgqs", grad_heads, value_piece, preferred_element_type=jnp.float32
            )
            grad_scores = (probabilities * (grad_probs - delta[..., None])).astype(jnp.bfloat16)
            grad_query_out = (
                grad_query_in
                + jnp.einsum(
                    "mkgqs,mskd->mqkgd", grad_scores, key_piece, preferred_element_type=jnp.float32
                )
                * score_scale
            )
            key_term = (
                jnp.einsum(
                    "mkgqs,mqkgd->mskd",
                    grad_scores,
                    query_heads,
                    preferred_element_type=jnp.float32,
                )
                * score_scale
            )
            value_term = jnp.einsum(
                "mkgqs,mqkgd->mskd",
                probabilities.astype(jnp.bfloat16),
                grad_heads,
                preferred_element_type=jnp.float32,
            )
            key_old = lax.dynamic_slice_in_dim(grad_key_in, begin, key_block, 1)
            value_old = lax.dynamic_slice_in_dim(grad_value_in, begin, key_block, 1)
            grad_key_out = lax.dynamic_update_slice_in_dim(
                grad_key_in, key_old + key_term, begin, 1
            )
            grad_value_out = lax.dynamic_update_slice_in_dim(
                grad_value_in, value_old + value_term, begin, 1
            )
            return (grad_query_out, grad_key_out, grad_value_out)

        return lax.cond(block_live(block_index), back_visit_block, lambda carry_in: carry_in, carry)

    back_start = (
        jnp.zeros((micro, slot_len, KV_HEADS, groups, HD), jnp.float32),
        jnp.zeros((micro, length, KV_HEADS, HD), jnp.float32),
        jnp.zeros((micro, length, KV_HEADS, HD), jnp.float32),
    )
    grad_query_rot, grad_key_all, grad_value_all = lax.fori_loop(
        0, block_count, back_step, back_start
    )
    grad_key_mine, grad_value_mine = (
        lax.psum_scatter(
            grad_key_all.reshape(micro, length, kv_width).astype(jnp.bfloat16),
            "group",
            scatter_dimension=1,
            tiled=True,
        ).astype(jnp.float32),
        lax.psum_scatter(
            grad_value_all.reshape(micro, length, kv_width).astype(jnp.bfloat16),
            "group",
            scatter_dimension=1,
            tiled=True,
        ).astype(jnp.float32),
    )
    grad_query_norm = rotate(
        grad_query_rot.reshape(rows, HEADS, HD), cosines[:, None, :], -sines[:, None, :]
    )
    grad_key_norm = rotate(
        grad_key_mine.reshape(rows, KV_HEADS, HD), cosines[:, None, :], -sines[:, None, :]
    )
    q_gain_total = jnp.sum(queries_normed * grad_query_norm, axis=(0, 1))
    k_gain_total = jnp.sum(keys_normed * grad_key_norm, axis=(0, 1))
    grad_queries = norm_back(queries, grad_query_norm * head_gain_q).reshape(rows, q_width)
    grad_keys = norm_back(keys_raw, grad_key_norm * head_gain_k).reshape(rows, kv_width)
    grad_qkv = jnp.concatenate(
        [grad_queries, grad_keys, grad_value_mine.reshape(rows, kv_width)], axis=1
    ).astype(jnp.bfloat16)
    qkv_full = matmul_left(first_low, grad_qkv)
    grad_first = matmul_right(grad_qkv, lax.all_gather(w_qkv, "group", axis=0, tiled=True))
    gain_first_full = jnp.sum(normed_first * grad_first, axis=0)
    input_grad = (
        (grad_middle + norm_back(source, grad_first * gain_first))
        .astype(jnp.bfloat16)
        .reshape(micro, slot_len, width)
    )
    owned = (
        lax.psum_scatter(
            gain_first_full.astype(jnp.bfloat16), "group", scatter_dimension=0, tiled=True
        ).astype(jnp.float32),
        lax.psum_scatter(
            qkv_full.astype(jnp.bfloat16), "group", scatter_dimension=0, tiled=True
        ).astype(jnp.float32),
        lax.psum_scatter(
            out_full.astype(jnp.bfloat16), "group", scatter_dimension=0, tiled=True
        ).astype(jnp.float32),
        lax.psum_scatter(
            gain_second_full.astype(jnp.bfloat16), "group", scatter_dimension=0, tiled=True
        ).astype(jnp.float32),
        lax.psum_scatter(
            gate_up_full.astype(jnp.bfloat16), "group", scatter_dimension=0, tiled=True
        ).astype(jnp.float32),
        lax.psum_scatter(
            down_full.astype(jnp.bfloat16), "group", scatter_dimension=0, tiled=True
        ).astype(jnp.float32),
    )
    summed = (
        lax.psum(owned[0].astype(jnp.bfloat16), "replica").astype(jnp.float32),
        lax.psum(owned[1].astype(jnp.bfloat16), "replica").astype(jnp.float32),
        lax.psum(owned[2].astype(jnp.bfloat16), "replica").astype(jnp.float32),
        lax.psum(owned[3].astype(jnp.bfloat16), "replica").astype(jnp.float32),
        lax.psum(owned[4].astype(jnp.bfloat16), "replica").astype(jnp.float32),
        lax.psum(owned[5].astype(jnp.bfloat16), "replica").astype(jnp.float32),
    )
    head_sums = lax.psum((q_gain_total, k_gain_total), ("group", "replica"))
    return (
        block_out,
        input_grad,
        summed[0],
        head_sums[0],
        head_sums[1],
        summed[1],
        summed[2],
        summed[3],
        summed[4],
        summed[5],
    )


MESH_ID = pl.DeviceIdType.MESH
HBM = pltpu.MemorySpace.HBM
VMEM_LIMIT = 64 * 1024 * 1024 - 65536
NZ = 4


class Place:
    def __init__(self):
        self.z = lax.axis_index("z")
        self.y = lax.axis_index("y")
        self.x = lax.axis_index("x")
        self.c = lax.axis_index("core")
        self.h = self.z // 2
        self.m = self.at(self.z)
        self.inner = {"z": self.at(self.m + 1)}
        self.outer = {"z": self.at(lax.rem(self.m + 3, 4))}
        self.across_x = {"x": 1 - self.x}
        self.across_y = {"y": 1 - self.y}
        self.partner = {"core": 1 - self.c}

    def at(self, t):
        return t * (1 - 2 * self.h) + 3 * self.h

    def greet(self):
        barrier = pltpu.get_barrier_semaphore()
        peers = [self.across_x, self.across_y, self.partner]
        for hop in range(1, NZ):
            there = lax.rem(self.z + hop, NZ)
            peers += [{"z": there}, {"z": there, "core": 1 - self.c}]
        for peer in peers:
            pl.semaphore_signal(barrier, inc=1, device_id=peer, device_id_type=MESH_ID)
        pl.semaphore_wait(barrier, len(peers))


def remote(src, dst, send, recv, peer):
    return pltpu.make_async_remote_copy(
        src_ref=src, dst_ref=dst, send_sem=send, recv_sem=recv, device_id=peer, device_id_type=MESH_ID
    )


KINDS = ("x", "y", "yx", "xy", "c", "cx", "cy", "cd")


def half_rows(ref, which):
    rows = ref.shape[0] // 2
    return ref.at[pl.ds(which * rows, rows), :]


class Gather:
    def __init__(self, me, shards, fulls, sems):
        self.me, self.shards, self.fulls = me, shards, fulls
        self.z_send, self.z_recv, self.f_send, self.xy_send, self.xy_recv = sems
        self.stage_t = (1 - me.m, 2, 3)
        self.stages = [(w, k) for w in range(len(shards)) for k in range(3)]

    def piece(self, c, x, y):
        return c * 4 + x * 2 + y

    def shard_z(self, k):
        return self.me.at(self.stage_t[k])

    def own_copy(self, w, peer, k, slot):
        me = self.me
        piece = self.piece(me.c, me.x, me.y)
        return remote(
            self.shards[w].at[piece],
            self.fulls[w].at[me.z, piece],
            self.z_send.at[w, slot],
            self.z_recv.at[w, k],
            peer,
        )

    def own(self, w):
        me = self.me
        self.own_copy(w, me.inner, me.m, 0).start()

        @pl.when(me.m == 1)
        def _():
            self.own_copy(w, me.outer, 0, 1).start()

    def place(self, w, k, cc, xx, yy):
        return self.fulls[w].at[self.shard_z(k), self.piece(cc, xx, yy)]

    def forward(self, w, k):
        me = self.me
        piece = self.place(w, k, me.c, me.x, me.y)
        peer, slot = ((me.inner, 2), (me.outer, 1), (me.outer, 2))[k]
        return remote(piece, piece, self.f_send.at[w, k], self.z_recv.at[w, slot], peer)

    def hop(self, w, k, kind):
        me = self.me
        c, x, y = me.c, me.x, me.y
        mine, px = self.place(w, k, c, x, y), self.place(w, k, c, 1 - x, y)
        py, pd = self.place(w, k, c, x, 1 - y), self.place(w, k, c, 1 - x, 1 - y)
        src, peer = {
            "x": (mine, me.across_x),
            "y": (mine, me.across_y),
            "yx": (half_rows(px, 0), me.across_y),
            "xy": (half_rows(py, 1), me.across_x),
            "c": (mine, me.partner),
            "cx": (px, me.partner),
            "cy": (py, me.partner),
            "cd": (pd, me.partner),
        }[kind]
        index = KINDS.index(kind)
        return remote(src, src, self.xy_send.at[w, k, index], self.xy_recv.at[w, k, index], peer)

    def arrived(self, w, k, kind):
        me = self.me
        c, x, y = me.c, me.x, me.y
        dst = {
            "x": lambda: self.place(w, k, c, 1 - x, y),
            "y": lambda: self.place(w, k, c, x, 1 - y),
            "yx": lambda: half_rows(self.place(w, k, c, 1 - x, 1 - y), 0),
            "xy": lambda: half_rows(self.place(w, k, c, 1 - x, 1 - y), 1),
            "c": lambda: self.place(w, k, 1 - c, x, y),
            "cx": lambda: self.place(w, k, 1 - c, 1 - x, y),
            "cy": lambda: self.place(w, k, 1 - c, x, 1 - y),
            "cd": lambda: self.place(w, k, 1 - c, 1 - x, 1 - y),
        }[kind]()
        index = KINDS.index(kind)
        remote(dst, dst, self.xy_send.at[w, k, index], self.xy_recv.at[w, k, index], me.partner).wait_recv()

    def relay(self, i):
        w, k = self.stages[i]
        me = self.me
        mine = self.place(w, k, me.c, me.x, me.y)
        remote(mine, mine, self.f_send.at[w, k], self.z_recv.at[w, k], me.partner).wait_recv()

        @pl.when(me.m == 1)
        def _():
            self.forward(w, k).start()

    def launch(self, i):
        w, k = self.stages[i]
        for kind in ("x", "y", "c"):
            self.hop(w, k, kind).start()

    def sx(self, i):
        w, k = self.stages[i]
        self.arrived(w, k, "x")
        self.hop(w, k, "yx").start()
        self.hop(w, k, "cx").start()

    def sy(self, i):
        w, k = self.stages[i]
        self.arrived(w, k, "y")
        self.hop(w, k, "xy").start()
        self.hop(w, k, "cy").start()

    def third(self, i):
        w, k = self.stages[i]
        self.arrived(w, k, "yx")
        self.arrived(w, k, "xy")
        self.hop(w, k, "cd").start()

    def require(self, w, k):
        for kind in ("c", "cx", "cy", "cd"):
            self.arrived(w, k, kind)

    def finish(self):
        me = self.me
        for w, k in self.stages:
            for kind in KINDS:
                self.hop(w, k, kind).wait_send()
        for w in range(len(self.shards)):
            self.own_copy(w, me.inner, me.m, 0).wait_send()

            @pl.when(me.m == 1)
            def _(w=w):
                self.own_copy(w, me.outer, 0, 1).wait_send()
                for k in range(3):
                    self.forward(w, k).wait_send()


class Route:
    def __init__(self, me):
        z, c = me.z, me.c
        odd = lax.rem(z, 2)
        self.stays = z // 2 == c
        self.order = (odd, 1 - odd)
        self.to = ({"z": 2 * c + odd, "core": z // 2}, {"z": 2 * c + 1 - odd, "core": z // 2})

    def start(self, copies):
        first_local, first, second = copies

        @pl.when(self.stays)
        def _():
            first_local.start()

        @pl.when(jnp.logical_not(self.stays))
        def _():
            first.start()

        second.start()

    def out(self, held, there, sems):
        a, b = self.order
        return (
            pltpu.make_async_copy(held.at[a], there.at[0], sems.at[0]),
            remote(held.at[a], there.at[0], sems.at[1], sems.at[2], self.to[0]),
            remote(held.at[b], there.at[1], sems.at[3], sems.at[4], self.to[1]),
        )

    def back(self, held, there, sems):
        odd = self.order[0]
        return (
            pltpu.make_async_copy(held.at[0], there.at[odd], sems.at[0]),
            remote(held.at[0], there.at[odd], sems.at[1], sems.at[2], self.to[0]),
            remote(held.at[1], there.at[odd], sems.at[3], sems.at[4], self.to[1]),
        )

    def wait(self, copies):
        first_local, first, second = copies

        @pl.when(self.stays)
        def _():
            first_local.wait()

        @pl.when(jnp.logical_not(self.stays))
        def _():
            first.wait()

        second.wait()


def turn(v):
    return pltpu.roll(v, HD // 2, 1)


def stacked(two_heads):
    return jnp.concatenate([two_heads[:, :HD], two_heads[:, HD:]], axis=0)


def pick(which, values):
    out = values[0]
    for i in range(1, len(values)):
        out = jnp.where(which == i, values[i], out)
    return out


def row_loop(rows, step, body):
    def run(i, carry):
        body(pl.ds(pl.multiple_of(i * step, step), step))
        return carry

    lax.fori_loop(0, rows // step, run, 0)


PER_HEAD = 4 * HD
HALF_HEADS = KV_HEADS // 2
BLOCKS = 4
COUNT = 4


def forward_kernel(scalars, gains, head_gains, cosines, sines, tokens, cotangent, *refs):
    shards = refs[:COUNT]
    (
        block_out,
        gains_all,
        source,
        grad,
        h1_out,
        raw_out,
        tok_out,
        probs_out,
        attended_out,
        middle_out,
        h2_out,
        gate_up_out,
    ) = refs[COUNT : COUNT + 12]
    fulls = refs[COUNT + 12 : 2 * COUNT + 12]
    (
        acc,
        acc_small,
        wide,
        narrow,
        x,
        h1,
        h2,
        tok,
        outgoing,
        raw,
        p0,
        p1,
        p2,
        p3,
        ordered,
        mixed,
        mixed_out,
        attended,
        middle,
        hidden,
        gate_up,
        low_out,
        z_send,
        z_recv,
        f_send,
        xy_send,
        xy_recv,
        load_sem,
        keep_sem,
        gain_sem,
        token_sem,
        cot_sem,
        swap_sem,
        save_sem,
        prob_sem,
        gate_sem,
    ) = refs[2 * COUNT + 12 :]
    prob_slots = (p0, p1, p2, p3)
    low, f32 = jnp.bfloat16, jnp.float32
    me = Place()
    z, c = me.z, me.c
    rows, width = x.shape
    block = rows // 2
    comm = Gather(me, shards, fulls, (z_send, z_recv, f_send, xy_send, xy_recv))
    route = Route(me)
    me.greet()
    gain_copies = []
    for j in range(1, NZ):
        there = {"z": lax.rem(z + j, NZ)}
        gain_copies.append(remote(gains, gains_all.at[z], gain_sem.at[0, j], gain_sem.at[1, j], there))
    for copy in gain_copies:
        copy.start()
    gains_all[pl.ds(z, 1)] = gains[...][None]
    token_copies = route.out(tokens, source, token_sem)
    cot_copies = route.out(cotangent, grad, cot_sem)

    def at_slot(slot):
        for name, index in FORWARD_PLAN.get(slot, ()):
            if name == "tok":
                route.start(token_copies)
            elif name == "cot":
                route.start(cot_copies)
            else:
                getattr(comm, name)(index)

    def buffer(w, kk):
        if w in (0, 2):
            return wide.at[kk % 2, :, :, pl.ds(0, shards[w].shape[2])]
        return narrow.at[kk % 2, :, pl.ds(0, shards[w].shape[1]), :]

    def load(w, kk):
        src = shards[w] if kk == 0 else fulls[w].at[comm.shard_z(kk - 1)]
        return pltpu.make_async_copy(src, buffer(w, kk), load_sem.at[w, kk])

    def keep(w):
        return pltpu.make_async_copy(buffer(w, 0), fulls[w].at[z], keep_sem.at[w])

    def fetch(w, kk):
        if kk > 0:
            comm.require(w, kk - 1)
        if kk == 2:
            keep(w).wait()
        load(w, kk).start()

    def chunk(w, kk, lhs, out, tile):
        depth = 8 * shards[w].shape[1]
        columns = shards[w].shape[2]
        own_z = z if kk == 0 else comm.shard_z(kk - 1)
        load(w, kk).wait()
        if kk == 0:
            keep(w).start()
        from_left = pl.ds(pl.multiple_of(own_z * depth, depth), depth)
        weight = buffer(w, kk)

        def body(i, carry):
            at = pl.ds(pl.multiple_of(i * tile, tile), tile)
            right = weight[:, :, at].reshape(depth, tile)
            part = jnp.dot(lhs[:, from_left], right, preferred_element_type=f32)
            if kk == 0:
                out[:, at] = part
            else:
                out[:, at] += part
            return carry

        lax.fori_loop(0, columns // tile, body, 0)

    def save(i, src, dst):
        return pltpu.make_async_copy(src, dst, save_sem.at[i])

    fetch(0, 0)
    fetch(1, 0)
    at_slot("start")
    fetch(0, 1)
    for j in range(1, NZ):
        gain_copies[j - 1].wait_send()
        there = gains_all.at[lax.rem(z + NZ - j, NZ)]
        remote(gains, there, gain_sem.at[0, j], gain_sem.at[1, j], me.partner).wait_recv()
    route.wait(token_copies)
    for part in range(2):
        pltpu.make_async_copy(source.at[part], x.at[pl.ds(part * block, block)], token_sem.at[5 + part]).start()
    for part in range(2):
        pltpu.make_async_copy(source.at[part], x.at[pl.ds(part * block, block)], token_sem.at[5 + part]).wait()

    def normed_times(v, index):
        v = v * lax.rsqrt(jnp.mean(v * v, axis=-1, keepdims=True) + EPSILON)
        gain = jnp.concatenate([gains_all[s, index : index + 1, :] for s in range(NZ)], axis=1)
        return (v * gain).astype(low)

    def first_norm(at):
        h1[at, :] = normed_times(x[at, :].astype(f32), 0)

    row_loop(rows, 64, first_norm)
    save(0, h1, h1_out).start()
    at_slot("tw")
    chunk(0, 0, h1, acc, 512)
    at_slot("q0")
    fetch(0, 2)
    chunk(0, 1, h1, acc, 512)
    at_slot("q1")
    fetch(0, 3)
    chunk(0, 2, h1, acc, 512)
    fetch(2, 0)
    at_slot("q2")
    chunk(0, 3, h1, acc, 512)
    at_slot("q3")

    def head(h, target, column):
        parts = []
        for start, size in ((h * 2 * HD, 2 * HD), ((HEADS + h) * HD, HD), ((HEADS + KV_HEADS + h) * HD, HD)):
            parts.append(acc[:, pl.ds(pl.multiple_of(start, HD), size)])
        half, at = h // HALF_HEADS, pl.multiple_of(lax.rem(h, HALF_HEADS) * PER_HEAD, PER_HEAD)
        for i, (v, gain_row) in enumerate(((parts[0][:, :HD], 0), (parts[0][:, HD:], 0), (parts[1], 1))):
            raw[half, :, pl.ds(pl.multiple_of(at + i * HD, HD), HD)] = v.astype(low)
            v = v * lax.rsqrt(jnp.mean(v * v, axis=-1, keepdims=True) + EPSILON)
            v = v * head_gains[gain_row : gain_row + 1, :]
            v = (v * cosines[...] + turn(v) * sines[...]).astype(low)
            for j in range(2):
                target[j, :, pl.ds(pl.multiple_of(column + i * HD, HD), HD)] = v[j * block : (j + 1) * block]
        v = parts[2].astype(low)
        for j in range(2):
            target[j, :, pl.ds(pl.multiple_of(column + 3 * HD, HD), HD)] = v[j * block : (j + 1) * block]

    def other_head(i, carry):
        head(i + HALF_HEADS * (1 - c), outgoing, i * PER_HEAD)
        return carry

    def own_head(i, carry):
        head(i + HALF_HEADS * c, tok, i * PER_HEAD)
        return carry

    lax.fori_loop(0, HALF_HEADS, other_head, 0)
    swap_out = remote(outgoing, tok.at[pl.ds(2, 2)], swap_sem.at[0], swap_sem.at[1], me.partner)
    swap_out.start()
    at_slot("r0")
    lax.fori_loop(0, HALF_HEADS, own_head, 0)
    save(1, raw, raw_out).start()
    at_slot("r1")
    swap_out.wait()
    save(2, tok, tok_out).start()
    at_slot("sw")

    scale = 1.0 / math.sqrt(HD)
    above = lax.rem(lax.broadcasted_iota(jnp.int32, (2 * block, block), 0), block)
    above = above < lax.broadcasted_iota(jnp.int32, (2 * block, block), 1)

    def save_probs(h, i):
        n = (i + 1) * block
        column = i * (i + 1) // 2 * block
        return pltpu.make_async_copy(prob_slots[i], probs_out.at[h, :, pl.ds(column, n)], prob_sem.at[i])

    def attend(h, carry):
        at = pl.multiple_of(h * PER_HEAD, PER_HEAD)
        for i in range(BLOCKS):
            ordered[i * block : (i + 1) * block] = pick(
                scalars[i], [tok[j, :, pl.ds(at, PER_HEAD)] for j in range(BLOCKS)]
            )
        for i in range(BLOCKS):
            n = (i + 1) * block
            query = stacked(ordered[i * block : n, : 2 * HD])
            keys, values = ordered[:n, 2 * HD : 3 * HD], ordered[:n, 3 * HD :]
            scores = lax.dot_general(query, keys, (((1,), (1,)), ((), ())), preferred_element_type=f32)
            last = jnp.where(above, MASKED, scores[:, i * block :])
            scores = last if i == 0 else jnp.concatenate([scores[:, : i * block], last], axis=1)
            top = jnp.max(scores, axis=-1, keepdims=True)
            weights = jnp.exp((scores - top) * scale)
            weights = weights * (1.0 / jnp.sum(weights, axis=-1, keepdims=True))
            probs = weights.astype(low)

            @pl.when(h > 0)
            def _():
                save_probs(h - 1, i).wait()

            prob_slots[i][...] = probs
            save_probs(h, i).start()
            out = jnp.dot(probs, values, preferred_element_type=f32).astype(low)
            there = pl.multiple_of(h * 2 * HD, 2 * HD)
            mixed[i * block : (i + 1) * block, pl.ds(there, HD)] = out[:block]
            mixed[i * block : (i + 1) * block, pl.ds(pl.multiple_of(there + HD, HD), HD)] = out[block:]
            for now in range(HALF_HEADS):
                slot_name = f"t{now}{i}"
                if slot_name in FORWARD_PLAN:

                    @pl.when(h == now)
                    def _(slot_name=slot_name):
                        at_slot(slot_name)

        return carry

    lax.fori_loop(0, HALF_HEADS, attend, 0)
    fetch(1, 1)
    half = HEADS * HD // 2
    mine = pl.ds(pl.multiple_of(c * half, half), half)
    for j in range(2):
        blocks = [mixed[i * block : (i + 1) * block] for i in range(BLOCKS)]
        mixed_out[j * block : (j + 1) * block] = pick(scalars[BLOCKS + 2 + j], blocks)
    for j in range(2):
        blocks = [mixed[i * block : (i + 1) * block] for i in range(BLOCKS)]
        attended[j * block : (j + 1) * block, mine] = pick(scalars[BLOCKS + j], blocks)
    mixed_swap = remote(mixed_out, attended.at[:, mine], swap_sem.at[2], swap_sem.at[3], me.partner)
    mixed_swap.start()
    at_slot("m")
    for i in range(BLOCKS):
        save_probs(HALF_HEADS - 1, i).wait()
    mixed_swap.wait()
    save(3, attended, attended_out).start()
    for kk in range(4):
        chunk(1, kk, attended, acc_small, 512)
        at_slot(f"o{kk}")
        if kk < 2:
            fetch(1, kk + 2)
        elif kk == 2:
            fetch(3, 0)

    def second_norm(at):
        v = x[at, :].astype(f32) + acc_small[at, :]
        middle[at, :] = v
        h2[at, :] = normed_times(v, 1)

    row_loop(rows, 64, second_norm)
    save(4, middle, middle_out).start()
    save(5, h2, h2_out).start()
    at_slot("n2")
    fetch(2, 1)
    chunk(2, 0, h2, acc, 512)
    at_slot("g0")
    fetch(2, 2)
    chunk(2, 1, h2, acc, 512)
    at_slot("g1")
    chunk(2, 2, h2, acc, 512)
    at_slot("g2")
    fetch(2, 3)
    chunk(2, 3, h2, acc, 512)
    at_slot("g3")

    def save_gate_up(i, part, slot):
        at = pl.multiple_of(part * FF + i * 512, 512)
        return pltpu.make_async_copy(gate_up.at[slot, part], gate_up_out.at[:, pl.ds(at, 512)], gate_sem.at[slot, part])

    def activate(i, carry):
        slot = lax.rem(i, 2)
        at = pl.multiple_of(i * 512, 512)

        @pl.when(i >= 2)
        def _():
            for part in range(2):
                save_gate_up(i - 2, part, slot).wait()

        gate = acc[:, pl.ds(at, 512)]
        up = acc[:, pl.ds(pl.multiple_of(FF + at, 512), 512)]
        gate_up[slot, 0] = gate.astype(low)
        gate_up[slot, 1] = up.astype(low)
        hidden[:, pl.ds(at, 512)] = (gate * jax.nn.sigmoid(gate) * up).astype(low)
        for part in range(2):
            save_gate_up(i, part, slot).start()
        return carry

    tiles = FF // 512
    lax.fori_loop(0, tiles, activate, 0)
    at_slot("ac")
    fetch(3, 1)
    chunk(3, 0, hidden, acc_small, 512)
    at_slot("d0")
    chunk(3, 1, hidden, acc_small, 512)
    at_slot("d1")
    fetch(3, 2)
    chunk(3, 2, hidden, acc_small, 512)
    at_slot("d2")
    fetch(3, 3)
    chunk(3, 3, hidden, acc_small, 512)
    at_slot("d3")

    def final(at):
        low_out[at, :] = (middle[at, :] + acc_small[at, :]).astype(low)

    row_loop(rows, 64, final)
    save(6, low_out, block_out).start()
    at_slot("fin")
    comm.finish()
    for slot in range(2):
        for part in range(2):
            save_gate_up(tiles - 2 + slot, part, slot).wait()
    for i, (src, dst) in enumerate(
        (
            (h1, h1_out),
            (raw, raw_out),
            (tok, tok_out),
            (attended, attended_out),
            (middle, middle_out),
            (h2, h2_out),
            (low_out, block_out),
        )
    ):
        save(i, src, dst).wait()
    route.wait(cot_copies)


FORWARD_PLAN = {
    "start": (("own", 0), ("own", 1), ("relay", 0), ("launch", 0), ("own", 2), ("relay", 2), ("launch", 2), ("relay", 1), ("sx", 2), ("tok", 0), ("sy", 0), ("relay", 3), ("relay", 6), ("launch", 1), ("launch", 3), ("sx", 0), ("sy", 1), ("sx", 1), ("third", 0), ("sy", 2), ("sy", 3), ("launch", 6), ("relay", 7), ("third", 2), ("own", 3), ("launch", 7), ("third", 1), ("sx", 3),),
    "q0": (("relay", 4),),
    "q1": (("launch", 4),),
    "q2": (("relay", 5), ("launch", 5),),
    "r0": (("relay", 10), ("relay", 9), ("sy", 6), ("sx", 6), ("sy", 4), ("third", 3), ("sy", 5),),
    "r1": (("launch", 9), ("sx", 4), ("sx", 5), ("launch", 10),),
    "t00": (("relay", 8),),
    "t01": (("launch", 8),),
    "m": (("third", 4), ("sy", 7), ("sx", 7), ("relay", 11), ("third", 6), ("sy", 10), ("third", 5), ("sy", 9), ("sy", 8), ("sx", 8), ("sx", 10), ("launch", 11), ("cot", 0), ("sx", 9),),
    "o3": (("third", 7),),
    "g0": (("third", 8),),
    "g1": (("sy", 11), ("sx", 11), ("third", 9),),
    "g2": (("third", 10),),
    "ac": (("third", 11),),
}


def run_forward(scalars, gains, head_gains, cosines, sines, tokens, cotangent, shards):
    low, f32 = jnp.bfloat16, jnp.float32
    _, slot_len, width = tokens.shape
    rows = 2 * slot_len
    cut = [s.reshape(8, s.shape[0] // 8, s.shape[1]) for s in shards]
    area = slot_len * BLOCKS * (BLOCKS + 1) // 2
    shape = jax.ShapeDtypeStruct
    outs = [
        shape((rows, width), low),
        shape((NZ, *gains.shape), f32),
        shape((2, slot_len, width), low),
        shape((2, slot_len, width), low),
        shape((rows, width), low),
        shape((2, rows, HALF_HEADS * PER_HEAD), low),
        shape((4, slot_len, HALF_HEADS * PER_HEAD), low),
        shape((HALF_HEADS, 2 * slot_len, area), low),
        shape((rows, HEADS * HD), low),
        shape((rows, width), f32),
        shape((rows, width), low),
        shape((rows, 2 * FF), low),
    ] + [shape((NZ, *s.shape), low) for s in cut]
    hbm = pl.BlockSpec(memory_space=HBM)
    vmem = pl.BlockSpec(memory_space=pltpu.VMEM)
    dma = pltpu.SemaphoreType.DMA
    out = pl.pallas_call(
        forward_kernel,
        out_shape=outs,
        in_specs=[pl.BlockSpec(memory_space=pltpu.SMEM)] + [vmem] * 4 + [hbm] * (2 + COUNT),
        out_specs=[hbm, vmem] + [hbm] * (10 + COUNT),
        scratch_shapes=[
            pltpu.VMEM((rows, 2 * FF), f32),
            pltpu.VMEM((rows, width), f32),
            pltpu.VMEM((2, 8, cut[2].shape[1], 2 * FF), low),
            pltpu.VMEM((2, 8, cut[3].shape[1], width), low),
            pltpu.VMEM((rows, width), low),
            pltpu.VMEM((rows, width), low),
            pltpu.VMEM((rows, width), low),
            pltpu.VMEM((4, slot_len, HALF_HEADS * PER_HEAD), low),
            pltpu.VMEM((2, slot_len, HALF_HEADS * PER_HEAD), low),
            pltpu.VMEM((2, rows, HALF_HEADS * PER_HEAD), low),
        ]
        + [pltpu.VMEM((2 * slot_len, (i + 1) * slot_len), low) for i in range(BLOCKS)]
        + [
            pltpu.VMEM((4 * slot_len, PER_HEAD), low),
            pltpu.VMEM((4 * slot_len, HEADS * HD // 2), low),
            pltpu.VMEM((rows, HEADS * HD // 2), low),
            pltpu.VMEM((rows, HEADS * HD), low),
            pltpu.VMEM((rows, width), f32),
            pltpu.VMEM((rows, FF), low),
            pltpu.VMEM((2, 2, rows, 512), low),
            pltpu.VMEM((rows, width), low),
            dma((COUNT, 2)),
            dma((COUNT, 3)),
            dma((COUNT, 3)),
            dma((COUNT, 3, len(KINDS))),
            dma((COUNT, 3, len(KINDS))),
            dma((COUNT, 4)),
            dma((COUNT,)),
            dma((2, NZ)),
            dma((7,)),
            dma((5,)),
            dma((4,)),
            dma((7,)),
            dma((BLOCKS,)),
            dma((2, 2)),
        ],
        compiler_params=pltpu.CompilerParams(collective_id=0, has_side_effects=True, vmem_limit_bytes=VMEM_LIMIT),
        name="forward",
    )(scalars, gains, head_gains, cosines, sines, tokens, cotangent, *cut)
    return out[:12], out[12:]


def add_rows(dst, src, rows):
    def body(i, carry):
        at = pl.ds(pl.multiple_of(i * 16, 16), 16)
        total = dst[at, :].astype(jnp.float32) + src[at, :].astype(jnp.float32)
        dst[at, :] = total.astype(dst.dtype)
        return carry

    lax.fori_loop(0, rows // 16, body, 0)


SPREAD = ("x", "y", "yx", "xy", "c", "cx", "cy", "cd")
ROUNDS = ("x1", "y1", "y2", "x2")


class Reduce:
    def __init__(self, me, shapes, refs, turned, sems):
        self.me, self.shapes, self.turned = me, shapes, turned
        self.stage, self.acc, self.rx1, self.ry1, self.rx2, self.ry2, self.rz, self.outs = refs
        (
            self.keep_sem,
            self.c_send,
            self.c_recv,
            self.r_send,
            self.r_recv,
            self.z_send,
            self.z_recv,
            self.o_send,
            self.o_recv,
        ) = sems
        self.stage_t = (3, 2, 1 - me.m, me.m)
        self.chunks = [(w, k) for w in range(len(shapes)) for k in range(4)]

    def zk(self, k):
        return self.me.at(self.stage_t[k])

    def product(self, n, rhs, columns, store):
        w, k = self.chunks[n]
        rows = self.shapes[w][0]
        half = self.shapes[w][1] // 2
        tile = min(half, 512)

        steps = half // tile
        parts = 2 if rows > 256 else 1
        high = rows // parts

        def body(i, carry):
            at = pl.multiple_of(lax.rem(i, steps) * tile, tile)
            down = pl.multiple_of(i // steps * high, high)
            part = jnp.dot(
                self.turned[n % 2, pl.ds(down, high)],
                rhs[:, pl.ds(pl.multiple_of(columns * half + at, tile), tile)],
                preferred_element_type=jnp.float32,
            )
            store(part.reshape(2 // parts, 2, rows // 4, tile), pl.ds(i // steps, 2 // parts), pl.ds(at, tile))
            return carry

        lax.fori_loop(0, parts * steps, body, 0)

    def to_partner(self, n):
        w, k = self.chunks[n]
        return remote(
            self.stage[w], self.acc[w].at[self.zk(k)], self.c_send.at[w, k], self.c_recv.at[w, k], self.me.partner
        )

    def turn_rows(self, n, lhs):
        w, k = self.chunks[n]
        rows = self.shapes[w][0]
        at = pl.multiple_of(self.zk(k) * rows, rows)
        self.turned[n % 2, :rows] = jnp.transpose(lhs[:, pl.ds(at, rows)])

    def theirs(self, n, rhs):
        w, k = self.chunks[n]
        if k > 0:
            self.to_partner(n - 1).wait_send()

        def store(part, side, at):
            self.stage[w][side, :, :, at] = part.astype(jnp.bfloat16)

        self.product(n, rhs, 1 - self.me.c, store)

    def ours(self, n, rhs):
        w, k = self.chunks[n]
        a = self.acc[w].at[self.zk(k)]
        self.to_partner(n).wait_recv()

        def store(part, side, at):
            a[side, :, :, at] = (part + a[side, :, :, at].astype(jnp.float32)).astype(jnp.bfloat16)

        self.product(n, rhs, self.me.c, store)

    def launch(self, n):
        w, k = self.chunks[n]
        self.exchange(w, k, "x1").start()
        self.exchange(w, k, "y1").start()

    def exchange(self, w, k, kind):
        me = self.me
        x, y = me.x, me.y
        a = self.acc[w].at[self.zk(k)]
        half = a.shape[-1] // 2
        lo, hi = pl.ds(0, half), pl.ds(half, half)
        src, dst, peer = {
            "x1": lambda: (a.at[1 - x, :, :, lo], self.rx1[w].at[k], me.across_x),
            "y1": lambda: (a.at[:, 1 - y, :, hi], self.ry1[w].at[k], me.across_y),
            "y2": lambda: (a.at[x, 1 - y, :, lo], self.ry2[w].at[k], me.across_y),
            "x2": lambda: (a.at[1 - x, y, :, hi], self.rx2[w].at[k], me.across_x),
        }[kind]()
        index = ROUNDS.index(kind)
        return remote(src, dst, self.r_send.at[w, k, index], self.r_recv.at[w, k, index], peer)

    def along(self, w, k, slot, peer):
        me = self.me
        return remote(
            self.acc[w].at[self.zk(k), me.x, me.y], self.rz[w].at[slot], self.z_send.at[w, k], self.z_recv.at[w, slot], peer
        )

    def s1(self, n):
        w, k = self.chunks[n]
        me = self.me
        a = self.acc[w].at[self.zk(k)]
        rows, half = a.shape[2], a.shape[3] // 2
        self.exchange(w, k, "x1").wait_recv()
        for j in range(2):
            add_rows(a.at[me.x, j, :, pl.ds(0, half)], self.rx1[w].at[k, j], rows)
        self.exchange(w, k, "y1").wait_recv()
        for i in range(2):
            add_rows(a.at[i, me.y, :, pl.ds(half, half)], self.ry1[w].at[k, i], rows)
        self.exchange(w, k, "y2").start()
        self.exchange(w, k, "x2").start()

    def s2(self, n):
        w, k = self.chunks[n]
        a = self.acc[w].at[self.zk(k), self.me.x, self.me.y]
        rows, half = a.shape[0], a.shape[1] // 2
        self.exchange(w, k, "y2").wait_recv()
        add_rows(a.at[:, pl.ds(0, half)], self.ry2[w].at[k], rows)
        self.exchange(w, k, "x2").wait_recv()
        add_rows(a.at[:, pl.ds(half, half)], self.rx2[w].at[k], rows)

    def s3(self, n):
        w, k = self.chunks[n]
        me = self.me
        a = self.acc[w].at[self.zk(k), me.x, me.y]
        rows = a.shape[0]

        def take(slot):
            there = self.rz[w].at[slot]
            remote(there, there, self.z_send.at[w, 0], self.z_recv.at[w, slot], me.partner).wait_recv()
            add_rows(a, there, rows)

        @pl.when(me.m == 0)
        def _():
            if k < 3:
                self.along(w, k, k, me.inner).start()
            else:
                take(0)

        @pl.when(me.m == 1)
        def _():
            if k == 0:
                take(0)
                self.along(w, k, 3, me.inner).start()
            elif k == 1:
                take(1)
                self.along(w, k, 4, me.inner).start()
            elif k == 2:
                take(3)
                self.along(w, k, 0, me.outer).start()
            else:
                take(2)
                take(4)

    def out_at(self, w, cc, xx, yy):
        half = self.shapes[w][1] // 2
        return self.outs[w].at[xx, yy, :, pl.ds(pl.multiple_of(cc * half, half), half)]

    def keep(self, w):
        me = self.me
        return pltpu.make_async_copy(
            self.acc[w].at[me.z, me.x, me.y], self.out_at(w, me.c, me.x, me.y), self.keep_sem.at[w]
        )

    def spread(self, w, kind):
        me = self.me
        c, x, y = me.c, me.x, me.y
        final, mine = self.acc[w].at[me.z, x, y], self.out_at(w, c, x, y)
        px, py = self.out_at(w, c, 1 - x, y), self.out_at(w, c, x, 1 - y)
        pd = self.out_at(w, c, 1 - x, 1 - y)
        src, dst, peer = {
            "x": (final, mine, me.across_x),
            "y": (final, mine, me.across_y),
            "c": (final, mine, me.partner),
            "yx": (half_rows(px, 0), half_rows(px, 0), me.across_y),
            "xy": (half_rows(py, 1), half_rows(py, 1), me.across_x),
            "cx": (px, px, me.partner),
            "cy": (py, py, me.partner),
            "cd": (pd, pd, me.partner),
        }[kind]
        index = SPREAD.index(kind)
        return remote(src, dst, self.o_send.at[w, index], self.o_recv.at[w, index], peer)

    def spread_arrived(self, w, kind):
        me = self.me
        c, x, y = me.c, me.x, me.y
        dst = {
            "x": lambda: self.out_at(w, c, 1 - x, y),
            "y": lambda: self.out_at(w, c, x, 1 - y),
            "yx": lambda: half_rows(self.out_at(w, c, 1 - x, 1 - y), 0),
            "xy": lambda: half_rows(self.out_at(w, c, 1 - x, 1 - y), 1),
            "c": lambda: self.out_at(w, 1 - c, x, y),
            "cx": lambda: self.out_at(w, 1 - c, 1 - x, y),
            "cy": lambda: self.out_at(w, 1 - c, x, 1 - y),
            "cd": lambda: self.out_at(w, 1 - c, 1 - x, 1 - y),
        }[kind]()
        index = SPREAD.index(kind)
        remote(dst, dst, self.o_send.at[w, index], self.o_recv.at[w, index], me.partner).wait_recv()

    def s4(self, w):
        self.keep(w).start()
        for kind in ("x", "y", "c"):
            self.spread(w, kind).start()

    def s5(self, w):
        self.spread_arrived(w, "x")
        self.spread(w, "yx").start()
        self.spread(w, "cx").start()
        self.spread_arrived(w, "y")
        self.spread(w, "xy").start()
        self.spread(w, "cy").start()

    def s6(self, w):
        self.spread_arrived(w, "yx")
        self.spread_arrived(w, "xy")
        self.spread(w, "cd").start()

    def finish(self):
        for n, (w, k) in enumerate(self.chunks):
            if k == 3:
                self.to_partner(n).wait_send()
            for kind in ROUNDS:
                self.exchange(w, k, kind).wait_send()
            if k < 3:
                self.along(w, k, k, self.me.inner).wait_send()
        for w in range(len(self.shapes)):
            self.keep(w).wait()
            for kind in SPREAD:
                self.spread(w, kind).wait_send()
            for kind in ("c", "cx", "cy", "cd"):
                self.spread_arrived(w, kind)


class Small:
    def __init__(self, me, mid, got, along, send, recv):
        self.me, self.mid, self.got, self.along_z, self.send, self.recv = me, mid, got, along, send, recv
        self.peers = (me.partner, me.across_x, me.across_y)

    def copy(self, step):
        return remote(self.mid.at[step], self.got.at[step], self.send.at[step], self.recv.at[step], self.peers[step])

    def along(self, j):
        there = {"z": lax.rem(self.me.z + 1 + j, NZ)}
        return remote(self.mid.at[3], self.along_z.at[self.me.z], self.send.at[3 + j], self.recv.at[3 + j], there)

    def step(self, n):
        if n < 6:
            step = n // 2
            if n % 2 == 0:
                self.copy(step).start()
            else:
                self.copy(step).wait()
                self.mid[step + 1] = self.mid[step] + self.got[step]
        elif n == 6:
            for j in range(3):
                self.along(j).start()
        else:
            for j in range(3):
                self.along(j).wait_send()
                there = self.along_z.at[lax.rem(self.me.z + 3 - j, NZ)]
                remote(there, there, self.send.at[3 + j], self.recv.at[3 + j], self.me.partner).wait_recv()
            self.along_z[pl.ds(self.me.z, 1)] = self.mid[pl.ds(3, 1)]

    def total(self):
        return (self.along_z[0] + self.along_z[1]) + (self.along_z[2] + self.along_z[3])


def backward_kernel(shapes, scalars, gains, head_gains, cosines, sines, *refs):
    (
        source,
        grad,
        h1_in,
        raw_in,
        tok_in,
        probs_in,
        attended_in,
        middle_in,
        h2_in,
        gate_up_in,
        block_rows_in,
        full_qkv,
        full_out,
        full_gate_up,
        full_down,
    ) = refs[:15]
    small_out, input_out, block_out = refs[15:18]
    outs = refs[18:22]
    rest = refs[22:]
    stage, acc, rz = rest[:4], rest[4:8], rest[8:12]
    rx1, ry1, rx2, ry2 = rest[12:14], rest[14:16], rest[16:18], rest[18:20]
    turned, wide, grad_mid, grads, outgoing, returned, small_mid, small_got, small_z, gain_sums, sums, input_low = rest[20:32]
    comm_sems = rest[32:41]
    (
        s_send,
        s_recv,
        load_sem,
        wide_sem,
        narrow_sem,
        gate_sem,
        prob_sem,
        tok_sem,
        raw_sem,
        swap_sem,
        out_sem,
        in_sem,
    ) = rest[41:]

    def like(refs, w):
        r, n = shapes[w]
        ref = refs[w % 2]
        if w < 2:
            return ref
        lead = (slice(None),) * (len(ref.shape) - 2)
        return ref.at[(*lead, pl.ds(0, r // 4), pl.ds(0, n // 4))]

    landing = [[like(group, w) for w in range(4)] for group in (rx1, ry1, rx2, ry2)]
    low, f32 = jnp.bfloat16, jnp.float32
    me = Place()
    z, c = me.z, me.c
    rows, width = grad_mid.shape
    block = rows // 2
    share = width // NZ
    comm = Reduce(me, shapes, (stage, acc, *landing, rz, outs), turned, comm_sems)
    small = Small(me, small_mid, small_got, small_z, s_send, s_recv)

    def at_slot(slot):
        for name, index in BACK_PLAN.get(slot, ()):
            if name == "small":
                small.step(index)
            elif name == "inback":
                route.start(input_back)
            else:
                getattr(comm, name)(index)

    route = Route(me)
    me.greet()
    block_back = route.back(block_rows_in, block_out, out_sem)
    input_back = route.back(input_low, input_out, in_sem)
    route.start(block_back)
    sums[...] = jnp.zeros_like(sums)
    gain_sums[...] = jnp.zeros_like(gain_sums)
    contract = (((1,), (1,)), ((), ()))
    depth = FF // NZ

    wide_loads = [(full_gate_up, k, t) for k in range(4) for t in range(3)]
    wide_loads += [(full_qkv, k, t) for k in range(4) for t in range(2)]
    wide_tile = wide.shape[3]

    def wide_load(j):
        full, k, t = wide_loads[j]
        src = full.at[comm.zk(k), :, :, pl.ds(t * wide_tile, wide_tile)]
        return pltpu.make_async_copy(src, wide.at[j % 2], wide_sem.at[j % 2])

    def against(j, count, left, target):
        full, k, _ = wide_loads[j]
        at = pl.ds(pl.multiple_of(comm.zk(k) * share, share), share)
        deep = wide_tile // 2

        def tile_load(t, slot):
            here = pl.ds(pl.multiple_of(t * wide_tile, wide_tile), wide_tile)
            return pltpu.make_async_copy(full.at[comm.zk(k), :, :, here], wide.at[slot], wide_sem.at[slot])

        def body(t, carry):
            slot = lax.rem(j + t, 2)
            tile_load(t, slot).wait()

            @pl.when(t + 1 < count)
            def _():
                tile_load(t + 1, 1 - slot).start()

            if j + count < len(wide_loads):

                @pl.when(t + 1 == count)
                def _():
                    wide_load(j + count).start()

            def half_tile(i, carry):
                from_tile = pl.ds(pl.multiple_of(i * deep, deep), deep)
                from_left = pl.ds(pl.multiple_of(t * wide_tile + i * deep, deep), deep)
                right = wide[slot, :, :, from_tile].reshape(share, deep)
                part = lax.dot_general(left[:, from_left], right, contract, preferred_element_type=f32)

                @pl.when(t + i == 0)
                def _():
                    target[:, at] = part

                @pl.when(t + i > 0)
                def _():
                    target[:, at] += part

                return carry

            return lax.fori_loop(0, 2, half_tile, carry)

        lax.fori_loop(0, count, body, 0)

    def gain_row(index):
        return jnp.concatenate([gains[s, index : index + 1, :] for s in range(NZ)], axis=1)

    def norm_parts(v):
        inverse = lax.rsqrt(jnp.mean(v * v, axis=-1, keepdims=True) + EPSILON)
        return v * inverse, inverse

    def norm_grad(normed, inverse, g):
        return inverse * (g - normed * jnp.mean(g * normed, axis=-1, keepdims=True))

    def load(i, src, dst):
        return pltpu.make_async_copy(src, dst, load_sem.at[i])

    def feed_forward(g, h2, grad_gate_up, narrow, gate_up, middle):
        g_loads = [load(i, grad.at[i], g.at[pl.ds(i * block, block)]) for i in range(2)]

        def narrow_load(k):
            return pltpu.make_async_copy(full_down.at[comm.zk(k)], narrow.at[k % 2], narrow_sem.at[k % 2])

        def gate_load(k, part):
            at = pl.multiple_of(part * FF + comm.zk(k) * depth, depth)
            src = gate_up_in.at[:, pl.ds(at, depth)]
            return pltpu.make_async_copy(src, gate_up.at[k % 2, part], gate_sem.at[k % 2, part])

        def fetch(k):
            narrow_load(k).start()
            for part in range(2):
                gate_load(k, part).start()

        for copy in g_loads:
            copy.start()
        fetch(0)
        fetch(1)
        load(2, h2_in, h2).start()
        load(3, middle_in, middle).start()
        wide_load(0).start()
        for copy in g_loads:
            copy.wait()
        tile = depth // 2

        def hidden_part(k):
            narrow_load(k).wait()
            for part in range(2):
                gate_load(k, part).wait()

            def body(step, carry):
                at = pl.multiple_of(step // 2 * tile, tile)
                here = pl.ds(pl.multiple_of(lax.rem(step, 2) * block, block), block)
                right = narrow[k % 2, pl.ds(step // 2 * 4, 4)].reshape(tile, width)
                grad_hidden = lax.dot_general(g[here, :], right, contract, preferred_element_type=f32)
                gate = gate_up[k % 2, 0, here, pl.ds(at, tile)].astype(f32)
                up = gate_up[k % 2, 1, here, pl.ds(at, tile)].astype(f32)
                sigmoid = jax.nn.sigmoid(gate)
                silu = gate * sigmoid
                turned[k % 2, pl.ds(at, tile), here] = jnp.transpose((silu * up).astype(low))
                there = pl.multiple_of(comm.zk(k) * depth + at, 128)
                grad_gate = grad_hidden * up * (sigmoid * (1.0 + gate * (1.0 - sigmoid)))
                grad_gate_up[here, pl.ds(there, tile)] = grad_gate.astype(low)
                grad_gate_up[here, pl.ds(pl.multiple_of(FF + there, 128), tile)] = (grad_hidden * silu).astype(low)
                return carry

            lax.fori_loop(0, 4, body, 0)
            if k + 2 < 4:
                fetch(k + 2)

        for n in range(4):
            hidden_part(n)
            comm.theirs(n, g)
            if n > 0:
                comm.ours(n - 1, g)
            comm.to_partner(n).start()
            at_slot(f"h{n}")
        load(2, h2_in, h2).wait()
        for n in range(4, 8):
            comm.turn_rows(n, h2)
            comm.theirs(n, grad_gate_up)
            comm.ours(n - 1, g if n == 4 else grad_gate_up)
            comm.to_partner(n).start()
            at_slot(f"g{n}")
            against((n - 4) * 3, 3, grad_gate_up, grad_mid)
            at_slot(f"a{n}")
        comm.ours(7, grad_gate_up)
        at_slot("g8")
        load(3, middle_in, middle).wait()

        def second_norm(at):
            normed, inverse = norm_parts(middle[at, :])
            grad_h2 = grad_mid[at, :]
            gain_sums[1:2, :] += jnp.sum(normed * grad_h2, axis=0, keepdims=True)
            grad_mid[at, :] = g[at, :].astype(f32) + norm_grad(normed, inverse, grad_h2 * gain_row(1))

        row_loop(rows, 64, second_norm)
        at_slot("n2")

    pl.run_scoped(
        feed_forward,
        pltpu.VMEM((rows, width), low),
        pltpu.VMEM((rows, width), low),
        pltpu.VMEM((rows, 2 * FF), low),
        pltpu.VMEM((2, *full_down.shape[1:]), low),
        pltpu.VMEM((2, 2, rows, depth), low),
        pltpu.VMEM((rows, width), f32),
    )

    half = HEADS * HD // 2

    def out_projection(attended, narrow, grad_low):
        def narrow_load(j):
            ours = j // 2
            where = 2 * ((1 - c) * (1 - ours) + c * ours) + j % 2
            return pltpu.make_async_copy(full_out.at[where], narrow.at[j % 2], narrow_sem.at[j % 2])

        narrow_load(0).start()
        narrow_load(1).start()
        load(0, attended_in, attended).start()

        def lower(at):
            grad_low[at, :] = grad_mid[at, :].astype(low)

        row_loop(rows, 64, lower)
        columns = half // 2
        swap = remote(outgoing, grads.at[pl.ds(2, 2)], swap_sem.at[0], swap_sem.at[1], me.partner)

        def project(j, carry):
            narrow_load(j).wait()
            right = narrow[j % 2].reshape(columns, width)
            part = lax.dot_general(grad_low[...], right, contract, preferred_element_type=f32).astype(low)
            there = pl.ds(pl.multiple_of(j % 2 * columns, columns), columns)

            @pl.when(j < 2)
            def _():
                for i in range(2):
                    outgoing[i, :, there] = part[i * block : (i + 1) * block]
                narrow_load(j + 2).start()

            @pl.when(j >= 2)
            def _():
                for i in range(2):
                    grads[i, :, there] = part[i * block : (i + 1) * block]

            @pl.when(j == 2)
            def _():
                swap.start()

            return carry

        lax.fori_loop(0, 4, project, 0)
        load(0, attended_in, attended).wait()
        at_slot("op")
        for n in range(8, 12):
            comm.turn_rows(n, attended)
            comm.theirs(n, grad_low)
            if n > 8:
                comm.ours(n - 1, grad_low)
            comm.to_partner(n).start()
            at_slot(f"o{n}")
        comm.ours(11, grad_low)
        swap.wait()
        at_slot("o12")

    pl.run_scoped(
        out_projection,
        pltpu.VMEM((rows, HEADS * HD), low),
        pltpu.VMEM((2, *full_out.shape[1:]), low),
        pltpu.VMEM((rows, width), low),
    )

    def sequence_part(own, leaving):
        swap = remote(leaving, returned, swap_sem.at[2], swap_sem.at[3], me.partner)

        def attention(tok, ordered, grad_ordered, p0, p1, p2, p3, grad_k, grad_v, placed):
            slots = (p0, p1, p2, p3)
            scale = 1.0 / math.sqrt(HD)

            def prob_load(h, i):
                n = (i + 1) * block
                src = probs_in.at[h, :, pl.ds(i * (i + 1) // 2 * block, n)]
                return pltpu.make_async_copy(src, slots[i], prob_sem.at[i])

            def tok_load(h, slot):
                at = pl.multiple_of(h * PER_HEAD, PER_HEAD)
                return pltpu.make_async_copy(tok_in.at[:, :, pl.ds(at, PER_HEAD)], tok.at[slot], tok_sem.at[slot])

            tok_load(0, 0).start()
            for i in reversed(range(BLOCKS)):
                prob_load(0, i).start()

            def one_head(h, carry):
                slot = lax.rem(h, 2)
                tok_load(h, slot).wait()

                @pl.when(h + 1 < HALF_HEADS)
                def _():
                    tok_load(h + 1, 1 - slot).start()

                at = pl.multiple_of(h * 2 * HD, 2 * HD)
                for i in range(BLOCKS):
                    here = slice(i * block, (i + 1) * block)
                    ordered[here] = pick(scalars[i], [tok[slot, j] for j in range(BLOCKS)])
                    grad_ordered[here] = pick(scalars[i], [grads[j, :, pl.ds(at, 2 * HD)] for j in range(BLOCKS)])
                for i in reversed(range(BLOCKS)):
                    n = (i + 1) * block
                    here = slice(i * block, n)
                    prob_load(h, i).wait()
                    query = stacked(ordered[here, : 2 * HD])
                    g = stacked(grad_ordered[here, :])
                    keys, values = ordered[:n, 2 * HD : 3 * HD], ordered[:n, 3 * HD :]
                    probs = slots[i][...]
                    weights = probs.astype(f32)
                    grad_probs = lax.dot_general(g, values, contract, preferred_element_type=f32)
                    delta = jnp.sum(weights * grad_probs, axis=-1, keepdims=True)
                    grad_scores = (weights * (grad_probs - delta)).astype(low)
                    grad_q = (jnp.dot(grad_scores, keys, preferred_element_type=f32) * scale).astype(low)
                    placed[here, :HD] = grad_q[:block]
                    placed[here, HD : 2 * HD] = grad_q[block:]
                    across = (((0,), (0,)), ((), ()))
                    part_k = lax.dot_general(query, grad_scores, across, preferred_element_type=f32)
                    part_v = lax.dot_general(g, probs, across, preferred_element_type=f32)
                    if i == BLOCKS - 1:
                        grad_k[...] = part_k
                        grad_v[...] = part_v
                    else:
                        grad_k[:, :n] += part_k
                        grad_v[:, :n] += part_v

                    @pl.when(h + 1 < HALF_HEADS)
                    def _():
                        prob_load(h + 1, i).start()

                    if i > 0:
                        for now in range(HALF_HEADS):
                            slot_name = f"t{now}{BLOCKS - 1 - i}"
                            if slot_name in BACK_PLAN:

                                @pl.when(h == now)
                                def _(slot_name=slot_name):
                                    at_slot(slot_name)

                for i in range(BLOCKS):
                    here = slice(i * block, (i + 1) * block)
                    placed[here, 2 * HD : 3 * HD] = jnp.transpose(grad_k[:, here] * scale).astype(low)
                    placed[here, 3 * HD :] = jnp.transpose(grad_v[:, here]).astype(low)
                columns = pl.ds(pl.multiple_of(h * PER_HEAD, PER_HEAD), PER_HEAD)
                for j in range(BLOCKS):
                    value = pick(scalars[BLOCKS + j], [placed[i * block : (i + 1) * block] for i in range(BLOCKS)])
                    target = own if j < 2 else leaving
                    target[j % 2 * block : (j % 2 + 1) * block, columns] = value
                for now in range(HALF_HEADS):
                    slot_name = f"t{now}{BLOCKS - 1}"
                    if slot_name in BACK_PLAN:

                        @pl.when(h == now)
                        def _(slot_name=slot_name):
                            at_slot(slot_name)

                return carry

            lax.fori_loop(0, HALF_HEADS, one_head, 0)
            swap.start()
            at_slot("sw")

        pl.run_scoped(
            attention,
            pltpu.VMEM((2, 4, block, PER_HEAD), low),
            pltpu.VMEM((4 * block, PER_HEAD), low),
            pltpu.VMEM((4 * block, 2 * HD), low),
            *[pltpu.VMEM((2 * block, (i + 1) * block), low) for i in range(BLOCKS)],
            pltpu.VMEM((HD, 4 * block), f32),
            pltpu.VMEM((HD, 4 * block), f32),
            pltpu.VMEM((4 * block, PER_HEAD), low),
        )

        def projection(grad_qkv, raw, h1, x, grad_first):
            load(0, h1_in, h1).start()
            for i in range(2):
                load(2 + i, source.at[i], x.at[pl.ds(i * block, block)]).start()

            def raw_load(j, slot):
                which = c + j // HALF_HEADS * (1 - 2 * c)
                at = pl.multiple_of(lax.rem(j, HALF_HEADS) * PER_HEAD, PER_HEAD)
                return pltpu.make_async_copy(raw_in.at[which, :, pl.ds(at, PER_HEAD)], raw.at[slot], raw_sem.at[slot])

            raw_load(0, 0).start()

            def one_head(j, came):
                slot = lax.rem(j, 2)
                raw_load(j, slot).wait()

                @pl.when(j + 1 < KV_HEADS)
                def _():
                    raw_load(j + 1, 1 - slot).start()

                at = pl.multiple_of(lax.rem(j, HALF_HEADS) * PER_HEAD, PER_HEAD)
                h = lax.rem(j, HALF_HEADS) + HALF_HEADS * (c + j // HALF_HEADS * (1 - 2 * c))
                places = (h * 2 * HD, (h * 2 + 1) * HD, (HEADS + h) * HD)
                for i, (row, place) in enumerate(zip((0, 0, 1), places)):
                    normed, inverse = norm_parts(raw[slot, :, i * HD : (i + 1) * HD].astype(f32))
                    g = came[:, pl.ds(pl.multiple_of(at + i * HD, HD), HD)].astype(f32)
                    g = g * cosines[...] - turn(g) * sines[...]
                    sums[row : row + 1, :] += jnp.sum(normed * g, axis=0, keepdims=True)
                    back = norm_grad(normed, inverse, g * head_gains[row : row + 1, :])
                    grad_qkv[:, pl.ds(pl.multiple_of(place, HD), HD)] = back.astype(low)
                there = pl.multiple_of((HEADS + KV_HEADS + h) * HD, HD)
                grad_qkv[:, pl.ds(there, HD)] = came[:, pl.ds(pl.multiple_of(at + 3 * HD, HD), HD)]

            def own_head(i, carry):
                one_head(i, own)
                return carry

            def other_head(i, carry):
                one_head(i + HALF_HEADS, returned)
                return carry

            lax.fori_loop(0, HALF_HEADS, own_head, 0)
            at_slot("b0")
            swap.wait()
            lax.fori_loop(0, HALF_HEADS, other_head, 0)
            load(0, h1_in, h1).wait()
            at_slot("b1")
            for n in range(12, 16):
                comm.turn_rows(n, h1)
                comm.theirs(n, grad_qkv)
                if n > 12:
                    comm.ours(n - 1, grad_qkv)
                comm.to_partner(n).start()
                at_slot(f"q{n}")
            comm.ours(15, grad_qkv)
            at_slot("q16")
            for k in range(4):
                against(12 + k * 2, 2, grad_qkv, grad_first)
                at_slot(f"f{k}")
            for i in range(2):
                load(2 + i, source.at[i], x.at[pl.ds(i * block, block)]).wait()
            for i in range(2):

                def first_norm(at, i=i):
                    here = pl.ds(pl.multiple_of(i * block + at.start, 64), 64)
                    normed, inverse = norm_parts(x[here, :].astype(f32))
                    g = grad_first[here, :]
                    gain_sums[0:1, :] += jnp.sum(normed * g, axis=0, keepdims=True)
                    total = grad_mid[here, :] + norm_grad(normed, inverse, g * gain_row(0))
                    input_low[i, at, :] = total.astype(low)

                row_loop(block, 64, first_norm)

        pl.run_scoped(
            projection,
            pltpu.VMEM((rows, (HEADS + 2 * KV_HEADS) * HD), low),
            pltpu.VMEM((2, rows, PER_HEAD), low),
            pltpu.VMEM((rows, width), low),
            pltpu.VMEM((rows, width), low),
            pltpu.VMEM((rows, width), f32),
        )

    pl.run_scoped(
        sequence_part,
        pltpu.VMEM((rows, HALF_HEADS * PER_HEAD), low),
        pltpu.VMEM((rows, HALF_HEADS * PER_HEAD), low),
    )

    small_mid[0] = jnp.zeros(small_mid.shape[1:], f32)
    for row in range(2):
        for i in range(width // HD):
            small_mid[0, row * 8 + i : row * 8 + i + 1, :] = gain_sums[row : row + 1, i * HD : (i + 1) * HD]
    small_mid[0, 16:24, :] = sums[...]
    at_slot("n1")
    small_got[0] = small.total()
    small_out[0:2, :] = small_got[0, pl.ds(2 * z, 2), :]
    small_out[2:4, :] = small_got[0, pl.ds(8 + 2 * z, 2), :]
    small_out[4:8, :] = small_got[0, 16:20, :]
    comm.finish()
    route.wait(block_back)
    route.wait(input_back)


BACK_PLAN = {
    "h1": (("launch", 0),),
    "h2": (("launch", 1),),
    "h3": (("launch", 2), ("s1", 1),),
    "g4": (("launch", 3),),
    "g5": (("launch", 4), ("s2", 1), ("s1", 2),),
    "g6": (("launch", 5), ("s1", 0),),
    "a7": (("launch", 6), ("s1", 4),),
    "o8": (("s1", 3), ("s2", 2),),
    "o9": (("s2", 0),),
    "o10": (("s3", 0), ("s1", 5), ("launch", 9),),
    "o11": (("s1", 6), ("s2", 3), ("s2", 4),),
    "t03": (("s3", 2), ("launch", 10),),
    "t11": (("launch", 8), ("s3", 1),),
    "t12": (("launch", 7), ("launch", 11),),
    "t22": (("s1", 10), ("s1", 9),),
    "t31": (("s1", 8),),
    "sw": (("s3", 3),),
    "b0": (("s4", 0),),
    "b1": (("s1", 11), ("s1", 7),),
    "q12": (("s3", 4), ("s5", 0),),
    "q13": (("launch", 12), ("s2", 5),),
    "q14": (("launch", 13), ("s3", 5), ("s2", 7),),
    "q15": (("s2", 6), ("s3", 6), ("s2", 8), ("s1", 12), ("s2", 9), ("s1", 13), ("launch", 14), ("s3", 9), ("s2", 11),),
    "q16": (("s3", 8), ("launch", 15),),
    "f0": (("s2", 13), ("s2", 10), ("s6", 0), ("s2", 12),),
    "f2": (("s3", 12), ("s3", 7), ("s1", 14), ("s3", 10), ("s4", 1),),
    "f3": (("s1", 15), ("s3", 13),),
    "n1": (("s2", 14), ("small", 0), ("s3", 14), ("small", 1), ("s3", 11), ("inback", 0), ("s5", 1), ("s2", 15), ("s3", 15), ("small", 2), ("s4", 3), ("small", 3), ("s4", 2), ("small", 4), ("s5", 3), ("s6", 1), ("small", 5), ("small", 6), ("s5", 2), ("s6", 3), ("small", 7), ("s6", 2),),
}


def run_backward(scalars, gains_all, head_gains, cosines, sines, saved, block_rows, fulls):
    low, f32 = jnp.bfloat16, jnp.float32
    source = saved[0]
    _, slot_len, width = source.shape
    rows = 2 * slot_len
    full_qkv, full_out, full_gate_up, full_down = fulls
    order = (full_down, full_gate_up, full_out, full_qkv)
    shapes = [(8 * f.shape[2], f.shape[3]) for f in order]
    shape = jax.ShapeDtypeStruct
    hbm = pl.BlockSpec(memory_space=HBM)
    vmem = pl.BlockSpec(memory_space=pltpu.VMEM)
    dma = pltpu.SemaphoreType.DMA
    count = len(shapes)

    def buffers(make, which):
        return [pltpu.VMEM(make(r // 4, n // 2), low) for r, n in which]

    out = pl.pallas_call(
        functools.partial(backward_kernel, shapes),
        out_shape=[
            shape((8, HD), f32),
            shape(source.shape, low),
            shape(source.shape, low),
            *[shape((2, 2, r // 4, n), low) for r, n in shapes],
        ],
        in_specs=[pl.BlockSpec(memory_space=pltpu.SMEM)] + [vmem] * 4 + [hbm] * 15,
        out_specs=[vmem] + [hbm] * 6,
        scratch_shapes=buffers(lambda r, n: (2, 2, r, n), shapes)
        + buffers(lambda r, n: (NZ, 2, 2, r, n), shapes)
        + buffers(lambda r, n: (5, r, n), shapes)
        + buffers(lambda r, n: (NZ, 2, r, n // 2), shapes[:2])
        + buffers(lambda r, n: (NZ, 2, r, n // 2), shapes[:2])
        + buffers(lambda r, n: (NZ, r, n // 2), shapes[:2])
        + buffers(lambda r, n: (NZ, r, n // 2), shapes[:2])
        + [
            pltpu.VMEM((2, max(r for r, _ in shapes), rows), low),
            pltpu.VMEM((2, 8, full_gate_up.shape[2], 2 * width), low),
            pltpu.VMEM((rows, width), f32),
            pltpu.VMEM((4, slot_len, HEADS * HD // 2), low),
            pltpu.VMEM((2, slot_len, HEADS * HD // 2), low),
            pltpu.VMEM((rows, HALF_HEADS * PER_HEAD), low),
            pltpu.VMEM((4, 24, HD), f32),
            pltpu.VMEM((3, 24, HD), f32),
            pltpu.VMEM((NZ, 24, HD), f32),
            pltpu.VMEM((8, width), f32),
            pltpu.VMEM((8, HD), f32),
            pltpu.VMEM((2, slot_len, width), low),
            dma((count,)),
            dma((count, 4)),
            dma((count, 4)),
            dma((count, 4, 4)),
            dma((count, 4, 4)),
            dma((count, 4)),
            dma((count, 5)),
            dma((count, len(SPREAD))),
            dma((count, len(SPREAD))),
            dma((6,)),
            dma((6,)),
            dma((4,)),
            dma((2,)),
            dma((2,)),
            dma((2, 2)),
            dma((BLOCKS,)),
            dma((2,)),
            dma((2,)),
            dma((4,)),
            dma((5,)),
            dma((5,)),
        ],
        compiler_params=pltpu.CompilerParams(collective_id=1, has_side_effects=True, vmem_limit_bytes=VMEM_LIMIT),
        name="backward",
    )(scalars, gains_all, head_gains, cosines, sines, *saved, block_rows, *fulls)
    return out[0], out[1], out[2], [o.reshape(r, n) for o, (r, n) in zip(out[3:], shapes)]


def swap(v):
    return lax.ppermute(v, "core", [(0, 1), (1, 0)])


def per_chip(
    tokens,
    cotangent,
    slot_order,
    attn_gain,
    q_gain,
    k_gain,
    w_qkv,
    w_out,
    mlp_gain,
    w_gate_up,
    w_down,
):
    z, core = lax.axis_index("z"), lax.axis_index("core")
    _, slot_len, width = tokens.shape
    f32, low = jnp.float32, jnp.bfloat16
    odd = z % 2
    orders = jnp.where(z // 2 == core, slot_order, swap(slot_order))
    order = lax.dynamic_index_in_dim(orders, odd, 0, False)
    slots = jnp.stack([2 * core + odd, 2 * core + 1 - odd, 2 - 2 * core + odd, 3 - 2 * core - odd])
    blocks = order[slots]
    where_is = jnp.sum(
        jnp.where(blocks[None, :] == jnp.arange(4)[:, None], jnp.arange(4)[None, :], 0), axis=1
    )
    scalars = jnp.concatenate([where_is, blocks, core[None], jnp.zeros((7,), jnp.int32)]).astype(jnp.int32)
    positions = (blocks[:2, None] * slot_len + jnp.arange(slot_len)[None, :]).reshape(-1)
    cos, sin = rope_tables(positions)
    cosines = jnp.concatenate([cos, cos], axis=1)
    sines = jnp.concatenate([-sin, sin], axis=1)
    gain_q, gain_k = q_gain.astype(f32)[None, :], k_gain.astype(f32)[None, :]
    head_gains = jnp.concatenate([gain_q, gain_k, jnp.zeros((6, HD), f32)], axis=0)
    gains = jnp.concatenate(
        [attn_gain.astype(f32)[None], mlp_gain.astype(f32)[None], jnp.zeros((6, attn_gain.shape[0]), f32)], axis=0
    )
    (block_rows, gains_all, *saved), fulls = run_forward(
        scalars, gains, head_gains, cosines, sines, tokens, cotangent, [w_qkv, w_out, w_gate_up, w_down]
    )
    sums, input_grad, block_out, (down_sum, gate_up_sum, out_sum, qkv_sum) = run_backward(
        scalars, gains_all, head_gains, cosines, sines, saved, block_rows.reshape(2, slot_len, width), fulls
    )
    return (
        block_out,
        input_grad,
        sums[:2].reshape(-1),
        sums[4],
        sums[5],
        qkv_sum.astype(f32),
        out_sum.astype(f32),
        sums[2:4].reshape(-1),
        gate_up_sum.astype(f32),
        down_sum.astype(f32),
    )


def solution(mesh):
    group, replica, body = "group", "replica", per_device
    if (mesh.shape["group"], mesh.shape["replica"]) == (NZ, 8):
        mesh = Mesh(mesh.devices.reshape(NZ, 2, 2, 2), ("z", "y", "x", "core"))
        group, replica, body = "z", ("y", "x", "core"), per_chip
    in_specs = (
        P(replica, group, None),
        P(replica, group, None),
        P(replica, None),
        P(group),
        P(),
        P(),
        P(group, None),
        P(group, None),
        P(group),
        P(group, None),
        P(group, None),
    )
    out_specs = (
        P(replica, group, None),
        P(replica, group, None),
        P(group),
        P(),
        P(),
        P(group, None),
        P(group, None),
        P(group),
        P(group, None),
        P(group, None),
    )
    return jax.shard_map(
        body, mesh=mesh, in_specs=in_specs, out_specs=out_specs, check_vma=False
    )
```
